256 devices in a mesh: sec: 32 (over x, z), op: 8 (over y, core).
Axes of the slice: x: 4, y: 4, z: 8, core: 2. Of those that a mesh axis runs over, the one named last changes fastest.
Arguments:
- state_start: bfloat16 [64, 256, 256], P('sec'), may hold values from -60 to 60
- left_ops: bfloat16 [64, 64, 256, 256], P('op', 'sec'), may hold values from -0.375 to 0.375
- right_ops: bfloat16 [64, 64, 256, 256], P('op', 'sec'), may hold values from -0.046875 to 0.046875
- shift: float32 [64], P('sec'), may hold values from 0.2 to 2.2
- partner: int32 [64, 64], P('op', 'sec'), may hold values from 0 to 5
- kept: int32 [64], P('sec'), may hold values from 128 to 256
Outputs:
- state_final: bfloat16 [64, 256, 256], P('sec')
- new_ops: bfloat16 [64, 64, 256, 256], P('op', 'sec')
The draws below stay inside these ranges and needn't reach their ends.
Inputs may be any that keep to these rules, and one draw needn't show every extreme that they name: `partner`: position in the window of 6 sector blocks.
All inputs are finite; a program needn't handle non-finite values.
Results may differ from the reference program's by a relative error of at most 0.015.
Values may be sent and summed in bfloat16 or wider, within the bound.
A program may use at most 64 MiB of HBM per device.

```python
import jax
import jax.numpy as jnp
from jax import lax

M = 256
SEC_DEV = 2
ITERS = 4
SECTORS = 64
TERMS = 64


def draw_state_start(key, part):
    position = jnp.arange(SECTORS, dtype=jnp.float32) / float(SECTORS - 1)
    scale = 1.0 + 3.0 * position
    values = jnp.clip(jax.random.normal(key, (SECTORS, M, M), jnp.float32), -6.0, 6.0)
    return (values * scale[:, None, None]).astype(jnp.bfloat16)


def draw_shift(key, part):
    position = jnp.arange(SECTORS, dtype=jnp.float32) / float(SECTORS - 1)
    base = 0.3 * jnp.exp(position * jnp.log(5.0))
    factor = jnp.exp(jax.random.uniform(key, (SECTORS,), jnp.float32, -0.22, 0.22))
    return (base * factor).astype(jnp.float32)


def plant(drawn, rng, low, high):
    longest = drawn.shape.index(max(drawn.shape))
    spots = []
    for shift in (0, 1):
        where = [jax.random.randint(jax.random.fold_in(rng, axis), (), 0, length) for axis, length in enumerate(drawn.shape)]
        where[longest] = (where[longest] + shift) % drawn.shape[longest]
        spots.append(tuple(where))
    return drawn.at[spots[0]].set(low).at[spots[1]].set(high)


def steps_of(own_key, extent, cuts, least, top_value):
    factor_of = 1.0
    for dim, parts in cuts:
        steps = jax.random.uniform(jax.random.fold_in(jax.random.fold_in(own_key, 6), dim), (parts,), jnp.float32, least / len(cuts), top_value / len(cuts))
        factor_of = factor_of * jnp.repeat(jnp.exp(steps), extent[dim] // parts).reshape((-1,) + (1,) * (len(extent) - 1 - dim))
    return factor_of


def normal_values(own_key, extent, spread, bound, pieces=(), kind=jnp.bfloat16):
    gain = steps_of(own_key, extent, pieces, -0.22, 0.18) if pieces else 1.0
    values = jax.random.normal(own_key, extent, jnp.float32) * spread * gain
    return jnp.minimum(jnp.maximum(values, -bound), bound).astype(kind)


def setup_inputs(seed: int = 0) -> dict:
    seeds = jax.random.split(jax.random.key(seed), 7)
    return {
        "state_start": draw_state_start(jax.random.fold_in(seeds[6], 71), 0),
        "left_ops": normal_values(seeds[1], (TERMS, SECTORS, M, M), M ** -0.5, 0.375, ((0, 8), (1, 32))),
        "right_ops": normal_values(seeds[2], (TERMS, SECTORS, M, M), (M * TERMS) ** -0.5, 0.046875, ((0, 8), (1, 32))),
        "shift": draw_shift(jax.random.fold_in(seeds[6], 71), 0),
        "partner": plant(jax.random.randint(seeds[4], (TERMS, SECTORS), 0, 3 * SEC_DEV), jax.random.fold_in(seeds[4], 1), 0, (3 * SEC_DEV) - 1).astype(jnp.int32),
        "kept": plant(jax.random.randint(seeds[5], (SECTORS,), M // 2, M + 1), jax.random.fold_in(seeds[5], 1), M // 2, M).astype(jnp.int32),
    }


step_size = 0.5

def reference(state_start, left_ops, right_ops, shift, partner, kept):
    sector_ids = jnp.arange(SECTORS, dtype=jnp.int32)
    window_base = (sector_ids // SEC_DEV - 1) * SEC_DEV
    source = ((window_base[None, :] + partner) % SECTORS).astype(jnp.int32)
    count = float(SECTORS * M * M)

    def sigma_of(state):
        state_wide = state.astype(jnp.float32)

        def add_term(total, inputs):
            left_one, right_one, index_one = inputs
            sources = state_wide[index_one]
            halfway = jnp.einsum('bij,bjk->bik', left_one.astype(jnp.float32), sources).astype(jnp.bfloat16)
            return (total + jnp.einsum('bij,bjk->bik', halfway.astype(jnp.float32), right_one.astype(jnp.float32)), None)
        total, _ = lax.scan(add_term, jnp.zeros((SECTORS, M, M), jnp.float32), (left_ops, right_ops, source))
        return total + shift[:, None, None] * state_wide
    state = state_start
    for iteration in range(ITERS):
        sigma = sigma_of(state)
        state_wide = state.astype(jnp.float32)
        energy_sum = jnp.sum(state_wide * sigma)
        norm_sum = jnp.sum(state_wide * state_wide)
        updated = state_wide - step_size * (sigma - energy_sum / norm_sum * state_wide)
        new_norm = jnp.sum(updated * updated)
        state = (updated * jnp.sqrt(count / new_norm)).astype(jnp.bfloat16)
    columns = jnp.arange(M, dtype=jnp.int32)
    keep_mask = (columns[None, :] < kept[:, None]).astype(jnp.bfloat16)
    kept_block = state * keep_mask[:, None, :]
    kept_wide = kept_block.astype(jnp.float32)
    out_scale = 1.0 / float(M) ** 0.5

    def renorm(carry, left_one):
        projected = jnp.einsum('bij,bjk->bik', left_one.astype(jnp.float32), kept_wide).astype(jnp.bfloat16)
        result = (jnp.einsum('bji,bjk->bik', kept_wide, projected.astype(jnp.float32)) * out_scale).astype(jnp.bfloat16)
        return (carry, result)
    _, renormed = lax.scan(renorm, jnp.float32(0.0), left_ops)
    new_ops = jnp.roll(renormed, SEC_DEV, axis=1)
    return (state, new_ops)
```

```python
import jax
import jax.numpy as jnp
from jax import lax
from jax.sharding import PartitionSpec as P

ITERS = 4


step_size = 0.5


def padded(cells, sides, width):
    for axis, dim in sides:
        count = lax.axis_size(axis)
        head = lax.slice_in_dim(cells, 0, width, axis=dim)
        tail = lax.slice_in_dim(cells, cells.shape[dim] - width, cells.shape[dim], axis=dim)
        cells = jnp.concatenate(
            [
                lax.ppermute(tail, axis, [(i, (i + 1) % count) for i in range(count)]),
                cells,
                lax.ppermute(head, axis, [((i + 1) % count, i) for i in range(count)]),
            ],
            axis=dim,
        )
    return cells


def shifted(block, axis, distance):
    devices = range(lax.axis_size(axis))
    route = [((i - distance) % len(devices), i) for i in devices]
    return lax.ppermute(block, axis, route)


def per_device(state_start, left_ops, right_ops, shift, partner, kept):
    sector_local = state_start.shape[0]
    width = state_start.shape[1]
    count = float(sector_local * lax.axis_size("sec") * width * width)
    shift_col = shift[:, None, None]
    first_op = lax.axis_index("op") == 0
    state = state_start
    for iteration in range(ITERS):
        window = padded(state, (("sec", 0),), sector_local)
        sources = window[partner]
        halfway = jnp.einsum(
            "tbij,tbjk->tbik", left_ops, sources, preferred_element_type=jnp.float32
        ).astype(jnp.bfloat16)
        partial_sigma = jnp.einsum(
            "tbij,tbjk->bik", halfway, right_ops, preferred_element_type=jnp.float32
        )
        state_wide = state.astype(jnp.float32)
        own_square = jnp.sum(state_wide * state_wide, axis=(1, 2))
        energy_part = jnp.sum(state_wide * partial_sigma) + jnp.where(
            first_op, jnp.sum(shift * own_square), 0.0
        )
        norm_part = jnp.where(first_op, jnp.sum(own_square), 0.0)
        energy_sum, norm_sum = lax.psum((energy_part, norm_part), ("sec", "op"))
        sigma = lax.psum(partial_sigma, "op") + shift_col * state_wide
        ratio = energy_sum / norm_sum
        updated = state_wide - step_size * (sigma - ratio * state_wide)
        if iteration < ITERS - 1:
            factor = jnp.sqrt(count / norm_sum)
        else:
            new_norm = lax.psum(
                jnp.where(first_op, jnp.sum(updated * updated), 0.0), ("sec", "op")
            )
            factor = jnp.sqrt(count / new_norm)
        state = (updated * factor).astype(jnp.bfloat16)
    columns = jnp.arange(width, dtype=jnp.int32)
    keep_mask = (columns[None, :] < kept[:, None]).astype(jnp.bfloat16)
    kept_block = state * keep_mask[:, None, :]
    out_scale = 1.0 / float(width) ** 0.5
    projected = jnp.einsum(
        "tbij,bjk->tbik", left_ops, kept_block, preferred_element_type=jnp.float32
    ).astype(jnp.bfloat16)
    renormed = (
        jnp.einsum("bji,tbjk->tbik", kept_block, projected, preferred_element_type=jnp.float32)
        * out_scale
    ).astype(jnp.bfloat16)
    new_ops = shifted(renormed, "sec", 1)
    return (state, new_ops)


def solution(mesh):
    in_specs = (
        P("sec", None, None),
        P("op", "sec", None, None),
        P("op", "sec", None, None),
        P("sec"),
        P("op", "sec"),
        P("sec"),
    )
    out_specs = (P("sec", None, None), P("op", "sec", None, None))
    return jax.shard_map(
        per_device, mesh=mesh, in_specs=in_specs, out_specs=out_specs, check_vma=False
    )
```

```python
import functools

import jax
import jax.numpy as jnp
from jax import lax
from jax.experimental import pallas as pl
from jax.experimental.pallas import tpu as pltpu
from jax.sharding import PartitionSpec as P

MESH = pl.DeviceIdType.MESH

ITERS = 4


step_size = 0.5


def padded(cells, sides, width):
    for axis, dim in sides:
        count = lax.axis_size(axis)
        head = lax.slice_in_dim(cells, 0, width, axis=dim)
        tail = lax.slice_in_dim(cells, cells.shape[dim] - width, cells.shape[dim], axis=dim)
        cells = jnp.concatenate(
            [
                lax.ppermute(tail, axis, [(i, (i + 1) % count) for i in range(count)]),
                cells,
                lax.ppermute(head, axis, [((i + 1) % count, i) for i in range(count)]),
            ],
            axis=dim,
        )
    return cells


def all_sum_kernel(n_sec, n_op, x_ref, o_ref, op_buf, sec_buf, mid, out_buf,
                   send_a, recv_a, send_b, recv_b, local_sem):
    me_sec = lax.axis_index("sec")
    me_op = lax.axis_index("op")
    barrier = pltpu.get_barrier_semaphore()
    for d in range(1, n_op):
        pl.semaphore_signal(barrier, 1, device_id=(me_sec, (me_op + d) % n_op),
                            device_id_type=MESH)
    for d in range(1, n_sec):
        pl.semaphore_signal(barrier, 1, device_id=((me_sec + d) % n_sec, me_op),
                            device_id_type=MESH)
    pl.semaphore_wait(barrier, n_op - 1 + n_sec - 1)

    def stage(n, me, src, buf, send, recv, peer_of):
        for d in range(1, n):
            pltpu.make_async_remote_copy(
                src_ref=src, dst_ref=buf.at[me], send_sem=send.at[d],
                recv_sem=recv.at[me], device_id=peer_of((me + d) % n),
                device_id_type=MESH).start()
        buf[me] = src[...]
        for d in range(1, n):
            slot = (me + n - d) % n
            pltpu.make_async_remote_copy(
                src_ref=src, dst_ref=buf.at[slot], send_sem=send.at[d],
                recv_sem=recv.at[slot], device_id=peer_of(slot),
                device_id_type=MESH).wait_recv()
        for d in range(1, n):
            pltpu.make_async_remote_copy(
                src_ref=src, dst_ref=buf.at[me], send_sem=send.at[d],
                recv_sem=recv.at[me], device_id=peer_of((me + d) % n),
                device_id_type=MESH).wait_send()
        total = buf[0]
        for j in range(1, n):
            total = total + buf[j]
        return total

    mid[...] = stage(n_op, me_op, x_ref, op_buf, send_a, recv_a,
                     lambda j: (me_sec, j))
    local = pltpu.make_async_copy(mid, out_buf, local_sem)
    local.start()
    local.wait()
    o_ref[...] = stage(n_sec, me_sec, out_buf, sec_buf, send_b, recv_b,
                       lambda j: (j, me_op))


def all_sum(values, n_sec, n_op):
    lane = lax.broadcasted_iota(jnp.int32, (8, 128), 1)
    tile = jnp.zeros((8, 128), jnp.float32)
    for k, v in enumerate(values):
        tile = jnp.where(lane == k, v, tile)
    tile_spec = pl.BlockSpec(memory_space=pltpu.VMEM)
    out = pl.pallas_call(
        functools.partial(all_sum_kernel, n_sec, n_op),
        out_shape=jax.ShapeDtypeStruct((8, 128), jnp.float32),
        in_specs=[tile_spec],
        out_specs=tile_spec,
        scratch_shapes=[
            pltpu.VMEM((n_op, 8, 128), jnp.float32),
            pltpu.VMEM((n_sec, 8, 128), jnp.float32),
            pltpu.VMEM((8, 128), jnp.float32),
            pltpu.VMEM((8, 128), jnp.float32),
            pltpu.SemaphoreType.DMA((n_op,)),
            pltpu.SemaphoreType.DMA((n_op,)),
            pltpu.SemaphoreType.DMA((n_sec,)),
            pltpu.SemaphoreType.DMA((n_sec,)),
            pltpu.SemaphoreType.DMA(()),
        ],
        compiler_params=pltpu.CompilerParams(collective_id=0, has_side_effects=True),
    )(tile)
    return tuple(out[0, k] for k in range(len(values)))


def shifted(block, axis, distance):
    devices = range(lax.axis_size(axis))
    route = [((i - distance) % len(devices), i) for i in devices]
    return lax.ppermute(block, axis, route)


def per_device(state_start, left_ops, right_ops, shift, partner, kept):
    sector_local = state_start.shape[0]
    width = state_start.shape[1]
    count = float(sector_local * lax.axis_size("sec") * width * width)
    shift_col = shift[:, None, None]
    first_op = lax.axis_index("op") == 0
    n_sec = lax.axis_size("sec")
    n_op = lax.axis_size("op")
    state = state_start
    for iteration in range(ITERS):
        window = padded(state, (("sec", 0),), sector_local)
        sources = window[partner]
        halfway = jnp.einsum(
            "tbij,tbjk->tbik", left_ops, sources, preferred_element_type=jnp.float32
        ).astype(jnp.bfloat16)
        partial_sigma = jnp.einsum(
            "tbij,tbjk->bik", halfway, right_ops, preferred_element_type=jnp.float32
        )
        state_wide = state.astype(jnp.float32)
        own_square = jnp.sum(state_wide * state_wide, axis=(1, 2))
        energy_part = jnp.sum(state_wide * partial_sigma) + jnp.where(
            first_op, jnp.sum(shift * own_square), 0.0
        )
        norm_part = jnp.where(first_op, jnp.sum(own_square), 0.0)
        energy_sum, norm_sum = all_sum((energy_part, norm_part), n_sec, n_op)
        sigma = lax.psum(partial_sigma, "op") + shift_col * state_wide
        ratio = energy_sum / norm_sum
        updated = state_wide - step_size * (sigma - ratio * state_wide)
        if iteration < ITERS - 1:
            factor = jnp.sqrt(count / norm_sum)
        else:
            (new_norm,) = all_sum(
                (jnp.where(first_op, jnp.sum(updated * updated), 0.0),), n_sec, n_op
            )
            factor = jnp.sqrt(count / new_norm)
        state = (updated * factor).astype(jnp.bfloat16)
    columns = jnp.arange(width, dtype=jnp.int32)
    keep_mask = (columns[None, :] < kept[:, None]).astype(jnp.bfloat16)
    kept_block = state * keep_mask[:, None, :]
    out_scale = 1.0 / float(width) ** 0.5
    projected = jnp.einsum(
        "tbij,bjk->tbik", left_ops, kept_block, preferred_element_type=jnp.float32
    ).astype(jnp.bfloat16)
    renormed = (
        jnp.einsum("bji,tbjk->tbik", kept_block, projected, preferred_element_type=jnp.float32)
        * out_scale
    ).astype(jnp.bfloat16)
    new_ops = shifted(renormed, "sec", 1)
    return (state, new_ops)


def solution(mesh):
    in_specs = (
        P("sec", None, None),
        P("op", "sec", None, None),
        P("op", "sec", None, None),
        P("sec"),
        P("op", "sec"),
        P("sec"),
    )
    out_specs = (P("sec", None, None), P("op", "sec", None, None))
    return jax.shard_map(
        per_device, mesh=mesh, in_specs=in_specs, out_specs=out_specs, check_vma=False
    )
```

```python
import functools

import jax
import jax.numpy as jnp
from jax import lax
from jax.experimental import pallas as pl
from jax.experimental.pallas import tpu as pltpu
from jax.sharding import PartitionSpec as P

MESH = pl.DeviceIdType.MESH

ITERS = 4


step_size = 0.5


def padded(cells, sides, width):
    for axis, dim in sides:
        count = lax.axis_size(axis)
        head = lax.slice_in_dim(cells, 0, width, axis=dim)
        tail = lax.slice_in_dim(cells, cells.shape[dim] - width, cells.shape[dim], axis=dim)
        cells = jnp.concatenate(
            [
                lax.ppermute(tail, axis, [(i, (i + 1) % count) for i in range(count)]),
                cells,
                lax.ppermute(head, axis, [((i + 1) % count, i) for i in range(count)]),
            ],
            axis=dim,
        )
    return cells


def all_sum_kernel(n_sec, n_op, x_ref, o_ref, op_buf, sec_buf, mid, out_buf,
                   send_a, recv_a, send_b, recv_b, local_sem):
    me_sec = lax.axis_index("sec")
    me_op = lax.axis_index("op")
    barrier = pltpu.get_barrier_semaphore()
    for d in range(1, n_op):
        pl.semaphore_signal(barrier, 1, device_id=(me_sec, (me_op + d) % n_op),
                            device_id_type=MESH)
    for d in range(1, n_sec):
        pl.semaphore_signal(barrier, 1, device_id=((me_sec + d) % n_sec, me_op),
                            device_id_type=MESH)
    pl.semaphore_wait(barrier, n_op - 1 + n_sec - 1)

    def stage(n, me, src, buf, send, recv, peer_of):
        for d in range(1, n):
            pltpu.make_async_remote_copy(
                src_ref=src, dst_ref=buf.at[me], send_sem=send.at[d],
                recv_sem=recv.at[me], device_id=peer_of((me + d) % n),
                device_id_type=MESH).start()
        buf[me] = src[...]
        for d in range(1, n):
            slot = (me + n - d) % n
            pltpu.make_async_remote_copy(
                src_ref=src, dst_ref=buf.at[slot], send_sem=send.at[d],
                recv_sem=recv.at[slot], device_id=peer_of(slot),
                device_id_type=MESH).wait_recv()
        for d in range(1, n):
            pltpu.make_async_remote_copy(
                src_ref=src, dst_ref=buf.at[me], send_sem=send.at[d],
                recv_sem=recv.at[me], device_id=peer_of((me + d) % n),
                device_id_type=MESH).wait_send()
        total = buf[0]
        for j in range(1, n):
            total = total + buf[j]
        return total

    mid[...] = stage(n_op, me_op, x_ref, op_buf, send_a, recv_a,
                     lambda j: (me_sec, j))
    local = pltpu.make_async_copy(mid, out_buf, local_sem)
    local.start()
    local.wait()
    o_ref[...] = stage(n_sec, me_sec, out_buf, sec_buf, send_b, recv_b,
                       lambda j: (j, me_op))


def all_sum(values, n_sec, n_op):
    lane = lax.broadcasted_iota(jnp.int32, (8, 128), 1)
    tile = jnp.zeros((8, 128), jnp.float32)
    for k, v in enumerate(values):
        tile = jnp.where(lane == k, v, tile)
    tile_spec = pl.BlockSpec(memory_space=pltpu.VMEM)
    out = pl.pallas_call(
        functools.partial(all_sum_kernel, n_sec, n_op),
        out_shape=jax.ShapeDtypeStruct((8, 128), jnp.float32),
        in_specs=[tile_spec],
        out_specs=tile_spec,
        scratch_shapes=[
            pltpu.VMEM((n_op, 8, 128), jnp.float32),
            pltpu.VMEM((n_sec, 8, 128), jnp.float32),
            pltpu.VMEM((8, 128), jnp.float32),
            pltpu.VMEM((8, 128), jnp.float32),
            pltpu.SemaphoreType.DMA((n_op,)),
            pltpu.SemaphoreType.DMA((n_op,)),
            pltpu.SemaphoreType.DMA((n_sec,)),
            pltpu.SemaphoreType.DMA((n_sec,)),
            pltpu.SemaphoreType.DMA(()),
        ],
        compiler_params=pltpu.CompilerParams(collective_id=0, has_side_effects=True),
    )(tile)
    return tuple(out[0, k] for k in range(len(values)))


def sigma_sum_kernel(n_sec, n_op, x_ref, t_ref, o_ref, s_ref,
                     rs_buf, red, red_out, ag_buf, op_buf, sec_buf, mid, mid_out,
                     send_rs, recv_rs, send_ag, recv_ag, send_a, recv_a,
                     send_b, recv_b, local_sem):
    me_sec = lax.axis_index("sec")
    me_op = lax.axis_index("op")
    barrier = pltpu.get_barrier_semaphore()
    for d in range(1, n_op):
        pl.semaphore_signal(barrier, 1, device_id=(me_sec, (me_op + d) % n_op),
                            device_id_type=MESH)
    for d in range(1, n_sec):
        pl.semaphore_signal(barrier, 1, device_id=((me_sec + d) % n_sec, me_op),
                            device_id_type=MESH)
    pl.semaphore_wait(barrier, n_op - 1 + n_sec - 1)

    def op_peer(j):
        return (me_sec, j)

    def sec_peer(j):
        return (j, me_op)

    def rs_copy(d):
        j = (me_op + d) % n_op
        return pltpu.make_async_remote_copy(
            src_ref=x_ref.at[j], dst_ref=rs_buf.at[me_op], send_sem=send_rs.at[d],
            recv_sem=recv_rs.at[me_op], device_id=op_peer(j), device_id_type=MESH)

    def rs_recv(d):
        slot = (me_op + n_op - d) % n_op
        return pltpu.make_async_remote_copy(
            src_ref=x_ref.at[me_op], dst_ref=rs_buf.at[slot], send_sem=send_rs.at[d],
            recv_sem=recv_rs.at[slot], device_id=op_peer(slot), device_id_type=MESH)

    def gather_copy(n, me, src, buf, send, recv, peer_of, d):
        return pltpu.make_async_remote_copy(
            src_ref=src, dst_ref=buf.at[me], send_sem=send.at[d],
            recv_sem=recv.at[me], device_id=peer_of((me + d) % n), device_id_type=MESH)

    def gather_recv(n, me, src, buf, send, recv, peer_of, d):
        slot = (me + n - d) % n
        return pltpu.make_async_remote_copy(
            src_ref=src, dst_ref=buf.at[slot], send_sem=send.at[d],
            recv_sem=recv.at[slot], device_id=peer_of(slot), device_id_type=MESH)

    def ordered_sum(buf, n):
        total = buf[0]
        for j in range(1, n):
            total = total + buf[j]
        return total

    for d in range(1, n_op):
        rs_copy(d).start()
    a_args = (n_op, me_op, t_ref, op_buf, send_a, recv_a, op_peer)
    for d in range(1, n_op):
        gather_copy(*a_args, d).start()
    rs_buf[me_op] = x_ref[me_op]
    op_buf[me_op] = t_ref[...]

    for d in range(1, n_op):
        gather_recv(*a_args, d).wait_recv()
    mid[...] = ordered_sum(op_buf, n_op)
    local = pltpu.make_async_copy(mid, mid_out, local_sem.at[0])
    local.start()
    local.wait()
    b_args = (n_sec, me_sec, mid_out, sec_buf, send_b, recv_b, sec_peer)
    for d in range(1, n_sec):
        gather_copy(*b_args, d).start()
    sec_buf[me_sec] = mid_out[...]

    for d in range(1, n_op):
        rs_recv(d).wait_recv()
    red[...] = ordered_sum(rs_buf, n_op)
    local = pltpu.make_async_copy(red, red_out, local_sem.at[1])
    local.start()
    local.wait()
    g_args = (n_op, me_op, red_out, ag_buf, send_ag, recv_ag, op_peer)
    for d in range(1, n_op):
        gather_copy(*g_args, d).start()
    ag_buf[me_op] = red_out[...]

    for d in range(1, n_sec):
        gather_recv(*b_args, d).wait_recv()
    s_ref[...] = ordered_sum(sec_buf, n_sec)
    for d in range(1, n_op):
        gather_recv(*g_args, d).wait_recv()
    o_ref[...] = ag_buf[...]

    for d in range(1, n_op):
        rs_copy(d).wait_send()
        gather_copy(*a_args, d).wait_send()
        gather_copy(*g_args, d).wait_send()
    for d in range(1, n_sec):
        gather_copy(*b_args, d).wait_send()


def sigma_sum(partial, values, n_sec, n_op):
    shape = partial.shape
    rows = shape[0] * shape[1] // n_op
    chunks = partial.reshape(n_op, rows, shape[2])
    lane = lax.broadcasted_iota(jnp.int32, (8, 128), 1)
    tile = jnp.zeros((8, 128), jnp.float32)
    for k, v in enumerate(values):
        tile = jnp.where(lane == k, v, tile)
    vmem = pl.BlockSpec(memory_space=pltpu.VMEM)
    total, sums = pl.pallas_call(
        functools.partial(sigma_sum_kernel, n_sec, n_op),
        out_shape=(
            jax.ShapeDtypeStruct(chunks.shape, jnp.float32),
            jax.ShapeDtypeStruct((8, 128), jnp.float32),
        ),
        in_specs=[vmem, vmem],
        out_specs=(vmem, vmem),
        scratch_shapes=[
            pltpu.VMEM(chunks.shape, jnp.float32),
            pltpu.VMEM((rows, shape[2]), jnp.float32),
            pltpu.VMEM((rows, shape[2]), jnp.float32),
            pltpu.VMEM(chunks.shape, jnp.float32),
            pltpu.VMEM((n_op, 8, 128), jnp.float32),
            pltpu.VMEM((n_sec, 8, 128), jnp.float32),
            pltpu.VMEM((8, 128), jnp.float32),
            pltpu.VMEM((8, 128), jnp.float32),
            pltpu.SemaphoreType.DMA((n_op,)),
            pltpu.SemaphoreType.DMA((n_op,)),
            pltpu.SemaphoreType.DMA((n_op,)),
            pltpu.SemaphoreType.DMA((n_op,)),
            pltpu.SemaphoreType.DMA((n_op,)),
            pltpu.SemaphoreType.DMA((n_op,)),
            pltpu.SemaphoreType.DMA((n_sec,)),
            pltpu.SemaphoreType.DMA((n_sec,)),
            pltpu.SemaphoreType.DMA((2,)),
        ],
        compiler_params=pltpu.CompilerParams(collective_id=1, has_side_effects=True),
    )(chunks, tile)
    return total.reshape(shape), tuple(sums[0, k] for k in range(len(values)))


def shifted(block, axis, distance):
    devices = range(lax.axis_size(axis))
    route = [((i - distance) % len(devices), i) for i in devices]
    return lax.ppermute(block, axis, route)


def per_device(state_start, left_ops, right_ops, shift, partner, kept):
    sector_local = state_start.shape[0]
    width = state_start.shape[1]
    count = float(sector_local * lax.axis_size("sec") * width * width)
    shift_col = shift[:, None, None]
    first_op = lax.axis_index("op") == 0
    n_sec = lax.axis_size("sec")
    n_op = lax.axis_size("op")
    state = state_start
    for iteration in range(ITERS):
        window = padded(state, (("sec", 0),), sector_local)
        sources = window[partner]
        halfway = jnp.einsum(
            "tbij,tbjk->tbik", left_ops, sources, preferred_element_type=jnp.float32
        ).astype(jnp.bfloat16)
        partial_sigma = jnp.einsum(
            "tbij,tbjk->bik", halfway, right_ops, preferred_element_type=jnp.float32
        )
        state_wide = state.astype(jnp.float32)
        own_square = jnp.sum(state_wide * state_wide, axis=(1, 2))
        energy_part = jnp.sum(state_wide * partial_sigma) + jnp.where(
            first_op, jnp.sum(shift * own_square), 0.0
        )
        norm_part = jnp.where(first_op, jnp.sum(own_square), 0.0)
        sigma_terms, (energy_sum, norm_sum) = sigma_sum(
            partial_sigma, (energy_part, norm_part), n_sec, n_op
        )
        sigma = sigma_terms + shift_col * state_wide
        ratio = energy_sum / norm_sum
        updated = state_wide - step_size * (sigma - ratio * state_wide)
        if iteration < ITERS - 1:
            factor = jnp.sqrt(count / norm_sum)
        else:
            (new_norm,) = all_sum(
                (jnp.where(first_op, jnp.sum(updated * updated), 0.0),), n_sec, n_op
            )
            factor = jnp.sqrt(count / new_norm)
        state = (updated * factor).astype(jnp.bfloat16)
    columns = jnp.arange(width, dtype=jnp.int32)
    keep_mask = (columns[None, :] < kept[:, None]).astype(jnp.bfloat16)
    kept_block = state * keep_mask[:, None, :]
    out_scale = 1.0 / float(width) ** 0.5
    projected = jnp.einsum(
        "tbij,bjk->tbik", left_ops, kept_block, preferred_element_type=jnp.float32
    ).astype(jnp.bfloat16)
    renormed = (
        jnp.einsum("bji,tbjk->tbik", kept_block, projected, preferred_element_type=jnp.float32)
        * out_scale
    ).astype(jnp.bfloat16)
    new_ops = shifted(renormed, "sec", 1)
    return (state, new_ops)


def solution(mesh):
    in_specs = (
        P("sec", None, None),
        P("op", "sec", None, None),
        P("op", "sec", None, None),
        P("sec"),
        P("op", "sec"),
        P("sec"),
    )
    out_specs = (P("sec", None, None), P("op", "sec", None, None))
    return jax.shard_map(
        per_device, mesh=mesh, in_specs=in_specs, out_specs=out_specs, check_vma=False
    )
```

```python
import functools

import jax
import jax.numpy as jnp
from jax import lax
from jax.experimental import pallas as pl
from jax.experimental.pallas import tpu as pltpu
from jax.sharding import PartitionSpec as P

MESH = pl.DeviceIdType.MESH

ITERS = 4


step_size = 0.5


def padded(cells, sides, width):
    for axis, dim in sides:
        count = lax.axis_size(axis)
        head = lax.slice_in_dim(cells, 0, width, axis=dim)
        tail = lax.slice_in_dim(cells, cells.shape[dim] - width, cells.shape[dim], axis=dim)
        cells = jnp.concatenate(
            [
                lax.ppermute(tail, axis, [(i, (i + 1) % count) for i in range(count)]),
                cells,
                lax.ppermute(head, axis, [((i + 1) % count, i) for i in range(count)]),
            ],
            axis=dim,
        )
    return cells


def all_sum_kernel(n_sec, n_op, x_ref, o_ref, op_buf, sec_buf, mid, out_buf,
                   send_a, recv_a, send_b, recv_b, local_sem):
    me_sec = lax.axis_index("sec")
    me_op = lax.axis_index("op")
    barrier = pltpu.get_barrier_semaphore()
    for d in range(1, n_op):
        pl.semaphore_signal(barrier, 1, device_id=(me_sec, (me_op + d) % n_op),
                            device_id_type=MESH)
    for d in range(1, n_sec):
        pl.semaphore_signal(barrier, 1, device_id=((me_sec + d) % n_sec, me_op),
                            device_id_type=MESH)
    pl.semaphore_wait(barrier, n_op - 1 + n_sec - 1)

    def stage(n, me, src, buf, send, recv, peer_of):
        for d in range(1, n):
            pltpu.make_async_remote_copy(
                src_ref=src, dst_ref=buf.at[me], send_sem=send.at[d],
                recv_sem=recv.at[me], device_id=peer_of((me + d) % n),
                device_id_type=MESH).start()
        buf[me] = src[...]
        for d in range(1, n):
            slot = (me + n - d) % n
            pltpu.make_async_remote_copy(
                src_ref=src, dst_ref=buf.at[slot], send_sem=send.at[d],
                recv_sem=recv.at[slot], device_id=peer_of(slot),
                device_id_type=MESH).wait_recv()
        for d in range(1, n):
            pltpu.make_async_remote_copy(
                src_ref=src, dst_ref=buf.at[me], send_sem=send.at[d],
                recv_sem=recv.at[me], device_id=peer_of((me + d) % n),
                device_id_type=MESH).wait_send()
        total = buf[0]
        for j in range(1, n):
            total = total + buf[j]
        return total

    mid[...] = stage(n_op, me_op, x_ref, op_buf, send_a, recv_a,
                     lambda j: (me_sec, j))
    local = pltpu.make_async_copy(mid, out_buf, local_sem)
    local.start()
    local.wait()
    o_ref[...] = stage(n_sec, me_sec, out_buf, sec_buf, send_b, recv_b,
                       lambda j: (j, me_op))


def all_sum(values, n_sec, n_op):
    lane = lax.broadcasted_iota(jnp.int32, (8, 128), 1)
    tile = jnp.zeros((8, 128), jnp.float32)
    for k, v in enumerate(values):
        tile = jnp.where(lane == k, v, tile)
    tile_spec = pl.BlockSpec(memory_space=pltpu.VMEM)
    out = pl.pallas_call(
        functools.partial(all_sum_kernel, n_sec, n_op),
        out_shape=jax.ShapeDtypeStruct((8, 128), jnp.float32),
        in_specs=[tile_spec],
        out_specs=tile_spec,
        scratch_shapes=[
            pltpu.VMEM((n_op, 8, 128), jnp.float32),
            pltpu.VMEM((n_sec, 8, 128), jnp.float32),
            pltpu.VMEM((8, 128), jnp.float32),
            pltpu.VMEM((8, 128), jnp.float32),
            pltpu.SemaphoreType.DMA((n_op,)),
            pltpu.SemaphoreType.DMA((n_op,)),
            pltpu.SemaphoreType.DMA((n_sec,)),
            pltpu.SemaphoreType.DMA((n_sec,)),
            pltpu.SemaphoreType.DMA(()),
        ],
        compiler_params=pltpu.CompilerParams(collective_id=0, has_side_effects=True),
    )(tile)
    return tuple(out[0, k] for k in range(len(values)))


def sigma_sum_kernel(n_sec, n_op, x_ref, t_ref, o_ref, s_ref,
                     rs_buf, red, red_out, ag_buf, op_buf, sec_buf, mid, mid_out,
                     send_rs, recv_rs, send_ag, recv_ag, send_a, recv_a,
                     send_b, recv_b, local_sem):
    me_sec = lax.axis_index("sec")
    me_op = lax.axis_index("op")
    barrier = pltpu.get_barrier_semaphore()
    for d in range(1, n_op):
        pl.semaphore_signal(barrier, 1, device_id=(me_sec, (me_op + d) % n_op),
                            device_id_type=MESH)
    for d in range(1, n_sec):
        pl.semaphore_signal(barrier, 1, device_id=((me_sec + d) % n_sec, me_op),
                            device_id_type=MESH)
    pl.semaphore_wait(barrier, n_op - 1 + n_sec - 1)

    def op_peer(j):
        return (me_sec, j)

    def sec_peer(j):
        return (j, me_op)

    def rs_copy(d):
        j = (me_op + d) % n_op
        return pltpu.make_async_remote_copy(
            src_ref=x_ref.at[j], dst_ref=rs_buf.at[me_op], send_sem=send_rs.at[d],
            recv_sem=recv_rs.at[me_op], device_id=op_peer(j), device_id_type=MESH)

    def rs_recv(d):
        slot = (me_op + n_op - d) % n_op
        return pltpu.make_async_remote_copy(
            src_ref=x_ref.at[me_op], dst_ref=rs_buf.at[slot], send_sem=send_rs.at[d],
            recv_sem=recv_rs.at[slot], device_id=op_peer(slot), device_id_type=MESH)

    def gather_copy(n, me, src, buf, send, recv, peer_of, d):
        return pltpu.make_async_remote_copy(
            src_ref=src, dst_ref=buf.at[me], send_sem=send.at[d],
            recv_sem=recv.at[me], device_id=peer_of((me + d) % n), device_id_type=MESH)

    def gather_recv(n, me, src, buf, send, recv, peer_of, d):
        slot = (me + n - d) % n
        return pltpu.make_async_remote_copy(
            src_ref=src, dst_ref=buf.at[slot], send_sem=send.at[d],
            recv_sem=recv.at[slot], device_id=peer_of(slot), device_id_type=MESH)

    def ordered_sum(buf, n):
        total = buf[0]
        for j in range(1, n):
            total = total + buf[j]
        return total

    for d in range(1, n_op):
        rs_copy(d).start()
    a_args = (n_op, me_op, t_ref, op_buf, send_a, recv_a, op_peer)
    for d in range(1, n_op):
        gather_copy(*a_args, d).start()
    rs_buf[me_op] = x_ref[me_op]
    op_buf[me_op] = t_ref[...]

    for d in range(1, n_op):
        gather_recv(*a_args, d).wait_recv()
    mid[...] = ordered_sum(op_buf, n_op)
    local = pltpu.make_async_copy(mid, mid_out, local_sem.at[0])
    local.start()
    local.wait()
    b_args = (n_sec, me_sec, mid_out, sec_buf, send_b, recv_b, sec_peer)
    for d in range(1, n_sec):
        gather_copy(*b_args, d).start()
    sec_buf[me_sec] = mid_out[...]

    for d in range(1, n_op):
        rs_recv(d).wait_recv()
    red[...] = ordered_sum(rs_buf, n_op)
    local = pltpu.make_async_copy(red, red_out, local_sem.at[1])
    local.start()
    local.wait()
    g_args = (n_op, me_op, red_out, ag_buf, send_ag, recv_ag, op_peer)
    for d in range(1, n_op):
        gather_copy(*g_args, d).start()
    ag_buf[me_op] = red_out[...]

    for d in range(1, n_sec):
        gather_recv(*b_args, d).wait_recv()
    s_ref[...] = ordered_sum(sec_buf, n_sec)
    for d in range(1, n_op):
        gather_recv(*g_args, d).wait_recv()
    o_ref[...] = ag_buf[...]

    for d in range(1, n_op):
        rs_copy(d).wait_send()
        gather_copy(*a_args, d).wait_send()
        gather_copy(*g_args, d).wait_send()
    for d in range(1, n_sec):
        gather_copy(*b_args, d).wait_send()


def sigma_sum(partial, values, n_sec, n_op):
    shape = partial.shape
    rows = shape[0] * shape[1] // n_op
    chunks = partial.reshape(n_op, rows, shape[2])
    lane = lax.broadcasted_iota(jnp.int32, (8, 128), 1)
    tile = jnp.zeros((8, 128), jnp.float32)
    for k, v in enumerate(values):
        tile = jnp.where(lane == k, v, tile)
    vmem = pl.BlockSpec(memory_space=pltpu.VMEM)
    total, sums = pl.pallas_call(
        functools.partial(sigma_sum_kernel, n_sec, n_op),
        out_shape=(
            jax.ShapeDtypeStruct(chunks.shape, jnp.float32),
            jax.ShapeDtypeStruct((8, 128), jnp.float32),
        ),
        in_specs=[vmem, vmem],
        out_specs=(vmem, vmem),
        scratch_shapes=[
            pltpu.VMEM(chunks.shape, jnp.float32),
            pltpu.VMEM((rows, shape[2]), jnp.float32),
            pltpu.VMEM((rows, shape[2]), jnp.float32),
            pltpu.VMEM(chunks.shape, jnp.float32),
            pltpu.VMEM((n_op, 8, 128), jnp.float32),
            pltpu.VMEM((n_sec, 8, 128), jnp.float32),
            pltpu.VMEM((8, 128), jnp.float32),
            pltpu.VMEM((8, 128), jnp.float32),
            pltpu.SemaphoreType.DMA((n_op,)),
            pltpu.SemaphoreType.DMA((n_op,)),
            pltpu.SemaphoreType.DMA((n_op,)),
            pltpu.SemaphoreType.DMA((n_op,)),
            pltpu.SemaphoreType.DMA((n_op,)),
            pltpu.SemaphoreType.DMA((n_op,)),
            pltpu.SemaphoreType.DMA((n_sec,)),
            pltpu.SemaphoreType.DMA((n_sec,)),
            pltpu.SemaphoreType.DMA((2,)),
        ],
        compiler_params=pltpu.CompilerParams(collective_id=1, has_side_effects=True),
    )(chunks, tile)
    return total.reshape(shape), tuple(sums[0, k] for k in range(len(values)))


def shifted(block, axis, distance):
    devices = range(lax.axis_size(axis))
    route = [((i - distance) % len(devices), i) for i in devices]
    return lax.ppermute(block, axis, route)


def per_device(state_start, left_ops, right_ops, shift, partner, kept):
    sector_local = state_start.shape[0]
    width = state_start.shape[1]
    count = float(sector_local * lax.axis_size("sec") * width * width)
    shift_col = shift[:, None, None]
    first_op = lax.axis_index("op") == 0
    n_sec = lax.axis_size("sec")
    n_op = lax.axis_size("op")
    left_prev = shifted(left_ops, "sec", 1)
    kept_prev = shifted(kept, "sec", 1)
    state = state_start
    for iteration in range(ITERS):
        window = padded(state, (("sec", 0),), sector_local)
        sources = window[partner]
        halfway = jnp.einsum(
            "tbij,tbjk->tbik", left_ops, sources, preferred_element_type=jnp.float32
        ).astype(jnp.bfloat16)
        partial_sigma = jnp.einsum(
            "tbij,tbjk->bik", halfway, right_ops, preferred_element_type=jnp.float32
        )
        state_wide = state.astype(jnp.float32)
        own_square = jnp.sum(state_wide * state_wide, axis=(1, 2))
        energy_part = jnp.sum(state_wide * partial_sigma) + jnp.where(
            first_op, jnp.sum(shift * own_square), 0.0
        )
        norm_part = jnp.where(first_op, jnp.sum(own_square), 0.0)
        sigma_terms, (energy_sum, norm_sum) = sigma_sum(
            partial_sigma, (energy_part, norm_part), n_sec, n_op
        )
        sigma = sigma_terms + shift_col * state_wide
        ratio = energy_sum / norm_sum
        updated = state_wide - step_size * (sigma - ratio * state_wide)
        if iteration < ITERS - 1:
            factor = jnp.sqrt(count / norm_sum)
        else:
            (new_norm,) = all_sum(
                (jnp.where(first_op, jnp.sum(updated * updated), 0.0),), n_sec, n_op
            )
            factor = jnp.sqrt(count / new_norm)
        state = (updated * factor).astype(jnp.bfloat16)
    columns = jnp.arange(width, dtype=jnp.int32)
    keep_mask = (columns[None, :] < kept_prev[:, None]).astype(jnp.bfloat16)
    kept_block = shifted(state, "sec", 1) * keep_mask[:, None, :]
    out_scale = 1.0 / float(width) ** 0.5
    projected = jnp.einsum(
        "tbij,bjk->tbik", left_prev, kept_block, preferred_element_type=jnp.float32
    ).astype(jnp.bfloat16)
    new_ops = (
        jnp.einsum("bji,tbjk->tbik", kept_block, projected, preferred_element_type=jnp.float32)
        * out_scale
    ).astype(jnp.bfloat16)
    return (state, new_ops)


def solution(mesh):
    in_specs = (
        P("sec", None, None),
        P("op", "sec", None, None),
        P("op", "sec", None, None),
        P("sec"),
        P("op", "sec"),
        P("sec"),
    )
    out_specs = (P("sec", None, None), P("op", "sec", None, None))
    return jax.shard_map(
        per_device, mesh=mesh, in_specs=in_specs, out_specs=out_specs, check_vma=False
    )
```

```python
import functools

import jax
import jax.numpy as jnp
from jax import lax
from jax.experimental import pallas as pl
from jax.experimental.pallas import tpu as pltpu
from jax.sharding import PartitionSpec as P

MESH = pl.DeviceIdType.MESH

ITERS = 4


step_size = 0.5


def padded(cells, sides, width):
    for axis, dim in sides:
        count = lax.axis_size(axis)
        head = lax.slice_in_dim(cells, 0, width, axis=dim)
        tail = lax.slice_in_dim(cells, cells.shape[dim] - width, cells.shape[dim], axis=dim)
        cells = jnp.concatenate(
            [
                lax.ppermute(tail, axis, [(i, (i + 1) % count) for i in range(count)]),
                cells,
                lax.ppermute(head, axis, [((i + 1) % count, i) for i in range(count)]),
            ],
            axis=dim,
        )
    return cells


def all_sum_kernel(n_sec, n_op, x_ref, o_ref, op_buf, sec_buf, mid, out_buf,
                   send_a, recv_a, send_b, recv_b, local_sem):
    me_sec = lax.axis_index("sec")
    me_op = lax.axis_index("op")
    barrier = pltpu.get_barrier_semaphore()
    for d in range(1, n_op):
        pl.semaphore_signal(barrier, 1, device_id=(me_sec, (me_op + d) % n_op),
                            device_id_type=MESH)
    for d in range(1, n_sec):
        pl.semaphore_signal(barrier, 1, device_id=((me_sec + d) % n_sec, me_op),
                            device_id_type=MESH)
    pl.semaphore_wait(barrier, n_op - 1 + n_sec - 1)

    def stage(n, me, src, buf, send, recv, peer_of):
        for d in range(1, n):
            pltpu.make_async_remote_copy(
                src_ref=src, dst_ref=buf.at[me], send_sem=send.at[d],
                recv_sem=recv.at[me], device_id=peer_of((me + d) % n),
                device_id_type=MESH).start()
        buf[me] = src[...]
        for d in range(1, n):
            slot = (me + n - d) % n
            pltpu.make_async_remote_copy(
                src_ref=src, dst_ref=buf.at[slot], send_sem=send.at[d],
                recv_sem=recv.at[slot], device_id=peer_of(slot),
                device_id_type=MESH).wait_recv()
        for d in range(1, n):
            pltpu.make_async_remote_copy(
                src_ref=src, dst_ref=buf.at[me], send_sem=send.at[d],
                recv_sem=recv.at[me], device_id=peer_of((me + d) % n),
                device_id_type=MESH).wait_send()
        total = buf[0]
        for j in range(1, n):
            total = total + buf[j]
        return total

    mid[...] = stage(n_op, me_op, x_ref, op_buf, send_a, recv_a,
                     lambda j: (me_sec, j))
    local = pltpu.make_async_copy(mid, out_buf, local_sem)
    local.start()
    local.wait()
    o_ref[...] = stage(n_sec, me_sec, out_buf, sec_buf, send_b, recv_b,
                       lambda j: (j, me_op))


def all_sum(values, n_sec, n_op):
    lane = lax.broadcasted_iota(jnp.int32, (8, 128), 1)
    tile = jnp.zeros((8, 128), jnp.float32)
    for k, v in enumerate(values):
        tile = jnp.where(lane == k, v, tile)
    tile_spec = pl.BlockSpec(memory_space=pltpu.VMEM)
    out = pl.pallas_call(
        functools.partial(all_sum_kernel, n_sec, n_op),
        out_shape=jax.ShapeDtypeStruct((8, 128), jnp.float32),
        in_specs=[tile_spec],
        out_specs=tile_spec,
        scratch_shapes=[
            pltpu.VMEM((n_op, 8, 128), jnp.float32),
            pltpu.VMEM((n_sec, 8, 128), jnp.float32),
            pltpu.VMEM((8, 128), jnp.float32),
            pltpu.VMEM((8, 128), jnp.float32),
            pltpu.SemaphoreType.DMA((n_op,)),
            pltpu.SemaphoreType.DMA((n_op,)),
            pltpu.SemaphoreType.DMA((n_sec,)),
            pltpu.SemaphoreType.DMA((n_sec,)),
            pltpu.SemaphoreType.DMA(()),
        ],
        compiler_params=pltpu.CompilerParams(collective_id=0, has_side_effects=True),
    )(tile)
    return tuple(out[0, k] for k in range(len(values)))


def sigma_sum_kernel(n_sec, n_op, x_ref, t_ref, o_ref, s_ref,
                     rs_buf, red, red_out, ag_buf, op_buf, sec_buf, mid, mid_out,
                     send_rs, recv_rs, send_ag, recv_ag, send_a, recv_a,
                     send_b, recv_b, local_sem):
    me_sec = lax.axis_index("sec")
    me_op = lax.axis_index("op")
    barrier = pltpu.get_barrier_semaphore()
    for d in range(1, n_op):
        pl.semaphore_signal(barrier, 1, device_id=(me_sec, (me_op + d) % n_op),
                            device_id_type=MESH)
    for d in range(1, n_sec):
        pl.semaphore_signal(barrier, 1, device_id=((me_sec + d) % n_sec, me_op),
                            device_id_type=MESH)
    pl.semaphore_wait(barrier, n_op - 1 + n_sec - 1)

    def op_peer(j):
        return (me_sec, j)

    def sec_peer(j):
        return (j, me_op)

    def rs_copy(d):
        j = (me_op + d) % n_op
        return pltpu.make_async_remote_copy(
            src_ref=x_ref.at[j], dst_ref=rs_buf.at[me_op], send_sem=send_rs.at[d],
            recv_sem=recv_rs.at[me_op], device_id=op_peer(j), device_id_type=MESH)

    def rs_recv(d):
        slot = (me_op + n_op - d) % n_op
        return pltpu.make_async_remote_copy(
            src_ref=x_ref.at[me_op], dst_ref=rs_buf.at[slot], send_sem=send_rs.at[d],
            recv_sem=recv_rs.at[slot], device_id=op_peer(slot), device_id_type=MESH)

    def gather_copy(n, me, src, buf, send, recv, peer_of, d):
        return pltpu.make_async_remote_copy(
            src_ref=src, dst_ref=buf.at[me], send_sem=send.at[d],
            recv_sem=recv.at[me], device_id=peer_of((me + d) % n), device_id_type=MESH)

    def gather_recv(n, me, src, buf, send, recv, peer_of, d):
        slot = (me + n - d) % n
        return pltpu.make_async_remote_copy(
            src_ref=src, dst_ref=buf.at[slot], send_sem=send.at[d],
            recv_sem=recv.at[slot], device_id=peer_of(slot), device_id_type=MESH)

    def ordered_sum(buf, n):
        total = buf[0]
        for j in range(1, n):
            total = total + buf[j]
        return total

    for d in range(1, n_op):
        rs_copy(d).start()
    a_args = (n_op, me_op, t_ref, op_buf, send_a, recv_a, op_peer)
    for d in range(1, n_op):
        gather_copy(*a_args, d).start()
    rs_buf[me_op] = x_ref[me_op]
    op_buf[me_op] = t_ref[...]

    for d in range(1, n_op):
        gather_recv(*a_args, d).wait_recv()
    mid[...] = ordered_sum(op_buf, n_op)
    local = pltpu.make_async_copy(mid, mid_out, local_sem.at[0])
    local.start()
    local.wait()
    b_args = (n_sec, me_sec, mid_out, sec_buf, send_b, recv_b, sec_peer)
    for d in range(1, n_sec):
        gather_copy(*b_args, d).start()
    sec_buf[me_sec] = mid_out[...]

    for d in range(1, n_op):
        rs_recv(d).wait_recv()
    red[...] = ordered_sum(rs_buf, n_op)
    local = pltpu.make_async_copy(red, red_out, local_sem.at[1])
    local.start()
    local.wait()
    g_args = (n_op, me_op, red_out, ag_buf, send_ag, recv_ag, op_peer)
    for d in range(1, n_op):
        gather_copy(*g_args, d).start()
    ag_buf[me_op] = red_out[...]

    for d in range(1, n_sec):
        gather_recv(*b_args, d).wait_recv()
    s_ref[...] = ordered_sum(sec_buf, n_sec)
    for d in range(1, n_op):
        gather_recv(*g_args, d).wait_recv()
    o_ref[...] = ag_buf[...]

    for d in range(1, n_op):
        rs_copy(d).wait_send()
        gather_copy(*a_args, d).wait_send()
        gather_copy(*g_args, d).wait_send()
    for d in range(1, n_sec):
        gather_copy(*b_args, d).wait_send()


def sigma_sum(partial, values, n_sec, n_op):
    shape = partial.shape
    rows = shape[0] * shape[1] // n_op
    chunks = partial.reshape(n_op, rows, shape[2])
    lane = lax.broadcasted_iota(jnp.int32, (8, 128), 1)
    tile = jnp.zeros((8, 128), jnp.float32)
    for k, v in enumerate(values):
        tile = jnp.where(lane == k, v, tile)
    vmem = pl.BlockSpec(memory_space=pltpu.VMEM)
    total, sums = pl.pallas_call(
        functools.partial(sigma_sum_kernel, n_sec, n_op),
        out_shape=(
            jax.ShapeDtypeStruct(chunks.shape, jnp.float32),
            jax.ShapeDtypeStruct((8, 128), jnp.float32),
        ),
        in_specs=[vmem, vmem],
        out_specs=(vmem, vmem),
        scratch_shapes=[
            pltpu.VMEM(chunks.shape, jnp.float32),
            pltpu.VMEM((rows, shape[2]), jnp.float32),
            pltpu.VMEM((rows, shape[2]), jnp.float32),
            pltpu.VMEM(chunks.shape, jnp.float32),
            pltpu.VMEM((n_op, 8, 128), jnp.float32),
            pltpu.VMEM((n_sec, 8, 128), jnp.float32),
            pltpu.VMEM((8, 128), jnp.float32),
            pltpu.VMEM((8, 128), jnp.float32),
            pltpu.SemaphoreType.DMA((n_op,)),
            pltpu.SemaphoreType.DMA((n_op,)),
            pltpu.SemaphoreType.DMA((n_op,)),
            pltpu.SemaphoreType.DMA((n_op,)),
            pltpu.SemaphoreType.DMA((n_op,)),
            pltpu.SemaphoreType.DMA((n_op,)),
            pltpu.SemaphoreType.DMA((n_sec,)),
            pltpu.SemaphoreType.DMA((n_sec,)),
            pltpu.SemaphoreType.DMA((2,)),
        ],
        compiler_params=pltpu.CompilerParams(collective_id=1, has_side_effects=True),
    )(chunks, tile)
    return total.reshape(shape), tuple(sums[0, k] for k in range(len(values)))


def step_kernel(n_sec, n_op, count, final, x_ref, st_ref, sh_ref, t_ref, *refs):
    if final:
        (win_ref, rs_buf, red, op_buf, sec_buf, mid, mid_out, op_buf2, sec_buf2,
         mid2, mid2_out, mid3, mid3_out, new_buf, new_out, win_buf, send_rs, recv_rs, send_a,
         recv_a, send_b, recv_b, send_a2, recv_a2, send_b2, recv_b2, send_w,
         recv_w, local_sem) = refs
    else:
        (win_ref, rs_buf, red, op_buf, sec_buf, mid, mid_out, new_buf, new_out,
         win_buf, send_rs, recv_rs, send_a, recv_a, send_b, recv_b, send_w,
         recv_w, local_sem) = refs
    me_sec = lax.axis_index("sec")
    me_op = lax.axis_index("op")
    prev_sec = (me_sec + n_sec - 1) % n_sec
    next_sec = (me_sec + 1) % n_sec
    barrier = pltpu.get_barrier_semaphore()
    greeted = 0
    for d in range(1, n_op):
        pl.semaphore_signal(barrier, 1, device_id=(me_sec, (me_op + d) % n_op),
                            device_id_type=MESH)
        greeted += 1
    for d in range(1, n_sec):
        pl.semaphore_signal(barrier, 1, device_id=((me_sec + d) % n_sec, me_op),
                            device_id_type=MESH)
        greeted += 1
    for side in (prev_sec, next_sec):
        for d in range(1, n_op):
            pl.semaphore_signal(barrier, 1, device_id=(side, (me_op + d) % n_op),
                                device_id_type=MESH)
            greeted += 1
    pl.semaphore_wait(barrier, greeted)

    def op_peer(j):
        return (me_sec, j)

    def sec_peer(j):
        return (j, me_op)

    def copy_to(src, dst, send, recv, peer):
        return pltpu.make_async_remote_copy(
            src_ref=src, dst_ref=dst, send_sem=send, recv_sem=recv,
            device_id=peer, device_id_type=MESH)

    def ordered_sum(buf, n):
        total = buf[0]
        for j in range(1, n):
            total = total + buf[j]
        return total

    def start_gather(n, me, src, buf, send, recv, peer_of):
        for d in range(1, n):
            copy_to(src, buf.at[me], send.at[d], recv.at[me], peer_of((me + d) % n)).start()
        buf[me] = src[...]

    def wait_gather(n, me, src, buf, send, recv, peer_of):
        for d in range(1, n):
            slot = (me + n - d) % n
            copy_to(src, buf.at[slot], send.at[d], recv.at[slot], peer_of(slot)).wait_recv()

    def drain_gather(n, me, src, buf, send, recv, peer_of):
        for d in range(1, n):
            copy_to(src, buf.at[me], send.at[d], recv.at[me], peer_of((me + d) % n)).wait_send()

    def settle(src, dst, sem):
        local = pltpu.make_async_copy(src, dst, sem)
        local.start()
        local.wait()

    def rs_copy(d):
        j = (me_op + d) % n_op
        return copy_to(x_ref.at[j], rs_buf.at[me_op], send_rs.at[d], recv_rs.at[me_op], op_peer(j))

    for d in range(1, n_op):
        rs_copy(d).start()
    a_args = (n_op, me_op, t_ref, op_buf, send_a, recv_a, op_peer)
    start_gather(*a_args)
    rs_buf[me_op] = x_ref[me_op]

    wait_gather(*a_args)
    mid[...] = ordered_sum(op_buf, n_op)
    settle(mid, mid_out, local_sem.at[0])
    b_args = (n_sec, me_sec, mid_out, sec_buf, send_b, recv_b, sec_peer)
    start_gather(*b_args)

    for d in range(1, n_op):
        slot = (me_op + n_op - d) % n_op
        copy_to(x_ref.at[me_op], rs_buf.at[slot], send_rs.at[d], recv_rs.at[slot],
                op_peer(slot)).wait_recv()
    red[...] = ordered_sum(rs_buf, n_op)

    wait_gather(*b_args)
    sums = ordered_sum(sec_buf, n_sec)
    energy_sum = sums[0:1, 0:1]
    norm_sum = sums[0:1, 1:2]
    state_wide = st_ref[me_op].astype(jnp.float32)
    sigma = red[...] + sh_ref[me_op] * state_wide
    updated = state_wide - step_size * (sigma - (energy_sum / norm_sum) * state_wide)
    if final:
        square = jnp.sum(jnp.sum(updated * updated, axis=1, keepdims=True), axis=0,
                         keepdims=True)
        lane = lax.broadcasted_iota(jnp.int32, (8, 128), 1)
        mid2[...] = jnp.where(lane == 0, square, 0.0)
        settle(mid2, mid2_out, local_sem.at[1])
        a2_args = (n_op, me_op, mid2_out, op_buf2, send_a2, recv_a2, op_peer)
        start_gather(*a2_args)
        wait_gather(*a2_args)
        mid3[...] = ordered_sum(op_buf2, n_op)
        settle(mid3, mid3_out, local_sem.at[3])
        b2_args = (n_sec, me_sec, mid3_out, sec_buf2, send_b2, recv_b2, sec_peer)
        start_gather(*b2_args)
        wait_gather(*b2_args)
        new_norm = ordered_sum(sec_buf2, n_sec)[0:1, 0:1]
        factor = jnp.sqrt(count / new_norm)
    else:
        factor = jnp.sqrt(count / norm_sum)
    new_buf[...] = (updated * factor).astype(new_buf.dtype)
    settle(new_buf, new_out, local_sem.at[2])

    sides = ((next_sec, 0),) if final else ((next_sec, 0), (prev_sec, 2 * n_op))
    sent = 0
    for side, base in sides:
        for j in range(n_op):
            copy_to(new_out, win_buf.at[base + me_op], send_w.at[sent],
                    recv_w.at[base + me_op], (side, j)).start()
            sent += 1
    for d in range(1, n_op):
        j = (me_op + d) % n_op
        copy_to(new_out, win_buf.at[n_op + me_op], send_w.at[sent],
                recv_w.at[n_op + me_op], op_peer(j)).start()
        sent += 1
    win_buf[n_op + me_op] = new_out[...]

    from_sides = ((prev_sec, 0),) if final else ((prev_sec, 0), (next_sec, 2 * n_op))
    for side, base in from_sides:
        for j in range(n_op):
            copy_to(new_out, win_buf.at[base + j], send_w.at[0], recv_w.at[base + j],
                    (side, j)).wait_recv()
    for d in range(1, n_op):
        slot = (me_op + n_op - d) % n_op
        copy_to(new_out, win_buf.at[n_op + slot], send_w.at[0], recv_w.at[n_op + slot],
                op_peer(slot)).wait_recv()
    win_ref[...] = win_buf[...]

    for d in range(1, n_op):
        rs_copy(d).wait_send()
    drain_gather(*a_args)
    drain_gather(*b_args)
    if final:
        drain_gather(*a2_args)
        drain_gather(*b2_args)
    for k in range(sent):
        copy_to(new_out, win_buf.at[n_op + me_op], send_w.at[k], recv_w.at[n_op + me_op],
                op_peer((me_op + 1) % n_op)).wait_send()


def step(partial, state, shift, values, count, final, n_sec, n_op):
    shape = partial.shape
    rows = shape[0] * shape[1] // n_op
    chunks = partial.reshape(n_op, rows, shape[2])
    state_chunks = state.reshape(n_op, rows, shape[2])
    shift_chunks = jnp.repeat(shift, n_op // shape[0])[:, None, None]
    lane = lax.broadcasted_iota(jnp.int32, (8, 128), 1)
    tile = jnp.zeros((8, 128), jnp.float32)
    for k, v in enumerate(values):
        tile = jnp.where(lane == k, v, tile)
    slots = (2 if final else 3) * n_op
    tile_shape = (rows, shape[2])
    scalar_bufs = [
        pltpu.VMEM((n_op, 8, 128), jnp.float32),
        pltpu.VMEM((n_sec, 8, 128), jnp.float32),
        pltpu.VMEM((8, 128), jnp.float32),
        pltpu.VMEM((8, 128), jnp.float32),
    ]
    scratch = [
        pltpu.VMEM(chunks.shape, jnp.float32),
        pltpu.VMEM(tile_shape, jnp.float32),
    ] + scalar_bufs + (scalar_bufs + scalar_bufs[2:] if final else []) + [
        pltpu.VMEM(tile_shape, jnp.bfloat16),
        pltpu.VMEM(tile_shape, jnp.bfloat16),
        pltpu.VMEM((slots, rows, shape[2]), jnp.bfloat16),
        pltpu.SemaphoreType.DMA((n_op,)),
        pltpu.SemaphoreType.DMA((n_op,)),
        pltpu.SemaphoreType.DMA((n_op,)),
        pltpu.SemaphoreType.DMA((n_op,)),
        pltpu.SemaphoreType.DMA((n_sec,)),
        pltpu.SemaphoreType.DMA((n_sec,)),
    ] + ([
        pltpu.SemaphoreType.DMA((n_op,)),
        pltpu.SemaphoreType.DMA((n_op,)),
        pltpu.SemaphoreType.DMA((n_sec,)),
        pltpu.SemaphoreType.DMA((n_sec,)),
    ] if final else []) + [
        pltpu.SemaphoreType.DMA((slots + n_op,)),
        pltpu.SemaphoreType.DMA((slots,)),
        pltpu.SemaphoreType.DMA((4,)),
    ]
    vmem = pl.BlockSpec(memory_space=pltpu.VMEM)
    window = pl.pallas_call(
        functools.partial(step_kernel, n_sec, n_op, count, final),
        out_shape=jax.ShapeDtypeStruct((slots, rows, shape[2]), jnp.bfloat16),
        in_specs=[vmem, vmem, vmem, vmem],
        out_specs=vmem,
        scratch_shapes=scratch,
        compiler_params=pltpu.CompilerParams(
            collective_id=3 if final else 2, has_side_effects=True
        ),
    )(chunks, state_chunks, shift_chunks, tile)
    return window.reshape(slots // (n_op // shape[0]), shape[1], shape[2])


def shifted(block, axis, distance):
    devices = range(lax.axis_size(axis))
    route = [((i - distance) % len(devices), i) for i in devices]
    return lax.ppermute(block, axis, route)


def per_device(state_start, left_ops, right_ops, shift, partner, kept):
    sector_local = state_start.shape[0]
    width = state_start.shape[1]
    count = float(sector_local * lax.axis_size("sec") * width * width)
    shift_col = shift[:, None, None]
    first_op = lax.axis_index("op") == 0
    n_sec = lax.axis_size("sec")
    n_op = lax.axis_size("op")
    left_prev = shifted(left_ops, "sec", 1)
    kept_prev = shifted(kept, "sec", 1)
    state = state_start
    window = padded(state, (("sec", 0),), sector_local)
    for iteration in range(ITERS):
        sources = window[partner]
        halfway = jnp.einsum(
            "tbij,tbjk->tbik", left_ops, sources, preferred_element_type=jnp.float32
        ).astype(jnp.bfloat16)
        partial_sigma = jnp.einsum(
            "tbij,tbjk->bik", halfway, right_ops, preferred_element_type=jnp.float32
        )
        state_wide = state.astype(jnp.float32)
        own_square = jnp.sum(state_wide * state_wide, axis=(1, 2))
        energy_part = jnp.sum(state_wide * partial_sigma) + jnp.where(
            first_op, jnp.sum(shift * own_square), 0.0
        )
        norm_part = jnp.where(first_op, jnp.sum(own_square), 0.0)
        final = iteration == ITERS - 1
        window = step(
            partial_sigma, state, shift, (energy_part, norm_part), count, final,
            n_sec, n_op,
        )
        state = window[sector_local : 2 * sector_local]
    state_prev = window[:sector_local]
    columns = jnp.arange(width, dtype=jnp.int32)
    keep_mask = (columns[None, :] < kept_prev[:, None]).astype(jnp.bfloat16)
    kept_block = state_prev * keep_mask[:, None, :]
    out_scale = 1.0 / float(width) ** 0.5
    projected = jnp.einsum(
        "tbij,bjk->tbik", left_prev, kept_block, preferred_element_type=jnp.float32
    ).astype(jnp.bfloat16)
    new_ops = (
        jnp.einsum("bji,tbjk->tbik", kept_block, projected, preferred_element_type=jnp.float32)
        * out_scale
    ).astype(jnp.bfloat16)
    return (state, new_ops)


def solution(mesh):
    in_specs = (
        P("sec", None, None),
        P("op", "sec", None, None),
        P("op", "sec", None, None),
        P("sec"),
        P("op", "sec"),
        P("sec"),
    )
    out_specs = (P("sec", None, None), P("op", "sec", None, None))
    return jax.shard_map(
        per_device, mesh=mesh, in_specs=in_specs, out_specs=out_specs, check_vma=False
    )
```

```python
import functools

import jax
import jax.numpy as jnp
from jax import lax
from jax.experimental import pallas as pl
from jax.experimental.pallas import tpu as pltpu
from jax.sharding import PartitionSpec as P

MESH = pl.DeviceIdType.MESH

ITERS = 4


step_size = 0.5


def padded(cells, sides, width):
    for axis, dim in sides:
        count = lax.axis_size(axis)
        head = lax.slice_in_dim(cells, 0, width, axis=dim)
        tail = lax.slice_in_dim(cells, cells.shape[dim] - width, cells.shape[dim], axis=dim)
        cells = jnp.concatenate(
            [
                lax.ppermute(tail, axis, [(i, (i + 1) % count) for i in range(count)]),
                cells,
                lax.ppermute(head, axis, [((i + 1) % count, i) for i in range(count)]),
            ],
            axis=dim,
        )
    return cells


def all_sum_kernel(n_sec, n_op, x_ref, o_ref, op_buf, sec_buf, mid, out_buf,
                   send_a, recv_a, send_b, recv_b, local_sem):
    me_sec = lax.axis_index("sec")
    me_op = lax.axis_index("op")
    barrier = pltpu.get_barrier_semaphore()
    for d in range(1, n_op):
        pl.semaphore_signal(barrier, 1, device_id=(me_sec, (me_op + d) % n_op),
                            device_id_type=MESH)
    for d in range(1, n_sec):
        pl.semaphore_signal(barrier, 1, device_id=((me_sec + d) % n_sec, me_op),
                            device_id_type=MESH)
    pl.semaphore_wait(barrier, n_op - 1 + n_sec - 1)

    def stage(n, me, src, buf, send, recv, peer_of):
        for d in range(1, n):
            pltpu.make_async_remote_copy(
                src_ref=src, dst_ref=buf.at[me], send_sem=send.at[d],
                recv_sem=recv.at[me], device_id=peer_of((me + d) % n),
                device_id_type=MESH).start()
        buf[me] = src[...]
        for d in range(1, n):
            slot = (me + n - d) % n
            pltpu.make_async_remote_copy(
                src_ref=src, dst_ref=buf.at[slot], send_sem=send.at[d],
                recv_sem=recv.at[slot], device_id=peer_of(slot),
                device_id_type=MESH).wait_recv()
        for d in range(1, n):
            pltpu.make_async_remote_copy(
                src_ref=src, dst_ref=buf.at[me], send_sem=send.at[d],
                recv_sem=recv.at[me], device_id=peer_of((me + d) % n),
                device_id_type=MESH).wait_send()
        total = buf[0]
        for j in range(1, n):
            total = total + buf[j]
        return total

    mid[...] = stage(n_op, me_op, x_ref, op_buf, send_a, recv_a,
                     lambda j: (me_sec, j))
    local = pltpu.make_async_copy(mid, out_buf, local_sem)
    local.start()
    local.wait()
    o_ref[...] = stage(n_sec, me_sec, out_buf, sec_buf, send_b, recv_b,
                       lambda j: (j, me_op))


def all_sum(values, n_sec, n_op):
    lane = lax.broadcasted_iota(jnp.int32, (8, 128), 1)
    tile = jnp.zeros((8, 128), jnp.float32)
    for k, v in enumerate(values):
        tile = jnp.where(lane == k, v, tile)
    tile_spec = pl.BlockSpec(memory_space=pltpu.VMEM)
    out = pl.pallas_call(
        functools.partial(all_sum_kernel, n_sec, n_op),
        out_shape=jax.ShapeDtypeStruct((8, 128), jnp.float32),
        in_specs=[tile_spec],
        out_specs=tile_spec,
        scratch_shapes=[
            pltpu.VMEM((n_op, 8, 128), jnp.float32),
            pltpu.VMEM((n_sec, 8, 128), jnp.float32),
            pltpu.VMEM((8, 128), jnp.float32),
            pltpu.VMEM((8, 128), jnp.float32),
            pltpu.SemaphoreType.DMA((n_op,)),
            pltpu.SemaphoreType.DMA((n_op,)),
            pltpu.SemaphoreType.DMA((n_sec,)),
            pltpu.SemaphoreType.DMA((n_sec,)),
            pltpu.SemaphoreType.DMA(()),
        ],
        compiler_params=pltpu.CompilerParams(collective_id=0, has_side_effects=True),
    )(tile)
    return tuple(out[0, k] for k in range(len(values)))


def sigma_sum_kernel(n_sec, n_op, x_ref, t_ref, o_ref, s_ref,
                     rs_buf, red, red_out, ag_buf, op_buf, sec_buf, mid, mid_out,
                     send_rs, recv_rs, send_ag, recv_ag, send_a, recv_a,
                     send_b, recv_b, local_sem):
    me_sec = lax.axis_index("sec")
    me_op = lax.axis_index("op")
    barrier = pltpu.get_barrier_semaphore()
    for d in range(1, n_op):
        pl.semaphore_signal(barrier, 1, device_id=(me_sec, (me_op + d) % n_op),
                            device_id_type=MESH)
    for d in range(1, n_sec):
        pl.semaphore_signal(barrier, 1, device_id=((me_sec + d) % n_sec, me_op),
                            device_id_type=MESH)
    pl.semaphore_wait(barrier, n_op - 1 + n_sec - 1)

    def op_peer(j):
        return (me_sec, j)

    def sec_peer(j):
        return (j, me_op)

    def total_of(v):
        return jnp.sum(jnp.sum(v, axis=1, keepdims=True), axis=0, keepdims=True)

    lane = lax.broadcasted_iota(jnp.int32, (8, 128), 1)
    own = st_ref[me_op].astype(jnp.float32)
    own_square = total_of(own * own)
    energy = sh_ref[me_op] * own_square
    for j in range(n_op):
        energy = energy + total_of(x_ref[j] * st_ref[j].astype(jnp.float32))
    t_ref[...] = jnp.where(lane == 0, energy, jnp.where(lane == 1, own_square, 0.0))
    settle(t_ref, t_out, local_sem.at[4])

    def rs_copy(d):
        j = (me_op + d) % n_op
        return pltpu.make_async_remote_copy(
            src_ref=x_ref.at[j], dst_ref=rs_buf.at[me_op], send_sem=send_rs.at[d],
            recv_sem=recv_rs.at[me_op], device_id=op_peer(j), device_id_type=MESH)

    def rs_recv(d):
        slot = (me_op + n_op - d) % n_op
        return pltpu.make_async_remote_copy(
            src_ref=x_ref.at[me_op], dst_ref=rs_buf.at[slot], send_sem=send_rs.at[d],
            recv_sem=recv_rs.at[slot], device_id=op_peer(slot), device_id_type=MESH)

    def gather_copy(n, me, src, buf, send, recv, peer_of, d):
        return pltpu.make_async_remote_copy(
            src_ref=src, dst_ref=buf.at[me], send_sem=send.at[d],
            recv_sem=recv.at[me], device_id=peer_of((me + d) % n), device_id_type=MESH)

    def gather_recv(n, me, src, buf, send, recv, peer_of, d):
        slot = (me + n - d) % n
        return pltpu.make_async_remote_copy(
            src_ref=src, dst_ref=buf.at[slot], send_sem=send.at[d],
            recv_sem=recv.at[slot], device_id=peer_of(slot), device_id_type=MESH)

    def ordered_sum(buf, n):
        total = buf[0]
        for j in range(1, n):
            total = total + buf[j]
        return total

    for d in range(1, n_op):
        rs_copy(d).start()
    a_args = (n_op, me_op, t_out, op_buf, send_a, recv_a, op_peer)
    for d in range(1, n_op):
        gather_copy(*a_args, d).start()
    rs_buf[me_op] = x_ref[me_op]
    op_buf[me_op] = t_ref[...]

    for d in range(1, n_op):
        gather_recv(*a_args, d).wait_recv()
    mid[...] = ordered_sum(op_buf, n_op)
    local = pltpu.make_async_copy(mid, mid_out, local_sem.at[0])
    local.start()
    local.wait()
    b_args = (n_sec, me_sec, mid_out, sec_buf, send_b, recv_b, sec_peer)
    for d in range(1, n_sec):
        gather_copy(*b_args, d).start()
    sec_buf[me_sec] = mid_out[...]

    for d in range(1, n_op):
        rs_recv(d).wait_recv()
    red[...] = ordered_sum(rs_buf, n_op)
    local = pltpu.make_async_copy(red, red_out, local_sem.at[1])
    local.start()
    local.wait()
    g_args = (n_op, me_op, red_out, ag_buf, send_ag, recv_ag, op_peer)
    for d in range(1, n_op):
        gather_copy(*g_args, d).start()
    ag_buf[me_op] = red_out[...]

    for d in range(1, n_sec):
        gather_recv(*b_args, d).wait_recv()
    s_ref[...] = ordered_sum(sec_buf, n_sec)
    for d in range(1, n_op):
        gather_recv(*g_args, d).wait_recv()
    o_ref[...] = ag_buf[...]

    for d in range(1, n_op):
        rs_copy(d).wait_send()
        gather_copy(*a_args, d).wait_send()
        gather_copy(*g_args, d).wait_send()
    for d in range(1, n_sec):
        gather_copy(*b_args, d).wait_send()


def sigma_sum(partial, values, n_sec, n_op):
    shape = partial.shape
    rows = shape[0] * shape[1] // n_op
    chunks = partial.reshape(n_op, rows, shape[2])
    lane = lax.broadcasted_iota(jnp.int32, (8, 128), 1)
    tile = jnp.zeros((8, 128), jnp.float32)
    for k, v in enumerate(values):
        tile = jnp.where(lane == k, v, tile)
    vmem = pl.BlockSpec(memory_space=pltpu.VMEM)
    total, sums = pl.pallas_call(
        functools.partial(sigma_sum_kernel, n_sec, n_op),
        out_shape=(
            jax.ShapeDtypeStruct(chunks.shape, jnp.float32),
            jax.ShapeDtypeStruct((8, 128), jnp.float32),
        ),
        in_specs=[vmem, vmem],
        out_specs=(vmem, vmem),
        scratch_shapes=[
            pltpu.VMEM(chunks.shape, jnp.float32),
            pltpu.VMEM((rows, shape[2]), jnp.float32),
            pltpu.VMEM((rows, shape[2]), jnp.float32),
            pltpu.VMEM(chunks.shape, jnp.float32),
            pltpu.VMEM((n_op, 8, 128), jnp.float32),
            pltpu.VMEM((n_sec, 8, 128), jnp.float32),
            pltpu.VMEM((8, 128), jnp.float32),
            pltpu.VMEM((8, 128), jnp.float32),
            pltpu.SemaphoreType.DMA((n_op,)),
            pltpu.SemaphoreType.DMA((n_op,)),
            pltpu.SemaphoreType.DMA((n_op,)),
            pltpu.SemaphoreType.DMA((n_op,)),
            pltpu.SemaphoreType.DMA((n_op,)),
            pltpu.SemaphoreType.DMA((n_op,)),
            pltpu.SemaphoreType.DMA((n_sec,)),
            pltpu.SemaphoreType.DMA((n_sec,)),
            pltpu.SemaphoreType.DMA((2,)),
        ],
        compiler_params=pltpu.CompilerParams(collective_id=1, has_side_effects=True),
    )(chunks, tile)
    return total.reshape(shape), tuple(sums[0, k] for k in range(len(values)))


def step_kernel(n_sec, n_op, count, final, x_ref, st_ref, sh_ref, *refs):
    if final:
        (win_ref, t_ref, t_out, rs_buf, red, op_buf, sec_buf, mid, mid_out, op_buf2,
         sec_buf2, mid2, mid2_out, mid3, mid3_out, new_buf, new_out, win_buf, send_rs, recv_rs, send_a,
         recv_a, send_b, recv_b, send_a2, recv_a2, send_b2, recv_b2, send_w,
         recv_w, local_sem) = refs
    else:
        (win_ref, t_ref, t_out, rs_buf, red, op_buf, sec_buf, mid, mid_out, new_buf,
         new_out, win_buf, send_rs, recv_rs, send_a, recv_a, send_b, recv_b, send_w,
         recv_w, local_sem) = refs
    me_sec = lax.axis_index("sec")
    me_op = lax.axis_index("op")
    prev_sec = (me_sec + n_sec - 1) % n_sec
    next_sec = (me_sec + 1) % n_sec
    barrier = pltpu.get_barrier_semaphore()
    greeted = 0
    for d in range(1, n_op):
        pl.semaphore_signal(barrier, 1, device_id=(me_sec, (me_op + d) % n_op),
                            device_id_type=MESH)
        greeted += 1
    for d in range(1, n_sec):
        pl.semaphore_signal(barrier, 1, device_id=((me_sec + d) % n_sec, me_op),
                            device_id_type=MESH)
        greeted += 1
    for side in (prev_sec, next_sec):
        for d in range(1, n_op):
            pl.semaphore_signal(barrier, 1, device_id=(side, (me_op + d) % n_op),
                                device_id_type=MESH)
            greeted += 1
    pl.semaphore_wait(barrier, greeted)

    def op_peer(j):
        return (me_sec, j)

    def sec_peer(j):
        return (j, me_op)

    def copy_to(src, dst, send, recv, peer):
        return pltpu.make_async_remote_copy(
            src_ref=src, dst_ref=dst, send_sem=send, recv_sem=recv,
            device_id=peer, device_id_type=MESH)

    def ordered_sum(buf, n):
        total = buf[0]
        for j in range(1, n):
            total = total + buf[j]
        return total

    def start_gather(n, me, src, buf, send, recv, peer_of):
        for d in range(1, n):
            copy_to(src, buf.at[me], send.at[d], recv.at[me], peer_of((me + d) % n)).start()
        buf[me] = src[...]

    def wait_gather(n, me, src, buf, send, recv, peer_of):
        for d in range(1, n):
            slot = (me + n - d) % n
            copy_to(src, buf.at[slot], send.at[d], recv.at[slot], peer_of(slot)).wait_recv()

    def drain_gather(n, me, src, buf, send, recv, peer_of):
        for d in range(1, n):
            copy_to(src, buf.at[me], send.at[d], recv.at[me], peer_of((me + d) % n)).wait_send()

    def settle(src, dst, sem):
        local = pltpu.make_async_copy(src, dst, sem)
        local.start()
        local.wait()

    def total_of(v):
        return jnp.sum(jnp.sum(v, axis=1, keepdims=True), axis=0, keepdims=True)

    lane = lax.broadcasted_iota(jnp.int32, (8, 128), 1)
    own = st_ref[me_op].astype(jnp.float32)
    own_square = total_of(own * own)
    energy = sh_ref[me_op] * own_square
    for j in range(n_op):
        energy = energy + total_of(x_ref[j] * st_ref[j].astype(jnp.float32))
    t_ref[...] = jnp.where(lane == 0, energy, jnp.where(lane == 1, own_square, 0.0))
    settle(t_ref, t_out, local_sem.at[4])

    def rs_copy(d):
        j = (me_op + d) % n_op
        return copy_to(x_ref.at[j], rs_buf.at[me_op], send_rs.at[d], recv_rs.at[me_op], op_peer(j))

    for d in range(1, n_op):
        rs_copy(d).start()
    a_args = (n_op, me_op, t_out, op_buf, send_a, recv_a, op_peer)
    start_gather(*a_args)
    rs_buf[me_op] = x_ref[me_op]

    wait_gather(*a_args)
    mid[...] = ordered_sum(op_buf, n_op)
    settle(mid, mid_out, local_sem.at[0])
    b_args = (n_sec, me_sec, mid_out, sec_buf, send_b, recv_b, sec_peer)
    start_gather(*b_args)

    for d in range(1, n_op):
        slot = (me_op + n_op - d) % n_op
        copy_to(x_ref.at[me_op], rs_buf.at[slot], send_rs.at[d], recv_rs.at[slot],
                op_peer(slot)).wait_recv()
    red[...] = ordered_sum(rs_buf, n_op)

    wait_gather(*b_args)
    sums = ordered_sum(sec_buf, n_sec)
    energy_sum = sums[0:1, 0:1]
    norm_sum = sums[0:1, 1:2]
    state_wide = st_ref[me_op].astype(jnp.float32)
    sigma = red[...] + sh_ref[me_op] * state_wide
    updated = state_wide - step_size * (sigma - (energy_sum / norm_sum) * state_wide)
    if final:
        square = total_of(updated * updated)
        mid2[...] = jnp.where(lane == 0, square, 0.0)
        settle(mid2, mid2_out, local_sem.at[1])
        a2_args = (n_op, me_op, mid2_out, op_buf2, send_a2, recv_a2, op_peer)
        start_gather(*a2_args)
        wait_gather(*a2_args)
        mid3[...] = ordered_sum(op_buf2, n_op)
        settle(mid3, mid3_out, local_sem.at[3])
        b2_args = (n_sec, me_sec, mid3_out, sec_buf2, send_b2, recv_b2, sec_peer)
        start_gather(*b2_args)
        wait_gather(*b2_args)
        new_norm = ordered_sum(sec_buf2, n_sec)[0:1, 0:1]
        factor = jnp.sqrt(count / new_norm)
    else:
        factor = jnp.sqrt(count / norm_sum)
    new_buf[...] = (updated * factor).astype(new_buf.dtype)
    settle(new_buf, new_out, local_sem.at[2])

    sides = ((next_sec, 0),) if final else ((next_sec, 0), (prev_sec, 2 * n_op))
    sent = 0
    for side, base in sides:
        for j in range(n_op):
            copy_to(new_out, win_buf.at[base + me_op], send_w.at[sent],
                    recv_w.at[base + me_op], (side, j)).start()
            sent += 1
    for d in range(1, n_op):
        j = (me_op + d) % n_op
        copy_to(new_out, win_buf.at[n_op + me_op], send_w.at[sent],
                recv_w.at[n_op + me_op], op_peer(j)).start()
        sent += 1
    win_buf[n_op + me_op] = new_out[...]

    from_sides = ((prev_sec, 0),) if final else ((prev_sec, 0), (next_sec, 2 * n_op))
    for side, base in from_sides:
        for j in range(n_op):
            copy_to(new_out, win_buf.at[base + j], send_w.at[0], recv_w.at[base + j],
                    (side, j)).wait_recv()
    for d in range(1, n_op):
        slot = (me_op + n_op - d) % n_op
        copy_to(new_out, win_buf.at[n_op + slot], send_w.at[0], recv_w.at[n_op + slot],
                op_peer(slot)).wait_recv()
    win_ref[...] = win_buf[...]

    for d in range(1, n_op):
        rs_copy(d).wait_send()
    drain_gather(*a_args)
    drain_gather(*b_args)
    if final:
        drain_gather(*a2_args)
        drain_gather(*b2_args)
    for k in range(sent):
        copy_to(new_out, win_buf.at[n_op + me_op], send_w.at[k], recv_w.at[n_op + me_op],
                op_peer((me_op + 1) % n_op)).wait_send()


def step(partial, state, shift, count, final, n_sec, n_op):
    shape = partial.shape
    rows = shape[0] * shape[1] // n_op
    chunks = partial.reshape(n_op, rows, shape[2])
    state_chunks = state.reshape(n_op, rows, shape[2])
    shift_chunks = jnp.repeat(shift, n_op // shape[0])[:, None, None]
    slots = (2 if final else 3) * n_op
    tile_shape = (rows, shape[2])
    scalar_bufs = [
        pltpu.VMEM((n_op, 8, 128), jnp.float32),
        pltpu.VMEM((n_sec, 8, 128), jnp.float32),
        pltpu.VMEM((8, 128), jnp.float32),
        pltpu.VMEM((8, 128), jnp.float32),
    ]
    scratch = [
        pltpu.VMEM((8, 128), jnp.float32),
        pltpu.VMEM((8, 128), jnp.float32),
        pltpu.VMEM(chunks.shape, jnp.float32),
        pltpu.VMEM(tile_shape, jnp.float32),
    ] + scalar_bufs + (scalar_bufs + scalar_bufs[2:] if final else []) + [
        pltpu.VMEM(tile_shape, jnp.bfloat16),
        pltpu.VMEM(tile_shape, jnp.bfloat16),
        pltpu.VMEM((slots, rows, shape[2]), jnp.bfloat16),
        pltpu.SemaphoreType.DMA((n_op,)),
        pltpu.SemaphoreType.DMA((n_op,)),
        pltpu.SemaphoreType.DMA((n_op,)),
        pltpu.SemaphoreType.DMA((n_op,)),
        pltpu.SemaphoreType.DMA((n_sec,)),
        pltpu.SemaphoreType.DMA((n_sec,)),
    ] + ([
        pltpu.SemaphoreType.DMA((n_op,)),
        pltpu.SemaphoreType.DMA((n_op,)),
        pltpu.SemaphoreType.DMA((n_sec,)),
        pltpu.SemaphoreType.DMA((n_sec,)),
    ] if final else []) + [
        pltpu.SemaphoreType.DMA((slots + n_op,)),
        pltpu.SemaphoreType.DMA((slots,)),
        pltpu.SemaphoreType.DMA((5,)),
    ]
    vmem = pl.BlockSpec(memory_space=pltpu.VMEM)
    window = pl.pallas_call(
        functools.partial(step_kernel, n_sec, n_op, count, final),
        out_shape=jax.ShapeDtypeStruct((slots, rows, shape[2]), jnp.bfloat16),
        in_specs=[vmem, vmem, vmem],
        out_specs=vmem,
        scratch_shapes=scratch,
        compiler_params=pltpu.CompilerParams(
            collective_id=3 if final else 2, has_side_effects=True
        ),
    )(chunks, state_chunks, shift_chunks)
    return window.reshape(slots // (n_op // shape[0]), shape[1], shape[2])


def shifted(block, axis, distance):
    devices = range(lax.axis_size(axis))
    route = [((i - distance) % len(devices), i) for i in devices]
    return lax.ppermute(block, axis, route)


def per_device(state_start, left_ops, right_ops, shift, partner, kept):
    sector_local = state_start.shape[0]
    width = state_start.shape[1]
    count = float(sector_local * lax.axis_size("sec") * width * width)
    n_sec = lax.axis_size("sec")
    n_op = lax.axis_size("op")
    left_prev = shifted(left_ops, "sec", 1)
    kept_prev = shifted(kept, "sec", 1)
    state = state_start
    window = padded(state, (("sec", 0),), sector_local)
    for iteration in range(ITERS):
        sources = window[partner]
        halfway = jnp.einsum(
            "tbij,tbjk->tbik", left_ops, sources, preferred_element_type=jnp.float32
        ).astype(jnp.bfloat16)
        partial_sigma = jnp.einsum(
            "tbij,tbjk->bik", halfway, right_ops, preferred_element_type=jnp.float32
        )
        final = iteration == ITERS - 1
        window = step(partial_sigma, state, shift, count, final, n_sec, n_op)
        state = window[sector_local : 2 * sector_local]
    state_prev = window[:sector_local]
    columns = jnp.arange(width, dtype=jnp.int32)
    keep_mask = (columns[None, :] < kept_prev[:, None]).astype(jnp.bfloat16)
    kept_block = state_prev * keep_mask[:, None, :]
    out_scale = 1.0 / float(width) ** 0.5
    projected = jnp.einsum(
        "tbij,bjk->tbik", left_prev, kept_block, preferred_element_type=jnp.float32
    ).astype(jnp.bfloat16)
    kept_turned = jnp.broadcast_to(
        jnp.swapaxes(kept_block, 1, 2)[None], left_prev.shape
    )
    new_ops = (
        jnp.einsum("tbij,tbjk->tbik", kept_turned, projected, preferred_element_type=jnp.float32)
        * out_scale
    ).astype(jnp.bfloat16)
    return (state, new_ops)


def solution(mesh):
    in_specs = (
        P("sec", None, None),
        P("op", "sec", None, None),
        P("op", "sec", None, None),
        P("sec"),
        P("op", "sec"),
        P("sec"),
    )
    out_specs = (P("sec", None, None), P("op", "sec", None, None))
    return jax.shard_map(
        per_device, mesh=mesh, in_specs=in_specs, out_specs=out_specs, check_vma=False
    )
```

```python
import functools

import jax
import jax.numpy as jnp
from jax import lax
from jax.experimental import pallas as pl
from jax.experimental.pallas import tpu as pltpu
from jax.sharding import PartitionSpec as P

MESH = pl.DeviceIdType.MESH

ITERS = 4


step_size = 0.5


def padded(cells, sides, width):
    for axis, dim in sides:
        count = lax.axis_size(axis)
        head = lax.slice_in_dim(cells, 0, width, axis=dim)
        tail = lax.slice_in_dim(cells, cells.shape[dim] - width, cells.shape[dim], axis=dim)
        cells = jnp.concatenate(
            [
                lax.ppermute(tail, axis, [(i, (i + 1) % count) for i in range(count)]),
                cells,
                lax.ppermute(head, axis, [((i + 1) % count, i) for i in range(count)]),
            ],
            axis=dim,
        )
    return cells


def all_sum_kernel(n_sec, n_op, x_ref, o_ref, op_buf, sec_buf, mid, out_buf,
                   send_a, recv_a, send_b, recv_b, local_sem):
    me_sec = lax.axis_index("sec")
    me_op = lax.axis_index("op")
    barrier = pltpu.get_barrier_semaphore()
    for d in range(1, n_op):
        pl.semaphore_signal(barrier, 1, device_id=(me_sec, (me_op + d) % n_op),
                            device_id_type=MESH)
    for d in range(1, n_sec):
        pl.semaphore_signal(barrier, 1, device_id=((me_sec + d) % n_sec, me_op),
                            device_id_type=MESH)
    pl.semaphore_wait(barrier, n_op - 1 + n_sec - 1)

    def stage(n, me, src, buf, send, recv, peer_of):
        for d in range(1, n):
            pltpu.make_async_remote_copy(
                src_ref=src, dst_ref=buf.at[me], send_sem=send.at[d],
                recv_sem=recv.at[me], device_id=peer_of((me + d) % n),
                device_id_type=MESH).start()
        buf[me] = src[...]
        for d in range(1, n):
            slot = (me + n - d) % n
            pltpu.make_async_remote_copy(
                src_ref=src, dst_ref=buf.at[slot], send_sem=send.at[d],
                recv_sem=recv.at[slot], device_id=peer_of(slot),
                device_id_type=MESH).wait_recv()
        for d in range(1, n):
            pltpu.make_async_remote_copy(
                src_ref=src, dst_ref=buf.at[me], send_sem=send.at[d],
                recv_sem=recv.at[me], device_id=peer_of((me + d) % n),
                device_id_type=MESH).wait_send()
        total = buf[0]
        for j in range(1, n):
            total = total + buf[j]
        return total

    mid[...] = stage(n_op, me_op, x_ref, op_buf, send_a, recv_a,
                     lambda j: (me_sec, j))
    local = pltpu.make_async_copy(mid, out_buf, local_sem)
    local.start()
    local.wait()
    o_ref[...] = stage(n_sec, me_sec, out_buf, sec_buf, send_b, recv_b,
                       lambda j: (j, me_op))


def all_sum(values, n_sec, n_op):
    lane = lax.broadcasted_iota(jnp.int32, (8, 128), 1)
    tile = jnp.zeros((8, 128), jnp.float32)
    for k, v in enumerate(values):
        tile = jnp.where(lane == k, v, tile)
    tile_spec = pl.BlockSpec(memory_space=pltpu.VMEM)
    out = pl.pallas_call(
        functools.partial(all_sum_kernel, n_sec, n_op),
        out_shape=jax.ShapeDtypeStruct((8, 128), jnp.float32),
        in_specs=[tile_spec],
        out_specs=tile_spec,
        scratch_shapes=[
            pltpu.VMEM((n_op, 8, 128), jnp.float32),
            pltpu.VMEM((n_sec, 8, 128), jnp.float32),
            pltpu.VMEM((8, 128), jnp.float32),
            pltpu.VMEM((8, 128), jnp.float32),
            pltpu.SemaphoreType.DMA((n_op,)),
            pltpu.SemaphoreType.DMA((n_op,)),
            pltpu.SemaphoreType.DMA((n_sec,)),
            pltpu.SemaphoreType.DMA((n_sec,)),
            pltpu.SemaphoreType.DMA(()),
        ],
        compiler_params=pltpu.CompilerParams(collective_id=0, has_side_effects=True),
    )(tile)
    return tuple(out[0, k] for k in range(len(values)))


def sigma_sum_kernel(n_sec, n_op, x_ref, t_ref, o_ref, s_ref,
                     rs_buf, red, red_out, ag_buf, op_buf, sec_buf, mid, mid_out,
                     send_rs, recv_rs, send_ag, recv_ag, send_a, recv_a,
                     send_b, recv_b, local_sem):
    me_sec = lax.axis_index("sec")
    me_op = lax.axis_index("op")
    barrier = pltpu.get_barrier_semaphore()
    for d in range(1, n_op):
        pl.semaphore_signal(barrier, 1, device_id=(me_sec, (me_op + d) % n_op),
                            device_id_type=MESH)
    for d in range(1, n_sec):
        pl.semaphore_signal(barrier, 1, device_id=((me_sec + d) % n_sec, me_op),
                            device_id_type=MESH)
    pl.semaphore_wait(barrier, n_op - 1 + n_sec - 1)

    def op_peer(j):
        return (me_sec, j)

    def sec_peer(j):
        return (j, me_op)

    def total_of(v):
        return jnp.sum(jnp.sum(v, axis=1, keepdims=True), axis=0, keepdims=True)

    lane = lax.broadcasted_iota(jnp.int32, (8, 128), 1)
    own = st_ref[me_op].astype(jnp.float32)
    own_square = total_of(own * own)
    energy = sh_ref[me_op] * own_square
    for j in range(n_op):
        energy = energy + total_of(x_ref[j] * st_ref[j].astype(jnp.float32))
    t_ref[...] = jnp.where(lane == 0, energy, jnp.where(lane == 1, own_square, 0.0))
    settle(t_ref, t_out, local_sem.at[4])

    def rs_copy(d):
        j = (me_op + d) % n_op
        return pltpu.make_async_remote_copy(
            src_ref=x_ref.at[j], dst_ref=rs_buf.at[me_op], send_sem=send_rs.at[d],
            recv_sem=recv_rs.at[me_op], device_id=op_peer(j), device_id_type=MESH)

    def rs_recv(d):
        slot = (me_op + n_op - d) % n_op
        return pltpu.make_async_remote_copy(
            src_ref=x_ref.at[me_op], dst_ref=rs_buf.at[slot], send_sem=send_rs.at[d],
            recv_sem=recv_rs.at[slot], device_id=op_peer(slot), device_id_type=MESH)

    def gather_copy(n, me, src, buf, send, recv, peer_of, d):
        return pltpu.make_async_remote_copy(
            src_ref=src, dst_ref=buf.at[me], send_sem=send.at[d],
            recv_sem=recv.at[me], device_id=peer_of((me + d) % n), device_id_type=MESH)

    def gather_recv(n, me, src, buf, send, recv, peer_of, d):
        slot = (me + n - d) % n
        return pltpu.make_async_remote_copy(
            src_ref=src, dst_ref=buf.at[slot], send_sem=send.at[d],
            recv_sem=recv.at[slot], device_id=peer_of(slot), device_id_type=MESH)

    def ordered_sum(buf, n):
        total = buf[0]
        for j in range(1, n):
            total = total + buf[j]
        return total

    for d in range(1, n_op):
        rs_copy(d).start()
    a_args = (n_op, me_op, t_out, op_buf, send_a, recv_a, op_peer)
    for d in range(1, n_op):
        gather_copy(*a_args, d).start()
    rs_buf[me_op] = x_ref[me_op]
    op_buf[me_op] = t_ref[...]

    for d in range(1, n_op):
        gather_recv(*a_args, d).wait_recv()
    mid[...] = ordered_sum(op_buf, n_op)
    local = pltpu.make_async_copy(mid, mid_out, local_sem.at[0])
    local.start()
    local.wait()
    b_args = (n_sec, me_sec, mid_out, sec_buf, send_b, recv_b, sec_peer)
    for d in range(1, n_sec):
        gather_copy(*b_args, d).start()
    sec_buf[me_sec] = mid_out[...]

    for d in range(1, n_op):
        rs_recv(d).wait_recv()
    red[...] = ordered_sum(rs_buf, n_op)
    local = pltpu.make_async_copy(red, red_out, local_sem.at[1])
    local.start()
    local.wait()
    g_args = (n_op, me_op, red_out, ag_buf, send_ag, recv_ag, op_peer)
    for d in range(1, n_op):
        gather_copy(*g_args, d).start()
    ag_buf[me_op] = red_out[...]

    for d in range(1, n_sec):
        gather_recv(*b_args, d).wait_recv()
    s_ref[...] = ordered_sum(sec_buf, n_sec)
    for d in range(1, n_op):
        gather_recv(*g_args, d).wait_recv()
    o_ref[...] = ag_buf[...]

    for d in range(1, n_op):
        rs_copy(d).wait_send()
        gather_copy(*a_args, d).wait_send()
        gather_copy(*g_args, d).wait_send()
    for d in range(1, n_sec):
        gather_copy(*b_args, d).wait_send()


def sigma_sum(partial, values, n_sec, n_op):
    shape = partial.shape
    rows = shape[0] * shape[1] // n_op
    chunks = partial.reshape(n_op, rows, shape[2])
    lane = lax.broadcasted_iota(jnp.int32, (8, 128), 1)
    tile = jnp.zeros((8, 128), jnp.float32)
    for k, v in enumerate(values):
        tile = jnp.where(lane == k, v, tile)
    vmem = pl.BlockSpec(memory_space=pltpu.VMEM)
    total, sums = pl.pallas_call(
        functools.partial(sigma_sum_kernel, n_sec, n_op),
        out_shape=(
            jax.ShapeDtypeStruct(chunks.shape, jnp.float32),
            jax.ShapeDtypeStruct((8, 128), jnp.float32),
        ),
        in_specs=[vmem, vmem],
        out_specs=(vmem, vmem),
        scratch_shapes=[
            pltpu.VMEM(chunks.shape, jnp.float32),
            pltpu.VMEM((rows, shape[2]), jnp.float32),
            pltpu.VMEM((rows, shape[2]), jnp.float32),
            pltpu.VMEM(chunks.shape, jnp.float32),
            pltpu.VMEM((n_op, 8, 128), jnp.float32),
            pltpu.VMEM((n_sec, 8, 128), jnp.float32),
            pltpu.VMEM((8, 128), jnp.float32),
            pltpu.VMEM((8, 128), jnp.float32),
            pltpu.SemaphoreType.DMA((n_op,)),
            pltpu.SemaphoreType.DMA((n_op,)),
            pltpu.SemaphoreType.DMA((n_op,)),
            pltpu.SemaphoreType.DMA((n_op,)),
            pltpu.SemaphoreType.DMA((n_op,)),
            pltpu.SemaphoreType.DMA((n_op,)),
            pltpu.SemaphoreType.DMA((n_sec,)),
            pltpu.SemaphoreType.DMA((n_sec,)),
            pltpu.SemaphoreType.DMA((2,)),
        ],
        compiler_params=pltpu.CompilerParams(collective_id=1, has_side_effects=True),
    )(chunks, tile)
    return total.reshape(shape), tuple(sums[0, k] for k in range(len(values)))


def step_kernel(n_sec, n_op, count, final, x_ref, st_ref, sh_ref, *refs):
    if final:
        (win_ref, t_ref, t_out, rs_buf, red, op_buf, sec_buf, mid, mid_out, op_buf2,
         sec_buf2, mid2, mid2_out, mid3, mid3_out, new_buf, new_out, win_buf, send_rs, recv_rs, send_a,
         recv_a, send_b, recv_b, send_a2, recv_a2, send_b2, recv_b2, send_w,
         recv_w, local_sem) = refs
    else:
        (win_ref, t_ref, t_out, rs_buf, red, op_buf, sec_buf, mid, mid_out, new_buf,
         new_out, win_buf, send_rs, recv_rs, send_a, recv_a, send_b, recv_b, send_w,
         recv_w, local_sem) = refs
    me_sec = lax.axis_index("sec")
    me_op = lax.axis_index("op")
    prev_sec = (me_sec + n_sec - 1) % n_sec
    next_sec = (me_sec + 1) % n_sec
    barrier = pltpu.get_barrier_semaphore()
    greeted = 0
    for d in range(1, n_op):
        pl.semaphore_signal(barrier, 1, device_id=(me_sec, (me_op + d) % n_op),
                            device_id_type=MESH)
        greeted += 1
    for d in range(1, n_sec):
        pl.semaphore_signal(barrier, 1, device_id=((me_sec + d) % n_sec, me_op),
                            device_id_type=MESH)
        greeted += 1
    for side in (prev_sec, next_sec):
        for d in range(1, n_op):
            pl.semaphore_signal(barrier, 1, device_id=(side, (me_op + d) % n_op),
                                device_id_type=MESH)
            greeted += 1
    pl.semaphore_wait(barrier, greeted)

    def op_peer(j):
        return (me_sec, j)

    def sec_peer(j):
        return (j, me_op)

    def copy_to(src, dst, send, recv, peer):
        return pltpu.make_async_remote_copy(
            src_ref=src, dst_ref=dst, send_sem=send, recv_sem=recv,
            device_id=peer, device_id_type=MESH)

    def ordered_sum(buf, n):
        total = buf[0]
        for j in range(1, n):
            total = total + buf[j]
        return total

    def start_gather(n, me, src, buf, send, recv, peer_of):
        for d in range(1, n):
            copy_to(src, buf.at[me], send.at[d], recv.at[me], peer_of((me + d) % n)).start()
        buf[me] = src[...]

    def wait_gather(n, me, src, buf, send, recv, peer_of):
        for d in range(1, n):
            slot = (me + n - d) % n
            copy_to(src, buf.at[slot], send.at[d], recv.at[slot], peer_of(slot)).wait_recv()

    def drain_gather(n, me, src, buf, send, recv, peer_of):
        for d in range(1, n):
            copy_to(src, buf.at[me], send.at[d], recv.at[me], peer_of((me + d) % n)).wait_send()

    def settle(src, dst, sem):
        local = pltpu.make_async_copy(src, dst, sem)
        local.start()
        local.wait()

    def total_of(v):
        return jnp.sum(jnp.sum(v, axis=1, keepdims=True), axis=0, keepdims=True)

    lane = lax.broadcasted_iota(jnp.int32, (8, 128), 1)
    own = st_ref[me_op].astype(jnp.float32)
    own_square = total_of(own * own)
    energy = sh_ref[me_op] * own_square
    for j in range(n_op):
        energy = energy + total_of(x_ref[j] * st_ref[j].astype(jnp.float32))
    t_ref[...] = jnp.where(lane == 0, energy, jnp.where(lane == 1, own_square, 0.0))
    settle(t_ref, t_out, local_sem.at[4])

    def rs_copy(d):
        j = (me_op + d) % n_op
        return copy_to(x_ref.at[j], rs_buf.at[me_op], send_rs.at[d], recv_rs.at[me_op], op_peer(j))

    for d in range(1, n_op):
        rs_copy(d).start()
    a_args = (n_op, me_op, t_out, op_buf, send_a, recv_a, op_peer)
    start_gather(*a_args)
    rs_buf[me_op] = x_ref[me_op]

    wait_gather(*a_args)
    mid[...] = ordered_sum(op_buf, n_op)
    settle(mid, mid_out, local_sem.at[0])
    b_args = (n_sec, me_sec, mid_out, sec_buf, send_b, recv_b, sec_peer)
    start_gather(*b_args)

    for d in range(1, n_op):
        slot = (me_op + n_op - d) % n_op
        copy_to(x_ref.at[me_op], rs_buf.at[slot], send_rs.at[d], recv_rs.at[slot],
                op_peer(slot)).wait_recv()
    red[...] = ordered_sum(rs_buf, n_op)

    wait_gather(*b_args)
    sums = ordered_sum(sec_buf, n_sec)
    energy_sum = sums[0:1, 0:1]
    norm_sum = sums[0:1, 1:2]
    state_wide = st_ref[me_op].astype(jnp.float32)
    sigma = red[...] + sh_ref[me_op] * state_wide
    updated = state_wide - step_size * (sigma - (energy_sum / norm_sum) * state_wide)
    if final:
        square = total_of(updated * updated)
        mid2[...] = jnp.where(lane == 0, square, 0.0)
        settle(mid2, mid2_out, local_sem.at[1])
        a2_args = (n_op, me_op, mid2_out, op_buf2, send_a2, recv_a2, op_peer)
        start_gather(*a2_args)
        wait_gather(*a2_args)
        mid3[...] = ordered_sum(op_buf2, n_op)
        settle(mid3, mid3_out, local_sem.at[3])
        b2_args = (n_sec, me_sec, mid3_out, sec_buf2, send_b2, recv_b2, sec_peer)
        start_gather(*b2_args)
        wait_gather(*b2_args)
        new_norm = ordered_sum(sec_buf2, n_sec)[0:1, 0:1]
        factor = jnp.sqrt(count / new_norm)
    else:
        factor = jnp.sqrt(count / norm_sum)
    new_buf[...] = (updated * factor).astype(new_buf.dtype)
    settle(new_buf, new_out, local_sem.at[2])

    sides = ((next_sec, 0),) if final else ((next_sec, 0), (prev_sec, 2 * n_op))
    sent = 0
    for side, base in sides:
        for j in range(n_op):
            copy_to(new_out, win_buf.at[base + me_op], send_w.at[sent],
                    recv_w.at[base + me_op], (side, j)).start()
            sent += 1
    for d in range(1, n_op):
        j = (me_op + d) % n_op
        copy_to(new_out, win_buf.at[n_op + me_op], send_w.at[sent],
                recv_w.at[n_op + me_op], op_peer(j)).start()
        sent += 1
    win_buf[n_op + me_op] = new_out[...]

    from_sides = ((prev_sec, 0),) if final else ((prev_sec, 0), (next_sec, 2 * n_op))
    for side, base in from_sides:
        for j in range(n_op):
            copy_to(new_out, win_buf.at[base + j], send_w.at[0], recv_w.at[base + j],
                    (side, j)).wait_recv()
    for d in range(1, n_op):
        slot = (me_op + n_op - d) % n_op
        copy_to(new_out, win_buf.at[n_op + slot], send_w.at[0], recv_w.at[n_op + slot],
                op_peer(slot)).wait_recv()
    win_ref[...] = win_buf[...]

    for d in range(1, n_op):
        rs_copy(d).wait_send()
    drain_gather(*a_args)
    drain_gather(*b_args)
    if final:
        drain_gather(*a2_args)
        drain_gather(*b2_args)
    for k in range(sent):
        copy_to(new_out, win_buf.at[n_op + me_op], send_w.at[k], recv_w.at[n_op + me_op],
                op_peer((me_op + 1) % n_op)).wait_send()


def step(partial, state, shift, count, final, n_sec, n_op):
    shape = partial.shape
    rows = shape[0] * shape[1] // n_op
    chunks = partial.reshape(n_op, rows, shape[2])
    state_chunks = state.reshape(n_op, rows, shape[2])
    shift_chunks = jnp.repeat(shift, n_op // shape[0])[:, None, None]
    slots = (2 if final else 3) * n_op
    tile_shape = (rows, shape[2])
    scalar_bufs = [
        pltpu.VMEM((n_op, 8, 128), jnp.float32),
        pltpu.VMEM((n_sec, 8, 128), jnp.float32),
        pltpu.VMEM((8, 128), jnp.float32),
        pltpu.VMEM((8, 128), jnp.float32),
    ]
    scratch = [
        pltpu.VMEM((8, 128), jnp.float32),
        pltpu.VMEM((8, 128), jnp.float32),
        pltpu.VMEM(chunks.shape, jnp.float32),
        pltpu.VMEM(tile_shape, jnp.float32),
    ] + scalar_bufs + (scalar_bufs + scalar_bufs[2:] if final else []) + [
        pltpu.VMEM(tile_shape, jnp.bfloat16),
        pltpu.VMEM(tile_shape, jnp.bfloat16),
        pltpu.VMEM((slots, rows, shape[2]), jnp.bfloat16),
        pltpu.SemaphoreType.DMA((n_op,)),
        pltpu.SemaphoreType.DMA((n_op,)),
        pltpu.SemaphoreType.DMA((n_op,)),
        pltpu.SemaphoreType.DMA((n_op,)),
        pltpu.SemaphoreType.DMA((n_sec,)),
        pltpu.SemaphoreType.DMA((n_sec,)),
    ] + ([
        pltpu.SemaphoreType.DMA((n_op,)),
        pltpu.SemaphoreType.DMA((n_op,)),
        pltpu.SemaphoreType.DMA((n_sec,)),
        pltpu.SemaphoreType.DMA((n_sec,)),
    ] if final else []) + [
        pltpu.SemaphoreType.DMA((slots + n_op,)),
        pltpu.SemaphoreType.DMA((slots,)),
        pltpu.SemaphoreType.DMA((5,)),
    ]
    vmem = pl.BlockSpec(memory_space=pltpu.VMEM)
    window = pl.pallas_call(
        functools.partial(step_kernel, n_sec, n_op, count, final),
        out_shape=jax.ShapeDtypeStruct((slots, rows, shape[2]), jnp.bfloat16),
        in_specs=[vmem, vmem, vmem],
        out_specs=vmem,
        scratch_shapes=scratch,
        compiler_params=pltpu.CompilerParams(
            collective_id=3 if final else 2, has_side_effects=True
        ),
    )(chunks, state_chunks, shift_chunks)
    return window.reshape(slots // (n_op // shape[0]), shape[1], shape[2])


def shifted(block, axis, distance):
    devices = range(lax.axis_size(axis))
    route = [((i - distance) % len(devices), i) for i in devices]
    return lax.ppermute(block, axis, route)


def per_device(state_start, left_ops, right_ops, shift, partner, kept):
    sector_local = state_start.shape[0]
    width = state_start.shape[1]
    count = float(sector_local * lax.axis_size("sec") * width * width)
    n_sec = lax.axis_size("sec")
    n_op = lax.axis_size("op")
    kept_prev = shifted(kept, "sec", 1)
    terms = left_ops.shape[0]
    cuts = [terms * k // ITERS for k in range(ITERS + 1)]
    left_pieces = []
    state = state_start
    window = padded(state, (("sec", 0),), sector_local)
    for iteration in range(ITERS):
        piece, window = lax.optimization_barrier(
            (left_ops[cuts[iteration] : cuts[iteration + 1]], window)
        )
        left_pieces.append(shifted(piece, "sec", 1))
        sources = window[partner]
        halfway = jnp.einsum(
            "tbij,tbjk->tbik", left_ops, sources, preferred_element_type=jnp.float32
        ).astype(jnp.bfloat16)
        partial_sigma = jnp.einsum(
            "tbij,tbjk->bik", halfway, right_ops, preferred_element_type=jnp.float32
        )
        final = iteration == ITERS - 1
        left_pieces[-1], partial_sigma = lax.optimization_barrier(
            (left_pieces[-1], partial_sigma)
        )
        window = step(partial_sigma, state, shift, count, final, n_sec, n_op)
        state = window[sector_local : 2 * sector_local]
    state_prev = window[:sector_local]
    left_prev = jnp.concatenate(left_pieces, axis=0)
    columns = jnp.arange(width, dtype=jnp.int32)
    keep_mask = (columns[None, :] < kept_prev[:, None]).astype(jnp.bfloat16)
    kept_block = state_prev * keep_mask[:, None, :]
    out_scale = 1.0 / float(width) ** 0.5
    projected = jnp.einsum(
        "tbij,bjk->tbik", left_prev, kept_block, preferred_element_type=jnp.float32
    ).astype(jnp.bfloat16)
    kept_turned = jnp.broadcast_to(
        jnp.swapaxes(kept_block, 1, 2)[None], left_prev.shape
    )
    new_ops = (
        jnp.einsum("tbij,tbjk->tbik", kept_turned, projected, preferred_element_type=jnp.float32)
        * out_scale
    ).astype(jnp.bfloat16)
    return (state, new_ops)


def solution(mesh):
    in_specs = (
        P("sec", None, None),
        P("op", "sec", None, None),
        P("op", "sec", None, None),
        P("sec"),
        P("op", "sec"),
        P("sec"),
    )
    out_specs = (P("sec", None, None), P("op", "sec", None, None))
    return jax.shard_map(
        per_device, mesh=mesh, in_specs=in_specs, out_specs=out_specs, check_vma=False
    )
```

```python
import functools

import jax
import jax.numpy as jnp
from jax import lax
from jax.experimental import pallas as pl
from jax.experimental.pallas import tpu as pltpu
from jax.sharding import PartitionSpec as P

MESH = pl.DeviceIdType.MESH

ITERS = 4


step_size = 0.5


def padded(cells, sides, width):
    for axis, dim in sides:
        count = lax.axis_size(axis)
        head = lax.slice_in_dim(cells, 0, width, axis=dim)
        tail = lax.slice_in_dim(cells, cells.shape[dim] - width, cells.shape[dim], axis=dim)
        cells = jnp.concatenate(
            [
                lax.ppermute(tail, axis, [(i, (i + 1) % count) for i in range(count)]),
                cells,
                lax.ppermute(head, axis, [((i + 1) % count, i) for i in range(count)]),
            ],
            axis=dim,
        )
    return cells


def all_sum_kernel(n_sec, n_op, x_ref, o_ref, op_buf, sec_buf, mid, out_buf,
                   send_a, recv_a, send_b, recv_b, local_sem):
    me_sec = lax.axis_index("sec")
    me_op = lax.axis_index("op")
    barrier = pltpu.get_barrier_semaphore()
    for d in range(1, n_op):
        pl.semaphore_signal(barrier, 1, device_id=(me_sec, (me_op + d) % n_op),
                            device_id_type=MESH)
    for d in range(1, n_sec):
        pl.semaphore_signal(barrier, 1, device_id=((me_sec + d) % n_sec, me_op),
                            device_id_type=MESH)
    pl.semaphore_wait(barrier, n_op - 1 + n_sec - 1)

    def stage(n, me, src, buf, send, recv, peer_of):
        for d in range(1, n):
            pltpu.make_async_remote_copy(
                src_ref=src, dst_ref=buf.at[me], send_sem=send.at[d],
                recv_sem=recv.at[me], device_id=peer_of((me + d) % n),
                device_id_type=MESH).start()
        buf[me] = src[...]
        for d in range(1, n):
            slot = (me + n - d) % n
            pltpu.make_async_remote_copy(
                src_ref=src, dst_ref=buf.at[slot], send_sem=send.at[d],
                recv_sem=recv.at[slot], device_id=peer_of(slot),
                device_id_type=MESH).wait_recv()
        for d in range(1, n):
            pltpu.make_async_remote_copy(
                src_ref=src, dst_ref=buf.at[me], send_sem=send.at[d],
                recv_sem=recv.at[me], device_id=peer_of((me + d) % n),
                device_id_type=MESH).wait_send()
        total = buf[0]
        for j in range(1, n):
            total = total + buf[j]
        return total

    mid[...] = stage(n_op, me_op, x_ref, op_buf, send_a, recv_a,
                     lambda j: (me_sec, j))
    local = pltpu.make_async_copy(mid, out_buf, local_sem)
    local.start()
    local.wait()
    o_ref[...] = stage(n_sec, me_sec, out_buf, sec_buf, send_b, recv_b,
                       lambda j: (j, me_op))


def all_sum(values, n_sec, n_op):
    lane = lax.broadcasted_iota(jnp.int32, (8, 128), 1)
    tile = jnp.zeros((8, 128), jnp.float32)
    for k, v in enumerate(values):
        tile = jnp.where(lane == k, v, tile)
    tile_spec = pl.BlockSpec(memory_space=pltpu.VMEM)
    out = pl.pallas_call(
        functools.partial(all_sum_kernel, n_sec, n_op),
        out_shape=jax.ShapeDtypeStruct((8, 128), jnp.float32),
        in_specs=[tile_spec],
        out_specs=tile_spec,
        scratch_shapes=[
            pltpu.VMEM((n_op, 8, 128), jnp.float32),
            pltpu.VMEM((n_sec, 8, 128), jnp.float32),
            pltpu.VMEM((8, 128), jnp.float32),
            pltpu.VMEM((8, 128), jnp.float32),
            pltpu.SemaphoreType.DMA((n_op,)),
            pltpu.SemaphoreType.DMA((n_op,)),
            pltpu.SemaphoreType.DMA((n_sec,)),
            pltpu.SemaphoreType.DMA((n_sec,)),
            pltpu.SemaphoreType.DMA(()),
        ],
        compiler_params=pltpu.CompilerParams(collective_id=0, has_side_effects=True),
    )(tile)
    return tuple(out[0, k] for k in range(len(values)))


def sigma_sum_kernel(n_sec, n_op, x_ref, t_ref, o_ref, s_ref,
                     rs_buf, red, red_out, ag_buf, op_buf, sec_buf, mid, mid_out,
                     send_rs, recv_rs, send_ag, recv_ag, send_a, recv_a,
                     send_b, recv_b, local_sem):
    me_sec = lax.axis_index("sec")
    me_op = lax.axis_index("op")
    barrier = pltpu.get_barrier_semaphore()
    for d in range(1, n_op):
        pl.semaphore_signal(barrier, 1, device_id=(me_sec, (me_op + d) % n_op),
                            device_id_type=MESH)
    for d in range(1, n_sec):
        pl.semaphore_signal(barrier, 1, device_id=((me_sec + d) % n_sec, me_op),
                            device_id_type=MESH)
    pl.semaphore_wait(barrier, n_op - 1 + n_sec - 1)

    def op_peer(j):
        return (me_sec, j)

    def sec_peer(j):
        return (j, me_op)

    def total_of(v):
        return jnp.sum(jnp.sum(v, axis=1, keepdims=True), axis=0, keepdims=True)

    lane = lax.broadcasted_iota(jnp.int32, (8, 128), 1)
    own = st_ref[n_op + me_op].astype(jnp.float32)
    own_square = total_of(own * own)
    energy = sh_ref[me_op] * own_square
    for j in range(n_op):
        energy = energy + total_of(x_ref[j] * st_ref[n_op + j].astype(jnp.float32))
    t_ref[...] = jnp.where(lane == 0, energy, jnp.where(lane == 1, own_square, 0.0))
    settle(t_ref, t_out, local_sem.at[4])

    def rs_copy(d):
        j = (me_op + d) % n_op
        return pltpu.make_async_remote_copy(
            src_ref=x_ref.at[j], dst_ref=rs_buf.at[me_op], send_sem=send_rs.at[d],
            recv_sem=recv_rs.at[me_op], device_id=op_peer(j), device_id_type=MESH)

    def rs_recv(d):
        slot = (me_op + n_op - d) % n_op
        return pltpu.make_async_remote_copy(
            src_ref=x_ref.at[me_op], dst_ref=rs_buf.at[slot], send_sem=send_rs.at[d],
            recv_sem=recv_rs.at[slot], device_id=op_peer(slot), device_id_type=MESH)

    def gather_copy(n, me, src, buf, send, recv, peer_of, d):
        return pltpu.make_async_remote_copy(
            src_ref=src, dst_ref=buf.at[me], send_sem=send.at[d],
            recv_sem=recv.at[me], device_id=peer_of((me + d) % n), device_id_type=MESH)

    def gather_recv(n, me, src, buf, send, recv, peer_of, d):
        slot = (me + n - d) % n
        return pltpu.make_async_remote_copy(
            src_ref=src, dst_ref=buf.at[slot], send_sem=send.at[d],
            recv_sem=recv.at[slot], device_id=peer_of(slot), device_id_type=MESH)

    def ordered_sum(buf, n):
        total = buf[0]
        for j in range(1, n):
            total = total + buf[j]
        return total

    for d in range(1, n_op):
        rs_copy(d).start()
    a_args = (n_op, me_op, t_out, op_buf, send_a, recv_a, op_peer)
    for d in range(1, n_op):
        gather_copy(*a_args, d).start()
    rs_buf[me_op] = x_ref[me_op]
    op_buf[me_op] = t_ref[...]

    for d in range(1, n_op):
        gather_recv(*a_args, d).wait_recv()
    mid[...] = ordered_sum(op_buf, n_op)
    local = pltpu.make_async_copy(mid, mid_out, local_sem.at[0])
    local.start()
    local.wait()
    b_args = (n_sec, me_sec, mid_out, sec_buf, send_b, recv_b, sec_peer)
    for d in range(1, n_sec):
        gather_copy(*b_args, d).start()
    sec_buf[me_sec] = mid_out[...]

    for d in range(1, n_op):
        rs_recv(d).wait_recv()
    red[...] = ordered_sum(rs_buf, n_op)
    local = pltpu.make_async_copy(red, red_out, local_sem.at[1])
    local.start()
    local.wait()
    g_args = (n_op, me_op, red_out, ag_buf, send_ag, recv_ag, op_peer)
    for d in range(1, n_op):
        gather_copy(*g_args, d).start()
    ag_buf[me_op] = red_out[...]

    for d in range(1, n_sec):
        gather_recv(*b_args, d).wait_recv()
    s_ref[...] = ordered_sum(sec_buf, n_sec)
    for d in range(1, n_op):
        gather_recv(*g_args, d).wait_recv()
    o_ref[...] = ag_buf[...]

    for d in range(1, n_op):
        rs_copy(d).wait_send()
        gather_copy(*a_args, d).wait_send()
        gather_copy(*g_args, d).wait_send()
    for d in range(1, n_sec):
        gather_copy(*b_args, d).wait_send()


def sigma_sum(partial, values, n_sec, n_op):
    shape = partial.shape
    rows = shape[0] * shape[1] // n_op
    chunks = partial.reshape(n_op, rows, shape[2])
    lane = lax.broadcasted_iota(jnp.int32, (8, 128), 1)
    tile = jnp.zeros((8, 128), jnp.float32)
    for k, v in enumerate(values):
        tile = jnp.where(lane == k, v, tile)
    vmem = pl.BlockSpec(memory_space=pltpu.VMEM)
    total, sums = pl.pallas_call(
        functools.partial(sigma_sum_kernel, n_sec, n_op),
        out_shape=(
            jax.ShapeDtypeStruct(chunks.shape, jnp.float32),
            jax.ShapeDtypeStruct((8, 128), jnp.float32),
        ),
        in_specs=[vmem, vmem],
        out_specs=(vmem, vmem),
        scratch_shapes=[
            pltpu.VMEM(chunks.shape, jnp.float32),
            pltpu.VMEM((rows, shape[2]), jnp.float32),
            pltpu.VMEM((rows, shape[2]), jnp.float32),
            pltpu.VMEM(chunks.shape, jnp.float32),
            pltpu.VMEM((n_op, 8, 128), jnp.float32),
            pltpu.VMEM((n_sec, 8, 128), jnp.float32),
            pltpu.VMEM((8, 128), jnp.float32),
            pltpu.VMEM((8, 128), jnp.float32),
            pltpu.SemaphoreType.DMA((n_op,)),
            pltpu.SemaphoreType.DMA((n_op,)),
            pltpu.SemaphoreType.DMA((n_op,)),
            pltpu.SemaphoreType.DMA((n_op,)),
            pltpu.SemaphoreType.DMA((n_op,)),
            pltpu.SemaphoreType.DMA((n_op,)),
            pltpu.SemaphoreType.DMA((n_sec,)),
            pltpu.SemaphoreType.DMA((n_sec,)),
            pltpu.SemaphoreType.DMA((2,)),
        ],
        compiler_params=pltpu.CompilerParams(collective_id=1, has_side_effects=True),
    )(chunks, tile)
    return total.reshape(shape), tuple(sums[0, k] for k in range(len(values)))


def step_kernel(n_sec, n_op, count, final, x_ref, st_ref, sh_ref, *refs):
    if final:
        (win_ref, t_ref, t_out, rs_buf, red, op_buf, sec_buf, mid, mid_out, op_buf2,
         sec_buf2, mid2, mid2_out, mid3, mid3_out, new_buf, new_out, win_buf, send_rs, recv_rs, send_a,
         recv_a, send_b, recv_b, send_a2, recv_a2, send_b2, recv_b2, send_w,
         recv_w, local_sem) = refs
    else:
        (win_ref, t_ref, t_out, rs_buf, red, op_buf, sec_buf, mid, mid_out, new_buf,
         new_out, win_buf, send_rs, recv_rs, send_a, recv_a, send_b, recv_b, send_w,
         recv_w, local_sem) = refs
    me_sec = lax.axis_index("sec")
    me_op = lax.axis_index("op")
    prev_sec = (me_sec + n_sec - 1) % n_sec
    next_sec = (me_sec + 1) % n_sec
    barrier = pltpu.get_barrier_semaphore()
    greeted = 0
    for d in range(1, n_op):
        pl.semaphore_signal(barrier, 1, device_id=(me_sec, (me_op + d) % n_op),
                            device_id_type=MESH)
        greeted += 1
    for d in range(1, n_sec):
        pl.semaphore_signal(barrier, 1, device_id=((me_sec + d) % n_sec, me_op),
                            device_id_type=MESH)
        greeted += 1
    for side in (prev_sec, next_sec):
        for d in range(1, n_op):
            pl.semaphore_signal(barrier, 1, device_id=(side, (me_op + d) % n_op),
                                device_id_type=MESH)
            greeted += 1
    pl.semaphore_wait(barrier, greeted)

    def op_peer(j):
        return (me_sec, j)

    def sec_peer(j):
        return (j, me_op)

    def copy_to(src, dst, send, recv, peer):
        return pltpu.make_async_remote_copy(
            src_ref=src, dst_ref=dst, send_sem=send, recv_sem=recv,
            device_id=peer, device_id_type=MESH)

    def ordered_sum(buf, n):
        total = buf[0]
        for j in range(1, n):
            total = total + buf[j]
        return total

    def start_gather(n, me, src, buf, send, recv, peer_of):
        for d in range(1, n):
            copy_to(src, buf.at[me], send.at[d], recv.at[me], peer_of((me + d) % n)).start()
        buf[me] = src[...]

    def wait_gather(n, me, src, buf, send, recv, peer_of):
        for d in range(1, n):
            slot = (me + n - d) % n
            copy_to(src, buf.at[slot], send.at[d], recv.at[slot], peer_of(slot)).wait_recv()

    def drain_gather(n, me, src, buf, send, recv, peer_of):
        for d in range(1, n):
            copy_to(src, buf.at[me], send.at[d], recv.at[me], peer_of((me + d) % n)).wait_send()

    def settle(src, dst, sem):
        local = pltpu.make_async_copy(src, dst, sem)
        local.start()
        local.wait()

    def total_of(v):
        return jnp.sum(jnp.sum(v, axis=1, keepdims=True), axis=0, keepdims=True)

    lane = lax.broadcasted_iota(jnp.int32, (8, 128), 1)
    own = st_ref[n_op + me_op].astype(jnp.float32)
    own_square = total_of(own * own)
    energy = sh_ref[me_op] * own_square
    for j in range(n_op):
        energy = energy + total_of(x_ref[j] * st_ref[n_op + j].astype(jnp.float32))
    t_ref[...] = jnp.where(lane == 0, energy, jnp.where(lane == 1, own_square, 0.0))
    settle(t_ref, t_out, local_sem.at[4])

    def rs_copy(d):
        j = (me_op + d) % n_op
        return copy_to(x_ref.at[j], rs_buf.at[me_op], send_rs.at[d], recv_rs.at[me_op], op_peer(j))

    for d in range(1, n_op):
        rs_copy(d).start()
    a_args = (n_op, me_op, t_out, op_buf, send_a, recv_a, op_peer)
    start_gather(*a_args)
    rs_buf[me_op] = x_ref[me_op]

    wait_gather(*a_args)
    mid[...] = ordered_sum(op_buf, n_op)
    settle(mid, mid_out, local_sem.at[0])
    b_args = (n_sec, me_sec, mid_out, sec_buf, send_b, recv_b, sec_peer)
    start_gather(*b_args)

    for d in range(1, n_op):
        slot = (me_op + n_op - d) % n_op
        copy_to(x_ref.at[me_op], rs_buf.at[slot], send_rs.at[d], recv_rs.at[slot],
                op_peer(slot)).wait_recv()
    red[...] = ordered_sum(rs_buf, n_op)

    wait_gather(*b_args)
    sums = ordered_sum(sec_buf, n_sec)
    energy_sum = sums[0:1, 0:1]
    norm_sum = sums[0:1, 1:2]
    state_wide = st_ref[n_op + me_op].astype(jnp.float32)
    sigma = red[...] + sh_ref[me_op] * state_wide
    updated = state_wide - step_size * (sigma - (energy_sum / norm_sum) * state_wide)
    if final:
        square = total_of(updated * updated)
        mid2[...] = jnp.where(lane == 0, square, 0.0)
        settle(mid2, mid2_out, local_sem.at[1])
        a2_args = (n_op, me_op, mid2_out, op_buf2, send_a2, recv_a2, op_peer)
        start_gather(*a2_args)
        wait_gather(*a2_args)
        mid3[...] = ordered_sum(op_buf2, n_op)
        settle(mid3, mid3_out, local_sem.at[3])
        b2_args = (n_sec, me_sec, mid3_out, sec_buf2, send_b2, recv_b2, sec_peer)
        start_gather(*b2_args)
        wait_gather(*b2_args)
        new_norm = ordered_sum(sec_buf2, n_sec)[0:1, 0:1]
        factor = jnp.sqrt(count / new_norm)
    else:
        factor = jnp.sqrt(count / norm_sum)
    new_buf[...] = (updated * factor).astype(new_buf.dtype)
    settle(new_buf, new_out, local_sem.at[2])

    sides = ((next_sec, 0),) if final else ((next_sec, 0), (prev_sec, 2 * n_op))
    sent = 0
    for side, base in sides:
        for j in range(n_op):
            copy_to(new_out, win_buf.at[base + me_op], send_w.at[sent],
                    recv_w.at[base + me_op], (side, j)).start()
            sent += 1
    for d in range(1, n_op):
        j = (me_op + d) % n_op
        copy_to(new_out, win_buf.at[n_op + me_op], send_w.at[sent],
                recv_w.at[n_op + me_op], op_peer(j)).start()
        sent += 1
    win_buf[n_op + me_op] = new_out[...]

    from_sides = ((prev_sec, 0),) if final else ((prev_sec, 0), (next_sec, 2 * n_op))
    for side, base in from_sides:
        for j in range(n_op):
            copy_to(new_out, win_buf.at[base + j], send_w.at[0], recv_w.at[base + j],
                    (side, j)).wait_recv()
    for d in range(1, n_op):
        slot = (me_op + n_op - d) % n_op
        copy_to(new_out, win_buf.at[n_op + slot], send_w.at[0], recv_w.at[n_op + slot],
                op_peer(slot)).wait_recv()
    win_ref[...] = win_buf[...]

    for d in range(1, n_op):
        rs_copy(d).wait_send()
    drain_gather(*a_args)
    drain_gather(*b_args)
    if final:
        drain_gather(*a2_args)
        drain_gather(*b2_args)
    for k in range(sent):
        copy_to(new_out, win_buf.at[n_op + me_op], send_w.at[k], recv_w.at[n_op + me_op],
                op_peer((me_op + 1) % n_op)).wait_send()


def step(partial, window, shift, count, final, n_sec, n_op):
    shape = partial.shape
    rows = shape[0] * shape[1] // n_op
    chunks = partial.reshape(n_op, rows, shape[2])
    state_chunks = window.reshape(-1, rows, shape[2])
    shift_chunks = jnp.repeat(shift, n_op // shape[0])[:, None, None]
    slots = (2 if final else 3) * n_op
    tile_shape = (rows, shape[2])
    scalar_bufs = [
        pltpu.VMEM((n_op, 8, 128), jnp.float32),
        pltpu.VMEM((n_sec, 8, 128), jnp.float32),
        pltpu.VMEM((8, 128), jnp.float32),
        pltpu.VMEM((8, 128), jnp.float32),
    ]
    scratch = [
        pltpu.VMEM((8, 128), jnp.float32),
        pltpu.VMEM((8, 128), jnp.float32),
        pltpu.VMEM(chunks.shape, jnp.float32),
        pltpu.VMEM(tile_shape, jnp.float32),
    ] + scalar_bufs + (scalar_bufs + scalar_bufs[2:] if final else []) + [
        pltpu.VMEM(tile_shape, jnp.bfloat16),
        pltpu.VMEM(tile_shape, jnp.bfloat16),
        pltpu.VMEM((slots, rows, shape[2]), jnp.bfloat16),
        pltpu.SemaphoreType.DMA((n_op,)),
        pltpu.SemaphoreType.DMA((n_op,)),
        pltpu.SemaphoreType.DMA((n_op,)),
        pltpu.SemaphoreType.DMA((n_op,)),
        pltpu.SemaphoreType.DMA((n_sec,)),
        pltpu.SemaphoreType.DMA((n_sec,)),
    ] + ([
        pltpu.SemaphoreType.DMA((n_op,)),
        pltpu.SemaphoreType.DMA((n_op,)),
        pltpu.SemaphoreType.DMA((n_sec,)),
        pltpu.SemaphoreType.DMA((n_sec,)),
    ] if final else []) + [
        pltpu.SemaphoreType.DMA((slots + n_op,)),
        pltpu.SemaphoreType.DMA((slots,)),
        pltpu.SemaphoreType.DMA((5,)),
    ]
    vmem = pl.BlockSpec(memory_space=pltpu.VMEM)
    window = pl.pallas_call(
        functools.partial(step_kernel, n_sec, n_op, count, final),
        out_shape=jax.ShapeDtypeStruct((slots, rows, shape[2]), jnp.bfloat16),
        in_specs=[vmem, vmem, vmem],
        out_specs=vmem,
        scratch_shapes=scratch,
        compiler_params=pltpu.CompilerParams(
            collective_id=3 if final else 2, has_side_effects=True
        ),
    )(chunks, state_chunks, shift_chunks)
    return window.reshape(slots // (n_op // shape[0]), shape[1], shape[2])


def sigma_part_kernel(partner_ref, win_ref, left_ref, right_ref, o_ref):
    b = pl.program_id(0)
    total = jnp.zeros(o_ref.shape[1:], jnp.float32)
    for t in range(left_ref.shape[0]):
        source = win_ref[partner_ref[t, b]]
        halfway = jnp.dot(left_ref[t, 0], source, preferred_element_type=jnp.float32)
        total = total + jnp.dot(halfway.astype(jnp.bfloat16), right_ref[t, 0],
                                preferred_element_type=jnp.float32)
    o_ref[0] = total


def sigma_part(window, left_ops, right_ops, partner):
    terms, sectors, m, _ = left_ops.shape
    op_spec = pl.BlockSpec((terms, 1, m, m), lambda b, p: (0, b, 0, 0))
    return pl.pallas_call(
        sigma_part_kernel,
        out_shape=jax.ShapeDtypeStruct((sectors, m, m), jnp.float32),
        grid_spec=pltpu.PrefetchScalarGridSpec(
            num_scalar_prefetch=1,
            grid=(sectors,),
            in_specs=[
                pl.BlockSpec(window.shape, lambda b, p: (0, 0, 0)),
                op_spec,
                op_spec,
            ],
            out_specs=pl.BlockSpec((1, m, m), lambda b, p: (b, 0, 0)),
        ),
        cost_estimate=pl.CostEstimate(
            flops=4 * terms * sectors * m * m * m,
            bytes_accessed=2 * left_ops.size * 2 + window.size * 2 + sectors * m * m * 4,
            transcendentals=0,
        ),
    )(partner, window, left_ops, right_ops)


def shifted(block, axis, distance):
    devices = range(lax.axis_size(axis))
    route = [((i - distance) % len(devices), i) for i in devices]
    return lax.ppermute(block, axis, route)


def per_device(state_start, left_ops, right_ops, shift, partner, kept):
    sector_local = state_start.shape[0]
    width = state_start.shape[1]
    count = float(sector_local * lax.axis_size("sec") * width * width)
    n_sec = lax.axis_size("sec")
    n_op = lax.axis_size("op")
    left_prev = shifted(left_ops, "sec", 1)
    kept_prev = shifted(kept, "sec", 1)
    state = state_start
    window = padded(state, (("sec", 0),), sector_local)
    for iteration in range(ITERS):
        partial_sigma = sigma_part(window, left_ops, right_ops, partner)
        final = iteration == ITERS - 1
        window = step(partial_sigma, window, shift, count, final, n_sec, n_op)
        state = window[sector_local : 2 * sector_local]
    state_prev = window[:sector_local]
    columns = jnp.arange(width, dtype=jnp.int32)
    keep_mask = (columns[None, :] < kept_prev[:, None]).astype(jnp.bfloat16)
    kept_block = state_prev * keep_mask[:, None, :]
    out_scale = 1.0 / float(width) ** 0.5
    projected = jnp.einsum(
        "tbij,bjk->tbik", left_prev, kept_block, preferred_element_type=jnp.float32
    ).astype(jnp.bfloat16)
    kept_turned = jnp.broadcast_to(
        jnp.swapaxes(kept_block, 1, 2)[None], left_prev.shape
    )
    new_ops = (
        jnp.einsum("tbij,tbjk->tbik", kept_turned, projected, preferred_element_type=jnp.float32)
        * out_scale
    ).astype(jnp.bfloat16)
    return (state, new_ops)


def solution(mesh):
    in_specs = (
        P("sec", None, None),
        P("op", "sec", None, None),
        P("op", "sec", None, None),
        P("sec"),
        P("op", "sec"),
        P("sec"),
    )
    out_specs = (P("sec", None, None), P("op", "sec", None, None))
    return jax.shard_map(
        per_device, mesh=mesh, in_specs=in_specs, out_specs=out_specs, check_vma=False
    )
```

```python
import functools

import jax
import jax.numpy as jnp
from jax import lax
from jax.experimental import pallas as pl
from jax.experimental.pallas import tpu as pltpu
from jax.sharding import PartitionSpec as P

MESH = pl.DeviceIdType.MESH

ITERS = 4


step_size = 0.5


def padded(cells, sides, width):
    for axis, dim in sides:
        count = lax.axis_size(axis)
        head = lax.slice_in_dim(cells, 0, width, axis=dim)
        tail = lax.slice_in_dim(cells, cells.shape[dim] - width, cells.shape[dim], axis=dim)
        cells = jnp.concatenate(
            [
                lax.ppermute(tail, axis, [(i, (i + 1) % count) for i in range(count)]),
                cells,
                lax.ppermute(head, axis, [((i + 1) % count, i) for i in range(count)]),
            ],
            axis=dim,
        )
    return cells


def all_sum_kernel(n_sec, n_op, x_ref, o_ref, op_buf, sec_buf, mid, out_buf,
                   send_a, recv_a, send_b, recv_b, local_sem):
    me_sec = lax.axis_index("sec")
    me_op = lax.axis_index("op")
    barrier = pltpu.get_barrier_semaphore()
    for d in range(1, n_op):
        pl.semaphore_signal(barrier, 1, device_id=(me_sec, (me_op + d) % n_op),
                            device_id_type=MESH)
    for d in range(1, n_sec):
        pl.semaphore_signal(barrier, 1, device_id=((me_sec + d) % n_sec, me_op),
                            device_id_type=MESH)
    pl.semaphore_wait(barrier, n_op - 1 + n_sec - 1)

    def stage(n, me, src, buf, send, recv, peer_of):
        for d in range(1, n):
            pltpu.make_async_remote_copy(
                src_ref=src, dst_ref=buf.at[me], send_sem=send.at[d],
                recv_sem=recv.at[me], device_id=peer_of((me + d) % n),
                device_id_type=MESH).start()
        buf[me] = src[...]
        for d in range(1, n):
            slot = (me + n - d) % n
            pltpu.make_async_remote_copy(
                src_ref=src, dst_ref=buf.at[slot], send_sem=send.at[d],
                recv_sem=recv.at[slot], device_id=peer_of(slot),
                device_id_type=MESH).wait_recv()
        for d in range(1, n):
            pltpu.make_async_remote_copy(
                src_ref=src, dst_ref=buf.at[me], send_sem=send.at[d],
                recv_sem=recv.at[me], device_id=peer_of((me + d) % n),
                device_id_type=MESH).wait_send()
        total = buf[0]
        for j in range(1, n):
            total = total + buf[j]
        return total

    mid[...] = stage(n_op, me_op, x_ref, op_buf, send_a, recv_a,
                     lambda j: (me_sec, j))
    local = pltpu.make_async_copy(mid, out_buf, local_sem)
    local.start()
    local.wait()
    o_ref[...] = stage(n_sec, me_sec, out_buf, sec_buf, send_b, recv_b,
                       lambda j: (j, me_op))


def all_sum(values, n_sec, n_op):
    lane = lax.broadcasted_iota(jnp.int32, (8, 128), 1)
    tile = jnp.zeros((8, 128), jnp.float32)
    for k, v in enumerate(values):
        tile = jnp.where(lane == k, v, tile)
    tile_spec = pl.BlockSpec(memory_space=pltpu.VMEM)
    out = pl.pallas_call(
        functools.partial(all_sum_kernel, n_sec, n_op),
        out_shape=jax.ShapeDtypeStruct((8, 128), jnp.float32),
        in_specs=[tile_spec],
        out_specs=tile_spec,
        scratch_shapes=[
            pltpu.VMEM((n_op, 8, 128), jnp.float32),
            pltpu.VMEM((n_sec, 8, 128), jnp.float32),
            pltpu.VMEM((8, 128), jnp.float32),
            pltpu.VMEM((8, 128), jnp.float32),
            pltpu.SemaphoreType.DMA((n_op,)),
            pltpu.SemaphoreType.DMA((n_op,)),
            pltpu.SemaphoreType.DMA((n_sec,)),
            pltpu.SemaphoreType.DMA((n_sec,)),
            pltpu.SemaphoreType.DMA(()),
        ],
        compiler_params=pltpu.CompilerParams(collective_id=0, has_side_effects=True),
    )(tile)
    return tuple(out[0, k] for k in range(len(values)))


def sigma_sum_kernel(n_sec, n_op, x_ref, t_ref, o_ref, s_ref,
                     rs_buf, red, red_out, ag_buf, op_buf, sec_buf, mid, mid_out,
                     send_rs, recv_rs, send_ag, recv_ag, send_a, recv_a,
                     send_b, recv_b, local_sem):
    me_sec = lax.axis_index("sec")
    me_op = lax.axis_index("op")
    barrier = pltpu.get_barrier_semaphore()
    for d in range(1, n_op):
        pl.semaphore_signal(barrier, 1, device_id=(me_sec, (me_op + d) % n_op),
                            device_id_type=MESH)
    for d in range(1, n_sec):
        pl.semaphore_signal(barrier, 1, device_id=((me_sec + d) % n_sec, me_op),
                            device_id_type=MESH)
    pl.semaphore_wait(barrier, n_op - 1 + n_sec - 1)

    def op_peer(j):
        return (me_sec, j)

    def sec_peer(j):
        return (j, me_op)

    def total_of(v):
        return jnp.sum(jnp.sum(v, axis=1, keepdims=True), axis=0, keepdims=True)

    lane = lax.broadcasted_iota(jnp.int32, (8, 128), 1)
    own = st_ref[n_op + me_op].astype(jnp.float32)
    own_square = total_of(own * own)
    energy = sh_ref[me_op] * own_square
    for j in range(n_op):
        energy = energy + total_of(x_ref[j] * st_ref[n_op + j].astype(jnp.float32))
    t_ref[...] = jnp.where(lane == 0, energy, jnp.where(lane == 1, own_square, 0.0))
    settle(t_ref, t_out, local_sem.at[4])

    def rs_copy(d):
        j = (me_op + d) % n_op
        return pltpu.make_async_remote_copy(
            src_ref=x_ref.at[j], dst_ref=rs_buf.at[me_op], send_sem=send_rs.at[d],
            recv_sem=recv_rs.at[me_op], device_id=op_peer(j), device_id_type=MESH)

    def rs_recv(d):
        slot = (me_op + n_op - d) % n_op
        return pltpu.make_async_remote_copy(
            src_ref=x_ref.at[me_op], dst_ref=rs_buf.at[slot], send_sem=send_rs.at[d],
            recv_sem=recv_rs.at[slot], device_id=op_peer(slot), device_id_type=MESH)

    def gather_copy(n, me, src, buf, send, recv, peer_of, d):
        return pltpu.make_async_remote_copy(
            src_ref=src, dst_ref=buf.at[me], send_sem=send.at[d],
            recv_sem=recv.at[me], device_id=peer_of((me + d) % n), device_id_type=MESH)

    def gather_recv(n, me, src, buf, send, recv, peer_of, d):
        slot = (me + n - d) % n
        return pltpu.make_async_remote_copy(
            src_ref=src, dst_ref=buf.at[slot], send_sem=send.at[d],
            recv_sem=recv.at[slot], device_id=peer_of(slot), device_id_type=MESH)

    def ordered_sum(buf, n):
        total = buf[0]
        for j in range(1, n):
            total = total + buf[j]
        return total

    for d in range(1, n_op):
        rs_copy(d).start()
    a_args = (n_op, me_op, t_out, op_buf, send_a, recv_a, op_peer)
    for d in range(1, n_op):
        gather_copy(*a_args, d).start()
    rs_buf[me_op] = x_ref[me_op]
    op_buf[me_op] = t_ref[...]

    for d in range(1, n_op):
        gather_recv(*a_args, d).wait_recv()
    mid[...] = ordered_sum(op_buf, n_op)
    local = pltpu.make_async_copy(mid, mid_out, local_sem.at[0])
    local.start()
    local.wait()
    b_args = (n_sec, me_sec, mid_out, sec_buf, send_b, recv_b, sec_peer)
    for d in range(1, n_sec):
        gather_copy(*b_args, d).start()
    sec_buf[me_sec] = mid_out[...]

    for d in range(1, n_op):
        rs_recv(d).wait_recv()
    red[...] = ordered_sum(rs_buf, n_op)
    local = pltpu.make_async_copy(red, red_out, local_sem.at[1])
    local.start()
    local.wait()
    g_args = (n_op, me_op, red_out, ag_buf, send_ag, recv_ag, op_peer)
    for d in range(1, n_op):
        gather_copy(*g_args, d).start()
    ag_buf[me_op] = red_out[...]

    for d in range(1, n_sec):
        gather_recv(*b_args, d).wait_recv()
    s_ref[...] = ordered_sum(sec_buf, n_sec)
    for d in range(1, n_op):
        gather_recv(*g_args, d).wait_recv()
    o_ref[...] = ag_buf[...]

    for d in range(1, n_op):
        rs_copy(d).wait_send()
        gather_copy(*a_args, d).wait_send()
        gather_copy(*g_args, d).wait_send()
    for d in range(1, n_sec):
        gather_copy(*b_args, d).wait_send()


def sigma_sum(partial, values, n_sec, n_op):
    shape = partial.shape
    rows = shape[0] * shape[1] // n_op
    chunks = partial.reshape(n_op, rows, shape[2])
    lane = lax.broadcasted_iota(jnp.int32, (8, 128), 1)
    tile = jnp.zeros((8, 128), jnp.float32)
    for k, v in enumerate(values):
        tile = jnp.where(lane == k, v, tile)
    vmem = pl.BlockSpec(memory_space=pltpu.VMEM)
    total, sums = pl.pallas_call(
        functools.partial(sigma_sum_kernel, n_sec, n_op),
        out_shape=(
            jax.ShapeDtypeStruct(chunks.shape, jnp.float32),
            jax.ShapeDtypeStruct((8, 128), jnp.float32),
        ),
        in_specs=[vmem, vmem],
        out_specs=(vmem, vmem),
        scratch_shapes=[
            pltpu.VMEM(chunks.shape, jnp.float32),
            pltpu.VMEM((rows, shape[2]), jnp.float32),
            pltpu.VMEM((rows, shape[2]), jnp.float32),
            pltpu.VMEM(chunks.shape, jnp.float32),
            pltpu.VMEM((n_op, 8, 128), jnp.float32),
            pltpu.VMEM((n_sec, 8, 128), jnp.float32),
            pltpu.VMEM((8, 128), jnp.float32),
            pltpu.VMEM((8, 128), jnp.float32),
            pltpu.SemaphoreType.DMA((n_op,)),
            pltpu.SemaphoreType.DMA((n_op,)),
            pltpu.SemaphoreType.DMA((n_op,)),
            pltpu.SemaphoreType.DMA((n_op,)),
            pltpu.SemaphoreType.DMA((n_op,)),
            pltpu.SemaphoreType.DMA((n_op,)),
            pltpu.SemaphoreType.DMA((n_sec,)),
            pltpu.SemaphoreType.DMA((n_sec,)),
            pltpu.SemaphoreType.DMA((2,)),
        ],
        compiler_params=pltpu.CompilerParams(collective_id=1, has_side_effects=True),
    )(chunks, tile)
    return total.reshape(shape), tuple(sums[0, k] for k in range(len(values)))


def step_kernel(n_sec, n_op, count, final, x_ref, st_ref, sh_ref, *refs):
    if final:
        (win_ref, t_ref, t_out, rs_buf, red, op_buf, sec_buf, mid, mid_out, op_buf2,
         sec_buf2, mid2, mid2_out, mid3, mid3_out, new_buf, new_out, win_buf, send_rs, recv_rs, send_a,
         recv_a, send_b, recv_b, send_a2, recv_a2, send_b2, recv_b2, send_w,
         recv_w, local_sem) = refs
    else:
        (win_ref, t_ref, t_out, rs_buf, red, op_buf, sec_buf, mid, mid_out, new_buf,
         new_out, win_buf, send_rs, recv_rs, send_a, recv_a, send_b, recv_b, send_w,
         recv_w, local_sem) = refs
    me_sec = lax.axis_index("sec")
    me_op = lax.axis_index("op")
    prev_sec = (me_sec + n_sec - 1) % n_sec
    next_sec = (me_sec + 1) % n_sec
    barrier = pltpu.get_barrier_semaphore()
    greeted = 0
    for d in range(1, n_op):
        pl.semaphore_signal(barrier, 1, device_id=(me_sec, (me_op + d) % n_op),
                            device_id_type=MESH)
        greeted += 1
    for d in range(1, n_sec):
        pl.semaphore_signal(barrier, 1, device_id=((me_sec + d) % n_sec, me_op),
                            device_id_type=MESH)
        greeted += 1
    for side in (prev_sec, next_sec):
        for d in range(1, n_op):
            pl.semaphore_signal(barrier, 1, device_id=(side, (me_op + d) % n_op),
                                device_id_type=MESH)
            greeted += 1
    pl.semaphore_wait(barrier, greeted)

    def op_peer(j):
        return (me_sec, j)

    def sec_peer(j):
        return (j, me_op)

    def copy_to(src, dst, send, recv, peer):
        return pltpu.make_async_remote_copy(
            src_ref=src, dst_ref=dst, send_sem=send, recv_sem=recv,
            device_id=peer, device_id_type=MESH)

    def ordered_sum(buf, n):
        total = buf[0]
        for j in range(1, n):
            total = total + buf[j]
        return total

    def start_gather(n, me, src, buf, send, recv, peer_of):
        for d in range(1, n):
            copy_to(src, buf.at[me], send.at[d], recv.at[me], peer_of((me + d) % n)).start()
        buf[me] = src[...]

    def wait_gather(n, me, src, buf, send, recv, peer_of):
        for d in range(1, n):
            slot = (me + n - d) % n
            copy_to(src, buf.at[slot], send.at[d], recv.at[slot], peer_of(slot)).wait_recv()

    def drain_gather(n, me, src, buf, send, recv, peer_of):
        for d in range(1, n):
            copy_to(src, buf.at[me], send.at[d], recv.at[me], peer_of((me + d) % n)).wait_send()

    def settle(src, dst, sem):
        local = pltpu.make_async_copy(src, dst, sem)
        local.start()
        local.wait()

    def total_of(v):
        return jnp.sum(jnp.sum(v, axis=1, keepdims=True), axis=0, keepdims=True)

    lane = lax.broadcasted_iota(jnp.int32, (8, 128), 1)
    own = st_ref[n_op + me_op].astype(jnp.float32)
    own_square = total_of(own * own)
    energy = sh_ref[me_op] * own_square
    for j in range(n_op):
        energy = energy + total_of(x_ref[j] * st_ref[n_op + j].astype(jnp.float32))
    t_ref[...] = jnp.where(lane == 0, energy, jnp.where(lane == 1, own_square, 0.0))
    settle(t_ref, t_out, local_sem.at[4])

    def rs_copy(d):
        j = (me_op + d) % n_op
        return copy_to(x_ref.at[j], rs_buf.at[me_op], send_rs.at[d], recv_rs.at[me_op], op_peer(j))

    for d in range(1, n_op):
        rs_copy(d).start()
    a_args = (n_op, me_op, t_out, op_buf, send_a, recv_a, op_peer)
    start_gather(*a_args)
    rs_buf[me_op] = x_ref[me_op]

    wait_gather(*a_args)
    mid[...] = ordered_sum(op_buf, n_op)
    settle(mid, mid_out, local_sem.at[0])
    b_args = (n_sec, me_sec, mid_out, sec_buf, send_b, recv_b, sec_peer)
    start_gather(*b_args)

    for d in range(1, n_op):
        slot = (me_op + n_op - d) % n_op
        copy_to(x_ref.at[me_op], rs_buf.at[slot], send_rs.at[d], recv_rs.at[slot],
                op_peer(slot)).wait_recv()
    red[...] = ordered_sum(rs_buf, n_op)

    wait_gather(*b_args)
    sums = ordered_sum(sec_buf, n_sec)
    energy_sum = sums[0:1, 0:1]
    norm_sum = sums[0:1, 1:2]
    state_wide = st_ref[n_op + me_op].astype(jnp.float32)
    sigma = red[...] + sh_ref[me_op] * state_wide
    updated = state_wide - step_size * (sigma - (energy_sum / norm_sum) * state_wide)
    if final:
        square = total_of(updated * updated)
        mid2[...] = jnp.where(lane == 0, square, 0.0)
        settle(mid2, mid2_out, local_sem.at[1])
        a2_args = (n_op, me_op, mid2_out, op_buf2, send_a2, recv_a2, op_peer)
        start_gather(*a2_args)
        wait_gather(*a2_args)
        mid3[...] = ordered_sum(op_buf2, n_op)
        settle(mid3, mid3_out, local_sem.at[3])
        b2_args = (n_sec, me_sec, mid3_out, sec_buf2, send_b2, recv_b2, sec_peer)
        start_gather(*b2_args)
        wait_gather(*b2_args)
        new_norm = ordered_sum(sec_buf2, n_sec)[0:1, 0:1]
        factor = jnp.sqrt(count / new_norm)
    else:
        factor = jnp.sqrt(count / norm_sum)
    new_buf[...] = (updated * factor).astype(new_buf.dtype)
    settle(new_buf, new_out, local_sem.at[2])

    sides = ((next_sec, 0),) if final else ((next_sec, 0), (prev_sec, 2 * n_op))
    sent = 0
    for side, base in sides:
        for j in range(n_op):
            copy_to(new_out, win_buf.at[base + me_op], send_w.at[sent],
                    recv_w.at[base + me_op], (side, j)).start()
            sent += 1
    for d in range(1, n_op):
        j = (me_op + d) % n_op
        copy_to(new_out, win_buf.at[n_op + me_op], send_w.at[sent],
                recv_w.at[n_op + me_op], op_peer(j)).start()
        sent += 1
    win_buf[n_op + me_op] = new_out[...]

    from_sides = ((prev_sec, 0),) if final else ((prev_sec, 0), (next_sec, 2 * n_op))
    for side, base in from_sides:
        for j in range(n_op):
            copy_to(new_out, win_buf.at[base + j], send_w.at[0], recv_w.at[base + j],
                    (side, j)).wait_recv()
    for d in range(1, n_op):
        slot = (me_op + n_op - d) % n_op
        copy_to(new_out, win_buf.at[n_op + slot], send_w.at[0], recv_w.at[n_op + slot],
                op_peer(slot)).wait_recv()
    win_ref[...] = win_buf[...]

    for d in range(1, n_op):
        rs_copy(d).wait_send()
    drain_gather(*a_args)
    drain_gather(*b_args)
    if final:
        drain_gather(*a2_args)
        drain_gather(*b2_args)
    for k in range(sent):
        copy_to(new_out, win_buf.at[n_op + me_op], send_w.at[k], recv_w.at[n_op + me_op],
                op_peer((me_op + 1) % n_op)).wait_send()


def step(partial, window, shift, count, final, n_sec, n_op):
    shape = partial.shape
    rows = shape[0] * shape[1] // n_op
    chunks = partial.reshape(n_op, rows, shape[2])
    state_chunks = window.reshape(-1, rows, shape[2])
    shift_chunks = jnp.repeat(shift, n_op // shape[0])[:, None, None]
    slots = (2 if final else 3) * n_op
    tile_shape = (rows, shape[2])
    scalar_bufs = [
        pltpu.VMEM((n_op, 8, 128), jnp.float32),
        pltpu.VMEM((n_sec, 8, 128), jnp.float32),
        pltpu.VMEM((8, 128), jnp.float32),
        pltpu.VMEM((8, 128), jnp.float32),
    ]
    scratch = [
        pltpu.VMEM((8, 128), jnp.float32),
        pltpu.VMEM((8, 128), jnp.float32),
        pltpu.VMEM(chunks.shape, jnp.float32),
        pltpu.VMEM(tile_shape, jnp.float32),
    ] + scalar_bufs + (scalar_bufs + scalar_bufs[2:] if final else []) + [
        pltpu.VMEM(tile_shape, jnp.bfloat16),
        pltpu.VMEM(tile_shape, jnp.bfloat16),
        pltpu.VMEM((slots, rows, shape[2]), jnp.bfloat16),
        pltpu.SemaphoreType.DMA((n_op,)),
        pltpu.SemaphoreType.DMA((n_op,)),
        pltpu.SemaphoreType.DMA((n_op,)),
        pltpu.SemaphoreType.DMA((n_op,)),
        pltpu.SemaphoreType.DMA((n_sec,)),
        pltpu.SemaphoreType.DMA((n_sec,)),
    ] + ([
        pltpu.SemaphoreType.DMA((n_op,)),
        pltpu.SemaphoreType.DMA((n_op,)),
        pltpu.SemaphoreType.DMA((n_sec,)),
        pltpu.SemaphoreType.DMA((n_sec,)),
    ] if final else []) + [
        pltpu.SemaphoreType.DMA((slots + n_op,)),
        pltpu.SemaphoreType.DMA((slots,)),
        pltpu.SemaphoreType.DMA((5,)),
    ]
    vmem = pl.BlockSpec(memory_space=pltpu.VMEM)
    window = pl.pallas_call(
        functools.partial(step_kernel, n_sec, n_op, count, final),
        out_shape=jax.ShapeDtypeStruct((slots, rows, shape[2]), jnp.bfloat16),
        in_specs=[vmem, vmem, vmem],
        out_specs=vmem,
        scratch_shapes=scratch,
        compiler_params=pltpu.CompilerParams(
            collective_id=3 if final else 2, has_side_effects=True
        ),
    )(chunks, state_chunks, shift_chunks)
    return window.reshape(slots // (n_op // shape[0]), shape[1], shape[2])


def sigma_part_kernel(partner_ref, win_ref, left_ref, right_ref, o_ref):
    b = pl.program_id(0)
    total = jnp.zeros(o_ref.shape[1:], jnp.float32)
    for t in range(left_ref.shape[0]):
        source = win_ref[partner_ref[t, b]]
        halfway = jnp.dot(left_ref[t, 0], source, preferred_element_type=jnp.float32)
        total = total + jnp.dot(halfway.astype(jnp.bfloat16), right_ref[t, 0],
                                preferred_element_type=jnp.float32)
    o_ref[0] = total


def sigma_part(window, left_ops, right_ops, partner):
    terms, sectors, m, _ = left_ops.shape
    op_spec = pl.BlockSpec((terms, 1, m, m), lambda b, p: (0, b, 0, 0))
    return pl.pallas_call(
        sigma_part_kernel,
        out_shape=jax.ShapeDtypeStruct((sectors, m, m), jnp.float32),
        grid_spec=pltpu.PrefetchScalarGridSpec(
            num_scalar_prefetch=1,
            grid=(sectors,),
            in_specs=[
                pl.BlockSpec(window.shape, lambda b, p: (0, 0, 0)),
                op_spec,
                op_spec,
            ],
            out_specs=pl.BlockSpec((1, m, m), lambda b, p: (b, 0, 0)),
        ),
        cost_estimate=pl.CostEstimate(
            flops=4 * terms * sectors * m * m * m,
            bytes_accessed=2 * left_ops.size * 2 + window.size * 2 + sectors * m * m * 4,
            transcendentals=0,
        ),
    )(partner, window, left_ops, right_ops)


def shifted(block, axis, distance):
    devices = range(lax.axis_size(axis))
    route = [((i - distance) % len(devices), i) for i in devices]
    return lax.ppermute(block, axis, route)


def per_device(state_start, left_ops, right_ops, shift, partner, kept):
    sector_local = state_start.shape[0]
    width = state_start.shape[1]
    count = float(sector_local * lax.axis_size("sec") * width * width)
    n_sec = lax.axis_size("sec")
    n_op = lax.axis_size("op")
    kept_prev = shifted(kept, "sec", 1)
    state = state_start
    window = padded(state, (("sec", 0),), sector_local)
    left_after, window, kept_prev = lax.optimization_barrier(
        (left_ops, window, kept_prev)
    )
    left_prev = shifted(left_after, "sec", 1)
    for iteration in range(ITERS):
        partial_sigma = sigma_part(window, left_ops, right_ops, partner)
        final = iteration == ITERS - 1
        window = step(partial_sigma, window, shift, count, final, n_sec, n_op)
        state = window[sector_local : 2 * sector_local]
    state_prev = window[:sector_local]
    columns = jnp.arange(width, dtype=jnp.int32)
    keep_mask = (columns[None, :] < kept_prev[:, None]).astype(jnp.bfloat16)
    kept_block = state_prev * keep_mask[:, None, :]
    out_scale = 1.0 / float(width) ** 0.5
    projected = jnp.einsum(
        "tbij,bjk->tbik", left_prev, kept_block, preferred_element_type=jnp.float32
    ).astype(jnp.bfloat16)
    kept_turned = jnp.broadcast_to(
        jnp.swapaxes(kept_block, 1, 2)[None], left_prev.shape
    )
    new_ops = (
        jnp.einsum("tbij,tbjk->tbik", kept_turned, projected, preferred_element_type=jnp.float32)
        * out_scale
    ).astype(jnp.bfloat16)
    return (state, new_ops)


def solution(mesh):
    in_specs = (
        P("sec", None, None),
        P("op", "sec", None, None),
        P("op", "sec", None, None),
        P("sec"),
        P("op", "sec"),
        P("sec"),
    )
    out_specs = (P("sec", None, None), P("op", "sec", None, None))
    return jax.shard_map(
        per_device, mesh=mesh, in_specs=in_specs, out_specs=out_specs, check_vma=False
    )
```

```python
import functools

import jax
import jax.numpy as jnp
from jax import lax
from jax.experimental import pallas as pl
from jax.experimental.pallas import tpu as pltpu
from jax.sharding import PartitionSpec as P

MESH = pl.DeviceIdType.MESH

ITERS = 4


step_size = 0.5


def padded(cells, sides, width):
    for axis, dim in sides:
        count = lax.axis_size(axis)
        head = lax.slice_in_dim(cells, 0, width, axis=dim)
        tail = lax.slice_in_dim(cells, cells.shape[dim] - width, cells.shape[dim], axis=dim)
        cells = jnp.concatenate(
            [
                lax.ppermute(tail, axis, [(i, (i + 1) % count) for i in range(count)]),
                cells,
                lax.ppermute(head, axis, [((i + 1) % count, i) for i in range(count)]),
            ],
            axis=dim,
        )
    return cells


def all_sum_kernel(n_sec, n_op, x_ref, o_ref, op_buf, sec_buf, mid, out_buf,
                   send_a, recv_a, send_b, recv_b, local_sem):
    me_sec = lax.axis_index("sec")
    me_op = lax.axis_index("op")
    barrier = pltpu.get_barrier_semaphore()
    for d in range(1, n_op):
        pl.semaphore_signal(barrier, 1, device_id=(me_sec, (me_op + d) % n_op),
                            device_id_type=MESH)
    for d in range(1, n_sec):
        pl.semaphore_signal(barrier, 1, device_id=((me_sec + d) % n_sec, me_op),
                            device_id_type=MESH)
    pl.semaphore_wait(barrier, n_op - 1 + n_sec - 1)

    def stage(n, me, src, buf, send, recv, peer_of):
        for d in range(1, n):
            pltpu.make_async_remote_copy(
                src_ref=src, dst_ref=buf.at[me], send_sem=send.at[d],
                recv_sem=recv.at[me], device_id=peer_of((me + d) % n),
                device_id_type=MESH).start()
        buf[me] = src[...]
        for d in range(1, n):
            slot = (me + n - d) % n
            pltpu.make_async_remote_copy(
                src_ref=src, dst_ref=buf.at[slot], send_sem=send.at[d],
                recv_sem=recv.at[slot], device_id=peer_of(slot),
                device_id_type=MESH).wait_recv()
        for d in range(1, n):
            pltpu.make_async_remote_copy(
                src_ref=src, dst_ref=buf.at[me], send_sem=send.at[d],
                recv_sem=recv.at[me], device_id=peer_of((me + d) % n),
                device_id_type=MESH).wait_send()
        total = buf[0]
        for j in range(1, n):
            total = total + buf[j]
        return total

    mid[...] = stage(n_op, me_op, x_ref, op_buf, send_a, recv_a,
                     lambda j: (me_sec, j))
    local = pltpu.make_async_copy(mid, out_buf, local_sem)
    local.start()
    local.wait()
    o_ref[...] = stage(n_sec, me_sec, out_buf, sec_buf, send_b, recv_b,
                       lambda j: (j, me_op))


def all_sum(values, n_sec, n_op):
    lane = lax.broadcasted_iota(jnp.int32, (8, 128), 1)
    tile = jnp.zeros((8, 128), jnp.float32)
    for k, v in enumerate(values):
        tile = jnp.where(lane == k, v, tile)
    tile_spec = pl.BlockSpec(memory_space=pltpu.VMEM)
    out = pl.pallas_call(
        functools.partial(all_sum_kernel, n_sec, n_op),
        out_shape=jax.ShapeDtypeStruct((8, 128), jnp.float32),
        in_specs=[tile_spec],
        out_specs=tile_spec,
        scratch_shapes=[
            pltpu.VMEM((n_op, 8, 128), jnp.float32),
            pltpu.VMEM((n_sec, 8, 128), jnp.float32),
            pltpu.VMEM((8, 128), jnp.float32),
            pltpu.VMEM((8, 128), jnp.float32),
            pltpu.SemaphoreType.DMA((n_op,)),
            pltpu.SemaphoreType.DMA((n_op,)),
            pltpu.SemaphoreType.DMA((n_sec,)),
            pltpu.SemaphoreType.DMA((n_sec,)),
            pltpu.SemaphoreType.DMA(()),
        ],
        compiler_params=pltpu.CompilerParams(collective_id=0, has_side_effects=True),
    )(tile)
    return tuple(out[0, k] for k in range(len(values)))


def sigma_sum_kernel(n_sec, n_op, x_ref, t_ref, o_ref, s_ref,
                     rs_buf, red, red_out, ag_buf, op_buf, sec_buf, mid, mid_out,
                     send_rs, recv_rs, send_ag, recv_ag, send_a, recv_a,
                     send_b, recv_b, local_sem):
    me_sec = lax.axis_index("sec")
    me_op = lax.axis_index("op")
    barrier = pltpu.get_barrier_semaphore()
    for d in range(1, n_op):
        pl.semaphore_signal(barrier, 1, device_id=(me_sec, (me_op + d) % n_op),
                            device_id_type=MESH)
    for d in range(1, n_sec):
        pl.semaphore_signal(barrier, 1, device_id=((me_sec + d) % n_sec, me_op),
                            device_id_type=MESH)
    pl.semaphore_wait(barrier, n_op - 1 + n_sec - 1)

    def op_peer(j):
        return (me_sec, j)

    def sec_peer(j):
        return (j, me_op)

    def total_of(v):
        return jnp.sum(jnp.sum(v, axis=1, keepdims=True), axis=0, keepdims=True)

    lane = lax.broadcasted_iota(jnp.int32, (8, 128), 1)
    own = st_ref[n_op + me_op].astype(jnp.float32)
    own_square = total_of(own * own)
    energy = sh_ref[me_op] * own_square
    for j in range(n_op):
        energy = energy + total_of(x_ref[j] * st_ref[n_op + j].astype(jnp.float32))
    t_ref[...] = jnp.where(lane == 0, energy, jnp.where(lane == 1, own_square, 0.0))
    settle(t_ref, t_out, local_sem.at[4])

    def rs_copy(d):
        j = (me_op + d) % n_op
        return pltpu.make_async_remote_copy(
            src_ref=x_ref.at[j], dst_ref=rs_buf.at[me_op], send_sem=send_rs.at[d],
            recv_sem=recv_rs.at[me_op], device_id=op_peer(j), device_id_type=MESH)

    def rs_recv(d):
        slot = (me_op + n_op - d) % n_op
        return pltpu.make_async_remote_copy(
            src_ref=x_ref.at[me_op], dst_ref=rs_buf.at[slot], send_sem=send_rs.at[d],
            recv_sem=recv_rs.at[slot], device_id=op_peer(slot), device_id_type=MESH)

    def gather_copy(n, me, src, buf, send, recv, peer_of, d):
        return pltpu.make_async_remote_copy(
            src_ref=src, dst_ref=buf.at[me], send_sem=send.at[d],
            recv_sem=recv.at[me], device_id=peer_of((me + d) % n), device_id_type=MESH)

    def gather_recv(n, me, src, buf, send, recv, peer_of, d):
        slot = (me + n - d) % n
        return pltpu.make_async_remote_copy(
            src_ref=src, dst_ref=buf.at[slot], send_sem=send.at[d],
            recv_sem=recv.at[slot], device_id=peer_of(slot), device_id_type=MESH)

    def ordered_sum(buf, n):
        total = buf[0]
        for j in range(1, n):
            total = total + buf[j]
        return total

    for d in range(1, n_op):
        rs_copy(d).start()
    a_args = (n_op, me_op, t_out, op_buf, send_a, recv_a, op_peer)
    for d in range(1, n_op):
        gather_copy(*a_args, d).start()
    rs_buf[me_op] = x_ref[me_op]
    op_buf[me_op] = t_ref[...]

    for d in range(1, n_op):
        gather_recv(*a_args, d).wait_recv()
    mid[...] = ordered_sum(op_buf, n_op)
    local = pltpu.make_async_copy(mid, mid_out, local_sem.at[0])
    local.start()
    local.wait()
    b_args = (n_sec, me_sec, mid_out, sec_buf, send_b, recv_b, sec_peer)
    for d in range(1, n_sec):
        gather_copy(*b_args, d).start()
    sec_buf[me_sec] = mid_out[...]

    for d in range(1, n_op):
        rs_recv(d).wait_recv()
    red[...] = ordered_sum(rs_buf, n_op)
    local = pltpu.make_async_copy(red, red_out, local_sem.at[1])
    local.start()
    local.wait()
    g_args = (n_op, me_op, red_out, ag_buf, send_ag, recv_ag, op_peer)
    for d in range(1, n_op):
        gather_copy(*g_args, d).start()
    ag_buf[me_op] = red_out[...]

    for d in range(1, n_sec):
        gather_recv(*b_args, d).wait_recv()
    s_ref[...] = ordered_sum(sec_buf, n_sec)
    for d in range(1, n_op):
        gather_recv(*g_args, d).wait_recv()
    o_ref[...] = ag_buf[...]

    for d in range(1, n_op):
        rs_copy(d).wait_send()
        gather_copy(*a_args, d).wait_send()
        gather_copy(*g_args, d).wait_send()
    for d in range(1, n_sec):
        gather_copy(*b_args, d).wait_send()


def sigma_sum(partial, values, n_sec, n_op):
    shape = partial.shape
    rows = shape[0] * shape[1] // n_op
    chunks = partial.reshape(n_op, rows, shape[2])
    lane = lax.broadcasted_iota(jnp.int32, (8, 128), 1)
    tile = jnp.zeros((8, 128), jnp.float32)
    for k, v in enumerate(values):
        tile = jnp.where(lane == k, v, tile)
    vmem = pl.BlockSpec(memory_space=pltpu.VMEM)
    total, sums = pl.pallas_call(
        functools.partial(sigma_sum_kernel, n_sec, n_op),
        out_shape=(
            jax.ShapeDtypeStruct(chunks.shape, jnp.float32),
            jax.ShapeDtypeStruct((8, 128), jnp.float32),
        ),
        in_specs=[vmem, vmem],
        out_specs=(vmem, vmem),
        scratch_shapes=[
            pltpu.VMEM(chunks.shape, jnp.float32),
            pltpu.VMEM((rows, shape[2]), jnp.float32),
            pltpu.VMEM((rows, shape[2]), jnp.float32),
            pltpu.VMEM(chunks.shape, jnp.float32),
            pltpu.VMEM((n_op, 8, 128), jnp.float32),
            pltpu.VMEM((n_sec, 8, 128), jnp.float32),
            pltpu.VMEM((8, 128), jnp.float32),
            pltpu.VMEM((8, 128), jnp.float32),
            pltpu.SemaphoreType.DMA((n_op,)),
            pltpu.SemaphoreType.DMA((n_op,)),
            pltpu.SemaphoreType.DMA((n_op,)),
            pltpu.SemaphoreType.DMA((n_op,)),
            pltpu.SemaphoreType.DMA((n_op,)),
            pltpu.SemaphoreType.DMA((n_op,)),
            pltpu.SemaphoreType.DMA((n_sec,)),
            pltpu.SemaphoreType.DMA((n_sec,)),
            pltpu.SemaphoreType.DMA((2,)),
        ],
        compiler_params=pltpu.CompilerParams(collective_id=1, has_side_effects=True),
    )(chunks, tile)
    return total.reshape(shape), tuple(sums[0, k] for k in range(len(values)))


def step_kernel(n_sec, n_op, count, final, x_ref, st_ref, sh_ref, piece_ref, *refs):
    if final:
        (win_ref, got_ref, t_ref, t_out, rs_buf, red, op_buf, sec_buf, mid, mid_out,
         op_buf2, sec_buf2, mid2, mid2_out, mid3, mid3_out, new_buf, new_out, win_buf,
         send_rs, recv_rs, send_a, recv_a, send_b, recv_b, send_a2, recv_a2, send_b2,
         recv_b2, send_w, recv_w, local_sem) = refs
    else:
        (win_ref, got_ref, t_ref, t_out, rs_buf, red, op_buf, sec_buf, mid, mid_out,
         new_buf, new_out, win_buf, send_rs, recv_rs, send_a, recv_a, send_b, recv_b, send_w,
         recv_w, local_sem) = refs
    me_sec = lax.axis_index("sec")
    me_op = lax.axis_index("op")
    prev_sec = (me_sec + n_sec - 1) % n_sec
    next_sec = (me_sec + 1) % n_sec
    barrier = pltpu.get_barrier_semaphore()
    greeted = 0
    for d in range(1, n_op):
        pl.semaphore_signal(barrier, 1, device_id=(me_sec, (me_op + d) % n_op),
                            device_id_type=MESH)
        greeted += 1
    for d in range(1, n_sec):
        pl.semaphore_signal(barrier, 1, device_id=((me_sec + d) % n_sec, me_op),
                            device_id_type=MESH)
        greeted += 1
    for side in (prev_sec, next_sec):
        for d in range(1, n_op):
            pl.semaphore_signal(barrier, 1, device_id=(side, (me_op + d) % n_op),
                                device_id_type=MESH)
            greeted += 1
    pl.semaphore_wait(barrier, greeted)

    def op_peer(j):
        return (me_sec, j)

    def sec_peer(j):
        return (j, me_op)

    def copy_to(src, dst, send, recv, peer):
        return pltpu.make_async_remote_copy(
            src_ref=src, dst_ref=dst, send_sem=send, recv_sem=recv,
            device_id=peer, device_id_type=MESH)

    def ordered_sum(buf, n):
        total = buf[0]
        for j in range(1, n):
            total = total + buf[j]
        return total

    def start_gather(n, me, src, buf, send, recv, peer_of):
        for d in range(1, n):
            copy_to(src, buf.at[me], send.at[d], recv.at[me], peer_of((me + d) % n)).start()
        buf[me] = src[...]

    def wait_gather(n, me, src, buf, send, recv, peer_of):
        for d in range(1, n):
            slot = (me + n - d) % n
            copy_to(src, buf.at[slot], send.at[d], recv.at[slot], peer_of(slot)).wait_recv()

    def drain_gather(n, me, src, buf, send, recv, peer_of):
        for d in range(1, n):
            copy_to(src, buf.at[me], send.at[d], recv.at[me], peer_of((me + d) % n)).wait_send()

    def settle(src, dst, sem):
        local = pltpu.make_async_copy(src, dst, sem)
        local.start()
        local.wait()

    def total_of(v):
        return jnp.sum(jnp.sum(v, axis=1, keepdims=True), axis=0, keepdims=True)

    lane = lax.broadcasted_iota(jnp.int32, (8, 128), 1)
    own = st_ref[n_op + me_op].astype(jnp.float32)
    own_square = total_of(own * own)
    energy = sh_ref[me_op] * own_square
    for j in range(n_op):
        energy = energy + total_of(x_ref[j] * st_ref[n_op + j].astype(jnp.float32))
    t_ref[...] = jnp.where(lane == 0, energy, jnp.where(lane == 1, own_square, 0.0))
    settle(t_ref, t_out, local_sem.at[4])

    def rs_copy(d):
        j = (me_op + d) % n_op
        return copy_to(x_ref.at[j], rs_buf.at[me_op], send_rs.at[d], recv_rs.at[me_op], op_peer(j))

    for d in range(1, n_op):
        rs_copy(d).start()
    a_args = (n_op, me_op, t_out, op_buf, send_a, recv_a, op_peer)
    start_gather(*a_args)
    rs_buf[me_op] = x_ref[me_op]

    operators = copy_to(piece_ref, got_ref, send_w.at[send_w.shape[0] - 1],
                        recv_w.at[recv_w.shape[0] - 1], (next_sec, me_op))
    operators.start()

    wait_gather(*a_args)
    mid[...] = ordered_sum(op_buf, n_op)
    settle(mid, mid_out, local_sem.at[0])
    b_args = (n_sec, me_sec, mid_out, sec_buf, send_b, recv_b, sec_peer)
    start_gather(*b_args)

    for d in range(1, n_op):
        slot = (me_op + n_op - d) % n_op
        copy_to(x_ref.at[me_op], rs_buf.at[slot], send_rs.at[d], recv_rs.at[slot],
                op_peer(slot)).wait_recv()
    red[...] = ordered_sum(rs_buf, n_op)

    wait_gather(*b_args)
    sums = ordered_sum(sec_buf, n_sec)
    energy_sum = sums[0:1, 0:1]
    norm_sum = sums[0:1, 1:2]
    state_wide = st_ref[n_op + me_op].astype(jnp.float32)
    sigma = red[...] + sh_ref[me_op] * state_wide
    updated = state_wide - step_size * (sigma - (energy_sum / norm_sum) * state_wide)
    if final:
        square = total_of(updated * updated)
        mid2[...] = jnp.where(lane == 0, square, 0.0)
        settle(mid2, mid2_out, local_sem.at[1])
        a2_args = (n_op, me_op, mid2_out, op_buf2, send_a2, recv_a2, op_peer)
        start_gather(*a2_args)
        wait_gather(*a2_args)
        mid3[...] = ordered_sum(op_buf2, n_op)
        settle(mid3, mid3_out, local_sem.at[3])
        b2_args = (n_sec, me_sec, mid3_out, sec_buf2, send_b2, recv_b2, sec_peer)
        start_gather(*b2_args)
        wait_gather(*b2_args)
        new_norm = ordered_sum(sec_buf2, n_sec)[0:1, 0:1]
        factor = jnp.sqrt(count / new_norm)
    else:
        factor = jnp.sqrt(count / norm_sum)
    new_buf[...] = (updated * factor).astype(new_buf.dtype)
    settle(new_buf, new_out, local_sem.at[2])

    sides = ((next_sec, 0),) if final else ((next_sec, 0), (prev_sec, 2 * n_op))
    sent = 0
    for side, base in sides:
        for j in range(n_op):
            copy_to(new_out, win_buf.at[base + me_op], send_w.at[sent],
                    recv_w.at[base + me_op], (side, j)).start()
            sent += 1
    for d in range(1, n_op):
        j = (me_op + d) % n_op
        copy_to(new_out, win_buf.at[n_op + me_op], send_w.at[sent],
                recv_w.at[n_op + me_op], op_peer(j)).start()
        sent += 1
    win_buf[n_op + me_op] = new_out[...]

    from_sides = ((prev_sec, 0),) if final else ((prev_sec, 0), (next_sec, 2 * n_op))
    for side, base in from_sides:
        for j in range(n_op):
            copy_to(new_out, win_buf.at[base + j], send_w.at[0], recv_w.at[base + j],
                    (side, j)).wait_recv()
    for d in range(1, n_op):
        slot = (me_op + n_op - d) % n_op
        copy_to(new_out, win_buf.at[n_op + slot], send_w.at[0], recv_w.at[n_op + slot],
                op_peer(slot)).wait_recv()
    win_ref[...] = win_buf[...]
    operators.wait_recv()

    operators.wait_send()
    for d in range(1, n_op):
        rs_copy(d).wait_send()
    drain_gather(*a_args)
    drain_gather(*b_args)
    if final:
        drain_gather(*a2_args)
        drain_gather(*b2_args)
    for k in range(sent):
        copy_to(new_out, win_buf.at[n_op + me_op], send_w.at[k], recv_w.at[n_op + me_op],
                op_peer((me_op + 1) % n_op)).wait_send()


def step(partial, window, shift, piece, count, final, n_sec, n_op):
    shape = partial.shape
    rows = shape[0] * shape[1] // n_op
    chunks = partial.reshape(n_op, rows, shape[2])
    state_chunks = window.reshape(-1, rows, shape[2])
    shift_chunks = jnp.repeat(shift, n_op // shape[0])[:, None, None]
    slots = (2 if final else 3) * n_op
    tile_shape = (rows, shape[2])
    scalar_bufs = [
        pltpu.VMEM((n_op, 8, 128), jnp.float32),
        pltpu.VMEM((n_sec, 8, 128), jnp.float32),
        pltpu.VMEM((8, 128), jnp.float32),
        pltpu.VMEM((8, 128), jnp.float32),
    ]
    scratch = [
        pltpu.VMEM((8, 128), jnp.float32),
        pltpu.VMEM((8, 128), jnp.float32),
        pltpu.VMEM(chunks.shape, jnp.float32),
        pltpu.VMEM(tile_shape, jnp.float32),
    ] + scalar_bufs + (scalar_bufs + scalar_bufs[2:] if final else []) + [
        pltpu.VMEM(tile_shape, jnp.bfloat16),
        pltpu.VMEM(tile_shape, jnp.bfloat16),
        pltpu.VMEM((slots, rows, shape[2]), jnp.bfloat16),
        pltpu.SemaphoreType.DMA((n_op,)),
        pltpu.SemaphoreType.DMA((n_op,)),
        pltpu.SemaphoreType.DMA((n_op,)),
        pltpu.SemaphoreType.DMA((n_op,)),
        pltpu.SemaphoreType.DMA((n_sec,)),
        pltpu.SemaphoreType.DMA((n_sec,)),
    ] + ([
        pltpu.SemaphoreType.DMA((n_op,)),
        pltpu.SemaphoreType.DMA((n_op,)),
        pltpu.SemaphoreType.DMA((n_sec,)),
        pltpu.SemaphoreType.DMA((n_sec,)),
    ] if final else []) + [
        pltpu.SemaphoreType.DMA((slots + n_op + 1,)),
        pltpu.SemaphoreType.DMA((slots + 1,)),
        pltpu.SemaphoreType.DMA((5,)),
    ]
    vmem = pl.BlockSpec(memory_space=pltpu.VMEM)
    anywhere = pl.BlockSpec(memory_space=pl.ANY)
    window, got = pl.pallas_call(
        functools.partial(step_kernel, n_sec, n_op, count, final),
        out_shape=(
            jax.ShapeDtypeStruct((slots, rows, shape[2]), jnp.bfloat16),
            jax.ShapeDtypeStruct(piece.shape, piece.dtype),
        ),
        in_specs=[vmem, vmem, vmem, anywhere],
        out_specs=(vmem, anywhere),
        scratch_shapes=scratch,
        compiler_params=pltpu.CompilerParams(
            collective_id=3 if final else 2, has_side_effects=True
        ),
    )(chunks, state_chunks, shift_chunks, piece)
    return window.reshape(slots // (n_op // shape[0]), shape[1], shape[2]), got


def sigma_part_kernel(partner_ref, win_ref, left_ref, right_ref, o_ref):
    b = pl.program_id(0)
    total = jnp.zeros(o_ref.shape[1:], jnp.float32)
    for t in range(left_ref.shape[0]):
        source = win_ref[partner_ref[t, b]]
        halfway = jnp.dot(left_ref[t, 0], source, preferred_element_type=jnp.float32)
        total = total + jnp.dot(halfway.astype(jnp.bfloat16), right_ref[t, 0],
                                preferred_element_type=jnp.float32)
    o_ref[0] = total


def sigma_part(window, left_ops, right_ops, partner):
    terms, sectors, m, _ = left_ops.shape
    op_spec = pl.BlockSpec((terms, 1, m, m), lambda b, p: (0, b, 0, 0))
    return pl.pallas_call(
        sigma_part_kernel,
        out_shape=jax.ShapeDtypeStruct((sectors, m, m), jnp.float32),
        grid_spec=pltpu.PrefetchScalarGridSpec(
            num_scalar_prefetch=1,
            grid=(sectors,),
            in_specs=[
                pl.BlockSpec(window.shape, lambda b, p: (0, 0, 0)),
                op_spec,
                op_spec,
            ],
            out_specs=pl.BlockSpec((1, m, m), lambda b, p: (b, 0, 0)),
        ),
        cost_estimate=pl.CostEstimate(
            flops=4 * terms * sectors * m * m * m,
            bytes_accessed=2 * left_ops.size * 2 + window.size * 2 + sectors * m * m * 4,
            transcendentals=0,
        ),
    )(partner, window, left_ops, right_ops)


def shifted(block, axis, distance):
    devices = range(lax.axis_size(axis))
    route = [((i - distance) % len(devices), i) for i in devices]
    return lax.ppermute(block, axis, route)


def per_device(state_start, left_ops, right_ops, shift, partner, kept):
    sector_local = state_start.shape[0]
    width = state_start.shape[1]
    count = float(sector_local * lax.axis_size("sec") * width * width)
    n_sec = lax.axis_size("sec")
    n_op = lax.axis_size("op")
    kept_prev = shifted(kept, "sec", 1)
    state = state_start
    window = padded(state, (("sec", 0),), sector_local)
    terms = left_ops.shape[0]
    cuts = [terms * k // ITERS for k in range(ITERS + 1)]
    left_pieces = []
    for iteration in range(ITERS):
        partial_sigma = sigma_part(window, left_ops, right_ops, partner)
        final = iteration == ITERS - 1
        window, got = step(
            partial_sigma, window, shift,
            left_ops[cuts[iteration] : cuts[iteration + 1]], count, final, n_sec, n_op,
        )
        left_pieces.append(got)
        state = window[sector_local : 2 * sector_local]
    state_prev = window[:sector_local]
    left_prev = jnp.concatenate(left_pieces, axis=0)
    columns = jnp.arange(width, dtype=jnp.int32)
    keep_mask = (columns[None, :] < kept_prev[:, None]).astype(jnp.bfloat16)
    kept_block = state_prev * keep_mask[:, None, :]
    out_scale = 1.0 / float(width) ** 0.5
    projected = jnp.einsum(
        "tbij,bjk->tbik", left_prev, kept_block, preferred_element_type=jnp.float32
    ).astype(jnp.bfloat16)
    kept_turned = jnp.broadcast_to(
        jnp.swapaxes(kept_block, 1, 2)[None], left_prev.shape
    )
    new_ops = (
        jnp.einsum("tbij,tbjk->tbik", kept_turned, projected, preferred_element_type=jnp.float32)
        * out_scale
    ).astype(jnp.bfloat16)
    return (state, new_ops)


def solution(mesh):
    in_specs = (
        P("sec", None, None),
        P("op", "sec", None, None),
        P("op", "sec", None, None),
        P("sec"),
        P("op", "sec"),
        P("sec"),
    )
    out_specs = (P("sec", None, None), P("op", "sec", None, None))
    return jax.shard_map(
        per_device, mesh=mesh, in_specs=in_specs, out_specs=out_specs, check_vma=False
    )
```

```python
import functools

import jax
import jax.numpy as jnp
from jax import lax
from jax.experimental import pallas as pl
from jax.experimental.pallas import tpu as pltpu
from jax.sharding import PartitionSpec as P

MESH = pl.DeviceIdType.MESH

ITERS = 4


step_size = 0.5


def padded(cells, sides, width):
    for axis, dim in sides:
        count = lax.axis_size(axis)
        head = lax.slice_in_dim(cells, 0, width, axis=dim)
        tail = lax.slice_in_dim(cells, cells.shape[dim] - width, cells.shape[dim], axis=dim)
        cells = jnp.concatenate(
            [
                lax.ppermute(tail, axis, [(i, (i + 1) % count) for i in range(count)]),
                cells,
                lax.ppermute(head, axis, [((i + 1) % count, i) for i in range(count)]),
            ],
            axis=dim,
        )
    return cells


def all_sum_kernel(n_sec, n_op, x_ref, o_ref, op_buf, sec_buf, mid, out_buf,
                   send_a, recv_a, send_b, recv_b, local_sem):
    me_sec = lax.axis_index("sec")
    me_op = lax.axis_index("op")
    barrier = pltpu.get_barrier_semaphore()
    for d in range(1, n_op):
        pl.semaphore_signal(barrier, 1, device_id=(me_sec, (me_op + d) % n_op),
                            device_id_type=MESH)
    for d in range(1, n_sec):
        pl.semaphore_signal(barrier, 1, device_id=((me_sec + d) % n_sec, me_op),
                            device_id_type=MESH)
    pl.semaphore_wait(barrier, n_op - 1 + n_sec - 1)

    def stage(n, me, src, buf, send, recv, peer_of):
        for d in range(1, n):
            pltpu.make_async_remote_copy(
                src_ref=src, dst_ref=buf.at[me], send_sem=send.at[d],
                recv_sem=recv.at[me], device_id=peer_of((me + d) % n),
                device_id_type=MESH).start()
        buf[me] = src[...]
        for d in range(1, n):
            slot = (me + n - d) % n
            pltpu.make_async_remote_copy(
                src_ref=src, dst_ref=buf.at[slot], send_sem=send.at[d],
                recv_sem=recv.at[slot], device_id=peer_of(slot),
                device_id_type=MESH).wait_recv()
        for d in range(1, n):
            pltpu.make_async_remote_copy(
                src_ref=src, dst_ref=buf.at[me], send_sem=send.at[d],
                recv_sem=recv.at[me], device_id=peer_of((me + d) % n),
                device_id_type=MESH).wait_send()
        total = buf[0]
        for j in range(1, n):
            total = total + buf[j]
        return total

    mid[...] = stage(n_op, me_op, x_ref, op_buf, send_a, recv_a,
                     lambda j: (me_sec, j))
    local = pltpu.make_async_copy(mid, out_buf, local_sem)
    local.start()
    local.wait()
    o_ref[...] = stage(n_sec, me_sec, out_buf, sec_buf, send_b, recv_b,
                       lambda j: (j, me_op))


def all_sum(values, n_sec, n_op):
    lane = lax.broadcasted_iota(jnp.int32, (8, 128), 1)
    tile = jnp.zeros((8, 128), jnp.float32)
    for k, v in enumerate(values):
        tile = jnp.where(lane == k, v, tile)
    tile_spec = pl.BlockSpec(memory_space=pltpu.VMEM)
    out = pl.pallas_call(
        functools.partial(all_sum_kernel, n_sec, n_op),
        out_shape=jax.ShapeDtypeStruct((8, 128), jnp.float32),
        in_specs=[tile_spec],
        out_specs=tile_spec,
        scratch_shapes=[
            pltpu.VMEM((n_op, 8, 128), jnp.float32),
            pltpu.VMEM((n_sec, 8, 128), jnp.float32),
            pltpu.VMEM((8, 128), jnp.float32),
            pltpu.VMEM((8, 128), jnp.float32),
            pltpu.SemaphoreType.DMA((n_op,)),
            pltpu.SemaphoreType.DMA((n_op,)),
            pltpu.SemaphoreType.DMA((n_sec,)),
            pltpu.SemaphoreType.DMA((n_sec,)),
            pltpu.SemaphoreType.DMA(()),
        ],
        compiler_params=pltpu.CompilerParams(collective_id=0, has_side_effects=True),
    )(tile)
    return tuple(out[0, k] for k in range(len(values)))


def sigma_sum_kernel(n_sec, n_op, x_ref, t_ref, o_ref, s_ref,
                     rs_buf, red, red_out, ag_buf, op_buf, sec_buf, mid, mid_out,
                     send_rs, recv_rs, send_ag, recv_ag, send_a, recv_a,
                     send_b, recv_b, local_sem):
    me_sec = lax.axis_index("sec")
    me_op = lax.axis_index("op")
    barrier = pltpu.get_barrier_semaphore()
    for d in range(1, n_op):
        pl.semaphore_signal(barrier, 1, device_id=(me_sec, (me_op + d) % n_op),
                            device_id_type=MESH)
    for d in range(1, n_sec):
        pl.semaphore_signal(barrier, 1, device_id=((me_sec + d) % n_sec, me_op),
                            device_id_type=MESH)
    pl.semaphore_wait(barrier, n_op - 1 + n_sec - 1)

    def op_peer(j):
        return (me_sec, j)

    def sec_peer(j):
        return (j, me_op)

    def total_of(v):
        return jnp.sum(jnp.sum(v, axis=1, keepdims=True), axis=0, keepdims=True)

    lane = lax.broadcasted_iota(jnp.int32, (8, 128), 1)
    own = st_ref[n_op + me_op].astype(jnp.float32)
    own_square = total_of(own * own)
    energy = sh_ref[me_op] * own_square
    for j in range(n_op):
        energy = energy + total_of(x_ref[j] * st_ref[n_op + j].astype(jnp.float32))
    t_ref[...] = jnp.where(lane == 0, energy, jnp.where(lane == 1, own_square, 0.0))
    settle(t_ref, t_out, local_sem.at[4])

    def rs_copy(d):
        j = (me_op + d) % n_op
        return pltpu.make_async_remote_copy(
            src_ref=x_ref.at[j], dst_ref=rs_buf.at[me_op], send_sem=send_rs.at[d],
            recv_sem=recv_rs.at[me_op], device_id=op_peer(j), device_id_type=MESH)

    def rs_recv(d):
        slot = (me_op + n_op - d) % n_op
        return pltpu.make_async_remote_copy(
            src_ref=x_ref.at[me_op], dst_ref=rs_buf.at[slot], send_sem=send_rs.at[d],
            recv_sem=recv_rs.at[slot], device_id=op_peer(slot), device_id_type=MESH)

    def gather_copy(n, me, src, buf, send, recv, peer_of, d):
        return pltpu.make_async_remote_copy(
            src_ref=src, dst_ref=buf.at[me], send_sem=send.at[d],
            recv_sem=recv.at[me], device_id=peer_of((me + d) % n), device_id_type=MESH)

    def gather_recv(n, me, src, buf, send, recv, peer_of, d):
        slot = (me + n - d) % n
        return pltpu.make_async_remote_copy(
            src_ref=src, dst_ref=buf.at[slot], send_sem=send.at[d],
            recv_sem=recv.at[slot], device_id=peer_of(slot), device_id_type=MESH)

    def ordered_sum(buf, n):
        total = buf[0]
        for j in range(1, n):
            total = total + buf[j]
        return total

    for d in range(1, n_op):
        rs_copy(d).start()
    a_args = (n_op, me_op, t_out, op_buf, send_a, recv_a, op_peer)
    for d in range(1, n_op):
        gather_copy(*a_args, d).start()
    rs_buf[me_op] = x_ref[me_op]
    op_buf[me_op] = t_ref[...]

    for d in range(1, n_op):
        gather_recv(*a_args, d).wait_recv()
    mid[...] = ordered_sum(op_buf, n_op)
    local = pltpu.make_async_copy(mid, mid_out, local_sem.at[0])
    local.start()
    local.wait()
    b_args = (n_sec, me_sec, mid_out, sec_buf, send_b, recv_b, sec_peer)
    for d in range(1, n_sec):
        gather_copy(*b_args, d).start()
    sec_buf[me_sec] = mid_out[...]

    for d in range(1, n_op):
        rs_recv(d).wait_recv()
    red[...] = ordered_sum(rs_buf, n_op)
    local = pltpu.make_async_copy(red, red_out, local_sem.at[1])
    local.start()
    local.wait()
    g_args = (n_op, me_op, red_out, ag_buf, send_ag, recv_ag, op_peer)
    for d in range(1, n_op):
        gather_copy(*g_args, d).start()
    ag_buf[me_op] = red_out[...]

    for d in range(1, n_sec):
        gather_recv(*b_args, d).wait_recv()
    s_ref[...] = ordered_sum(sec_buf, n_sec)
    for d in range(1, n_op):
        gather_recv(*g_args, d).wait_recv()
    o_ref[...] = ag_buf[...]

    for d in range(1, n_op):
        rs_copy(d).wait_send()
        gather_copy(*a_args, d).wait_send()
        gather_copy(*g_args, d).wait_send()
    for d in range(1, n_sec):
        gather_copy(*b_args, d).wait_send()


def sigma_sum(partial, values, n_sec, n_op):
    shape = partial.shape
    rows = shape[0] * shape[1] // n_op
    chunks = partial.reshape(n_op, rows, shape[2])
    lane = lax.broadcasted_iota(jnp.int32, (8, 128), 1)
    tile = jnp.zeros((8, 128), jnp.float32)
    for k, v in enumerate(values):
        tile = jnp.where(lane == k, v, tile)
    vmem = pl.BlockSpec(memory_space=pltpu.VMEM)
    total, sums = pl.pallas_call(
        functools.partial(sigma_sum_kernel, n_sec, n_op),
        out_shape=(
            jax.ShapeDtypeStruct(chunks.shape, jnp.float32),
            jax.ShapeDtypeStruct((8, 128), jnp.float32),
        ),
        in_specs=[vmem, vmem],
        out_specs=(vmem, vmem),
        scratch_shapes=[
            pltpu.VMEM(chunks.shape, jnp.float32),
            pltpu.VMEM((rows, shape[2]), jnp.float32),
            pltpu.VMEM((rows, shape[2]), jnp.float32),
            pltpu.VMEM(chunks.shape, jnp.float32),
            pltpu.VMEM((n_op, 8, 128), jnp.float32),
            pltpu.VMEM((n_sec, 8, 128), jnp.float32),
            pltpu.VMEM((8, 128), jnp.float32),
            pltpu.VMEM((8, 128), jnp.float32),
            pltpu.SemaphoreType.DMA((n_op,)),
            pltpu.SemaphoreType.DMA((n_op,)),
            pltpu.SemaphoreType.DMA((n_op,)),
            pltpu.SemaphoreType.DMA((n_op,)),
            pltpu.SemaphoreType.DMA((n_op,)),
            pltpu.SemaphoreType.DMA((n_op,)),
            pltpu.SemaphoreType.DMA((n_sec,)),
            pltpu.SemaphoreType.DMA((n_sec,)),
            pltpu.SemaphoreType.DMA((2,)),
        ],
        compiler_params=pltpu.CompilerParams(collective_id=1, has_side_effects=True),
    )(chunks, tile)
    return total.reshape(shape), tuple(sums[0, k] for k in range(len(values)))


def step_kernel(n_sec, n_op, count, final, x_ref, st_ref, sh_ref, piece_ref, *refs):
    if final:
        (win_ref, got_ref, t_ref, t_out, rs_buf, red, op_buf, sec_buf, mid, mid_out,
         op_buf2, sec_buf2, mid2, mid2_out, mid3, mid3_out, new_buf, new_out, win_buf,
         part, part_out, part2, part2_out,
         send_rs, recv_rs, send_a, recv_a, send_b, recv_b, send_a2, recv_a2, send_b2,
         recv_b2, send_w, recv_w, local_sem) = refs
    else:
        (win_ref, got_ref, t_ref, t_out, rs_buf, red, op_buf, sec_buf, mid, mid_out,
         new_buf, new_out, win_buf, part, part_out, send_rs, recv_rs, send_a, recv_a, send_b, recv_b, send_w,
         recv_w, local_sem) = refs
    me_sec = lax.axis_index("sec")
    me_op = lax.axis_index("op")
    prev_sec = (me_sec + n_sec - 1) % n_sec
    next_sec = (me_sec + 1) % n_sec
    barrier = pltpu.get_barrier_semaphore()
    row_len = 8 if n_sec % 8 == 0 else (2 if n_sec % 2 == 0 else n_sec)
    n_rows = n_sec // row_len
    row = me_sec // row_len
    col = me_sec % row_len
    greet = [(me_sec, (me_op + d) % n_op) for d in range(1, n_op)]
    greet += [(row * row_len + (col + d) % row_len, me_op) for d in range(1, row_len)]
    greet += [(((row + d) % n_rows) * row_len + col, me_op) for d in range(1, n_rows)]
    greet += [(side, j) for side in (prev_sec, next_sec) for j in range(n_op)]
    for peer in greet:
        pl.semaphore_signal(barrier, 1, device_id=peer, device_id_type=MESH)
    greeted = len(greet)
    pl.semaphore_wait(barrier, greeted)

    def op_peer(j):
        return (me_sec, j)

    def sec_peer(j):
        return (j, me_op)

    def copy_to(src, dst, send, recv, peer):
        return pltpu.make_async_remote_copy(
            src_ref=src, dst_ref=dst, send_sem=send, recv_sem=recv,
            device_id=peer, device_id_type=MESH)

    def ordered_sum(buf, n):
        total = buf[0]
        for j in range(1, n):
            total = total + buf[j]
        return total

    def start_gather(n, me, src, buf, send, recv, peer_of):
        for d in range(1, n):
            copy_to(src, buf.at[me], send.at[d], recv.at[me], peer_of((me + d) % n)).start()
        buf[me] = src[...]

    def wait_gather(n, me, src, buf, send, recv, peer_of):
        for d in range(1, n):
            slot = (me + n - d) % n
            copy_to(src, buf.at[slot], send.at[d], recv.at[slot], peer_of(slot)).wait_recv()

    def drain_gather(n, me, src, buf, send, recv, peer_of):
        for d in range(1, n):
            copy_to(src, buf.at[me], send.at[d], recv.at[me], peer_of((me + d) % n)).wait_send()

    def settle(src, dst, sem):
        local = pltpu.make_async_copy(src, dst, sem)
        local.start()
        local.wait()

    def total_of(v):
        return jnp.sum(jnp.sum(v, axis=1, keepdims=True), axis=0, keepdims=True)

    lane = lax.broadcasted_iota(jnp.int32, (8, 128), 1)
    own = st_ref[n_op + me_op].astype(jnp.float32)
    own_square = total_of(own * own)
    energy = sh_ref[me_op] * own_square
    for j in range(n_op):
        energy = energy + total_of(x_ref[j] * st_ref[n_op + j].astype(jnp.float32))
    t_ref[...] = jnp.where(lane == 0, energy, jnp.where(lane == 1, own_square, 0.0))
    settle(t_ref, t_out, local_sem.at[4])

    def row_peer(c):
        return (row * row_len + c, me_op)

    def col_peer(r):
        return (r * row_len + col, me_op)

    def start_rows(src, buf, send, recv):
        for d in range(1, row_len):
            copy_to(src, buf.at[col], send.at[d], recv.at[col],
                    row_peer((col + d) % row_len)).start()
        buf[col] = src[...]

    def finish_sec(src, buf, send, recv, mid_sum, mid_out, sem):
        for d in range(1, row_len):
            slot = (col + row_len - d) % row_len
            copy_to(src, buf.at[slot], send.at[d], recv.at[slot], row_peer(slot)).wait_recv()
        mid_sum[...] = ordered_sum(buf, row_len)
        settle(mid_sum, mid_out, sem)
        for d in range(1, n_rows):
            copy_to(mid_out, buf.at[row_len + row], send.at[row_len + d],
                    recv.at[row_len + row], col_peer((row + d) % n_rows)).start()
        buf[row_len + row] = mid_out[...]
        for d in range(1, n_rows):
            slot = (row + n_rows - d) % n_rows
            copy_to(mid_out, buf.at[row_len + slot], send.at[row_len + d],
                    recv.at[row_len + slot], col_peer(slot)).wait_recv()
        total = buf[row_len]
        for r in range(1, n_rows):
            total = total + buf[row_len + r]
        return total

    def drain_sec(src, buf, send, recv, mid_out):
        for d in range(1, row_len):
            copy_to(src, buf.at[col], send.at[d], recv.at[col],
                    row_peer((col + d) % row_len)).wait_send()
        for d in range(1, n_rows):
            copy_to(mid_out, buf.at[row_len + row], send.at[row_len + d],
                    recv.at[row_len + row], col_peer((row + d) % n_rows)).wait_send()

    def rs_copy(d):
        j = (me_op + d) % n_op
        return copy_to(x_ref.at[j], rs_buf.at[me_op], send_rs.at[d], recv_rs.at[me_op], op_peer(j))

    for d in range(1, n_op):
        rs_copy(d).start()
    a_args = (n_op, me_op, t_out, op_buf, send_a, recv_a, op_peer)
    start_gather(*a_args)
    rs_buf[me_op] = x_ref[me_op]

    operators = copy_to(piece_ref, got_ref, send_w.at[send_w.shape[0] - 1],
                        recv_w.at[recv_w.shape[0] - 1], (next_sec, me_op))
    operators.start()

    wait_gather(*a_args)
    mid[...] = ordered_sum(op_buf, n_op)
    settle(mid, mid_out, local_sem.at[0])
    start_rows(mid_out, sec_buf, send_b, recv_b)

    for d in range(1, n_op):
        slot = (me_op + n_op - d) % n_op
        copy_to(x_ref.at[me_op], rs_buf.at[slot], send_rs.at[d], recv_rs.at[slot],
                op_peer(slot)).wait_recv()
    red[...] = ordered_sum(rs_buf, n_op)

    sums = finish_sec(mid_out, sec_buf, send_b, recv_b, part, part_out, local_sem.at[5])
    energy_sum = sums[0:1, 0:1]
    norm_sum = sums[0:1, 1:2]
    state_wide = st_ref[n_op + me_op].astype(jnp.float32)
    sigma = red[...] + sh_ref[me_op] * state_wide
    updated = state_wide - step_size * (sigma - (energy_sum / norm_sum) * state_wide)
    if final:
        square = total_of(updated * updated)
        mid2[...] = jnp.where(lane == 0, square, 0.0)
        settle(mid2, mid2_out, local_sem.at[1])
        a2_args = (n_op, me_op, mid2_out, op_buf2, send_a2, recv_a2, op_peer)
        start_gather(*a2_args)
        wait_gather(*a2_args)
        mid3[...] = ordered_sum(op_buf2, n_op)
        settle(mid3, mid3_out, local_sem.at[3])
        start_rows(mid3_out, sec_buf2, send_b2, recv_b2)
        new_norm = finish_sec(mid3_out, sec_buf2, send_b2, recv_b2, part2, part2_out,
                              local_sem.at[6])[0:1, 0:1]
        factor = jnp.sqrt(count / new_norm)
    else:
        factor = jnp.sqrt(count / norm_sum)
    new_buf[...] = (updated * factor).astype(new_buf.dtype)
    settle(new_buf, new_out, local_sem.at[2])

    sides = ((next_sec, 0),) if final else ((next_sec, 0), (prev_sec, 2 * n_op))
    sent = 0
    for side, base in sides:
        for j in range(n_op):
            copy_to(new_out, win_buf.at[base + me_op], send_w.at[sent],
                    recv_w.at[base + me_op], (side, j)).start()
            sent += 1
    for d in range(1, n_op):
        j = (me_op + d) % n_op
        copy_to(new_out, win_buf.at[n_op + me_op], send_w.at[sent],
                recv_w.at[n_op + me_op], op_peer(j)).start()
        sent += 1
    win_buf[n_op + me_op] = new_out[...]

    from_sides = ((prev_sec, 0),) if final else ((prev_sec, 0), (next_sec, 2 * n_op))
    for side, base in from_sides:
        for j in range(n_op):
            copy_to(new_out, win_buf.at[base + j], send_w.at[0], recv_w.at[base + j],
                    (side, j)).wait_recv()
    for d in range(1, n_op):
        slot = (me_op + n_op - d) % n_op
        copy_to(new_out, win_buf.at[n_op + slot], send_w.at[0], recv_w.at[n_op + slot],
                op_peer(slot)).wait_recv()
    win_ref[...] = win_buf[...]
    operators.wait_recv()

    operators.wait_send()
    for d in range(1, n_op):
        rs_copy(d).wait_send()
    drain_gather(*a_args)
    drain_sec(mid_out, sec_buf, send_b, recv_b, part_out)
    if final:
        drain_gather(*a2_args)
        drain_sec(mid3_out, sec_buf2, send_b2, recv_b2, part2_out)
    for k in range(sent):
        copy_to(new_out, win_buf.at[n_op + me_op], send_w.at[k], recv_w.at[n_op + me_op],
                op_peer((me_op + 1) % n_op)).wait_send()


def step(partial, window, shift, piece, count, final, n_sec, n_op):
    shape = partial.shape
    rows = shape[0] * shape[1] // n_op
    chunks = partial.reshape(n_op, rows, shape[2])
    state_chunks = window.reshape(-1, rows, shape[2])
    shift_chunks = jnp.repeat(shift, n_op // shape[0])[:, None, None]
    slots = (2 if final else 3) * n_op
    tile_shape = (rows, shape[2])
    scalar_bufs = [
        pltpu.VMEM((n_op, 8, 128), jnp.float32),
        pltpu.VMEM((n_sec, 8, 128), jnp.float32),
        pltpu.VMEM((8, 128), jnp.float32),
        pltpu.VMEM((8, 128), jnp.float32),
    ]
    scratch = [
        pltpu.VMEM((8, 128), jnp.float32),
        pltpu.VMEM((8, 128), jnp.float32),
        pltpu.VMEM(chunks.shape, jnp.float32),
        pltpu.VMEM(tile_shape, jnp.float32),
    ] + scalar_bufs + (scalar_bufs + scalar_bufs[2:] if final else []) + [
        pltpu.VMEM(tile_shape, jnp.bfloat16),
        pltpu.VMEM(tile_shape, jnp.bfloat16),
        pltpu.VMEM((slots, rows, shape[2]), jnp.bfloat16),
    ] + [pltpu.VMEM((8, 128), jnp.float32)] * (4 if final else 2) + [
        pltpu.SemaphoreType.DMA((n_op,)),
        pltpu.SemaphoreType.DMA((n_op,)),
        pltpu.SemaphoreType.DMA((n_op,)),
        pltpu.SemaphoreType.DMA((n_op,)),
        pltpu.SemaphoreType.DMA((n_sec,)),
        pltpu.SemaphoreType.DMA((n_sec,)),
    ] + ([
        pltpu.SemaphoreType.DMA((n_op,)),
        pltpu.SemaphoreType.DMA((n_op,)),
        pltpu.SemaphoreType.DMA((n_sec,)),
        pltpu.SemaphoreType.DMA((n_sec,)),
    ] if final else []) + [
        pltpu.SemaphoreType.DMA((slots + n_op + 1,)),
        pltpu.SemaphoreType.DMA((slots + 1,)),
        pltpu.SemaphoreType.DMA((7,)),
    ]
    vmem = pl.BlockSpec(memory_space=pltpu.VMEM)
    anywhere = pl.BlockSpec(memory_space=pl.ANY)
    window, got = pl.pallas_call(
        functools.partial(step_kernel, n_sec, n_op, count, final),
        out_shape=(
            jax.ShapeDtypeStruct((slots, rows, shape[2]), jnp.bfloat16),
            jax.ShapeDtypeStruct(piece.shape, piece.dtype),
        ),
        in_specs=[vmem, vmem, vmem, anywhere],
        out_specs=(vmem, anywhere),
        scratch_shapes=scratch,
        compiler_params=pltpu.CompilerParams(
            collective_id=3 if final else 2, has_side_effects=True
        ),
    )(chunks, state_chunks, shift_chunks, piece)
    return window.reshape(slots // (n_op // shape[0]), shape[1], shape[2]), got


def sigma_part_kernel(partner_ref, win_ref, left_ref, right_ref, o_ref):
    b = pl.program_id(0)
    total = jnp.zeros(o_ref.shape[1:], jnp.float32)
    for t in range(left_ref.shape[0]):
        source = win_ref[partner_ref[t, b]]
        halfway = jnp.dot(left_ref[t, 0], source, preferred_element_type=jnp.float32)
        total = total + jnp.dot(halfway.astype(jnp.bfloat16), right_ref[t, 0],
                                preferred_element_type=jnp.float32)
    o_ref[0] = total


def sigma_part(window, left_ops, right_ops, partner):
    terms, sectors, m, _ = left_ops.shape
    op_spec = pl.BlockSpec((terms, 1, m, m), lambda b, p: (0, b, 0, 0))
    return pl.pallas_call(
        sigma_part_kernel,
        out_shape=jax.ShapeDtypeStruct((sectors, m, m), jnp.float32),
        grid_spec=pltpu.PrefetchScalarGridSpec(
            num_scalar_prefetch=1,
            grid=(sectors,),
            in_specs=[
                pl.BlockSpec(window.shape, lambda b, p: (0, 0, 0)),
                op_spec,
                op_spec,
            ],
            out_specs=pl.BlockSpec((1, m, m), lambda b, p: (b, 0, 0)),
        ),
        cost_estimate=pl.CostEstimate(
            flops=4 * terms * sectors * m * m * m,
            bytes_accessed=2 * left_ops.size * 2 + window.size * 2 + sectors * m * m * 4,
            transcendentals=0,
        ),
    )(partner, window, left_ops, right_ops)


def shifted(block, axis, distance):
    devices = range(lax.axis_size(axis))
    route = [((i - distance) % len(devices), i) for i in devices]
    return lax.ppermute(block, axis, route)


def per_device(state_start, left_ops, right_ops, shift, partner, kept):
    sector_local = state_start.shape[0]
    width = state_start.shape[1]
    count = float(sector_local * lax.axis_size("sec") * width * width)
    n_sec = lax.axis_size("sec")
    n_op = lax.axis_size("op")
    kept_prev = shifted(kept, "sec", 1)
    state = state_start
    window = padded(state, (("sec", 0),), sector_local)
    terms = left_ops.shape[0]
    cuts = [terms * k // ITERS for k in range(ITERS + 1)]
    left_pieces = []
    for iteration in range(ITERS):
        partial_sigma = sigma_part(window, left_ops, right_ops, partner)
        final = iteration == ITERS - 1
        window, got = step(
            partial_sigma, window, shift,
            left_ops[cuts[iteration] : cuts[iteration + 1]], count, final, n_sec, n_op,
        )
        left_pieces.append(got)
        state = window[sector_local : 2 * sector_local]
    state_prev = window[:sector_local]
    left_prev = jnp.concatenate(left_pieces, axis=0)
    columns = jnp.arange(width, dtype=jnp.int32)
    keep_mask = (columns[None, :] < kept_prev[:, None]).astype(jnp.bfloat16)
    kept_block = state_prev * keep_mask[:, None, :]
    out_scale = 1.0 / float(width) ** 0.5
    projected = jnp.einsum(
        "tbij,bjk->tbik", left_prev, kept_block, preferred_element_type=jnp.float32
    ).astype(jnp.bfloat16)
    kept_turned = jnp.broadcast_to(
        jnp.swapaxes(kept_block, 1, 2)[None], left_prev.shape
    )
    new_ops = (
        jnp.einsum("tbij,tbjk->tbik", kept_turned, projected, preferred_element_type=jnp.float32)
        * out_scale
    ).astype(jnp.bfloat16)
    return (state, new_ops)


def solution(mesh):
    in_specs = (
        P("sec", None, None),
        P("op", "sec", None, None),
        P("op", "sec", None, None),
        P("sec"),
        P("op", "sec"),
        P("sec"),
    )
    out_specs = (P("sec", None, None), P("op", "sec", None, None))
    return jax.shard_map(
        per_device, mesh=mesh, in_specs=in_specs, out_specs=out_specs, check_vma=False
    )
```

```python
import functools

import jax
import jax.numpy as jnp
from jax import lax
from jax.experimental import pallas as pl
from jax.experimental.pallas import tpu as pltpu
from jax.sharding import PartitionSpec as P

MESH = pl.DeviceIdType.MESH

ITERS = 4


step_size = 0.5


def padded(cells, sides, width):
    for axis, dim in sides:
        count = lax.axis_size(axis)
        head = lax.slice_in_dim(cells, 0, width, axis=dim)
        tail = lax.slice_in_dim(cells, cells.shape[dim] - width, cells.shape[dim], axis=dim)
        cells = jnp.concatenate(
            [
                lax.ppermute(tail, axis, [(i, (i + 1) % count) for i in range(count)]),
                cells,
                lax.ppermute(head, axis, [((i + 1) % count, i) for i in range(count)]),
            ],
            axis=dim,
        )
    return cells


def all_sum_kernel(n_sec, n_op, x_ref, o_ref, op_buf, sec_buf, mid, out_buf,
                   send_a, recv_a, send_b, recv_b, local_sem):
    me_sec = lax.axis_index("sec")
    me_op = lax.axis_index("op")
    barrier = pltpu.get_barrier_semaphore()
    for d in range(1, n_op):
        pl.semaphore_signal(barrier, 1, device_id=(me_sec, (me_op + d) % n_op),
                            device_id_type=MESH)
    for d in range(1, n_sec):
        pl.semaphore_signal(barrier, 1, device_id=((me_sec + d) % n_sec, me_op),
                            device_id_type=MESH)
    pl.semaphore_wait(barrier, n_op - 1 + n_sec - 1)

    def stage(n, me, src, buf, send, recv, peer_of):
        for d in range(1, n):
            pltpu.make_async_remote_copy(
                src_ref=src, dst_ref=buf.at[me], send_sem=send.at[d],
                recv_sem=recv.at[me], device_id=peer_of((me + d) % n),
                device_id_type=MESH).start()
        buf[me] = src[...]
        for d in range(1, n):
            slot = (me + n - d) % n
            pltpu.make_async_remote_copy(
                src_ref=src, dst_ref=buf.at[slot], send_sem=send.at[d],
                recv_sem=recv.at[slot], device_id=peer_of(slot),
                device_id_type=MESH).wait_recv()
        for d in range(1, n):
            pltpu.make_async_remote_copy(
                src_ref=src, dst_ref=buf.at[me], send_sem=send.at[d],
                recv_sem=recv.at[me], device_id=peer_of((me + d) % n),
                device_id_type=MESH).wait_send()
        total = buf[0]
        for j in range(1, n):
            total = total + buf[j]
        return total

    mid[...] = stage(n_op, me_op, x_ref, op_buf, send_a, recv_a,
                     lambda j: (me_sec, j))
    local = pltpu.make_async_copy(mid, out_buf, local_sem)
    local.start()
    local.wait()
    o_ref[...] = stage(n_sec, me_sec, out_buf, sec_buf, send_b, recv_b,
                       lambda j: (j, me_op))


def all_sum(values, n_sec, n_op):
    lane = lax.broadcasted_iota(jnp.int32, (8, 128), 1)
    tile = jnp.zeros((8, 128), jnp.float32)
    for k, v in enumerate(values):
        tile = jnp.where(lane == k, v, tile)
    tile_spec = pl.BlockSpec(memory_space=pltpu.VMEM)
    out = pl.pallas_call(
        functools.partial(all_sum_kernel, n_sec, n_op),
        out_shape=jax.ShapeDtypeStruct((8, 128), jnp.float32),
        in_specs=[tile_spec],
        out_specs=tile_spec,
        scratch_shapes=[
            pltpu.VMEM((n_op, 8, 128), jnp.float32),
            pltpu.VMEM((n_sec, 8, 128), jnp.float32),
            pltpu.VMEM((8, 128), jnp.float32),
            pltpu.VMEM((8, 128), jnp.float32),
            pltpu.SemaphoreType.DMA((n_op,)),
            pltpu.SemaphoreType.DMA((n_op,)),
            pltpu.SemaphoreType.DMA((n_sec,)),
            pltpu.SemaphoreType.DMA((n_sec,)),
            pltpu.SemaphoreType.DMA(()),
        ],
        compiler_params=pltpu.CompilerParams(collective_id=0, has_side_effects=True),
    )(tile)
    return tuple(out[0, k] for k in range(len(values)))


def sigma_sum_kernel(n_sec, n_op, x_ref, t_ref, o_ref, s_ref,
                     rs_buf, red, red_out, ag_buf, op_buf, sec_buf, mid, mid_out,
                     send_rs, recv_rs, send_ag, recv_ag, send_a, recv_a,
                     send_b, recv_b, local_sem):
    me_sec = lax.axis_index("sec")
    me_op = lax.axis_index("op")
    barrier = pltpu.get_barrier_semaphore()
    for d in range(1, n_op):
        pl.semaphore_signal(barrier, 1, device_id=(me_sec, (me_op + d) % n_op),
                            device_id_type=MESH)
    for d in range(1, n_sec):
        pl.semaphore_signal(barrier, 1, device_id=((me_sec + d) % n_sec, me_op),
                            device_id_type=MESH)
    pl.semaphore_wait(barrier, n_op - 1 + n_sec - 1)

    def op_peer(j):
        return (me_sec, j)

    def sec_peer(j):
        return (j, me_op)

    def total_of(v):
        return jnp.sum(jnp.sum(v, axis=1, keepdims=True), axis=0, keepdims=True)

    lane = lax.broadcasted_iota(jnp.int32, (8, 128), 1)
    own = st_ref[n_op + me_op].astype(jnp.float32)
    own_square = total_of(own * own)
    energy = sh_ref[me_op] * own_square
    for j in range(n_op):
        energy = energy + total_of(x_ref[j] * st_ref[n_op + j].astype(jnp.float32))
    t_ref[...] = jnp.where(lane == 0, energy, jnp.where(lane == 1, own_square, 0.0))
    settle(t_ref, t_out, local_sem.at[4])

    def rs_copy(d):
        j = (me_op + d) % n_op
        return pltpu.make_async_remote_copy(
            src_ref=x_ref.at[j], dst_ref=rs_buf.at[me_op], send_sem=send_rs.at[d],
            recv_sem=recv_rs.at[me_op], device_id=op_peer(j), device_id_type=MESH)

    def rs_recv(d):
        slot = (me_op + n_op - d) % n_op
        return pltpu.make_async_remote_copy(
            src_ref=x_ref.at[me_op], dst_ref=rs_buf.at[slot], send_sem=send_rs.at[d],
            recv_sem=recv_rs.at[slot], device_id=op_peer(slot), device_id_type=MESH)

    def gather_copy(n, me, src, buf, send, recv, peer_of, d):
        return pltpu.make_async_remote_copy(
            src_ref=src, dst_ref=buf.at[me], send_sem=send.at[d],
            recv_sem=recv.at[me], device_id=peer_of((me + d) % n), device_id_type=MESH)

    def gather_recv(n, me, src, buf, send, recv, peer_of, d):
        slot = (me + n - d) % n
        return pltpu.make_async_remote_copy(
            src_ref=src, dst_ref=buf.at[slot], send_sem=send.at[d],
            recv_sem=recv.at[slot], device_id=peer_of(slot), device_id_type=MESH)

    def ordered_sum(buf, n):
        total = buf[0]
        for j in range(1, n):
            total = total + buf[j]
        return total

    for d in range(1, n_op):
        rs_copy(d).start()
    a_args = (n_op, me_op, t_out, op_buf, send_a, recv_a, op_peer)
    for d in range(1, n_op):
        gather_copy(*a_args, d).start()
    rs_buf[me_op] = x_ref[me_op]
    op_buf[me_op] = t_ref[...]

    for d in range(1, n_op):
        gather_recv(*a_args, d).wait_recv()
    mid[...] = ordered_sum(op_buf, n_op)
    local = pltpu.make_async_copy(mid, mid_out, local_sem.at[0])
    local.start()
    local.wait()
    b_args = (n_sec, me_sec, mid_out, sec_buf, send_b, recv_b, sec_peer)
    for d in range(1, n_sec):
        gather_copy(*b_args, d).start()
    sec_buf[me_sec] = mid_out[...]

    for d in range(1, n_op):
        rs_recv(d).wait_recv()
    red[...] = ordered_sum(rs_buf, n_op)
    local = pltpu.make_async_copy(red, red_out, local_sem.at[1])
    local.start()
    local.wait()
    g_args = (n_op, me_op, red_out, ag_buf, send_ag, recv_ag, op_peer)
    for d in range(1, n_op):
        gather_copy(*g_args, d).start()
    ag_buf[me_op] = red_out[...]

    for d in range(1, n_sec):
        gather_recv(*b_args, d).wait_recv()
    s_ref[...] = ordered_sum(sec_buf, n_sec)
    for d in range(1, n_op):
        gather_recv(*g_args, d).wait_recv()
    o_ref[...] = ag_buf[...]

    for d in range(1, n_op):
        rs_copy(d).wait_send()
        gather_copy(*a_args, d).wait_send()
        gather_copy(*g_args, d).wait_send()
    for d in range(1, n_sec):
        gather_copy(*b_args, d).wait_send()


def sigma_sum(partial, values, n_sec, n_op):
    shape = partial.shape
    rows = shape[0] * shape[1] // n_op
    chunks = partial.reshape(n_op, rows, shape[2])
    lane = lax.broadcasted_iota(jnp.int32, (8, 128), 1)
    tile = jnp.zeros((8, 128), jnp.float32)
    for k, v in enumerate(values):
        tile = jnp.where(lane == k, v, tile)
    vmem = pl.BlockSpec(memory_space=pltpu.VMEM)
    total, sums = pl.pallas_call(
        functools.partial(sigma_sum_kernel, n_sec, n_op),
        out_shape=(
            jax.ShapeDtypeStruct(chunks.shape, jnp.float32),
            jax.ShapeDtypeStruct((8, 128), jnp.float32),
        ),
        in_specs=[vmem, vmem],
        out_specs=(vmem, vmem),
        scratch_shapes=[
            pltpu.VMEM(chunks.shape, jnp.float32),
            pltpu.VMEM((rows, shape[2]), jnp.float32),
            pltpu.VMEM((rows, shape[2]), jnp.float32),
            pltpu.VMEM(chunks.shape, jnp.float32),
            pltpu.VMEM((n_op, 8, 128), jnp.float32),
            pltpu.VMEM((n_sec, 8, 128), jnp.float32),
            pltpu.VMEM((8, 128), jnp.float32),
            pltpu.VMEM((8, 128), jnp.float32),
            pltpu.SemaphoreType.DMA((n_op,)),
            pltpu.SemaphoreType.DMA((n_op,)),
            pltpu.SemaphoreType.DMA((n_op,)),
            pltpu.SemaphoreType.DMA((n_op,)),
            pltpu.SemaphoreType.DMA((n_op,)),
            pltpu.SemaphoreType.DMA((n_op,)),
            pltpu.SemaphoreType.DMA((n_sec,)),
            pltpu.SemaphoreType.DMA((n_sec,)),
            pltpu.SemaphoreType.DMA((2,)),
        ],
        compiler_params=pltpu.CompilerParams(collective_id=1, has_side_effects=True),
    )(chunks, tile)
    return total.reshape(shape), tuple(sums[0, k] for k in range(len(values)))


def step_kernel(n_sec, n_op, count, final, x_ref, st_ref, sh_ref, piece_ref, *refs):
    if final:
        (win_ref, got_ref, t_ref, t_out, rs_buf, red, op_buf, sec_buf, mid, mid_out,
         op_buf2, sec_buf2, mid2, mid2_out, mid3, mid3_out, new_buf, new_out, win_buf,
         part, part_out, part2, part2_out,
         send_rs, recv_rs, send_a, recv_a, send_b, recv_b, send_a2, recv_a2, send_b2,
         recv_b2, send_w, recv_w, local_sem) = refs
    else:
        (win_ref, got_ref, t_ref, t_out, rs_buf, red, op_buf, sec_buf, mid, mid_out,
         new_buf, new_out, win_buf, part, part_out, send_rs, recv_rs, send_a, recv_a, send_b, recv_b, send_w,
         recv_w, local_sem) = refs
    me_sec = lax.axis_index("sec")
    me_op = lax.axis_index("op")
    prev_sec = (me_sec + n_sec - 1) % n_sec
    next_sec = (me_sec + 1) % n_sec
    barrier = pltpu.get_barrier_semaphore()
    row_len = 8 if n_sec % 8 == 0 else (2 if n_sec % 2 == 0 else n_sec)
    n_rows = n_sec // row_len
    row = me_sec // row_len
    col = me_sec % row_len
    greet = [(me_sec, (me_op + d) % n_op) for d in range(1, n_op)]
    greet += [(row * row_len + (col + d) % row_len, me_op) for d in range(1, row_len)]
    greet += [(((row + d) % n_rows) * row_len + col, me_op) for d in range(1, n_rows)]
    greet += [(side, j) for side in (prev_sec, next_sec) for j in range(n_op)]
    for peer in greet:
        pl.semaphore_signal(barrier, 1, device_id=peer, device_id_type=MESH)
    greeted = len(greet)
    pl.semaphore_wait(barrier, greeted)

    def op_peer(j):
        return (me_sec, j)

    def sec_peer(j):
        return (j, me_op)

    def copy_to(src, dst, send, recv, peer):
        return pltpu.make_async_remote_copy(
            src_ref=src, dst_ref=dst, send_sem=send, recv_sem=recv,
            device_id=peer, device_id_type=MESH)

    def ordered_sum(buf, n):
        total = buf[0]
        for j in range(1, n):
            total = total + buf[j]
        return total

    def start_gather(n, me, src, buf, send, recv, peer_of):
        for d in range(1, n):
            copy_to(src, buf.at[me], send.at[d], recv.at[me], peer_of((me + d) % n)).start()
        buf[me] = src[...]

    def wait_gather(n, me, src, buf, send, recv, peer_of):
        for d in range(1, n):
            slot = (me + n - d) % n
            copy_to(src, buf.at[slot], send.at[d], recv.at[slot], peer_of(slot)).wait_recv()

    def drain_gather(n, me, src, buf, send, recv, peer_of):
        for d in range(1, n):
            copy_to(src, buf.at[me], send.at[d], recv.at[me], peer_of((me + d) % n)).wait_send()

    def settle(src, dst, sem):
        local = pltpu.make_async_copy(src, dst, sem)
        local.start()
        local.wait()

    def total_of(v):
        return jnp.sum(jnp.sum(v, axis=1, keepdims=True), axis=0, keepdims=True)

    lane = lax.broadcasted_iota(jnp.int32, (8, 128), 1)
    own = st_ref[n_op + me_op].astype(jnp.float32)
    own_square = total_of(own * own)
    energy = sh_ref[me_op] * own_square
    for j in range(n_op):
        energy = energy + total_of(x_ref[j] * st_ref[n_op + j].astype(jnp.float32))
    t_ref[...] = jnp.where(lane == 0, energy, jnp.where(lane == 1, own_square, 0.0))
    settle(t_ref, t_out, local_sem.at[4])

    def row_peer(c):
        return (row * row_len + c, me_op)

    def col_peer(r):
        return (r * row_len + col, me_op)

    def start_rows(src, buf, send, recv):
        for d in range(1, row_len):
            copy_to(src, buf.at[col], send.at[d], recv.at[col],
                    row_peer((col + d) % row_len)).start()
        buf[col] = src[...]

    def finish_sec(src, buf, send, recv, mid_sum, mid_out, sem):
        for d in range(1, row_len):
            slot = (col + row_len - d) % row_len
            copy_to(src, buf.at[slot], send.at[d], recv.at[slot], row_peer(slot)).wait_recv()
        mid_sum[...] = ordered_sum(buf, row_len)
        settle(mid_sum, mid_out, sem)
        for d in range(1, n_rows):
            copy_to(mid_out, buf.at[row_len + row], send.at[row_len + d],
                    recv.at[row_len + row], col_peer((row + d) % n_rows)).start()
        buf[row_len + row] = mid_out[...]
        for d in range(1, n_rows):
            slot = (row + n_rows - d) % n_rows
            copy_to(mid_out, buf.at[row_len + slot], send.at[row_len + d],
                    recv.at[row_len + slot], col_peer(slot)).wait_recv()
        total = buf[row_len]
        for r in range(1, n_rows):
            total = total + buf[row_len + r]
        return total

    def drain_sec(src, buf, send, recv, mid_out):
        for d in range(1, row_len):
            copy_to(src, buf.at[col], send.at[d], recv.at[col],
                    row_peer((col + d) % row_len)).wait_send()
        for d in range(1, n_rows):
            copy_to(mid_out, buf.at[row_len + row], send.at[row_len + d],
                    recv.at[row_len + row], col_peer((row + d) % n_rows)).wait_send()

    def rs_copy(d):
        j = (me_op + d) % n_op
        return copy_to(x_ref.at[j], rs_buf.at[me_op], send_rs.at[d], recv_rs.at[me_op], op_peer(j))

    for d in range(1, n_op):
        rs_copy(d).start()
    a_args = (n_op, me_op, t_out, op_buf, send_a, recv_a, op_peer)
    start_gather(*a_args)
    rs_buf[me_op] = x_ref[me_op]

    operators = copy_to(piece_ref, got_ref, send_w.at[send_w.shape[0] - 1],
                        recv_w.at[recv_w.shape[0] - 1], (next_sec, me_op))
    operators.start()

    wait_gather(*a_args)
    mid[...] = ordered_sum(op_buf, n_op)
    settle(mid, mid_out, local_sem.at[0])
    start_rows(mid_out, sec_buf, send_b, recv_b)

    for d in range(1, n_op):
        slot = (me_op + n_op - d) % n_op
        copy_to(x_ref.at[me_op], rs_buf.at[slot], send_rs.at[d], recv_rs.at[slot],
                op_peer(slot)).wait_recv()
    red[...] = ordered_sum(rs_buf, n_op)

    sums = finish_sec(mid_out, sec_buf, send_b, recv_b, part, part_out, local_sem.at[5])
    energy_sum = sums[0:1, 0:1]
    norm_sum = sums[0:1, 1:2]
    state_wide = st_ref[n_op + me_op].astype(jnp.float32)
    sigma = red[...] + sh_ref[me_op] * state_wide
    updated = state_wide - step_size * (sigma - (energy_sum / norm_sum) * state_wide)
    factor = jnp.sqrt(count / norm_sum)
    if final:
        square = total_of(updated * updated)
    new_buf[...] = (updated * factor).astype(new_buf.dtype)
    settle(new_buf, new_out, local_sem.at[2])

    sides = ((next_sec, 0),) if final else ((next_sec, 0), (prev_sec, 2 * n_op))
    sent = 0
    for side, base in sides:
        for j in range(n_op):
            copy_to(new_out, win_buf.at[base + me_op], send_w.at[sent],
                    recv_w.at[base + me_op], (side, j)).start()
            sent += 1
    for d in range(1, n_op):
        j = (me_op + d) % n_op
        copy_to(new_out, win_buf.at[n_op + me_op], send_w.at[sent],
                recv_w.at[n_op + me_op], op_peer(j)).start()
        sent += 1
    win_buf[n_op + me_op] = new_out[...]

    if final:
        mid2[...] = jnp.where(lane == 0, square, 0.0)
        settle(mid2, mid2_out, local_sem.at[1])
        a2_args = (n_op, me_op, mid2_out, op_buf2, send_a2, recv_a2, op_peer)
        start_gather(*a2_args)
        wait_gather(*a2_args)
        mid3[...] = ordered_sum(op_buf2, n_op)
        settle(mid3, mid3_out, local_sem.at[3])
        start_rows(mid3_out, sec_buf2, send_b2, recv_b2)
        new_norm = finish_sec(mid3_out, sec_buf2, send_b2, recv_b2, part2, part2_out,
                              local_sem.at[6])[0:1, 0:1]
        rescale = jnp.sqrt(count / new_norm) / factor

    from_sides = ((prev_sec, 0),) if final else ((prev_sec, 0), (next_sec, 2 * n_op))
    for side, base in from_sides:
        for j in range(n_op):
            copy_to(new_out, win_buf.at[base + j], send_w.at[0], recv_w.at[base + j],
                    (side, j)).wait_recv()
    for d in range(1, n_op):
        slot = (me_op + n_op - d) % n_op
        copy_to(new_out, win_buf.at[n_op + slot], send_w.at[0], recv_w.at[n_op + slot],
                op_peer(slot)).wait_recv()
    if final:
        for k in range(win_ref.shape[0]):
            win_ref[k] = (win_buf[k].astype(jnp.float32) * rescale).astype(win_ref.dtype)
    else:
        win_ref[...] = win_buf[...]
    operators.wait_recv()

    operators.wait_send()
    for d in range(1, n_op):
        rs_copy(d).wait_send()
    drain_gather(*a_args)
    drain_sec(mid_out, sec_buf, send_b, recv_b, part_out)
    if final:
        drain_gather(*a2_args)
        drain_sec(mid3_out, sec_buf2, send_b2, recv_b2, part2_out)
    for k in range(sent):
        copy_to(new_out, win_buf.at[n_op + me_op], send_w.at[k], recv_w.at[n_op + me_op],
                op_peer((me_op + 1) % n_op)).wait_send()


def step(partial, window, shift, piece, count, final, n_sec, n_op):
    shape = partial.shape
    rows = shape[0] * shape[1] // n_op
    chunks = partial.reshape(n_op, rows, shape[2])
    state_chunks = window.reshape(-1, rows, shape[2])
    shift_chunks = jnp.repeat(shift, n_op // shape[0])[:, None, None]
    slots = (2 if final else 3) * n_op
    tile_shape = (rows, shape[2])
    scalar_bufs = [
        pltpu.VMEM((n_op, 8, 128), jnp.float32),
        pltpu.VMEM((n_sec, 8, 128), jnp.float32),
        pltpu.VMEM((8, 128), jnp.float32),
        pltpu.VMEM((8, 128), jnp.float32),
    ]
    scratch = [
        pltpu.VMEM((8, 128), jnp.float32),
        pltpu.VMEM((8, 128), jnp.float32),
        pltpu.VMEM(chunks.shape, jnp.float32),
        pltpu.VMEM(tile_shape, jnp.float32),
    ] + scalar_bufs + (scalar_bufs + scalar_bufs[2:] if final else []) + [
        pltpu.VMEM(tile_shape, jnp.bfloat16),
        pltpu.VMEM(tile_shape, jnp.bfloat16),
        pltpu.VMEM((slots, rows, shape[2]), jnp.bfloat16),
    ] + [pltpu.VMEM((8, 128), jnp.float32)] * (4 if final else 2) + [
        pltpu.SemaphoreType.DMA((n_op,)),
        pltpu.SemaphoreType.DMA((n_op,)),
        pltpu.SemaphoreType.DMA((n_op,)),
        pltpu.SemaphoreType.DMA((n_op,)),
        pltpu.SemaphoreType.DMA((n_sec,)),
        pltpu.SemaphoreType.DMA((n_sec,)),
    ] + ([
        pltpu.SemaphoreType.DMA((n_op,)),
        pltpu.SemaphoreType.DMA((n_op,)),
        pltpu.SemaphoreType.DMA((n_sec,)),
        pltpu.SemaphoreType.DMA((n_sec,)),
    ] if final else []) + [
        pltpu.SemaphoreType.DMA((slots + n_op + 1,)),
        pltpu.SemaphoreType.DMA((slots + 1,)),
        pltpu.SemaphoreType.DMA((7,)),
    ]
    vmem = pl.BlockSpec(memory_space=pltpu.VMEM)
    anywhere = pl.BlockSpec(memory_space=pl.ANY)
    window, got = pl.pallas_call(
        functools.partial(step_kernel, n_sec, n_op, count, final),
        out_shape=(
            jax.ShapeDtypeStruct((slots, rows, shape[2]), jnp.bfloat16),
            jax.ShapeDtypeStruct(piece.shape, piece.dtype),
        ),
        in_specs=[vmem, vmem, vmem, anywhere],
        out_specs=(vmem, anywhere),
        scratch_shapes=scratch,
        compiler_params=pltpu.CompilerParams(
            collective_id=3 if final else 2, has_side_effects=True
        ),
    )(chunks, state_chunks, shift_chunks, piece)
    return window.reshape(slots // (n_op // shape[0]), shape[1], shape[2]), got


def sigma_part_kernel(partner_ref, win_ref, left_ref, right_ref, o_ref):
    b = pl.program_id(0)
    total = jnp.zeros(o_ref.shape[1:], jnp.float32)
    for t in range(left_ref.shape[0]):
        source = win_ref[partner_ref[t, b]]
        halfway = jnp.dot(left_ref[t, 0], source, preferred_element_type=jnp.float32)
        total = total + jnp.dot(halfway.astype(jnp.bfloat16), right_ref[t, 0],
                                preferred_element_type=jnp.float32)
    o_ref[0] = total


def sigma_part(window, left_ops, right_ops, partner):
    terms, sectors, m, _ = left_ops.shape
    op_spec = pl.BlockSpec((terms, 1, m, m), lambda b, p: (0, b, 0, 0))
    return pl.pallas_call(
        sigma_part_kernel,
        out_shape=jax.ShapeDtypeStruct((sectors, m, m), jnp.float32),
        grid_spec=pltpu.PrefetchScalarGridSpec(
            num_scalar_prefetch=1,
            grid=(sectors,),
            in_specs=[
                pl.BlockSpec(window.shape, lambda b, p: (0, 0, 0)),
                op_spec,
                op_spec,
            ],
            out_specs=pl.BlockSpec((1, m, m), lambda b, p: (b, 0, 0)),
        ),
        cost_estimate=pl.CostEstimate(
            flops=4 * terms * sectors * m * m * m,
            bytes_accessed=2 * left_ops.size * 2 + window.size * 2 + sectors * m * m * 4,
            transcendentals=0,
        ),
    )(partner, window, left_ops, right_ops)


def shifted(block, axis, distance):
    devices = range(lax.axis_size(axis))
    route = [((i - distance) % len(devices), i) for i in devices]
    return lax.ppermute(block, axis, route)


def per_device(state_start, left_ops, right_ops, shift, partner, kept):
    sector_local = state_start.shape[0]
    width = state_start.shape[1]
    count = float(sector_local * lax.axis_size("sec") * width * width)
    n_sec = lax.axis_size("sec")
    n_op = lax.axis_size("op")
    kept_prev = shifted(kept, "sec", 1)
    state = state_start
    window = padded(state, (("sec", 0),), sector_local)
    terms = left_ops.shape[0]
    cuts = [terms * k // ITERS for k in range(ITERS + 1)]
    left_pieces = []
    for iteration in range(ITERS):
        partial_sigma = sigma_part(window, left_ops, right_ops, partner)
        final = iteration == ITERS - 1
        window, got = step(
            partial_sigma, window, shift,
            left_ops[cuts[iteration] : cuts[iteration + 1]], count, final, n_sec, n_op,
        )
        left_pieces.append(got)
        state = window[sector_local : 2 * sector_local]
    state_prev = window[:sector_local]
    left_prev = jnp.concatenate(left_pieces, axis=0)
    columns = jnp.arange(width, dtype=jnp.int32)
    keep_mask = (columns[None, :] < kept_prev[:, None]).astype(jnp.bfloat16)
    kept_block = state_prev * keep_mask[:, None, :]
    out_scale = 1.0 / float(width) ** 0.5
    projected = jnp.einsum(
        "tbij,bjk->tbik", left_prev, kept_block, preferred_element_type=jnp.float32
    ).astype(jnp.bfloat16)
    kept_turned = jnp.broadcast_to(
        jnp.swapaxes(kept_block, 1, 2)[None], left_prev.shape
    )
    new_ops = (
        jnp.einsum("tbij,tbjk->tbik", kept_turned, projected, preferred_element_type=jnp.float32)
        * out_scale
    ).astype(jnp.bfloat16)
    return (state, new_ops)


def solution(mesh):
    in_specs = (
        P("sec", None, None),
        P("op", "sec", None, None),
        P("op", "sec", None, None),
        P("sec"),
        P("op", "sec"),
        P("sec"),
    )
    out_specs = (P("sec", None, None), P("op", "sec", None, None))
    return jax.shard_map(
        per_device, mesh=mesh, in_specs=in_specs, out_specs=out_specs, check_vma=False
    )
```

```python
import functools

import jax
import jax.numpy as jnp
from jax import lax
from jax.experimental import pallas as pl
from jax.experimental.pallas import tpu as pltpu
from jax.sharding import PartitionSpec as P

MESH = pl.DeviceIdType.MESH

ITERS = 4


step_size = 0.5


def padded(cells, sides, width):
    for axis, dim in sides:
        count = lax.axis_size(axis)
        head = lax.slice_in_dim(cells, 0, width, axis=dim)
        tail = lax.slice_in_dim(cells, cells.shape[dim] - width, cells.shape[dim], axis=dim)
        cells = jnp.concatenate(
            [
                lax.ppermute(tail, axis, [(i, (i + 1) % count) for i in range(count)]),
                cells,
                lax.ppermute(head, axis, [((i + 1) % count, i) for i in range(count)]),
            ],
            axis=dim,
        )
    return cells


def all_sum_kernel(n_sec, n_op, x_ref, o_ref, op_buf, sec_buf, mid, out_buf,
                   send_a, recv_a, send_b, recv_b, local_sem):
    me_sec = lax.axis_index("sec")
    me_op = lax.axis_index("op")
    barrier = pltpu.get_barrier_semaphore()
    for d in range(1, n_op):
        pl.semaphore_signal(barrier, 1, device_id=(me_sec, (me_op + d) % n_op),
                            device_id_type=MESH)
    for d in range(1, n_sec):
        pl.semaphore_signal(barrier, 1, device_id=((me_sec + d) % n_sec, me_op),
                            device_id_type=MESH)
    pl.semaphore_wait(barrier, n_op - 1 + n_sec - 1)

    def stage(n, me, src, buf, send, recv, peer_of):
        for d in range(1, n):
            pltpu.make_async_remote_copy(
                src_ref=src, dst_ref=buf.at[me], send_sem=send.at[d],
                recv_sem=recv.at[me], device_id=peer_of((me + d) % n),
                device_id_type=MESH).start()
        buf[me] = src[...]
        for d in range(1, n):
            slot = (me + n - d) % n
            pltpu.make_async_remote_copy(
                src_ref=src, dst_ref=buf.at[slot], send_sem=send.at[d],
                recv_sem=recv.at[slot], device_id=peer_of(slot),
                device_id_type=MESH).wait_recv()
        for d in range(1, n):
            pltpu.make_async_remote_copy(
                src_ref=src, dst_ref=buf.at[me], send_sem=send.at[d],
                recv_sem=recv.at[me], device_id=peer_of((me + d) % n),
                device_id_type=MESH).wait_send()
        total = buf[0]
        for j in range(1, n):
            total = total + buf[j]
        return total

    mid[...] = stage(n_op, me_op, x_ref, op_buf, send_a, recv_a,
                     lambda j: (me_sec, j))
    local = pltpu.make_async_copy(mid, out_buf, local_sem)
    local.start()
    local.wait()
    o_ref[...] = stage(n_sec, me_sec, out_buf, sec_buf, send_b, recv_b,
                       lambda j: (j, me_op))


def all_sum(values, n_sec, n_op):
    lane = lax.broadcasted_iota(jnp.int32, (8, 128), 1)
    tile = jnp.zeros((8, 128), jnp.float32)
    for k, v in enumerate(values):
        tile = jnp.where(lane == k, v, tile)
    tile_spec = pl.BlockSpec(memory_space=pltpu.VMEM)
    out = pl.pallas_call(
        functools.partial(all_sum_kernel, n_sec, n_op),
        out_shape=jax.ShapeDtypeStruct((8, 128), jnp.float32),
        in_specs=[tile_spec],
        out_specs=tile_spec,
        scratch_shapes=[
            pltpu.VMEM((n_op, 8, 128), jnp.float32),
            pltpu.VMEM((n_sec, 8, 128), jnp.float32),
            pltpu.VMEM((8, 128), jnp.float32),
            pltpu.VMEM((8, 128), jnp.float32),
            pltpu.SemaphoreType.DMA((n_op,)),
            pltpu.SemaphoreType.DMA((n_op,)),
            pltpu.SemaphoreType.DMA((n_sec,)),
            pltpu.SemaphoreType.DMA((n_sec,)),
            pltpu.SemaphoreType.DMA(()),
        ],
        compiler_params=pltpu.CompilerParams(collective_id=0, has_side_effects=True),
    )(tile)
    return tuple(out[0, k] for k in range(len(values)))


def sigma_sum_kernel(n_sec, n_op, x_ref, t_ref, o_ref, s_ref,
                     rs_buf, red, red_out, ag_buf, op_buf, sec_buf, mid, mid_out,
                     send_rs, recv_rs, send_ag, recv_ag, send_a, recv_a,
                     send_b, recv_b, local_sem):
    me_sec = lax.axis_index("sec")
    me_op = lax.axis_index("op")
    barrier = pltpu.get_barrier_semaphore()
    for d in range(1, n_op):
        pl.semaphore_signal(barrier, 1, device_id=(me_sec, (me_op + d) % n_op),
                            device_id_type=MESH)
    for d in range(1, n_sec):
        pl.semaphore_signal(barrier, 1, device_id=((me_sec + d) % n_sec, me_op),
                            device_id_type=MESH)
    pl.semaphore_wait(barrier, n_op - 1 + n_sec - 1)

    def op_peer(j):
        return (me_sec, j)

    def sec_peer(j):
        return (j, me_op)

    def total_of(v):
        return jnp.sum(jnp.sum(v, axis=1, keepdims=True), axis=0, keepdims=True)

    lane = lax.broadcasted_iota(jnp.int32, (8, 128), 1)
    own = st_ref[n_op + me_op].astype(jnp.float32)
    own_square = total_of(own * own)
    energy = sh_ref[me_op] * own_square
    for j in range(n_op):
        energy = energy + total_of(x_ref[j] * st_ref[n_op + j].astype(jnp.float32))
    t_ref[...] = jnp.where(lane == 0, energy, jnp.where(lane == 1, own_square, 0.0))
    settle(t_ref, t_out, local_sem.at[4])

    def rs_copy(d):
        j = (me_op + d) % n_op
        return pltpu.make_async_remote_copy(
            src_ref=x_ref.at[j], dst_ref=rs_buf.at[me_op], send_sem=send_rs.at[d],
            recv_sem=recv_rs.at[me_op], device_id=op_peer(j), device_id_type=MESH)

    def rs_recv(d):
        slot = (me_op + n_op - d) % n_op
        return pltpu.make_async_remote_copy(
            src_ref=x_ref.at[me_op], dst_ref=rs_buf.at[slot], send_sem=send_rs.at[d],
            recv_sem=recv_rs.at[slot], device_id=op_peer(slot), device_id_type=MESH)

    def gather_copy(n, me, src, buf, send, recv, peer_of, d):
        return pltpu.make_async_remote_copy(
            src_ref=src, dst_ref=buf.at[me], send_sem=send.at[d],
            recv_sem=recv.at[me], device_id=peer_of((me + d) % n), device_id_type=MESH)

    def gather_recv(n, me, src, buf, send, recv, peer_of, d):
        slot = (me + n - d) % n
        return pltpu.make_async_remote_copy(
            src_ref=src, dst_ref=buf.at[slot], send_sem=send.at[d],
            recv_sem=recv.at[slot], device_id=peer_of(slot), device_id_type=MESH)

    def ordered_sum(buf, n):
        total = buf[0]
        for j in range(1, n):
            total = total + buf[j]
        return total

    for d in range(1, n_op):
        rs_copy(d).start()
    a_args = (n_op, me_op, t_out, op_buf, send_a, recv_a, op_peer)
    for d in range(1, n_op):
        gather_copy(*a_args, d).start()
    rs_buf[me_op] = x_ref[me_op]
    op_buf[me_op] = t_ref[...]

    for d in range(1, n_op):
        gather_recv(*a_args, d).wait_recv()
    mid[...] = ordered_sum(op_buf, n_op)
    local = pltpu.make_async_copy(mid, mid_out, local_sem.at[0])
    local.start()
    local.wait()
    b_args = (n_sec, me_sec, mid_out, sec_buf, send_b, recv_b, sec_peer)
    for d in range(1, n_sec):
        gather_copy(*b_args, d).start()
    sec_buf[me_sec] = mid_out[...]

    for d in range(1, n_op):
        rs_recv(d).wait_recv()
    red[...] = ordered_sum(rs_buf, n_op)
    local = pltpu.make_async_copy(red, red_out, local_sem.at[1])
    local.start()
    local.wait()
    g_args = (n_op, me_op, red_out, ag_buf, send_ag, recv_ag, op_peer)
    for d in range(1, n_op):
        gather_copy(*g_args, d).start()
    ag_buf[me_op] = red_out[...]

    for d in range(1, n_sec):
        gather_recv(*b_args, d).wait_recv()
    s_ref[...] = ordered_sum(sec_buf, n_sec)
    for d in range(1, n_op):
        gather_recv(*g_args, d).wait_recv()
    o_ref[...] = ag_buf[...]

    for d in range(1, n_op):
        rs_copy(d).wait_send()
        gather_copy(*a_args, d).wait_send()
        gather_copy(*g_args, d).wait_send()
    for d in range(1, n_sec):
        gather_copy(*b_args, d).wait_send()


def sigma_sum(partial, values, n_sec, n_op):
    shape = partial.shape
    rows = shape[0] * shape[1] // n_op
    chunks = partial.reshape(n_op, rows, shape[2])
    lane = lax.broadcasted_iota(jnp.int32, (8, 128), 1)
    tile = jnp.zeros((8, 128), jnp.float32)
    for k, v in enumerate(values):
        tile = jnp.where(lane == k, v, tile)
    vmem = pl.BlockSpec(memory_space=pltpu.VMEM)
    total, sums = pl.pallas_call(
        functools.partial(sigma_sum_kernel, n_sec, n_op),
        out_shape=(
            jax.ShapeDtypeStruct(chunks.shape, jnp.float32),
            jax.ShapeDtypeStruct((8, 128), jnp.float32),
        ),
        in_specs=[vmem, vmem],
        out_specs=(vmem, vmem),
        scratch_shapes=[
            pltpu.VMEM(chunks.shape, jnp.float32),
            pltpu.VMEM((rows, shape[2]), jnp.float32),
            pltpu.VMEM((rows, shape[2]), jnp.float32),
            pltpu.VMEM(chunks.shape, jnp.float32),
            pltpu.VMEM((n_op, 8, 128), jnp.float32),
            pltpu.VMEM((n_sec, 8, 128), jnp.float32),
            pltpu.VMEM((8, 128), jnp.float32),
            pltpu.VMEM((8, 128), jnp.float32),
            pltpu.SemaphoreType.DMA((n_op,)),
            pltpu.SemaphoreType.DMA((n_op,)),
            pltpu.SemaphoreType.DMA((n_op,)),
            pltpu.SemaphoreType.DMA((n_op,)),
            pltpu.SemaphoreType.DMA((n_op,)),
            pltpu.SemaphoreType.DMA((n_op,)),
            pltpu.SemaphoreType.DMA((n_sec,)),
            pltpu.SemaphoreType.DMA((n_sec,)),
            pltpu.SemaphoreType.DMA((2,)),
        ],
        compiler_params=pltpu.CompilerParams(collective_id=1, has_side_effects=True),
    )(chunks, tile)
    return total.reshape(shape), tuple(sums[0, k] for k in range(len(values)))


def step_kernel(n_sec, n_op, count, final, x_ref, st_ref, sh_ref, piece_ref, *refs):
    if final:
        (win_ref, got_ref, t_ref, t_out, rs_buf, red, op_buf, sec_buf, mid, mid_out,
         op_buf2, sec_buf2, mid2, mid2_out, mid3, mid3_out, new_buf, new_out, win_buf,
         part, part_out, part2, part2_out,
         send_rs, recv_rs, send_a, recv_a, send_b, recv_b, send_a2, recv_a2, send_b2,
         recv_b2, send_w, recv_w, local_sem) = refs
    else:
        (win_ref, got_ref, t_ref, t_out, rs_buf, red, op_buf, sec_buf, mid, mid_out,
         new_buf, new_out, win_buf, part, part_out, send_rs, recv_rs, send_a, recv_a, send_b, recv_b, send_w,
         recv_w, local_sem) = refs
    me_sec = lax.axis_index("sec")
    me_op = lax.axis_index("op")
    prev_sec = (me_sec + n_sec - 1) % n_sec
    next_sec = (me_sec + 1) % n_sec
    barrier = pltpu.get_barrier_semaphore()
    row_len = 8 if n_sec % 8 == 0 else (2 if n_sec % 2 == 0 else n_sec)
    n_rows = n_sec // row_len
    row = me_sec // row_len
    col = me_sec % row_len
    greet = [(me_sec, (me_op + d) % n_op) for d in range(1, n_op)]
    greet += [(row * row_len + (col + d) % row_len, me_op) for d in range(1, row_len)]
    greet += [(((row + d) % n_rows) * row_len + col, me_op) for d in range(1, n_rows)]
    greet += [(side, j) for side in (prev_sec, next_sec) for j in range(n_op)]
    for peer in greet:
        pl.semaphore_signal(barrier, 1, device_id=peer, device_id_type=MESH)
    greeted = len(greet)
    pl.semaphore_wait(barrier, greeted)

    def op_peer(j):
        return (me_sec, j)

    def sec_peer(j):
        return (j, me_op)

    def copy_to(src, dst, send, recv, peer):
        return pltpu.make_async_remote_copy(
            src_ref=src, dst_ref=dst, send_sem=send, recv_sem=recv,
            device_id=peer, device_id_type=MESH)

    def ordered_sum(buf, n):
        total = buf[0]
        for j in range(1, n):
            total = total + buf[j]
        return total

    def start_gather(n, me, src, buf, send, recv, peer_of):
        for d in range(1, n):
            copy_to(src, buf.at[me], send.at[d], recv.at[me], peer_of((me + d) % n)).start()
        buf[me] = src[...]

    def wait_gather(n, me, src, buf, send, recv, peer_of):
        for d in range(1, n):
            slot = (me + n - d) % n
            copy_to(src, buf.at[slot], send.at[d], recv.at[slot], peer_of(slot)).wait_recv()

    def drain_gather(n, me, src, buf, send, recv, peer_of):
        for d in range(1, n):
            copy_to(src, buf.at[me], send.at[d], recv.at[me], peer_of((me + d) % n)).wait_send()

    def settle(src, dst, sem):
        local = pltpu.make_async_copy(src, dst, sem)
        local.start()
        local.wait()

    def total_of(v):
        return jnp.sum(jnp.sum(v, axis=1, keepdims=True), axis=0, keepdims=True)

    lane = lax.broadcasted_iota(jnp.int32, (8, 128), 1)
    own = st_ref[n_op + me_op].astype(jnp.float32)
    own_square = total_of(own * own)
    energy = sh_ref[me_op] * own_square
    for j in range(n_op):
        energy = energy + total_of(x_ref[j] * st_ref[n_op + j].astype(jnp.float32))
    t_ref[...] = jnp.where(lane == 0, energy, jnp.where(lane == 1, own_square, 0.0))
    settle(t_ref, t_out, local_sem.at[4])

    def row_peer(c):
        return (row * row_len + c, me_op)

    def col_peer(r):
        return (r * row_len + col, me_op)

    def start_rows(src, buf, send, recv):
        for d in range(1, row_len):
            copy_to(src, buf.at[col], send.at[d], recv.at[col],
                    row_peer((col + d) % row_len)).start()
        buf[col] = src[...]

    def finish_sec(src, buf, send, recv, mid_sum, mid_out, sem):
        for d in range(1, row_len):
            slot = (col + row_len - d) % row_len
            copy_to(src, buf.at[slot], send.at[d], recv.at[slot], row_peer(slot)).wait_recv()
        mid_sum[...] = ordered_sum(buf, row_len)
        settle(mid_sum, mid_out, sem)
        for d in range(1, n_rows):
            copy_to(mid_out, buf.at[row_len + row], send.at[row_len + d],
                    recv.at[row_len + row], col_peer((row + d) % n_rows)).start()
        buf[row_len + row] = mid_out[...]
        for d in range(1, n_rows):
            slot = (row + n_rows - d) % n_rows
            copy_to(mid_out, buf.at[row_len + slot], send.at[row_len + d],
                    recv.at[row_len + slot], col_peer(slot)).wait_recv()
        total = buf[row_len]
        for r in range(1, n_rows):
            total = total + buf[row_len + r]
        return total

    def drain_sec(src, buf, send, recv, mid_out):
        for d in range(1, row_len):
            copy_to(src, buf.at[col], send.at[d], recv.at[col],
                    row_peer((col + d) % row_len)).wait_send()
        for d in range(1, n_rows):
            copy_to(mid_out, buf.at[row_len + row], send.at[row_len + d],
                    recv.at[row_len + row], col_peer((row + d) % n_rows)).wait_send()

    def rs_copy(d):
        j = (me_op + d) % n_op
        return copy_to(x_ref.at[j], rs_buf.at[me_op], send_rs.at[d], recv_rs.at[me_op], op_peer(j))

    for d in range(1, n_op):
        rs_copy(d).start()
    a_args = (n_op, me_op, t_out, op_buf, send_a, recv_a, op_peer)
    start_gather(*a_args)
    rs_buf[me_op] = x_ref[me_op]

    operators = copy_to(piece_ref, got_ref, send_w.at[send_w.shape[0] - 1],
                        recv_w.at[recv_w.shape[0] - 1], (next_sec, me_op))
    operators.start()

    wait_gather(*a_args)
    mid[...] = ordered_sum(op_buf, n_op)
    settle(mid, mid_out, local_sem.at[0])
    start_rows(mid_out, sec_buf, send_b, recv_b)

    for d in range(1, n_op):
        slot = (me_op + n_op - d) % n_op
        copy_to(x_ref.at[me_op], rs_buf.at[slot], send_rs.at[d], recv_rs.at[slot],
                op_peer(slot)).wait_recv()
    red[...] = ordered_sum(rs_buf, n_op)

    sums = finish_sec(mid_out, sec_buf, send_b, recv_b, part, part_out, local_sem.at[5])
    energy_sum = sums[0:1, 0:1]
    norm_sum = sums[0:1, 1:2]
    state_wide = st_ref[n_op + me_op].astype(jnp.float32)
    sigma = red[...] + sh_ref[me_op] * state_wide
    updated = state_wide - step_size * (sigma - (energy_sum / norm_sum) * state_wide)
    factor = jnp.sqrt(count / norm_sum)
    if final:
        square = total_of(updated * updated)
    new_buf[...] = (updated * factor).astype(new_buf.dtype)
    settle(new_buf, new_out, local_sem.at[2])

    sides = ((next_sec, 0),) if final else ((next_sec, 0), (prev_sec, 2 * n_op))
    sent = 0
    for side, base in sides:
        for j in range(n_op):
            copy_to(new_out, win_buf.at[base + me_op], send_w.at[sent],
                    recv_w.at[base + me_op], (side, j)).start()
            sent += 1
    for d in range(1, n_op):
        j = (me_op + d) % n_op
        copy_to(new_out, win_buf.at[n_op + me_op], send_w.at[sent],
                recv_w.at[n_op + me_op], op_peer(j)).start()
        sent += 1
    win_buf[n_op + me_op] = new_out[...]

    if final:
        mid2[...] = jnp.where(lane == 0, square, 0.0)
        settle(mid2, mid2_out, local_sem.at[1])
        a2_args = (n_op, me_op, mid2_out, op_buf2, send_a2, recv_a2, op_peer)
        start_gather(*a2_args)
        wait_gather(*a2_args)
        mid3[...] = ordered_sum(op_buf2, n_op)
        settle(mid3, mid3_out, local_sem.at[3])
        start_rows(mid3_out, sec_buf2, send_b2, recv_b2)
        new_norm = finish_sec(mid3_out, sec_buf2, send_b2, recv_b2, part2, part2_out,
                              local_sem.at[6])[0:1, 0:1]
        rescale = jnp.sqrt(count / new_norm) / factor

    from_sides = ((prev_sec, 0),) if final else ((prev_sec, 0), (next_sec, 2 * n_op))
    for side, base in from_sides:
        for j in range(n_op):
            copy_to(new_out, win_buf.at[base + j], send_w.at[0], recv_w.at[base + j],
                    (side, j)).wait_recv()
    for d in range(1, n_op):
        slot = (me_op + n_op - d) % n_op
        copy_to(new_out, win_buf.at[n_op + slot], send_w.at[0], recv_w.at[n_op + slot],
                op_peer(slot)).wait_recv()
    if final:
        for k in range(win_ref.shape[0]):
            win_ref[k] = (win_buf[k].astype(jnp.float32) * rescale).astype(win_ref.dtype)
    else:
        win_ref[...] = win_buf[...]
    operators.wait_recv()

    operators.wait_send()
    for d in range(1, n_op):
        rs_copy(d).wait_send()
    drain_gather(*a_args)
    drain_sec(mid_out, sec_buf, send_b, recv_b, part_out)
    if final:
        drain_gather(*a2_args)
        drain_sec(mid3_out, sec_buf2, send_b2, recv_b2, part2_out)
    for k in range(sent):
        copy_to(new_out, win_buf.at[n_op + me_op], send_w.at[k], recv_w.at[n_op + me_op],
                op_peer((me_op + 1) % n_op)).wait_send()


def step(partial, window, shift, piece, count, final, n_sec, n_op):
    shape = partial.shape
    rows = shape[0] * shape[1] // n_op
    chunks = partial.reshape(n_op, rows, shape[2])
    state_chunks = window.reshape(-1, rows, shape[2])
    shift_chunks = jnp.repeat(shift, n_op // shape[0])[:, None, None]
    slots = (2 if final else 3) * n_op
    tile_shape = (rows, shape[2])
    scalar_bufs = [
        pltpu.VMEM((n_op, 8, 128), jnp.float32),
        pltpu.VMEM((n_sec, 8, 128), jnp.float32),
        pltpu.VMEM((8, 128), jnp.float32),
        pltpu.VMEM((8, 128), jnp.float32),
    ]
    scratch = [
        pltpu.VMEM((8, 128), jnp.float32),
        pltpu.VMEM((8, 128), jnp.float32),
        pltpu.VMEM(chunks.shape, jnp.float32),
        pltpu.VMEM(tile_shape, jnp.float32),
    ] + scalar_bufs + (scalar_bufs + scalar_bufs[2:] if final else []) + [
        pltpu.VMEM(tile_shape, jnp.bfloat16),
        pltpu.VMEM(tile_shape, jnp.bfloat16),
        pltpu.VMEM((slots, rows, shape[2]), jnp.bfloat16),
    ] + [pltpu.VMEM((8, 128), jnp.float32)] * (4 if final else 2) + [
        pltpu.SemaphoreType.DMA((n_op,)),
        pltpu.SemaphoreType.DMA((n_op,)),
        pltpu.SemaphoreType.DMA((n_op,)),
        pltpu.SemaphoreType.DMA((n_op,)),
        pltpu.SemaphoreType.DMA((n_sec,)),
        pltpu.SemaphoreType.DMA((n_sec,)),
    ] + ([
        pltpu.SemaphoreType.DMA((n_op,)),
        pltpu.SemaphoreType.DMA((n_op,)),
        pltpu.SemaphoreType.DMA((n_sec,)),
        pltpu.SemaphoreType.DMA((n_sec,)),
    ] if final else []) + [
        pltpu.SemaphoreType.DMA((slots + n_op + 1,)),
        pltpu.SemaphoreType.DMA((slots + 1,)),
        pltpu.SemaphoreType.DMA((7,)),
    ]
    vmem = pl.BlockSpec(memory_space=pltpu.VMEM)
    anywhere = pl.BlockSpec(memory_space=pl.ANY)
    window, got = pl.pallas_call(
        functools.partial(step_kernel, n_sec, n_op, count, final),
        out_shape=(
            jax.ShapeDtypeStruct((slots, rows, shape[2]), jnp.bfloat16),
            jax.ShapeDtypeStruct(piece.shape, piece.dtype),
        ),
        in_specs=[vmem, vmem, vmem, anywhere],
        out_specs=(vmem, anywhere),
        scratch_shapes=scratch,
        compiler_params=pltpu.CompilerParams(
            collective_id=3 if final else 2, has_side_effects=True
        ),
    )(chunks, state_chunks, shift_chunks, piece)
    return window.reshape(slots // (n_op // shape[0]), shape[1], shape[2]), got


def sigma_part_kernel(partner_ref, win_ref, left_ref, right_ref, o_ref):
    b = pl.program_id(0)
    total = jnp.zeros(o_ref.shape[1:], jnp.float32)
    for t in range(left_ref.shape[0]):
        source = win_ref[partner_ref[t, b]]
        halfway = jnp.dot(left_ref[t, 0], source, preferred_element_type=jnp.float32)
        total = total + jnp.dot(halfway.astype(jnp.bfloat16), right_ref[t, 0],
                                preferred_element_type=jnp.float32)
    o_ref[0] = total


def sigma_part(window, left_ops, right_ops, partner):
    terms, sectors, m, _ = left_ops.shape
    op_spec = pl.BlockSpec((terms, 1, m, m), lambda b, p: (0, b, 0, 0))
    return pl.pallas_call(
        sigma_part_kernel,
        out_shape=jax.ShapeDtypeStruct((sectors, m, m), jnp.float32),
        grid_spec=pltpu.PrefetchScalarGridSpec(
            num_scalar_prefetch=1,
            grid=(sectors,),
            in_specs=[
                pl.BlockSpec(window.shape, lambda b, p: (0, 0, 0)),
                op_spec,
                op_spec,
            ],
            out_specs=pl.BlockSpec((1, m, m), lambda b, p: (b, 0, 0)),
        ),
        cost_estimate=pl.CostEstimate(
            flops=4 * terms * sectors * m * m * m,
            bytes_accessed=2 * left_ops.size * 2 + window.size * 2 + sectors * m * m * 4,
            transcendentals=0,
        ),
    )(partner, window, left_ops, right_ops)


def halo_kernel(n_sec, st_ref, win_ref, win_buf, send, recv):
    me_sec = lax.axis_index("sec")
    me_op = lax.axis_index("op")
    prev_sec = (me_sec + n_sec - 1) % n_sec
    next_sec = (me_sec + 1) % n_sec
    barrier = pltpu.get_barrier_semaphore()
    for side in (prev_sec, next_sec):
        pl.semaphore_signal(barrier, 1, device_id=(side, me_op), device_id_type=MESH)
    pl.semaphore_wait(barrier, 2)
    copies = [
        pltpu.make_async_remote_copy(
            src_ref=st_ref, dst_ref=win_buf.at[slot], send_sem=send.at[k],
            recv_sem=recv.at[slot], device_id=(side, me_op), device_id_type=MESH)
        for k, (side, slot) in enumerate(((next_sec, 0), (prev_sec, 2)))
    ]
    for c in copies:
        c.start()
    win_buf[1] = st_ref[...]
    for c in copies:
        c.wait_recv()
    win_ref[...] = win_buf[...]
    for c in copies:
        c.wait_send()


def halo(state, n_sec):
    vmem = pl.BlockSpec(memory_space=pltpu.VMEM)
    window = pl.pallas_call(
        functools.partial(halo_kernel, n_sec),
        out_shape=jax.ShapeDtypeStruct((3,) + state.shape, state.dtype),
        in_specs=[vmem],
        out_specs=vmem,
        scratch_shapes=[
            pltpu.VMEM((3,) + state.shape, state.dtype),
            pltpu.SemaphoreType.DMA((2,)),
            pltpu.SemaphoreType.DMA((3,)),
        ],
        compiler_params=pltpu.CompilerParams(collective_id=4, has_side_effects=True),
    )(state)
    return window.reshape((3 * state.shape[0],) + state.shape[1:])


def shifted(block, axis, distance):
    devices = range(lax.axis_size(axis))
    route = [((i - distance) % len(devices), i) for i in devices]
    return lax.ppermute(block, axis, route)


def per_device(state_start, left_ops, right_ops, shift, partner, kept):
    sector_local = state_start.shape[0]
    width = state_start.shape[1]
    count = float(sector_local * lax.axis_size("sec") * width * width)
    n_sec = lax.axis_size("sec")
    n_op = lax.axis_size("op")
    kept_prev = shifted(kept, "sec", 1)
    state = state_start
    window = halo(state, n_sec)
    terms = left_ops.shape[0]
    cuts = [terms * k // ITERS for k in range(ITERS + 1)]
    left_pieces = []
    for iteration in range(ITERS):
        partial_sigma = sigma_part(window, left_ops, right_ops, partner)
        final = iteration == ITERS - 1
        window, got = step(
            partial_sigma, window, shift,
            left_ops[cuts[iteration] : cuts[iteration + 1]], count, final, n_sec, n_op,
        )
        left_pieces.append(got)
        state = window[sector_local : 2 * sector_local]
    state_prev = window[:sector_local]
    left_prev = jnp.concatenate(left_pieces, axis=0)
    columns = jnp.arange(width, dtype=jnp.int32)
    keep_mask = (columns[None, :] < kept_prev[:, None]).astype(jnp.bfloat16)
    kept_block = state_prev * keep_mask[:, None, :]
    out_scale = 1.0 / float(width) ** 0.5
    projected = jnp.einsum(
        "tbij,bjk->tbik", left_prev, kept_block, preferred_element_type=jnp.float32
    ).astype(jnp.bfloat16)
    kept_turned = jnp.broadcast_to(
        jnp.swapaxes(kept_block, 1, 2)[None], left_prev.shape
    )
    new_ops = (
        jnp.einsum("tbij,tbjk->tbik", kept_turned, projected, preferred_element_type=jnp.float32)
        * out_scale
    ).astype(jnp.bfloat16)
    return (state, new_ops)


def solution(mesh):
    in_specs = (
        P("sec", None, None),
        P("op", "sec", None, None),
        P("op", "sec", None, None),
        P("sec"),
        P("op", "sec"),
        P("sec"),
    )
    out_specs = (P("sec", None, None), P("op", "sec", None, None))
    return jax.shard_map(
        per_device, mesh=mesh, in_specs=in_specs, out_specs=out_specs, check_vma=False
    )
```

```python
import functools

import jax
import jax.numpy as jnp
from jax import lax
from jax.experimental import pallas as pl
from jax.experimental.pallas import tpu as pltpu
from jax.sharding import PartitionSpec as P

MESH = pl.DeviceIdType.MESH

ITERS = 4


step_size = 0.5


def padded(cells, sides, width):
    for axis, dim in sides:
        count = lax.axis_size(axis)
        head = lax.slice_in_dim(cells, 0, width, axis=dim)
        tail = lax.slice_in_dim(cells, cells.shape[dim] - width, cells.shape[dim], axis=dim)
        cells = jnp.concatenate(
            [
                lax.ppermute(tail, axis, [(i, (i + 1) % count) for i in range(count)]),
                cells,
                lax.ppermute(head, axis, [((i + 1) % count, i) for i in range(count)]),
            ],
            axis=dim,
        )
    return cells


def all_sum_kernel(n_sec, n_op, x_ref, o_ref, op_buf, sec_buf, mid, out_buf,
                   send_a, recv_a, send_b, recv_b, local_sem):
    me_sec = lax.axis_index("sec")
    me_op = lax.axis_index("op")
    barrier = pltpu.get_barrier_semaphore()
    for d in range(1, n_op):
        pl.semaphore_signal(barrier, 1, device_id=(me_sec, (me_op + d) % n_op),
                            device_id_type=MESH)
    for d in range(1, n_sec):
        pl.semaphore_signal(barrier, 1, device_id=((me_sec + d) % n_sec, me_op),
                            device_id_type=MESH)
    pl.semaphore_wait(barrier, n_op - 1 + n_sec - 1)

    def stage(n, me, src, buf, send, recv, peer_of):
        for d in range(1, n):
            pltpu.make_async_remote_copy(
                src_ref=src, dst_ref=buf.at[me], send_sem=send.at[d],
                recv_sem=recv.at[me], device_id=peer_of((me + d) % n),
                device_id_type=MESH).start()
        buf[me] = src[...]
        for d in range(1, n):
            slot = (me + n - d) % n
            pltpu.make_async_remote_copy(
                src_ref=src, dst_ref=buf.at[slot], send_sem=send.at[d],
                recv_sem=recv.at[slot], device_id=peer_of(slot),
                device_id_type=MESH).wait_recv()
        for d in range(1, n):
            pltpu.make_async_remote_copy(
                src_ref=src, dst_ref=buf.at[me], send_sem=send.at[d],
                recv_sem=recv.at[me], device_id=peer_of((me + d) % n),
                device_id_type=MESH).wait_send()
        total = buf[0]
        for j in range(1, n):
            total = total + buf[j]
        return total

    mid[...] = stage(n_op, me_op, x_ref, op_buf, send_a, recv_a,
                     lambda j: (me_sec, j))
    local = pltpu.make_async_copy(mid, out_buf, local_sem)
    local.start()
    local.wait()
    o_ref[...] = stage(n_sec, me_sec, out_buf, sec_buf, send_b, recv_b,
                       lambda j: (j, me_op))


def all_sum(values, n_sec, n_op):
    lane = lax.broadcasted_iota(jnp.int32, (8, 128), 1)
    tile = jnp.zeros((8, 128), jnp.float32)
    for k, v in enumerate(values):
        tile = jnp.where(lane == k, v, tile)
    tile_spec = pl.BlockSpec(memory_space=pltpu.VMEM)
    out = pl.pallas_call(
        functools.partial(all_sum_kernel, n_sec, n_op),
        out_shape=jax.ShapeDtypeStruct((8, 128), jnp.float32),
        in_specs=[tile_spec],
        out_specs=tile_spec,
        scratch_shapes=[
            pltpu.VMEM((n_op, 8, 128), jnp.float32),
            pltpu.VMEM((n_sec, 8, 128), jnp.float32),
            pltpu.VMEM((8, 128), jnp.float32),
            pltpu.VMEM((8, 128), jnp.float32),
            pltpu.SemaphoreType.DMA((n_op,)),
            pltpu.SemaphoreType.DMA((n_op,)),
            pltpu.SemaphoreType.DMA((n_sec,)),
            pltpu.SemaphoreType.DMA((n_sec,)),
            pltpu.SemaphoreType.DMA(()),
        ],
        compiler_params=pltpu.CompilerParams(collective_id=0, has_side_effects=True),
    )(tile)
    return tuple(out[0, k] for k in range(len(values)))


def sigma_sum_kernel(n_sec, n_op, x_ref, t_ref, o_ref, s_ref,
                     rs_buf, red, red_out, ag_buf, op_buf, sec_buf, mid, mid_out,
                     send_rs, recv_rs, send_ag, recv_ag, send_a, recv_a,
                     send_b, recv_b, local_sem):
    me_sec = lax.axis_index("sec")
    me_op = lax.axis_index("op")
    barrier = pltpu.get_barrier_semaphore()
    for d in range(1, n_op):
        pl.semaphore_signal(barrier, 1, device_id=(me_sec, (me_op + d) % n_op),
                            device_id_type=MESH)
    for d in range(1, n_sec):
        pl.semaphore_signal(barrier, 1, device_id=((me_sec + d) % n_sec, me_op),
                            device_id_type=MESH)
    pl.semaphore_wait(barrier, n_op - 1 + n_sec - 1)

    def op_peer(j):
        return (me_sec, j)

    def sec_peer(j):
        return (j, me_op)

    def total_of(v):
        return jnp.sum(jnp.sum(v, axis=1, keepdims=True), axis=0, keepdims=True)

    lane = lax.broadcasted_iota(jnp.int32, (8, 128), 1)
    own = st_ref[n_op + me_op].astype(jnp.float32)
    own_square = total_of(own * own)
    energy = sh_ref[me_op] * own_square
    for j in range(n_op):
        energy = energy + total_of(x_ref[j] * st_ref[n_op + j].astype(jnp.float32))
    t_ref[...] = jnp.where(lane == 0, energy, jnp.where(lane == 1, own_square, 0.0))
    settle(t_ref, t_out, local_sem.at[4])

    def rs_copy(d):
        j = (me_op + d) % n_op
        return pltpu.make_async_remote_copy(
            src_ref=x_ref.at[j], dst_ref=rs_buf.at[me_op], send_sem=send_rs.at[d],
            recv_sem=recv_rs.at[me_op], device_id=op_peer(j), device_id_type=MESH)

    def rs_recv(d):
        slot = (me_op + n_op - d) % n_op
        return pltpu.make_async_remote_copy(
            src_ref=x_ref.at[me_op], dst_ref=rs_buf.at[slot], send_sem=send_rs.at[d],
            recv_sem=recv_rs.at[slot], device_id=op_peer(slot), device_id_type=MESH)

    def gather_copy(n, me, src, buf, send, recv, peer_of, d):
        return pltpu.make_async_remote_copy(
            src_ref=src, dst_ref=buf.at[me], send_sem=send.at[d],
            recv_sem=recv.at[me], device_id=peer_of((me + d) % n), device_id_type=MESH)

    def gather_recv(n, me, src, buf, send, recv, peer_of, d):
        slot = (me + n - d) % n
        return pltpu.make_async_remote_copy(
            src_ref=src, dst_ref=buf.at[slot], send_sem=send.at[d],
            recv_sem=recv.at[slot], device_id=peer_of(slot), device_id_type=MESH)

    def ordered_sum(buf, n):
        total = buf[0]
        for j in range(1, n):
            total = total + buf[j]
        return total

    for d in range(1, n_op):
        rs_copy(d).start()
    a_args = (n_op, me_op, t_out, op_buf, send_a, recv_a, op_peer)
    for d in range(1, n_op):
        gather_copy(*a_args, d).start()
    rs_buf[me_op] = x_ref[me_op]
    op_buf[me_op] = t_ref[...]

    for d in range(1, n_op):
        gather_recv(*a_args, d).wait_recv()
    mid[...] = ordered_sum(op_buf, n_op)
    local = pltpu.make_async_copy(mid, mid_out, local_sem.at[0])
    local.start()
    local.wait()
    b_args = (n_sec, me_sec, mid_out, sec_buf, send_b, recv_b, sec_peer)
    for d in range(1, n_sec):
        gather_copy(*b_args, d).start()
    sec_buf[me_sec] = mid_out[...]

    for d in range(1, n_op):
        rs_recv(d).wait_recv()
    red[...] = ordered_sum(rs_buf, n_op)
    local = pltpu.make_async_copy(red, red_out, local_sem.at[1])
    local.start()
    local.wait()
    g_args = (n_op, me_op, red_out, ag_buf, send_ag, recv_ag, op_peer)
    for d in range(1, n_op):
        gather_copy(*g_args, d).start()
    ag_buf[me_op] = red_out[...]

    for d in range(1, n_sec):
        gather_recv(*b_args, d).wait_recv()
    s_ref[...] = ordered_sum(sec_buf, n_sec)
    for d in range(1, n_op):
        gather_recv(*g_args, d).wait_recv()
    o_ref[...] = ag_buf[...]

    for d in range(1, n_op):
        rs_copy(d).wait_send()
        gather_copy(*a_args, d).wait_send()
        gather_copy(*g_args, d).wait_send()
    for d in range(1, n_sec):
        gather_copy(*b_args, d).wait_send()


def sigma_sum(partial, values, n_sec, n_op):
    shape = partial.shape
    rows = shape[0] * shape[1] // n_op
    chunks = partial.reshape(n_op, rows, shape[2])
    lane = lax.broadcasted_iota(jnp.int32, (8, 128), 1)
    tile = jnp.zeros((8, 128), jnp.float32)
    for k, v in enumerate(values):
        tile = jnp.where(lane == k, v, tile)
    vmem = pl.BlockSpec(memory_space=pltpu.VMEM)
    total, sums = pl.pallas_call(
        functools.partial(sigma_sum_kernel, n_sec, n_op),
        out_shape=(
            jax.ShapeDtypeStruct(chunks.shape, jnp.float32),
            jax.ShapeDtypeStruct((8, 128), jnp.float32),
        ),
        in_specs=[vmem, vmem],
        out_specs=(vmem, vmem),
        scratch_shapes=[
            pltpu.VMEM(chunks.shape, jnp.float32),
            pltpu.VMEM((rows, shape[2]), jnp.float32),
            pltpu.VMEM((rows, shape[2]), jnp.float32),
            pltpu.VMEM(chunks.shape, jnp.float32),
            pltpu.VMEM((n_op, 8, 128), jnp.float32),
            pltpu.VMEM((n_sec, 8, 128), jnp.float32),
            pltpu.VMEM((8, 128), jnp.float32),
            pltpu.VMEM((8, 128), jnp.float32),
            pltpu.SemaphoreType.DMA((n_op,)),
            pltpu.SemaphoreType.DMA((n_op,)),
            pltpu.SemaphoreType.DMA((n_op,)),
            pltpu.SemaphoreType.DMA((n_op,)),
            pltpu.SemaphoreType.DMA((n_op,)),
            pltpu.SemaphoreType.DMA((n_op,)),
            pltpu.SemaphoreType.DMA((n_sec,)),
            pltpu.SemaphoreType.DMA((n_sec,)),
            pltpu.SemaphoreType.DMA((2,)),
        ],
        compiler_params=pltpu.CompilerParams(collective_id=1, has_side_effects=True),
    )(chunks, tile)
    return total.reshape(shape), tuple(sums[0, k] for k in range(len(values)))


def step_kernel(n_sec, n_op, count, final, x_ref, st_ref, sh_ref, piece_ref, *refs):
    if final:
        (win_ref, got_ref, t_ref, t_out, rs_buf, red, op_buf, sec_buf, mid, mid_out,
         op_buf2, sec_buf2, mid2, mid2_out, mid3, mid3_out, new_buf, new_out, win_buf,
         part, part_out, part2, part2_out,
         send_rs, recv_rs, send_a, recv_a, send_b, recv_b, send_a2, recv_a2, send_b2,
         recv_b2, send_w, recv_w, local_sem) = refs
    else:
        (win_ref, got_ref, t_ref, t_out, rs_buf, red, op_buf, sec_buf, mid, mid_out,
         new_buf, new_out, win_buf, part, part_out, send_rs, recv_rs, send_a, recv_a, send_b, recv_b, send_w,
         recv_w, local_sem) = refs
    me_sec = lax.axis_index("sec")
    me_op = lax.axis_index("op")
    prev_sec = (me_sec + n_sec - 1) % n_sec
    next_sec = (me_sec + 1) % n_sec
    barrier = pltpu.get_barrier_semaphore()
    row_len = 8 if n_sec % 8 == 0 else (2 if n_sec % 2 == 0 else n_sec)
    n_rows = n_sec // row_len
    row = me_sec // row_len
    col = me_sec % row_len
    greet = [(me_sec, (me_op + d) % n_op) for d in range(1, n_op)]
    greet += [(row * row_len + (col + d) % row_len, me_op) for d in range(1, row_len)]
    greet += [(((row + d) % n_rows) * row_len + col, me_op) for d in range(1, n_rows)]
    greet += [(side, j) for side in (prev_sec, next_sec) for j in range(n_op)]
    for peer in greet:
        pl.semaphore_signal(barrier, 1, device_id=peer, device_id_type=MESH)
    greeted = len(greet)
    pl.semaphore_wait(barrier, greeted)

    def op_peer(j):
        return (me_sec, j)

    def sec_peer(j):
        return (j, me_op)

    def copy_to(src, dst, send, recv, peer):
        return pltpu.make_async_remote_copy(
            src_ref=src, dst_ref=dst, send_sem=send, recv_sem=recv,
            device_id=peer, device_id_type=MESH)

    def ordered_sum(buf, n):
        total = buf[0]
        for j in range(1, n):
            total = total + buf[j]
        return total

    def start_gather(n, me, src, buf, send, recv, peer_of):
        for d in range(1, n):
            copy_to(src, buf.at[me], send.at[d], recv.at[me], peer_of((me + d) % n)).start()
        buf[me] = src[...]

    def wait_gather(n, me, src, buf, send, recv, peer_of):
        for d in range(1, n):
            slot = (me + n - d) % n
            copy_to(src, buf.at[slot], send.at[d], recv.at[slot], peer_of(slot)).wait_recv()

    def drain_gather(n, me, src, buf, send, recv, peer_of):
        for d in range(1, n):
            copy_to(src, buf.at[me], send.at[d], recv.at[me], peer_of((me + d) % n)).wait_send()

    def settle(src, dst, sem):
        local = pltpu.make_async_copy(src, dst, sem)
        local.start()
        local.wait()

    def total_of(v):
        return jnp.sum(jnp.sum(v, axis=1, keepdims=True), axis=0, keepdims=True)

    lane = lax.broadcasted_iota(jnp.int32, (8, 128), 1)
    own = st_ref[n_op + me_op].astype(jnp.float32)
    own_square = total_of(own * own)
    energy = sh_ref[me_op] * own_square
    for j in range(n_op):
        energy = energy + total_of(x_ref[j] * st_ref[n_op + j].astype(jnp.float32))
    t_ref[...] = jnp.where(lane == 0, energy, jnp.where(lane == 1, own_square, 0.0))
    settle(t_ref, t_out, local_sem.at[4])

    def row_peer(c):
        return (row * row_len + c, me_op)

    def col_peer(r):
        return (r * row_len + col, me_op)

    def start_rows(src, buf, send, recv):
        for d in range(1, row_len):
            copy_to(src, buf.at[col], send.at[d], recv.at[col],
                    row_peer((col + d) % row_len)).start()
        buf[col] = src[...]

    def finish_sec(src, buf, send, recv, mid_sum, mid_out, sem):
        for d in range(1, row_len):
            slot = (col + row_len - d) % row_len
            copy_to(src, buf.at[slot], send.at[d], recv.at[slot], row_peer(slot)).wait_recv()
        mid_sum[...] = ordered_sum(buf, row_len)
        settle(mid_sum, mid_out, sem)
        for d in range(1, n_rows):
            copy_to(mid_out, buf.at[row_len + row], send.at[row_len + d],
                    recv.at[row_len + row], col_peer((row + d) % n_rows)).start()
        buf[row_len + row] = mid_out[...]
        for d in range(1, n_rows):
            slot = (row + n_rows - d) % n_rows
            copy_to(mid_out, buf.at[row_len + slot], send.at[row_len + d],
                    recv.at[row_len + slot], col_peer(slot)).wait_recv()
        total = buf[row_len]
        for r in range(1, n_rows):
            total = total + buf[row_len + r]
        return total

    def drain_sec(src, buf, send, recv, mid_out):
        for d in range(1, row_len):
            copy_to(src, buf.at[col], send.at[d], recv.at[col],
                    row_peer((col + d) % row_len)).wait_send()
        for d in range(1, n_rows):
            copy_to(mid_out, buf.at[row_len + row], send.at[row_len + d],
                    recv.at[row_len + row], col_peer((row + d) % n_rows)).wait_send()

    def rs_copy(d):
        j = (me_op + d) % n_op
        return copy_to(x_ref.at[j], rs_buf.at[me_op], send_rs.at[d], recv_rs.at[me_op], op_peer(j))

    for d in range(1, n_op):
        rs_copy(d).start()
    a_args = (n_op, me_op, t_out, op_buf, send_a, recv_a, op_peer)
    start_gather(*a_args)
    rs_buf[me_op] = x_ref[me_op]

    operators = copy_to(piece_ref, got_ref, send_w.at[send_w.shape[0] - 1],
                        recv_w.at[recv_w.shape[0] - 1], (next_sec, me_op))
    operators.start()

    wait_gather(*a_args)
    mid[...] = ordered_sum(op_buf, n_op)
    settle(mid, mid_out, local_sem.at[0])
    start_rows(mid_out, sec_buf, send_b, recv_b)

    for d in range(1, n_op):
        slot = (me_op + n_op - d) % n_op
        copy_to(x_ref.at[me_op], rs_buf.at[slot], send_rs.at[d], recv_rs.at[slot],
                op_peer(slot)).wait_recv()
    red[...] = ordered_sum(rs_buf, n_op)

    sums = finish_sec(mid_out, sec_buf, send_b, recv_b, part, part_out, local_sem.at[5])
    energy_sum = sums[0:1, 0:1]
    norm_sum = sums[0:1, 1:2]
    state_wide = st_ref[n_op + me_op].astype(jnp.float32)
    sigma = red[...] + sh_ref[me_op] * state_wide
    updated = state_wide - step_size * (sigma - (energy_sum / norm_sum) * state_wide)
    factor = jnp.sqrt(count / norm_sum)
    if final:
        square = total_of(updated * updated)
    new_buf[...] = (updated * factor).astype(new_buf.dtype)
    settle(new_buf, new_out, local_sem.at[2])

    sides = ((next_sec, 0),) if final else ((next_sec, 0), (prev_sec, 2 * n_op))
    sent = 0
    for side, base in sides:
        for j in range(n_op):
            copy_to(new_out, win_buf.at[base + me_op], send_w.at[sent],
                    recv_w.at[base + me_op], (side, j)).start()
            sent += 1
    for d in range(1, n_op):
        j = (me_op + d) % n_op
        copy_to(new_out, win_buf.at[n_op + me_op], send_w.at[sent],
                recv_w.at[n_op + me_op], op_peer(j)).start()
        sent += 1
    win_buf[n_op + me_op] = new_out[...]

    if final:
        mid2[...] = jnp.where(lane == 0, square, 0.0)
        settle(mid2, mid2_out, local_sem.at[1])
        a2_args = (n_op, me_op, mid2_out, op_buf2, send_a2, recv_a2, op_peer)
        start_gather(*a2_args)
        wait_gather(*a2_args)
        mid3[...] = ordered_sum(op_buf2, n_op)
        settle(mid3, mid3_out, local_sem.at[3])
        start_rows(mid3_out, sec_buf2, send_b2, recv_b2)
        new_norm = finish_sec(mid3_out, sec_buf2, send_b2, recv_b2, part2, part2_out,
                              local_sem.at[6])[0:1, 0:1]
        rescale = jnp.sqrt(count / new_norm) / factor

    from_sides = ((prev_sec, 0),) if final else ((prev_sec, 0), (next_sec, 2 * n_op))
    for side, base in from_sides:
        for j in range(n_op):
            copy_to(new_out, win_buf.at[base + j], send_w.at[0], recv_w.at[base + j],
                    (side, j)).wait_recv()
    for d in range(1, n_op):
        slot = (me_op + n_op - d) % n_op
        copy_to(new_out, win_buf.at[n_op + slot], send_w.at[0], recv_w.at[n_op + slot],
                op_peer(slot)).wait_recv()
    if final:
        for k in range(win_ref.shape[0]):
            win_ref[k] = (win_buf[k].astype(jnp.float32) * rescale).astype(win_ref.dtype)
    else:
        win_ref[...] = win_buf[...]
    operators.wait_recv()

    operators.wait_send()
    for d in range(1, n_op):
        rs_copy(d).wait_send()
    drain_gather(*a_args)
    drain_sec(mid_out, sec_buf, send_b, recv_b, part_out)
    if final:
        drain_gather(*a2_args)
        drain_sec(mid3_out, sec_buf2, send_b2, recv_b2, part2_out)
    for k in range(sent):
        copy_to(new_out, win_buf.at[n_op + me_op], send_w.at[k], recv_w.at[n_op + me_op],
                op_peer((me_op + 1) % n_op)).wait_send()


def step(partial, window, shift, piece, count, final, n_sec, n_op):
    shape = partial.shape
    rows = shape[0] * shape[1] // n_op
    chunks = partial.reshape(n_op, rows, shape[2])
    state_chunks = window.reshape(-1, rows, shape[2])
    shift_chunks = jnp.repeat(shift, n_op // shape[0])[:, None, None]
    slots = (2 if final else 3) * n_op
    tile_shape = (rows, shape[2])
    scalar_bufs = [
        pltpu.VMEM((n_op, 8, 128), jnp.float32),
        pltpu.VMEM((n_sec, 8, 128), jnp.float32),
        pltpu.VMEM((8, 128), jnp.float32),
        pltpu.VMEM((8, 128), jnp.float32),
    ]
    scratch = [
        pltpu.VMEM((8, 128), jnp.float32),
        pltpu.VMEM((8, 128), jnp.float32),
        pltpu.VMEM(chunks.shape, jnp.float32),
        pltpu.VMEM(tile_shape, jnp.float32),
    ] + scalar_bufs + (scalar_bufs + scalar_bufs[2:] if final else []) + [
        pltpu.VMEM(tile_shape, jnp.bfloat16),
        pltpu.VMEM(tile_shape, jnp.bfloat16),
        pltpu.VMEM((slots, rows, shape[2]), jnp.bfloat16),
    ] + [pltpu.VMEM((8, 128), jnp.float32)] * (4 if final else 2) + [
        pltpu.SemaphoreType.DMA((n_op,)),
        pltpu.SemaphoreType.DMA((n_op,)),
        pltpu.SemaphoreType.DMA((n_op,)),
        pltpu.SemaphoreType.DMA((n_op,)),
        pltpu.SemaphoreType.DMA((n_sec,)),
        pltpu.SemaphoreType.DMA((n_sec,)),
    ] + ([
        pltpu.SemaphoreType.DMA((n_op,)),
        pltpu.SemaphoreType.DMA((n_op,)),
        pltpu.SemaphoreType.DMA((n_sec,)),
        pltpu.SemaphoreType.DMA((n_sec,)),
    ] if final else []) + [
        pltpu.SemaphoreType.DMA((slots + n_op + 1,)),
        pltpu.SemaphoreType.DMA((slots + 1,)),
        pltpu.SemaphoreType.DMA((7,)),
    ]
    vmem = pl.BlockSpec(memory_space=pltpu.VMEM)
    anywhere = pl.BlockSpec(memory_space=pl.ANY)
    window, got = pl.pallas_call(
        functools.partial(step_kernel, n_sec, n_op, count, final),
        out_shape=(
            jax.ShapeDtypeStruct((slots, rows, shape[2]), jnp.bfloat16),
            jax.ShapeDtypeStruct(piece.shape, piece.dtype),
        ),
        in_specs=[vmem, vmem, vmem, anywhere],
        out_specs=(vmem, anywhere),
        scratch_shapes=scratch,
        compiler_params=pltpu.CompilerParams(
            collective_id=3 if final else 2, has_side_effects=True
        ),
    )(chunks, state_chunks, shift_chunks, piece)
    return window.reshape(slots // (n_op // shape[0]), shape[1], shape[2]), got


def sigma_part_kernel(partner_ref, win_ref, left_ref, right_ref, o_ref):
    b = pl.program_id(0)
    h = pl.program_id(1)
    share = left_ref.shape[0]

    @pl.when(h == 0)
    def _():
        o_ref[...] = jnp.zeros_like(o_ref)

    total = o_ref[0]
    for t in range(share):
        source = win_ref[partner_ref[h * share + t, b]]
        halfway = jnp.dot(left_ref[t, 0], source, preferred_element_type=jnp.float32)
        total = total + jnp.dot(halfway.astype(jnp.bfloat16), right_ref[t, 0],
                                preferred_element_type=jnp.float32)
    o_ref[0] = total


def sigma_part(window, left_ops, right_ops, partner):
    terms, sectors, m, _ = left_ops.shape
    halves = 2 if terms % 2 == 0 else 1
    op_spec = pl.BlockSpec((terms // halves, 1, m, m), lambda b, h, p: (h, b, 0, 0))
    return pl.pallas_call(
        sigma_part_kernel,
        out_shape=jax.ShapeDtypeStruct((sectors, m, m), jnp.float32),
        grid_spec=pltpu.PrefetchScalarGridSpec(
            num_scalar_prefetch=1,
            grid=(sectors, halves),
            in_specs=[
                pl.BlockSpec(window.shape, lambda b, h, p: (0, 0, 0)),
                op_spec,
                op_spec,
            ],
            out_specs=pl.BlockSpec((1, m, m), lambda b, h, p: (b, 0, 0)),
        ),
        cost_estimate=pl.CostEstimate(
            flops=4 * terms * sectors * m * m * m,
            bytes_accessed=2 * left_ops.size * 2 + window.size * 2 + sectors * m * m * 4,
            transcendentals=0,
        ),
    )(partner, window, left_ops, right_ops)


def shifted(block, axis, distance):
    devices = range(lax.axis_size(axis))
    route = [((i - distance) % len(devices), i) for i in devices]
    return lax.ppermute(block, axis, route)


def per_device(state_start, left_ops, right_ops, shift, partner, kept):
    sector_local = state_start.shape[0]
    width = state_start.shape[1]
    count = float(sector_local * lax.axis_size("sec") * width * width)
    n_sec = lax.axis_size("sec")
    n_op = lax.axis_size("op")
    kept_prev = shifted(kept, "sec", 1)
    state = state_start
    window = padded(state, (("sec", 0),), sector_local)
    terms = left_ops.shape[0]
    cuts = [terms * k // ITERS for k in range(ITERS + 1)]
    left_pieces = []
    for iteration in range(ITERS):
        partial_sigma = sigma_part(window, left_ops, right_ops, partner)
        final = iteration == ITERS - 1
        window, got = step(
            partial_sigma, window, shift,
            left_ops[cuts[iteration] : cuts[iteration + 1]], count, final, n_sec, n_op,
        )
        left_pieces.append(got)
        state = window[sector_local : 2 * sector_local]
    state_prev = window[:sector_local]
    left_prev = jnp.concatenate(left_pieces, axis=0)
    columns = jnp.arange(width, dtype=jnp.int32)
    keep_mask = (columns[None, :] < kept_prev[:, None]).astype(jnp.bfloat16)
    kept_block = state_prev * keep_mask[:, None, :]
    out_scale = 1.0 / float(width) ** 0.5
    projected = jnp.einsum(
        "tbij,bjk->tbik", left_prev, kept_block, preferred_element_type=jnp.float32
    ).astype(jnp.bfloat16)
    kept_turned = jnp.broadcast_to(
        jnp.swapaxes(kept_block, 1, 2)[None], left_prev.shape
    )
    new_ops = (
        jnp.einsum("tbij,tbjk->tbik", kept_turned, projected, preferred_element_type=jnp.float32)
        * out_scale
    ).astype(jnp.bfloat16)
    return (state, new_ops)


def solution(mesh):
    in_specs = (
        P("sec", None, None),
        P("op", "sec", None, None),
        P("op", "sec", None, None),
        P("sec"),
        P("op", "sec"),
        P("sec"),
    )
    out_specs = (P("sec", None, None), P("op", "sec", None, None))
    return jax.shard_map(
        per_device, mesh=mesh, in_specs=in_specs, out_specs=out_specs, check_vma=False
    )
```

```python
import functools

import jax
import jax.numpy as jnp
from jax import lax
from jax.experimental import pallas as pl
from jax.experimental.pallas import tpu as pltpu
from jax.sharding import PartitionSpec as P

MESH = pl.DeviceIdType.MESH

ITERS = 4


step_size = 0.5


def padded(cells, sides, width):
    for axis, dim in sides:
        count = lax.axis_size(axis)
        head = lax.slice_in_dim(cells, 0, width, axis=dim)
        tail = lax.slice_in_dim(cells, cells.shape[dim] - width, cells.shape[dim], axis=dim)
        cells = jnp.concatenate(
            [
                lax.ppermute(tail, axis, [(i, (i + 1) % count) for i in range(count)]),
                cells,
                lax.ppermute(head, axis, [((i + 1) % count, i) for i in range(count)]),
            ],
            axis=dim,
        )
    return cells


def all_sum_kernel(n_sec, n_op, x_ref, o_ref, op_buf, sec_buf, mid, out_buf,
                   send_a, recv_a, send_b, recv_b, local_sem):
    me_sec = lax.axis_index("sec")
    me_op = lax.axis_index("op")
    barrier = pltpu.get_barrier_semaphore()
    for d in range(1, n_op):
        pl.semaphore_signal(barrier, 1, device_id=(me_sec, (me_op + d) % n_op),
                            device_id_type=MESH)
    for d in range(1, n_sec):
        pl.semaphore_signal(barrier, 1, device_id=((me_sec + d) % n_sec, me_op),
                            device_id_type=MESH)
    pl.semaphore_wait(barrier, n_op - 1 + n_sec - 1)

    def stage(n, me, src, buf, send, recv, peer_of):
        for d in range(1, n):
            pltpu.make_async_remote_copy(
                src_ref=src, dst_ref=buf.at[me], send_sem=send.at[d],
                recv_sem=recv.at[me], device_id=peer_of((me + d) % n),
                device_id_type=MESH).start()
        buf[me] = src[...]
        for d in range(1, n):
            slot = (me + n - d) % n
            pltpu.make_async_remote_copy(
                src_ref=src, dst_ref=buf.at[slot], send_sem=send.at[d],
                recv_sem=recv.at[slot], device_id=peer_of(slot),
                device_id_type=MESH).wait_recv()
        for d in range(1, n):
            pltpu.make_async_remote_copy(
                src_ref=src, dst_ref=buf.at[me], send_sem=send.at[d],
                recv_sem=recv.at[me], device_id=peer_of((me + d) % n),
                device_id_type=MESH).wait_send()
        total = buf[0]
        for j in range(1, n):
            total = total + buf[j]
        return total

    mid[...] = stage(n_op, me_op, x_ref, op_buf, send_a, recv_a,
                     lambda j: (me_sec, j))
    local = pltpu.make_async_copy(mid, out_buf, local_sem)
    local.start()
    local.wait()
    o_ref[...] = stage(n_sec, me_sec, out_buf, sec_buf, send_b, recv_b,
                       lambda j: (j, me_op))


def all_sum(values, n_sec, n_op):
    lane = lax.broadcasted_iota(jnp.int32, (8, 128), 1)
    tile = jnp.zeros((8, 128), jnp.float32)
    for k, v in enumerate(values):
        tile = jnp.where(lane == k, v, tile)
    tile_spec = pl.BlockSpec(memory_space=pltpu.VMEM)
    out = pl.pallas_call(
        functools.partial(all_sum_kernel, n_sec, n_op),
        out_shape=jax.ShapeDtypeStruct((8, 128), jnp.float32),
        in_specs=[tile_spec],
        out_specs=tile_spec,
        scratch_shapes=[
            pltpu.VMEM((n_op, 8, 128), jnp.float32),
            pltpu.VMEM((n_sec, 8, 128), jnp.float32),
            pltpu.VMEM((8, 128), jnp.float32),
            pltpu.VMEM((8, 128), jnp.float32),
            pltpu.SemaphoreType.DMA((n_op,)),
            pltpu.SemaphoreType.DMA((n_op,)),
            pltpu.SemaphoreType.DMA((n_sec,)),
            pltpu.SemaphoreType.DMA((n_sec,)),
            pltpu.SemaphoreType.DMA(()),
        ],
        compiler_params=pltpu.CompilerParams(collective_id=0, has_side_effects=True),
    )(tile)
    return tuple(out[0, k] for k in range(len(values)))


def sigma_sum_kernel(n_sec, n_op, x_ref, t_ref, o_ref, s_ref,
                     rs_buf, red, red_out, ag_buf, op_buf, sec_buf, mid, mid_out,
                     send_rs, recv_rs, send_ag, recv_ag, send_a, recv_a,
                     send_b, recv_b, local_sem):
    me_sec = lax.axis_index("sec")
    me_op = lax.axis_index("op")
    barrier = pltpu.get_barrier_semaphore()
    for d in range(1, n_op):
        pl.semaphore_signal(barrier, 1, device_id=(me_sec, (me_op + d) % n_op),
                            device_id_type=MESH)
    for d in range(1, n_sec):
        pl.semaphore_signal(barrier, 1, device_id=((me_sec + d) % n_sec, me_op),
                            device_id_type=MESH)
    pl.semaphore_wait(barrier, n_op - 1 + n_sec - 1)

    def op_peer(j):
        return (me_sec, j)

    def sec_peer(j):
        return (j, me_op)

    def total_of(v):
        return jnp.sum(jnp.sum(v, axis=1, keepdims=True), axis=0, keepdims=True)

    lane = lax.broadcasted_iota(jnp.int32, (8, 128), 1)
    own = st_ref[n_op + me_op].astype(jnp.float32)
    own_square = total_of(own * own)
    energy = sh_ref[me_op] * own_square
    for j in range(n_op):
        energy = energy + total_of(x_ref[j] * st_ref[n_op + j].astype(jnp.float32))
    t_ref[...] = jnp.where(lane == 0, energy, jnp.where(lane == 1, own_square, 0.0))
    settle(t_ref, t_out, local_sem.at[4])

    def rs_copy(d):
        j = (me_op + d) % n_op
        return pltpu.make_async_remote_copy(
            src_ref=x_ref.at[j], dst_ref=rs_buf.at[me_op], send_sem=send_rs.at[d],
            recv_sem=recv_rs.at[me_op], device_id=op_peer(j), device_id_type=MESH)

    def rs_recv(d):
        slot = (me_op + n_op - d) % n_op
        return pltpu.make_async_remote_copy(
            src_ref=x_ref.at[me_op], dst_ref=rs_buf.at[slot], send_sem=send_rs.at[d],
            recv_sem=recv_rs.at[slot], device_id=op_peer(slot), device_id_type=MESH)

    def gather_copy(n, me, src, buf, send, recv, peer_of, d):
        return pltpu.make_async_remote_copy(
            src_ref=src, dst_ref=buf.at[me], send_sem=send.at[d],
            recv_sem=recv.at[me], device_id=peer_of((me + d) % n), device_id_type=MESH)

    def gather_recv(n, me, src, buf, send, recv, peer_of, d):
        slot = (me + n - d) % n
        return pltpu.make_async_remote_copy(
            src_ref=src, dst_ref=buf.at[slot], send_sem=send.at[d],
            recv_sem=recv.at[slot], device_id=peer_of(slot), device_id_type=MESH)

    def ordered_sum(buf, n):
        total = buf[0]
        for j in range(1, n):
            total = total + buf[j]
        return total

    for d in range(1, n_op):
        rs_copy(d).start()
    a_args = (n_op, me_op, t_out, op_buf, send_a, recv_a, op_peer)
    for d in range(1, n_op):
        gather_copy(*a_args, d).start()
    rs_buf[me_op] = x_ref[me_op]
    op_buf[me_op] = t_ref[...]

    for d in range(1, n_op):
        gather_recv(*a_args, d).wait_recv()
    mid[...] = ordered_sum(op_buf, n_op)
    local = pltpu.make_async_copy(mid, mid_out, local_sem.at[0])
    local.start()
    local.wait()
    b_args = (n_sec, me_sec, mid_out, sec_buf, send_b, recv_b, sec_peer)
    for d in range(1, n_sec):
        gather_copy(*b_args, d).start()
    sec_buf[me_sec] = mid_out[...]

    for d in range(1, n_op):
        rs_recv(d).wait_recv()
    red[...] = ordered_sum(rs_buf, n_op)
    local = pltpu.make_async_copy(red, red_out, local_sem.at[1])
    local.start()
    local.wait()
    g_args = (n_op, me_op, red_out, ag_buf, send_ag, recv_ag, op_peer)
    for d in range(1, n_op):
        gather_copy(*g_args, d).start()
    ag_buf[me_op] = red_out[...]

    for d in range(1, n_sec):
        gather_recv(*b_args, d).wait_recv()
    s_ref[...] = ordered_sum(sec_buf, n_sec)
    for d in range(1, n_op):
        gather_recv(*g_args, d).wait_recv()
    o_ref[...] = ag_buf[...]

    for d in range(1, n_op):
        rs_copy(d).wait_send()
        gather_copy(*a_args, d).wait_send()
        gather_copy(*g_args, d).wait_send()
    for d in range(1, n_sec):
        gather_copy(*b_args, d).wait_send()


def sigma_sum(partial, values, n_sec, n_op):
    shape = partial.shape
    rows = shape[0] * shape[1] // n_op
    chunks = partial.reshape(n_op, rows, shape[2])
    lane = lax.broadcasted_iota(jnp.int32, (8, 128), 1)
    tile = jnp.zeros((8, 128), jnp.float32)
    for k, v in enumerate(values):
        tile = jnp.where(lane == k, v, tile)
    vmem = pl.BlockSpec(memory_space=pltpu.VMEM)
    total, sums = pl.pallas_call(
        functools.partial(sigma_sum_kernel, n_sec, n_op),
        out_shape=(
            jax.ShapeDtypeStruct(chunks.shape, jnp.float32),
            jax.ShapeDtypeStruct((8, 128), jnp.float32),
        ),
        in_specs=[vmem, vmem],
        out_specs=(vmem, vmem),
        scratch_shapes=[
            pltpu.VMEM(chunks.shape, jnp.float32),
            pltpu.VMEM((rows, shape[2]), jnp.float32),
            pltpu.VMEM((rows, shape[2]), jnp.float32),
            pltpu.VMEM(chunks.shape, jnp.float32),
            pltpu.VMEM((n_op, 8, 128), jnp.float32),
            pltpu.VMEM((n_sec, 8, 128), jnp.float32),
            pltpu.VMEM((8, 128), jnp.float32),
            pltpu.VMEM((8, 128), jnp.float32),
            pltpu.SemaphoreType.DMA((n_op,)),
            pltpu.SemaphoreType.DMA((n_op,)),
            pltpu.SemaphoreType.DMA((n_op,)),
            pltpu.SemaphoreType.DMA((n_op,)),
            pltpu.SemaphoreType.DMA((n_op,)),
            pltpu.SemaphoreType.DMA((n_op,)),
            pltpu.SemaphoreType.DMA((n_sec,)),
            pltpu.SemaphoreType.DMA((n_sec,)),
            pltpu.SemaphoreType.DMA((2,)),
        ],
        compiler_params=pltpu.CompilerParams(collective_id=1, has_side_effects=True),
    )(chunks, tile)
    return total.reshape(shape), tuple(sums[0, k] for k in range(len(values)))


def step_kernel(n_sec, n_op, count, final, x_ref, st_ref, sh_ref, piece_ref, *refs):
    if final:
        (win_ref, got_ref, t_ref, t_out, rs_buf, red, op_buf, sec_buf, mid, mid_out,
         op_buf2, sec_buf2, mid2, mid2_out, mid3, mid3_out, new_buf, new_out, win_buf,
         part, part_out, part2, part2_out,
         send_rs, recv_rs, send_a, recv_a, send_b, recv_b, send_a2, recv_a2, send_b2,
         recv_b2, send_w, recv_w, local_sem) = refs
    else:
        (win_ref, got_ref, t_ref, t_out, rs_buf, red, op_buf, sec_buf, mid, mid_out,
         new_buf, new_out, win_buf, part, part_out, send_rs, recv_rs, send_a, recv_a, send_b, recv_b, send_w,
         recv_w, local_sem) = refs
    me_sec = lax.axis_index("sec")
    me_op = lax.axis_index("op")
    prev_sec = (me_sec + n_sec - 1) % n_sec
    next_sec = (me_sec + 1) % n_sec
    barrier = pltpu.get_barrier_semaphore()
    row_len = 8 if n_sec % 8 == 0 else (2 if n_sec % 2 == 0 else n_sec)
    n_rows = n_sec // row_len
    row = me_sec // row_len
    col = me_sec % row_len
    greet = [(me_sec, (me_op + d) % n_op) for d in range(1, n_op)]
    greet += [(row * row_len + (col + d) % row_len, me_op) for d in range(1, row_len)]
    greet += [(((row + d) % n_rows) * row_len + col, me_op) for d in range(1, n_rows)]
    greet += [(side, j) for side in (prev_sec, next_sec) for j in range(n_op)]
    for peer in greet:
        pl.semaphore_signal(barrier, 1, device_id=peer, device_id_type=MESH)
    greeted = len(greet)

    def op_peer(j):
        return (me_sec, j)

    def sec_peer(j):
        return (j, me_op)

    def copy_to(src, dst, send, recv, peer):
        return pltpu.make_async_remote_copy(
            src_ref=src, dst_ref=dst, send_sem=send, recv_sem=recv,
            device_id=peer, device_id_type=MESH)

    def ordered_sum(buf, n):
        total = buf[0]
        for j in range(1, n):
            total = total + buf[j]
        return total

    def start_gather(n, me, src, buf, send, recv, peer_of):
        for d in range(1, n):
            copy_to(src, buf.at[me], send.at[d], recv.at[me], peer_of((me + d) % n)).start()
        buf[me] = src[...]

    def wait_gather(n, me, src, buf, send, recv, peer_of):
        for d in range(1, n):
            slot = (me + n - d) % n
            copy_to(src, buf.at[slot], send.at[d], recv.at[slot], peer_of(slot)).wait_recv()

    def drain_gather(n, me, src, buf, send, recv, peer_of):
        for d in range(1, n):
            copy_to(src, buf.at[me], send.at[d], recv.at[me], peer_of((me + d) % n)).wait_send()

    def settle(src, dst, sem):
        local = pltpu.make_async_copy(src, dst, sem)
        local.start()
        local.wait()

    def total_of(v):
        return jnp.sum(jnp.sum(v, axis=1, keepdims=True), axis=0, keepdims=True)

    lane = lax.broadcasted_iota(jnp.int32, (8, 128), 1)
    own = st_ref[n_op + me_op].astype(jnp.float32)
    own_square = total_of(own * own)
    energy = sh_ref[me_op] * own_square
    for j in range(n_op):
        energy = energy + total_of(x_ref[j] * st_ref[n_op + j].astype(jnp.float32))
    t_ref[...] = jnp.where(lane == 0, energy, jnp.where(lane == 1, own_square, 0.0))
    settle(t_ref, t_out, local_sem.at[4])

    def row_peer(c):
        return (row * row_len + c, me_op)

    def col_peer(r):
        return (r * row_len + col, me_op)

    def start_rows(src, buf, send, recv):
        for d in range(1, row_len):
            copy_to(src, buf.at[col], send.at[d], recv.at[col],
                    row_peer((col + d) % row_len)).start()
        buf[col] = src[...]

    def finish_sec(src, buf, send, recv, mid_sum, mid_out, sem):
        for d in range(1, row_len):
            slot = (col + row_len - d) % row_len
            copy_to(src, buf.at[slot], send.at[d], recv.at[slot], row_peer(slot)).wait_recv()
        mid_sum[...] = ordered_sum(buf, row_len)
        settle(mid_sum, mid_out, sem)
        for d in range(1, n_rows):
            copy_to(mid_out, buf.at[row_len + row], send.at[row_len + d],
                    recv.at[row_len + row], col_peer((row + d) % n_rows)).start()
        buf[row_len + row] = mid_out[...]
        for d in range(1, n_rows):
            slot = (row + n_rows - d) % n_rows
            copy_to(mid_out, buf.at[row_len + slot], send.at[row_len + d],
                    recv.at[row_len + slot], col_peer(slot)).wait_recv()
        total = buf[row_len]
        for r in range(1, n_rows):
            total = total + buf[row_len + r]
        return total

    def drain_sec(src, buf, send, recv, mid_out):
        for d in range(1, row_len):
            copy_to(src, buf.at[col], send.at[d], recv.at[col],
                    row_peer((col + d) % row_len)).wait_send()
        for d in range(1, n_rows):
            copy_to(mid_out, buf.at[row_len + row], send.at[row_len + d],
                    recv.at[row_len + row], col_peer((row + d) % n_rows)).wait_send()

    def rs_copy(d):
        j = (me_op + d) % n_op
        return copy_to(x_ref.at[j], rs_buf.at[me_op], send_rs.at[d], recv_rs.at[me_op], op_peer(j))

    pl.semaphore_wait(barrier, greeted)
    for d in range(1, n_op):
        rs_copy(d).start()
    a_args = (n_op, me_op, t_out, op_buf, send_a, recv_a, op_peer)
    start_gather(*a_args)
    rs_buf[me_op] = x_ref[me_op]

    operators = copy_to(piece_ref, got_ref, send_w.at[send_w.shape[0] - 1],
                        recv_w.at[recv_w.shape[0] - 1], (next_sec, me_op))
    operators.start()

    wait_gather(*a_args)
    mid[...] = ordered_sum(op_buf, n_op)
    settle(mid, mid_out, local_sem.at[0])
    start_rows(mid_out, sec_buf, send_b, recv_b)

    for d in range(1, n_op):
        slot = (me_op + n_op - d) % n_op
        copy_to(x_ref.at[me_op], rs_buf.at[slot], send_rs.at[d], recv_rs.at[slot],
                op_peer(slot)).wait_recv()
    red[...] = ordered_sum(rs_buf, n_op)

    sums = finish_sec(mid_out, sec_buf, send_b, recv_b, part, part_out, local_sem.at[5])
    energy_sum = sums[0:1, 0:1]
    norm_sum = sums[0:1, 1:2]
    state_wide = st_ref[n_op + me_op].astype(jnp.float32)
    sigma = red[...] + sh_ref[me_op] * state_wide
    updated = state_wide - step_size * (sigma - (energy_sum / norm_sum) * state_wide)
    factor = jnp.sqrt(count / norm_sum)
    if final:
        square = total_of(updated * updated)
    new_buf[...] = (updated * factor).astype(new_buf.dtype)
    settle(new_buf, new_out, local_sem.at[2])

    sides = ((next_sec, 0),) if final else ((next_sec, 0), (prev_sec, 2 * n_op))
    sent = 0
    for side, base in sides:
        for j in range(n_op):
            copy_to(new_out, win_buf.at[base + me_op], send_w.at[sent],
                    recv_w.at[base + me_op], (side, j)).start()
            sent += 1
    for d in range(1, n_op):
        j = (me_op + d) % n_op
        copy_to(new_out, win_buf.at[n_op + me_op], send_w.at[sent],
                recv_w.at[n_op + me_op], op_peer(j)).start()
        sent += 1
    win_buf[n_op + me_op] = new_out[...]

    if final:
        mid2[...] = jnp.where(lane == 0, square, 0.0)
        settle(mid2, mid2_out, local_sem.at[1])
        a2_args = (n_op, me_op, mid2_out, op_buf2, send_a2, recv_a2, op_peer)
        start_gather(*a2_args)
        wait_gather(*a2_args)
        mid3[...] = ordered_sum(op_buf2, n_op)
        settle(mid3, mid3_out, local_sem.at[3])
        start_rows(mid3_out, sec_buf2, send_b2, recv_b2)
        new_norm = finish_sec(mid3_out, sec_buf2, send_b2, recv_b2, part2, part2_out,
                              local_sem.at[6])[0:1, 0:1]
        rescale = jnp.sqrt(count / new_norm) / factor

    from_sides = ((prev_sec, 0),) if final else ((prev_sec, 0), (next_sec, 2 * n_op))
    for side, base in from_sides:
        for j in range(n_op):
            copy_to(new_out, win_buf.at[base + j], send_w.at[0], recv_w.at[base + j],
                    (side, j)).wait_recv()
    for d in range(1, n_op):
        slot = (me_op + n_op - d) % n_op
        copy_to(new_out, win_buf.at[n_op + slot], send_w.at[0], recv_w.at[n_op + slot],
                op_peer(slot)).wait_recv()
    if final:
        for k in range(win_ref.shape[0]):
            win_ref[k] = (win_buf[k].astype(jnp.float32) * rescale).astype(win_ref.dtype)
    else:
        win_ref[...] = win_buf[...]
    operators.wait_recv()

    operators.wait_send()
    for d in range(1, n_op):
        rs_copy(d).wait_send()
    drain_gather(*a_args)
    drain_sec(mid_out, sec_buf, send_b, recv_b, part_out)
    if final:
        drain_gather(*a2_args)
        drain_sec(mid3_out, sec_buf2, send_b2, recv_b2, part2_out)
    for k in range(sent):
        copy_to(new_out, win_buf.at[n_op + me_op], send_w.at[k], recv_w.at[n_op + me_op],
                op_peer((me_op + 1) % n_op)).wait_send()


def step(partial, window, shift, piece, count, final, n_sec, n_op):
    shape = partial.shape
    rows = shape[0] * shape[1] // n_op
    chunks = partial.reshape(n_op, rows, shape[2])
    state_chunks = window.reshape(-1, rows, shape[2])
    shift_chunks = jnp.repeat(shift, n_op // shape[0])[:, None, None]
    slots = (2 if final else 3) * n_op
    tile_shape = (rows, shape[2])
    scalar_bufs = [
        pltpu.VMEM((n_op, 8, 128), jnp.float32),
        pltpu.VMEM((n_sec, 8, 128), jnp.float32),
        pltpu.VMEM((8, 128), jnp.float32),
        pltpu.VMEM((8, 128), jnp.float32),
    ]
    scratch = [
        pltpu.VMEM((8, 128), jnp.float32),
        pltpu.VMEM((8, 128), jnp.float32),
        pltpu.VMEM(chunks.shape, jnp.float32),
        pltpu.VMEM(tile_shape, jnp.float32),
    ] + scalar_bufs + (scalar_bufs + scalar_bufs[2:] if final else []) + [
        pltpu.VMEM(tile_shape, jnp.bfloat16),
        pltpu.VMEM(tile_shape, jnp.bfloat16),
        pltpu.VMEM((slots, rows, shape[2]), jnp.bfloat16),
    ] + [pltpu.VMEM((8, 128), jnp.float32)] * (4 if final else 2) + [
        pltpu.SemaphoreType.DMA((n_op,)),
        pltpu.SemaphoreType.DMA((n_op,)),
        pltpu.SemaphoreType.DMA((n_op,)),
        pltpu.SemaphoreType.DMA((n_op,)),
        pltpu.SemaphoreType.DMA((n_sec,)),
        pltpu.SemaphoreType.DMA((n_sec,)),
    ] + ([
        pltpu.SemaphoreType.DMA((n_op,)),
        pltpu.SemaphoreType.DMA((n_op,)),
        pltpu.SemaphoreType.DMA((n_sec,)),
        pltpu.SemaphoreType.DMA((n_sec,)),
    ] if final else []) + [
        pltpu.SemaphoreType.DMA((slots + n_op + 1,)),
        pltpu.SemaphoreType.DMA((slots + 1,)),
        pltpu.SemaphoreType.DMA((7,)),
    ]
    vmem = pl.BlockSpec(memory_space=pltpu.VMEM)
    anywhere = pl.BlockSpec(memory_space=pl.ANY)
    window, got = pl.pallas_call(
        functools.partial(step_kernel, n_sec, n_op, count, final),
        out_shape=(
            jax.ShapeDtypeStruct((slots, rows, shape[2]), jnp.bfloat16),
            jax.ShapeDtypeStruct(piece.shape, piece.dtype),
        ),
        in_specs=[vmem, vmem, vmem, anywhere],
        out_specs=(vmem, anywhere),
        scratch_shapes=scratch,
        compiler_params=pltpu.CompilerParams(
            collective_id=3 if final else 2, has_side_effects=True
        ),
    )(chunks, state_chunks, shift_chunks, piece)
    return window.reshape(slots // (n_op // shape[0]), shape[1], shape[2]), got


def sigma_part_kernel(partner_ref, win_ref, left_ref, right_ref, o_ref):
    b = pl.program_id(0)
    total = jnp.zeros(o_ref.shape[1:], jnp.float32)
    for t in range(left_ref.shape[0]):
        source = win_ref[partner_ref[t, b]]
        halfway = jnp.dot(left_ref[t, 0], source, preferred_element_type=jnp.float32)
        total = total + jnp.dot(halfway.astype(jnp.bfloat16), right_ref[t, 0],
                                preferred_element_type=jnp.float32)
    o_ref[0] = total


def sigma_part(window, left_ops, right_ops, partner):
    terms, sectors, m, _ = left_ops.shape
    op_spec = pl.BlockSpec((terms, 1, m, m), lambda b, p: (0, b, 0, 0))
    return pl.pallas_call(
        sigma_part_kernel,
        out_shape=jax.ShapeDtypeStruct((sectors, m, m), jnp.float32),
        grid_spec=pltpu.PrefetchScalarGridSpec(
            num_scalar_prefetch=1,
            grid=(sectors,),
            in_specs=[
                pl.BlockSpec(window.shape, lambda b, p: (0, 0, 0)),
                op_spec,
                op_spec,
            ],
            out_specs=pl.BlockSpec((1, m, m), lambda b, p: (b, 0, 0)),
        ),
        cost_estimate=pl.CostEstimate(
            flops=4 * terms * sectors * m * m * m,
            bytes_accessed=2 * left_ops.size * 2 + window.size * 2 + sectors * m * m * 4,
            transcendentals=0,
        ),
    )(partner, window, left_ops, right_ops)


def shifted(block, axis, distance):
    devices = range(lax.axis_size(axis))
    route = [((i - distance) % len(devices), i) for i in devices]
    return lax.ppermute(block, axis, route)


def per_device(state_start, left_ops, right_ops, shift, partner, kept):
    sector_local = state_start.shape[0]
    width = state_start.shape[1]
    count = float(sector_local * lax.axis_size("sec") * width * width)
    n_sec = lax.axis_size("sec")
    n_op = lax.axis_size("op")
    kept_prev = shifted(kept, "sec", 1)
    state = state_start
    window = padded(state, (("sec", 0),), sector_local)
    terms = left_ops.shape[0]
    cuts = [terms * k // ITERS for k in range(ITERS + 1)]
    left_pieces = []
    for iteration in range(ITERS):
        partial_sigma = sigma_part(window, left_ops, right_ops, partner)
        final = iteration == ITERS - 1
        window, got = step(
            partial_sigma, window, shift,
            left_ops[cuts[iteration] : cuts[iteration + 1]], count, final, n_sec, n_op,
        )
        left_pieces.append(got)
        state = window[sector_local : 2 * sector_local]
    state_prev = window[:sector_local]
    left_prev = jnp.concatenate(left_pieces, axis=0)
    columns = jnp.arange(width, dtype=jnp.int32)
    keep_mask = (columns[None, :] < kept_prev[:, None]).astype(jnp.bfloat16)
    kept_block = state_prev * keep_mask[:, None, :]
    out_scale = 1.0 / float(width) ** 0.5
    projected = jnp.einsum(
        "tbij,bjk->tbik", left_prev, kept_block, preferred_element_type=jnp.float32
    ).astype(jnp.bfloat16)
    kept_turned = jnp.broadcast_to(
        jnp.swapaxes(kept_block, 1, 2)[None], left_prev.shape
    )
    new_ops = (
        jnp.einsum("tbij,tbjk->tbik", kept_turned, projected, preferred_element_type=jnp.float32)
        * out_scale
    ).astype(jnp.bfloat16)
    return (state, new_ops)


def solution(mesh):
    in_specs = (
        P("sec", None, None),
        P("op", "sec", None, None),
        P("op", "sec", None, None),
        P("sec"),
        P("op", "sec"),
        P("sec"),
    )
    out_specs = (P("sec", None, None), P("op", "sec", None, None))
    return jax.shard_map(
        per_device, mesh=mesh, in_specs=in_specs, out_specs=out_specs, check_vma=False
    )
```

```python
import functools

import jax
import jax.numpy as jnp
from jax import lax
from jax.experimental import pallas as pl
from jax.experimental.pallas import tpu as pltpu
from jax.sharding import PartitionSpec as P

MESH = pl.DeviceIdType.MESH

ITERS = 4


step_size = 0.5


def padded(cells, sides, width):
    for axis, dim in sides:
        count = lax.axis_size(axis)
        head = lax.slice_in_dim(cells, 0, width, axis=dim)
        tail = lax.slice_in_dim(cells, cells.shape[dim] - width, cells.shape[dim], axis=dim)
        cells = jnp.concatenate(
            [
                lax.ppermute(tail, axis, [(i, (i + 1) % count) for i in range(count)]),
                cells,
                lax.ppermute(head, axis, [((i + 1) % count, i) for i in range(count)]),
            ],
            axis=dim,
        )
    return cells


def all_sum_kernel(n_sec, n_op, x_ref, o_ref, op_buf, sec_buf, mid, out_buf,
                   send_a, recv_a, send_b, recv_b, local_sem):
    me_sec = lax.axis_index("sec")
    me_op = lax.axis_index("op")
    barrier = pltpu.get_barrier_semaphore()
    for d in range(1, n_op):
        pl.semaphore_signal(barrier, 1, device_id=(me_sec, (me_op + d) % n_op),
                            device_id_type=MESH)
    for d in range(1, n_sec):
        pl.semaphore_signal(barrier, 1, device_id=((me_sec + d) % n_sec, me_op),
                            device_id_type=MESH)
    pl.semaphore_wait(barrier, n_op - 1 + n_sec - 1)

    def stage(n, me, src, buf, send, recv, peer_of):
        for d in range(1, n):
            pltpu.make_async_remote_copy(
                src_ref=src, dst_ref=buf.at[me], send_sem=send.at[d],
                recv_sem=recv.at[me], device_id=peer_of((me + d) % n),
                device_id_type=MESH).start()
        buf[me] = src[...]
        for d in range(1, n):
            slot = (me + n - d) % n
            pltpu.make_async_remote_copy(
                src_ref=src, dst_ref=buf.at[slot], send_sem=send.at[d],
                recv_sem=recv.at[slot], device_id=peer_of(slot),
                device_id_type=MESH).wait_recv()
        for d in range(1, n):
            pltpu.make_async_remote_copy(
                src_ref=src, dst_ref=buf.at[me], send_sem=send.at[d],
                recv_sem=recv.at[me], device_id=peer_of((me + d) % n),
                device_id_type=MESH).wait_send()
        total = buf[0]
        for j in range(1, n):
            total = total + buf[j]
        return total

    mid[...] = stage(n_op, me_op, x_ref, op_buf, send_a, recv_a,
                     lambda j: (me_sec, j))
    local = pltpu.make_async_copy(mid, out_buf, local_sem)
    local.start()
    local.wait()
    o_ref[...] = stage(n_sec, me_sec, out_buf, sec_buf, send_b, recv_b,
                       lambda j: (j, me_op))


def all_sum(values, n_sec, n_op):
    lane = lax.broadcasted_iota(jnp.int32, (8, 128), 1)
    tile = jnp.zeros((8, 128), jnp.float32)
    for k, v in enumerate(values):
        tile = jnp.where(lane == k, v, tile)
    tile_spec = pl.BlockSpec(memory_space=pltpu.VMEM)
    out = pl.pallas_call(
        functools.partial(all_sum_kernel, n_sec, n_op),
        out_shape=jax.ShapeDtypeStruct((8, 128), jnp.float32),
        in_specs=[tile_spec],
        out_specs=tile_spec,
        scratch_shapes=[
            pltpu.VMEM((n_op, 8, 128), jnp.float32),
            pltpu.VMEM((n_sec, 8, 128), jnp.float32),
            pltpu.VMEM((8, 128), jnp.float32),
            pltpu.VMEM((8, 128), jnp.float32),
            pltpu.SemaphoreType.DMA((n_op,)),
            pltpu.SemaphoreType.DMA((n_op,)),
            pltpu.SemaphoreType.DMA((n_sec,)),
            pltpu.SemaphoreType.DMA((n_sec,)),
            pltpu.SemaphoreType.DMA(()),
        ],
        compiler_params=pltpu.CompilerParams(collective_id=0, has_side_effects=True),
    )(tile)
    return tuple(out[0, k] for k in range(len(values)))


def sigma_sum_kernel(n_sec, n_op, x_ref, t_ref, o_ref, s_ref,
                     rs_buf, red, red_out, ag_buf, op_buf, sec_buf, mid, mid_out,
                     send_rs, recv_rs, send_ag, recv_ag, send_a, recv_a,
                     send_b, recv_b, local_sem):
    me_sec = lax.axis_index("sec")
    me_op = lax.axis_index("op")
    barrier = pltpu.get_barrier_semaphore()
    for d in range(1, n_op):
        pl.semaphore_signal(barrier, 1, device_id=(me_sec, (me_op + d) % n_op),
                            device_id_type=MESH)
    for d in range(1, n_sec):
        pl.semaphore_signal(barrier, 1, device_id=((me_sec + d) % n_sec, me_op),
                            device_id_type=MESH)
    pl.semaphore_wait(barrier, n_op - 1 + n_sec - 1)

    def op_peer(j):
        return (me_sec, j)

    def sec_peer(j):
        return (j, me_op)

    def total_of(v):
        return jnp.sum(jnp.sum(v, axis=1, keepdims=True), axis=0, keepdims=True)

    lane = lax.broadcasted_iota(jnp.int32, (8, 128), 1)
    own = st_ref[n_op + me_op].astype(jnp.float32)
    own_square = total_of(own * own)
    energy = sh_ref[me_op] * own_square
    for j in range(n_op):
        energy = energy + total_of(x_ref[j] * st_ref[n_op + j].astype(jnp.float32))
    t_ref[...] = jnp.where(lane == 0, energy, jnp.where(lane == 1, own_square, 0.0))
    settle(t_ref, t_out, local_sem.at[4])

    def rs_copy(d):
        j = (me_op + d) % n_op
        return pltpu.make_async_remote_copy(
            src_ref=x_ref.at[j], dst_ref=rs_buf.at[me_op], send_sem=send_rs.at[d],
            recv_sem=recv_rs.at[me_op], device_id=op_peer(j), device_id_type=MESH)

    def rs_recv(d):
        slot = (me_op + n_op - d) % n_op
        return pltpu.make_async_remote_copy(
            src_ref=x_ref.at[me_op], dst_ref=rs_buf.at[slot], send_sem=send_rs.at[d],
            recv_sem=recv_rs.at[slot], device_id=op_peer(slot), device_id_type=MESH)

    def gather_copy(n, me, src, buf, send, recv, peer_of, d):
        return pltpu.make_async_remote_copy(
            src_ref=src, dst_ref=buf.at[me], send_sem=send.at[d],
            recv_sem=recv.at[me], device_id=peer_of((me + d) % n), device_id_type=MESH)

    def gather_recv(n, me, src, buf, send, recv, peer_of, d):
        slot = (me + n - d) % n
        return pltpu.make_async_remote_copy(
            src_ref=src, dst_ref=buf.at[slot], send_sem=send.at[d],
            recv_sem=recv.at[slot], device_id=peer_of(slot), device_id_type=MESH)

    def ordered_sum(buf, n):
        total = buf[0]
        for j in range(1, n):
            total = total + buf[j]
        return total

    for d in range(1, n_op):
        rs_copy(d).start()
    a_args = (n_op, me_op, t_out, op_buf, send_a, recv_a, op_peer)
    for d in range(1, n_op):
        gather_copy(*a_args, d).start()
    rs_buf[me_op] = x_ref[me_op]
    op_buf[me_op] = t_ref[...]

    for d in range(1, n_op):
        gather_recv(*a_args, d).wait_recv()
    mid[...] = ordered_sum(op_buf, n_op)
    local = pltpu.make_async_copy(mid, mid_out, local_sem.at[0])
    local.start()
    local.wait()
    b_args = (n_sec, me_sec, mid_out, sec_buf, send_b, recv_b, sec_peer)
    for d in range(1, n_sec):
        gather_copy(*b_args, d).start()
    sec_buf[me_sec] = mid_out[...]

    for d in range(1, n_op):
        rs_recv(d).wait_recv()
    red[...] = ordered_sum(rs_buf, n_op)
    local = pltpu.make_async_copy(red, red_out, local_sem.at[1])
    local.start()
    local.wait()
    g_args = (n_op, me_op, red_out, ag_buf, send_ag, recv_ag, op_peer)
    for d in range(1, n_op):
        gather_copy(*g_args, d).start()
    ag_buf[me_op] = red_out[...]

    for d in range(1, n_sec):
        gather_recv(*b_args, d).wait_recv()
    s_ref[...] = ordered_sum(sec_buf, n_sec)
    for d in range(1, n_op):
        gather_recv(*g_args, d).wait_recv()
    o_ref[...] = ag_buf[...]

    for d in range(1, n_op):
        rs_copy(d).wait_send()
        gather_copy(*a_args, d).wait_send()
        gather_copy(*g_args, d).wait_send()
    for d in range(1, n_sec):
        gather_copy(*b_args, d).wait_send()


def sigma_sum(partial, values, n_sec, n_op):
    shape = partial.shape
    rows = shape[0] * shape[1] // n_op
    chunks = partial.reshape(n_op, rows, shape[2])
    lane = lax.broadcasted_iota(jnp.int32, (8, 128), 1)
    tile = jnp.zeros((8, 128), jnp.float32)
    for k, v in enumerate(values):
        tile = jnp.where(lane == k, v, tile)
    vmem = pl.BlockSpec(memory_space=pltpu.VMEM)
    total, sums = pl.pallas_call(
        functools.partial(sigma_sum_kernel, n_sec, n_op),
        out_shape=(
            jax.ShapeDtypeStruct(chunks.shape, jnp.float32),
            jax.ShapeDtypeStruct((8, 128), jnp.float32),
        ),
        in_specs=[vmem, vmem],
        out_specs=(vmem, vmem),
        scratch_shapes=[
            pltpu.VMEM(chunks.shape, jnp.float32),
            pltpu.VMEM((rows, shape[2]), jnp.float32),
            pltpu.VMEM((rows, shape[2]), jnp.float32),
            pltpu.VMEM(chunks.shape, jnp.float32),
            pltpu.VMEM((n_op, 8, 128), jnp.float32),
            pltpu.VMEM((n_sec, 8, 128), jnp.float32),
            pltpu.VMEM((8, 128), jnp.float32),
            pltpu.VMEM((8, 128), jnp.float32),
            pltpu.SemaphoreType.DMA((n_op,)),
            pltpu.SemaphoreType.DMA((n_op,)),
            pltpu.SemaphoreType.DMA((n_op,)),
            pltpu.SemaphoreType.DMA((n_op,)),
            pltpu.SemaphoreType.DMA((n_op,)),
            pltpu.SemaphoreType.DMA((n_op,)),
            pltpu.SemaphoreType.DMA((n_sec,)),
            pltpu.SemaphoreType.DMA((n_sec,)),
            pltpu.SemaphoreType.DMA((2,)),
        ],
        compiler_params=pltpu.CompilerParams(collective_id=1, has_side_effects=True),
    )(chunks, tile)
    return total.reshape(shape), tuple(sums[0, k] for k in range(len(values)))


def step_kernel(n_sec, n_op, count, final, x_ref, st_ref, sh_ref, piece_ref, *refs):
    if final:
        (win_ref, got_ref, t_ref, t_out, rs_buf, red, op_buf, sec_buf, mid, mid_out,
         op_buf2, sec_buf2, mid2, mid2_out, mid3, mid3_out, new_buf, new_out, win_buf,
         part, part_out, part2, part2_out,
         send_rs, recv_rs, send_a, recv_a, send_b, recv_b, send_a2, recv_a2, send_b2,
         recv_b2, send_w, recv_w, local_sem) = refs
    else:
        (win_ref, got_ref, t_ref, t_out, rs_buf, red, op_buf, sec_buf, mid, mid_out,
         new_buf, new_out, win_buf, part, part_out, send_rs, recv_rs, send_a, recv_a, send_b, recv_b, send_w,
         recv_w, local_sem) = refs
    me_sec = lax.axis_index("sec")
    me_op = lax.axis_index("op")
    prev_sec = (me_sec + n_sec - 1) % n_sec
    next_sec = (me_sec + 1) % n_sec
    barrier = pltpu.get_barrier_semaphore()
    row_len = 8 if n_sec % 8 == 0 else (2 if n_sec % 2 == 0 else n_sec)
    n_rows = n_sec // row_len
    row = me_sec // row_len
    col = me_sec % row_len
    greet = [(me_sec, (me_op + d) % n_op) for d in range(1, n_op)]
    greet += [(row * row_len + (col + d) % row_len, me_op) for d in range(1, row_len)]
    greet += [(((row + d) % n_rows) * row_len + col, me_op) for d in range(1, n_rows)]
    greet += [(side, j) for side in (prev_sec, next_sec) for j in range(n_op)]
    for peer in greet:
        pl.semaphore_signal(barrier, 1, device_id=peer, device_id_type=MESH)
    greeted = len(greet)

    def op_peer(j):
        return (me_sec, j)

    def sec_peer(j):
        return (j, me_op)

    def copy_to(src, dst, send, recv, peer):
        return pltpu.make_async_remote_copy(
            src_ref=src, dst_ref=dst, send_sem=send, recv_sem=recv,
            device_id=peer, device_id_type=MESH)

    def ordered_sum(buf, n):
        total = buf[0]
        for j in range(1, n):
            total = total + buf[j]
        return total

    def start_gather(n, me, src, buf, send, recv, peer_of):
        for d in range(1, n):
            copy_to(src, buf.at[me], send.at[d], recv.at[me], peer_of((me + d) % n)).start()
        buf[me] = src[...]

    def wait_gather(n, me, src, buf, send, recv, peer_of):
        for d in range(1, n):
            slot = (me + n - d) % n
            copy_to(src, buf.at[slot], send.at[d], recv.at[slot], peer_of(slot)).wait_recv()

    def drain_gather(n, me, src, buf, send, recv, peer_of):
        for d in range(1, n):
            copy_to(src, buf.at[me], send.at[d], recv.at[me], peer_of((me + d) % n)).wait_send()

    def settle(src, dst, sem):
        local = pltpu.make_async_copy(src, dst, sem)
        local.start()
        local.wait()

    def total_of(v):
        return jnp.sum(jnp.sum(v, axis=1, keepdims=True), axis=0, keepdims=True)

    lane = lax.broadcasted_iota(jnp.int32, (8, 128), 1)
    own = st_ref[n_op + me_op].astype(jnp.float32)
    own_square = total_of(own * own)
    energy = sh_ref[me_op] * own_square
    for j in range(n_op):
        energy = energy + total_of(x_ref[j] * st_ref[n_op + j].astype(jnp.float32))
    t_ref[...] = jnp.where(lane == 0, energy, jnp.where(lane == 1, own_square, 0.0))
    settle(t_ref, t_out, local_sem.at[4])

    def row_peer(c):
        return (row * row_len + c, me_op)

    def col_peer(r):
        return (r * row_len + col, me_op)

    def start_rows(src, buf, send, recv):
        for d in range(1, row_len):
            copy_to(src, buf.at[col], send.at[d], recv.at[col],
                    row_peer((col + d) % row_len)).start()
        buf[col] = src[...]

    def finish_sec(src, buf, send, recv, mid_sum, mid_out, sem):
        for d in range(1, row_len):
            slot = (col + row_len - d) % row_len
            copy_to(src, buf.at[slot], send.at[d], recv.at[slot], row_peer(slot)).wait_recv()
        mid_sum[...] = ordered_sum(buf, row_len)
        settle(mid_sum, mid_out, sem)
        for d in range(1, n_rows):
            copy_to(mid_out, buf.at[row_len + row], send.at[row_len + d],
                    recv.at[row_len + row], col_peer((row + d) % n_rows)).start()
        buf[row_len + row] = mid_out[...]
        for d in range(1, n_rows):
            slot = (row + n_rows - d) % n_rows
            copy_to(mid_out, buf.at[row_len + slot], send.at[row_len + d],
                    recv.at[row_len + slot], col_peer(slot)).wait_recv()
        total = buf[row_len]
        for r in range(1, n_rows):
            total = total + buf[row_len + r]
        return total

    def drain_sec(src, buf, send, recv, mid_out):
        for d in range(1, row_len):
            copy_to(src, buf.at[col], send.at[d], recv.at[col],
                    row_peer((col + d) % row_len)).wait_send()
        for d in range(1, n_rows):
            copy_to(mid_out, buf.at[row_len + row], send.at[row_len + d],
                    recv.at[row_len + row], col_peer((row + d) % n_rows)).wait_send()

    def rs_copy(d):
        j = (me_op + d) % n_op
        return copy_to(x_ref.at[j], rs_buf.at[me_op], send_rs.at[d], recv_rs.at[me_op], op_peer(j))

    pl.semaphore_wait(barrier, greeted)
    a_args = (n_op, me_op, t_out, op_buf, send_a, recv_a, op_peer)
    start_gather(*a_args)
    for d in range(1, n_op):
        rs_copy(d).start()
    rs_buf[me_op] = x_ref[me_op]

    operators = copy_to(piece_ref, got_ref, send_w.at[send_w.shape[0] - 1],
                        recv_w.at[recv_w.shape[0] - 1], (next_sec, me_op))
    operators.start()

    wait_gather(*a_args)
    mid[...] = ordered_sum(op_buf, n_op)
    settle(mid, mid_out, local_sem.at[0])
    start_rows(mid_out, sec_buf, send_b, recv_b)

    for d in range(1, n_op):
        slot = (me_op + n_op - d) % n_op
        copy_to(x_ref.at[me_op], rs_buf.at[slot], send_rs.at[d], recv_rs.at[slot],
                op_peer(slot)).wait_recv()
    red[...] = ordered_sum(rs_buf, n_op)

    sums = finish_sec(mid_out, sec_buf, send_b, recv_b, part, part_out, local_sem.at[5])
    energy_sum = sums[0:1, 0:1]
    norm_sum = sums[0:1, 1:2]
    state_wide = st_ref[n_op + me_op].astype(jnp.float32)
    sigma = red[...] + sh_ref[me_op] * state_wide
    updated = state_wide - step_size * (sigma - (energy_sum / norm_sum) * state_wide)
    factor = jnp.sqrt(count / norm_sum)
    if final:
        square = total_of(updated * updated)
    new_buf[...] = (updated * factor).astype(new_buf.dtype)
    settle(new_buf, new_out, local_sem.at[2])

    sides = ((next_sec, 0),) if final else ((next_sec, 0), (prev_sec, 2 * n_op))
    sent = 0
    for side, base in sides:
        for j in range(n_op):
            copy_to(new_out, win_buf.at[base + me_op], send_w.at[sent],
                    recv_w.at[base + me_op], (side, j)).start()
            sent += 1
    for d in range(1, n_op):
        j = (me_op + d) % n_op
        copy_to(new_out, win_buf.at[n_op + me_op], send_w.at[sent],
                recv_w.at[n_op + me_op], op_peer(j)).start()
        sent += 1
    win_buf[n_op + me_op] = new_out[...]

    if final:
        mid2[...] = jnp.where(lane == 0, square, 0.0)
        settle(mid2, mid2_out, local_sem.at[1])
        a2_args = (n_op, me_op, mid2_out, op_buf2, send_a2, recv_a2, op_peer)
        start_gather(*a2_args)
        wait_gather(*a2_args)
        mid3[...] = ordered_sum(op_buf2, n_op)
        settle(mid3, mid3_out, local_sem.at[3])
        start_rows(mid3_out, sec_buf2, send_b2, recv_b2)
        new_norm = finish_sec(mid3_out, sec_buf2, send_b2, recv_b2, part2, part2_out,
                              local_sem.at[6])[0:1, 0:1]
        rescale = jnp.sqrt(count / new_norm) / factor

    from_sides = ((prev_sec, 0),) if final else ((prev_sec, 0), (next_sec, 2 * n_op))
    for side, base in from_sides:
        for j in range(n_op):
            copy_to(new_out, win_buf.at[base + j], send_w.at[0], recv_w.at[base + j],
                    (side, j)).wait_recv()
    for d in range(1, n_op):
        slot = (me_op + n_op - d) % n_op
        copy_to(new_out, win_buf.at[n_op + slot], send_w.at[0], recv_w.at[n_op + slot],
                op_peer(slot)).wait_recv()
    if final:
        for k in range(win_ref.shape[0]):
            win_ref[k] = (win_buf[k].astype(jnp.float32) * rescale).astype(win_ref.dtype)
    else:
        win_ref[...] = win_buf[...]
    operators.wait_recv()

    operators.wait_send()
    for d in range(1, n_op):
        rs_copy(d).wait_send()
    drain_gather(*a_args)
    drain_sec(mid_out, sec_buf, send_b, recv_b, part_out)
    if final:
        drain_gather(*a2_args)
        drain_sec(mid3_out, sec_buf2, send_b2, recv_b2, part2_out)
    for k in range(sent):
        copy_to(new_out, win_buf.at[n_op + me_op], send_w.at[k], recv_w.at[n_op + me_op],
                op_peer((me_op + 1) % n_op)).wait_send()


def step(partial, window, shift, piece, count, final, n_sec, n_op):
    shape = partial.shape
    rows = shape[0] * shape[1] // n_op
    chunks = partial.reshape(n_op, rows, shape[2])
    state_chunks = window.reshape(-1, rows, shape[2])
    shift_chunks = jnp.repeat(shift, n_op // shape[0])[:, None, None]
    slots = (2 if final else 3) * n_op
    tile_shape = (rows, shape[2])
    scalar_bufs = [
        pltpu.VMEM((n_op, 8, 128), jnp.float32),
        pltpu.VMEM((n_sec, 8, 128), jnp.float32),
        pltpu.VMEM((8, 128), jnp.float32),
        pltpu.VMEM((8, 128), jnp.float32),
    ]
    scratch = [
        pltpu.VMEM((8, 128), jnp.float32),
        pltpu.VMEM((8, 128), jnp.float32),
        pltpu.VMEM(chunks.shape, jnp.float32),
        pltpu.VMEM(tile_shape, jnp.float32),
    ] + scalar_bufs + (scalar_bufs + scalar_bufs[2:] if final else []) + [
        pltpu.VMEM(tile_shape, jnp.bfloat16),
        pltpu.VMEM(tile_shape, jnp.bfloat16),
        pltpu.VMEM((slots, rows, shape[2]), jnp.bfloat16),
    ] + [pltpu.VMEM((8, 128), jnp.float32)] * (4 if final else 2) + [
        pltpu.SemaphoreType.DMA((n_op,)),
        pltpu.SemaphoreType.DMA((n_op,)),
        pltpu.SemaphoreType.DMA((n_op,)),
        pltpu.SemaphoreType.DMA((n_op,)),
        pltpu.SemaphoreType.DMA((n_sec,)),
        pltpu.SemaphoreType.DMA((n_sec,)),
    ] + ([
        pltpu.SemaphoreType.DMA((n_op,)),
        pltpu.SemaphoreType.DMA((n_op,)),
        pltpu.SemaphoreType.DMA((n_sec,)),
        pltpu.SemaphoreType.DMA((n_sec,)),
    ] if final else []) + [
        pltpu.SemaphoreType.DMA((slots + n_op + 1,)),
        pltpu.SemaphoreType.DMA((slots + 1,)),
        pltpu.SemaphoreType.DMA((7,)),
    ]
    vmem = pl.BlockSpec(memory_space=pltpu.VMEM)
    anywhere = pl.BlockSpec(memory_space=pl.ANY)
    window, got = pl.pallas_call(
        functools.partial(step_kernel, n_sec, n_op, count, final),
        out_shape=(
            jax.ShapeDtypeStruct((slots, rows, shape[2]), jnp.bfloat16),
            jax.ShapeDtypeStruct(piece.shape, piece.dtype),
        ),
        in_specs=[vmem, vmem, vmem, anywhere],
        out_specs=(vmem, anywhere),
        scratch_shapes=scratch,
        compiler_params=pltpu.CompilerParams(
            collective_id=3 if final else 2, has_side_effects=True
        ),
    )(chunks, state_chunks, shift_chunks, piece)
    return window.reshape(slots // (n_op // shape[0]), shape[1], shape[2]), got


def sigma_part_kernel(partner_ref, win_ref, left_ref, right_ref, o_ref):
    b = pl.program_id(0)
    total = jnp.zeros(o_ref.shape[1:], jnp.float32)
    for t in range(left_ref.shape[0]):
        source = win_ref[partner_ref[t, b]]
        halfway = jnp.dot(left_ref[t, 0], source, preferred_element_type=jnp.float32)
        total = total + jnp.dot(halfway.astype(jnp.bfloat16), right_ref[t, 0],
                                preferred_element_type=jnp.float32)
    o_ref[0] = total


def sigma_part(window, left_ops, right_ops, partner):
    terms, sectors, m, _ = left_ops.shape
    op_spec = pl.BlockSpec((terms, 1, m, m), lambda b, p: (0, b, 0, 0))
    return pl.pallas_call(
        sigma_part_kernel,
        out_shape=jax.ShapeDtypeStruct((sectors, m, m), jnp.float32),
        grid_spec=pltpu.PrefetchScalarGridSpec(
            num_scalar_prefetch=1,
            grid=(sectors,),
            in_specs=[
                pl.BlockSpec(window.shape, lambda b, p: (0, 0, 0)),
                op_spec,
                op_spec,
            ],
            out_specs=pl.BlockSpec((1, m, m), lambda b, p: (b, 0, 0)),
        ),
        cost_estimate=pl.CostEstimate(
            flops=4 * terms * sectors * m * m * m,
            bytes_accessed=2 * left_ops.size * 2 + window.size * 2 + sectors * m * m * 4,
            transcendentals=0,
        ),
    )(partner, window, left_ops, right_ops)


def shifted(block, axis, distance):
    devices = range(lax.axis_size(axis))
    route = [((i - distance) % len(devices), i) for i in devices]
    return lax.ppermute(block, axis, route)


def per_device(state_start, left_ops, right_ops, shift, partner, kept):
    sector_local = state_start.shape[0]
    width = state_start.shape[1]
    count = float(sector_local * lax.axis_size("sec") * width * width)
    n_sec = lax.axis_size("sec")
    n_op = lax.axis_size("op")
    kept_prev = shifted(kept, "sec", 1)
    state = state_start
    window = padded(state, (("sec", 0),), sector_local)
    terms = left_ops.shape[0]
    cuts = [terms * k // ITERS for k in range(ITERS + 1)]
    left_pieces = []
    for iteration in range(ITERS):
        partial_sigma = sigma_part(window, left_ops, right_ops, partner)
        final = iteration == ITERS - 1
        window, got = step(
            partial_sigma, window, shift,
            left_ops[cuts[iteration] : cuts[iteration + 1]], count, final, n_sec, n_op,
        )
        left_pieces.append(got)
        state = window[sector_local : 2 * sector_local]
    state_prev = window[:sector_local]
    left_prev = jnp.concatenate(left_pieces, axis=0)
    columns = jnp.arange(width, dtype=jnp.int32)
    keep_mask = (columns[None, :] < kept_prev[:, None]).astype(jnp.bfloat16)
    kept_block = state_prev * keep_mask[:, None, :]
    out_scale = 1.0 / float(width) ** 0.5
    projected = jnp.einsum(
        "tbij,bjk->tbik", left_prev, kept_block, preferred_element_type=jnp.float32
    ).astype(jnp.bfloat16)
    kept_turned = jnp.broadcast_to(
        jnp.swapaxes(kept_block, 1, 2)[None], left_prev.shape
    )
    new_ops = (
        jnp.einsum("tbij,tbjk->tbik", kept_turned, projected, preferred_element_type=jnp.float32)
        * out_scale
    ).astype(jnp.bfloat16)
    return (state, new_ops)


def solution(mesh):
    in_specs = (
        P("sec", None, None),
        P("op", "sec", None, None),
        P("op", "sec", None, None),
        P("sec"),
        P("op", "sec"),
        P("sec"),
    )
    out_specs = (P("sec", None, None), P("op", "sec", None, None))
    return jax.shard_map(
        per_device, mesh=mesh, in_specs=in_specs, out_specs=out_specs, check_vma=False
    )
```

```python
import functools

import jax
import jax.numpy as jnp
from jax import lax
from jax.experimental import pallas as pl
from jax.experimental.pallas import tpu as pltpu
from jax.sharding import PartitionSpec as P

MESH = pl.DeviceIdType.MESH

ITERS = 4


step_size = 0.5


def padded(cells, sides, width):
    for axis, dim in sides:
        count = lax.axis_size(axis)
        head = lax.slice_in_dim(cells, 0, width, axis=dim)
        tail = lax.slice_in_dim(cells, cells.shape[dim] - width, cells.shape[dim], axis=dim)
        cells = jnp.concatenate(
            [
                lax.ppermute(tail, axis, [(i, (i + 1) % count) for i in range(count)]),
                cells,
                lax.ppermute(head, axis, [((i + 1) % count, i) for i in range(count)]),
            ],
            axis=dim,
        )
    return cells


def all_sum_kernel(n_sec, n_op, x_ref, o_ref, op_buf, sec_buf, mid, out_buf,
                   send_a, recv_a, send_b, recv_b, local_sem):
    me_sec = lax.axis_index("sec")
    me_op = lax.axis_index("op")
    barrier = pltpu.get_barrier_semaphore()
    for d in range(1, n_op):
        pl.semaphore_signal(barrier, 1, device_id=(me_sec, (me_op + d) % n_op),
                            device_id_type=MESH)
    for d in range(1, n_sec):
        pl.semaphore_signal(barrier, 1, device_id=((me_sec + d) % n_sec, me_op),
                            device_id_type=MESH)
    pl.semaphore_wait(barrier, n_op - 1 + n_sec - 1)

    def stage(n, me, src, buf, send, recv, peer_of):
        for d in range(1, n):
            pltpu.make_async_remote_copy(
                src_ref=src, dst_ref=buf.at[me], send_sem=send.at[d],
                recv_sem=recv.at[me], device_id=peer_of((me + d) % n),
                device_id_type=MESH).start()
        buf[me] = src[...]
        for d in range(1, n):
            slot = (me + n - d) % n
            pltpu.make_async_remote_copy(
                src_ref=src, dst_ref=buf.at[slot], send_sem=send.at[d],
                recv_sem=recv.at[slot], device_id=peer_of(slot),
                device_id_type=MESH).wait_recv()
        for d in range(1, n):
            pltpu.make_async_remote_copy(
                src_ref=src, dst_ref=buf.at[me], send_sem=send.at[d],
                recv_sem=recv.at[me], device_id=peer_of((me + d) % n),
                device_id_type=MESH).wait_send()
        total = buf[0]
        for j in range(1, n):
            total = total + buf[j]
        return total

    mid[...] = stage(n_op, me_op, x_ref, op_buf, send_a, recv_a,
                     lambda j: (me_sec, j))
    local = pltpu.make_async_copy(mid, out_buf, local_sem)
    local.start()
    local.wait()
    o_ref[...] = stage(n_sec, me_sec, out_buf, sec_buf, send_b, recv_b,
                       lambda j: (j, me_op))


def all_sum(values, n_sec, n_op):
    lane = lax.broadcasted_iota(jnp.int32, (8, 128), 1)
    tile = jnp.zeros((8, 128), jnp.float32)
    for k, v in enumerate(values):
        tile = jnp.where(lane == k, v, tile)
    tile_spec = pl.BlockSpec(memory_space=pltpu.VMEM)
    out = pl.pallas_call(
        functools.partial(all_sum_kernel, n_sec, n_op),
        out_shape=jax.ShapeDtypeStruct((8, 128), jnp.float32),
        in_specs=[tile_spec],
        out_specs=tile_spec,
        scratch_shapes=[
            pltpu.VMEM((n_op, 8, 128), jnp.float32),
            pltpu.VMEM((n_sec, 8, 128), jnp.float32),
            pltpu.VMEM((8, 128), jnp.float32),
            pltpu.VMEM((8, 128), jnp.float32),
            pltpu.SemaphoreType.DMA((n_op,)),
            pltpu.SemaphoreType.DMA((n_op,)),
            pltpu.SemaphoreType.DMA((n_sec,)),
            pltpu.SemaphoreType.DMA((n_sec,)),
            pltpu.SemaphoreType.DMA(()),
        ],
        compiler_params=pltpu.CompilerParams(collective_id=0, has_side_effects=True),
    )(tile)
    return tuple(out[0, k] for k in range(len(values)))


def sigma_sum_kernel(n_sec, n_op, x_ref, t_ref, o_ref, s_ref,
                     rs_buf, red, red_out, ag_buf, op_buf, sec_buf, mid, mid_out,
                     send_rs, recv_rs, send_ag, recv_ag, send_a, recv_a,
                     send_b, recv_b, local_sem):
    me_sec = lax.axis_index("sec")
    me_op = lax.axis_index("op")
    barrier = pltpu.get_barrier_semaphore()
    for d in range(1, n_op):
        pl.semaphore_signal(barrier, 1, device_id=(me_sec, (me_op + d) % n_op),
                            device_id_type=MESH)
    for d in range(1, n_sec):
        pl.semaphore_signal(barrier, 1, device_id=((me_sec + d) % n_sec, me_op),
                            device_id_type=MESH)
    pl.semaphore_wait(barrier, n_op - 1 + n_sec - 1)

    def op_peer(j):
        return (me_sec, j)

    def sec_peer(j):
        return (j, me_op)

    def total_of(v):
        return jnp.sum(jnp.sum(v, axis=1, keepdims=True), axis=0, keepdims=True)

    lane = lax.broadcasted_iota(jnp.int32, (8, 128), 1)
    own = st_ref[n_op + me_op].astype(jnp.float32)
    own_square = total_of(own * own)
    energy = sh_ref[me_op] * own_square
    for j in range(n_op):
        energy = energy + total_of(x_ref[j] * st_ref[n_op + j].astype(jnp.float32))
    t_ref[...] = jnp.where(lane == 0, energy, jnp.where(lane == 1, own_square, 0.0))
    settle(t_ref, t_out, local_sem.at[4])

    def rs_copy(d):
        j = (me_op + d) % n_op
        return pltpu.make_async_remote_copy(
            src_ref=x_ref.at[j], dst_ref=rs_buf.at[me_op], send_sem=send_rs.at[d],
            recv_sem=recv_rs.at[me_op], device_id=op_peer(j), device_id_type=MESH)

    def rs_recv(d):
        slot = (me_op + n_op - d) % n_op
        return pltpu.make_async_remote_copy(
            src_ref=x_ref.at[me_op], dst_ref=rs_buf.at[slot], send_sem=send_rs.at[d],
            recv_sem=recv_rs.at[slot], device_id=op_peer(slot), device_id_type=MESH)

    def gather_copy(n, me, src, buf, send, recv, peer_of, d):
        return pltpu.make_async_remote_copy(
            src_ref=src, dst_ref=buf.at[me], send_sem=send.at[d],
            recv_sem=recv.at[me], device_id=peer_of((me + d) % n), device_id_type=MESH)

    def gather_recv(n, me, src, buf, send, recv, peer_of, d):
        slot = (me + n - d) % n
        return pltpu.make_async_remote_copy(
            src_ref=src, dst_ref=buf.at[slot], send_sem=send.at[d],
            recv_sem=recv.at[slot], device_id=peer_of(slot), device_id_type=MESH)

    def ordered_sum(buf, n):
        total = buf[0]
        for j in range(1, n):
            total = total + buf[j]
        return total

    for d in range(1, n_op):
        rs_copy(d).start()
    a_args = (n_op, me_op, t_out, op_buf, send_a, recv_a, op_peer)
    for d in range(1, n_op):
        gather_copy(*a_args, d).start()
    rs_buf[me_op] = x_ref[me_op]
    op_buf[me_op] = t_ref[...]

    for d in range(1, n_op):
        gather_recv(*a_args, d).wait_recv()
    mid[...] = ordered_sum(op_buf, n_op)
    local = pltpu.make_async_copy(mid, mid_out, local_sem.at[0])
    local.start()
    local.wait()
    b_args = (n_sec, me_sec, mid_out, sec_buf, send_b, recv_b, sec_peer)
    for d in range(1, n_sec):
        gather_copy(*b_args, d).start()
    sec_buf[me_sec] = mid_out[...]

    for d in range(1, n_op):
        rs_recv(d).wait_recv()
    red[...] = ordered_sum(rs_buf, n_op)
    local = pltpu.make_async_copy(red, red_out, local_sem.at[1])
    local.start()
    local.wait()
    g_args = (n_op, me_op, red_out, ag_buf, send_ag, recv_ag, op_peer)
    for d in range(1, n_op):
        gather_copy(*g_args, d).start()
    ag_buf[me_op] = red_out[...]

    for d in range(1, n_sec):
        gather_recv(*b_args, d).wait_recv()
    s_ref[...] = ordered_sum(sec_buf, n_sec)
    for d in range(1, n_op):
        gather_recv(*g_args, d).wait_recv()
    o_ref[...] = ag_buf[...]

    for d in range(1, n_op):
        rs_copy(d).wait_send()
        gather_copy(*a_args, d).wait_send()
        gather_copy(*g_args, d).wait_send()
    for d in range(1, n_sec):
        gather_copy(*b_args, d).wait_send()


def sigma_sum(partial, values, n_sec, n_op):
    shape = partial.shape
    rows = shape[0] * shape[1] // n_op
    chunks = partial.reshape(n_op, rows, shape[2])
    lane = lax.broadcasted_iota(jnp.int32, (8, 128), 1)
    tile = jnp.zeros((8, 128), jnp.float32)
    for k, v in enumerate(values):
        tile = jnp.where(lane == k, v, tile)
    vmem = pl.BlockSpec(memory_space=pltpu.VMEM)
    total, sums = pl.pallas_call(
        functools.partial(sigma_sum_kernel, n_sec, n_op),
        out_shape=(
            jax.ShapeDtypeStruct(chunks.shape, jnp.float32),
            jax.ShapeDtypeStruct((8, 128), jnp.float32),
        ),
        in_specs=[vmem, vmem],
        out_specs=(vmem, vmem),
        scratch_shapes=[
            pltpu.VMEM(chunks.shape, jnp.float32),
            pltpu.VMEM((rows, shape[2]), jnp.float32),
            pltpu.VMEM((rows, shape[2]), jnp.float32),
            pltpu.VMEM(chunks.shape, jnp.float32),
            pltpu.VMEM((n_op, 8, 128), jnp.float32),
            pltpu.VMEM((n_sec, 8, 128), jnp.float32),
            pltpu.VMEM((8, 128), jnp.float32),
            pltpu.VMEM((8, 128), jnp.float32),
            pltpu.SemaphoreType.DMA((n_op,)),
            pltpu.SemaphoreType.DMA((n_op,)),
            pltpu.SemaphoreType.DMA((n_op,)),
            pltpu.SemaphoreType.DMA((n_op,)),
            pltpu.SemaphoreType.DMA((n_op,)),
            pltpu.SemaphoreType.DMA((n_op,)),
            pltpu.SemaphoreType.DMA((n_sec,)),
            pltpu.SemaphoreType.DMA((n_sec,)),
            pltpu.SemaphoreType.DMA((2,)),
        ],
        compiler_params=pltpu.CompilerParams(collective_id=1, has_side_effects=True),
    )(chunks, tile)
    return total.reshape(shape), tuple(sums[0, k] for k in range(len(values)))


def step_kernel(n_sec, n_op, count, final, x_ref, st_ref, sh_ref, piece_ref, *refs):
    if final:
        (win_ref, got_ref, t_ref, t_out, rs_buf, red, op_buf, sec_buf, mid, mid_out,
         op_buf2, sec_buf2, mid2, mid2_out, mid3, mid3_out, new_buf, new_out, win_buf,
         part, part_out, part2, part2_out,
         send_rs, recv_rs, send_a, recv_a, send_b, recv_b, send_a2, recv_a2, send_b2,
         recv_b2, send_w, recv_w, local_sem) = refs
    else:
        (win_ref, got_ref, t_ref, t_out, rs_buf, red, op_buf, sec_buf, mid, mid_out,
         new_buf, new_out, win_buf, part, part_out, send_rs, recv_rs, send_a, recv_a, send_b, recv_b, send_w,
         recv_w, local_sem) = refs
    me_sec = lax.axis_index("sec")
    me_op = lax.axis_index("op")
    prev_sec = (me_sec + n_sec - 1) % n_sec
    next_sec = (me_sec + 1) % n_sec
    barrier = pltpu.get_barrier_semaphore()
    row_len = 8 if n_sec % 8 == 0 else (2 if n_sec % 2 == 0 else n_sec)
    n_rows = n_sec // row_len
    row = me_sec // row_len
    col = me_sec % row_len
    greet = [(me_sec, (me_op + d) % n_op) for d in range(1, n_op)]
    greet += [(row * row_len + (col + d) % row_len, me_op) for d in range(1, row_len)]
    greet += [(((row + d) % n_rows) * row_len + col, me_op) for d in range(1, n_rows)]
    greet += [(side, j) for side in (prev_sec, next_sec) for j in range(n_op)]
    for peer in greet:
        pl.semaphore_signal(barrier, 1, device_id=peer, device_id_type=MESH)
    greeted = len(greet)

    def op_peer(j):
        return (me_sec, j)

    def sec_peer(j):
        return (j, me_op)

    def copy_to(src, dst, send, recv, peer):
        return pltpu.make_async_remote_copy(
            src_ref=src, dst_ref=dst, send_sem=send, recv_sem=recv,
            device_id=peer, device_id_type=MESH)

    def ordered_sum(buf, n):
        total = buf[0]
        for j in range(1, n):
            total = total + buf[j]
        return total

    def start_gather(n, me, src, buf, send, recv, peer_of):
        for d in range(1, n):
            copy_to(src, buf.at[me], send.at[d], recv.at[me], peer_of((me + d) % n)).start()
        buf[me] = src[...]

    def wait_gather(n, me, src, buf, send, recv, peer_of):
        for d in range(1, n):
            slot = (me + n - d) % n
            copy_to(src, buf.at[slot], send.at[d], recv.at[slot], peer_of(slot)).wait_recv()

    def drain_gather(n, me, src, buf, send, recv, peer_of):
        for d in range(1, n):
            copy_to(src, buf.at[me], send.at[d], recv.at[me], peer_of((me + d) % n)).wait_send()

    def settle(src, dst, sem):
        local = pltpu.make_async_copy(src, dst, sem)
        local.start()
        local.wait()

    def total_of(v):
        return jnp.sum(jnp.sum(v, axis=1, keepdims=True), axis=0, keepdims=True)

    lane = lax.broadcasted_iota(jnp.int32, (8, 128), 1)
    own = st_ref[n_op + me_op].astype(jnp.float32)
    own_square = total_of(own * own)
    energy = sh_ref[me_op] * own_square
    for j in range(n_op):
        energy = energy + total_of(x_ref[j] * st_ref[n_op + j].astype(jnp.float32))
    t_ref[...] = jnp.where(lane == 0, energy, jnp.where(lane == 1, own_square, 0.0))
    settle(t_ref, t_out, local_sem.at[4])

    def row_peer(c):
        return (row * row_len + c, me_op)

    def col_peer(r):
        return (r * row_len + col, me_op)

    def start_rows(src, buf, send, recv):
        for d in range(1, row_len):
            copy_to(src, buf.at[col], send.at[d], recv.at[col],
                    row_peer((col + d) % row_len)).start()
        buf[col] = src[...]

    def finish_sec(src, buf, send, recv, mid_sum, mid_out, sem):
        for d in range(1, row_len):
            slot = (col + row_len - d) % row_len
            copy_to(src, buf.at[slot], send.at[d], recv.at[slot], row_peer(slot)).wait_recv()
        mid_sum[...] = ordered_sum(buf, row_len)
        settle(mid_sum, mid_out, sem)
        for d in range(1, n_rows):
            copy_to(mid_out, buf.at[row_len + row], send.at[row_len + d],
                    recv.at[row_len + row], col_peer((row + d) % n_rows)).start()
        buf[row_len + row] = mid_out[...]
        for d in range(1, n_rows):
            slot = (row + n_rows - d) % n_rows
            copy_to(mid_out, buf.at[row_len + slot], send.at[row_len + d],
                    recv.at[row_len + slot], col_peer(slot)).wait_recv()
        total = buf[row_len]
        for r in range(1, n_rows):
            total = total + buf[row_len + r]
        return total

    def drain_sec(src, buf, send, recv, mid_out):
        for d in range(1, row_len):
            copy_to(src, buf.at[col], send.at[d], recv.at[col],
                    row_peer((col + d) % row_len)).wait_send()
        for d in range(1, n_rows):
            copy_to(mid_out, buf.at[row_len + row], send.at[row_len + d],
                    recv.at[row_len + row], col_peer((row + d) % n_rows)).wait_send()

    def rs_copy(d):
        j = (me_op + d) % n_op
        return copy_to(x_ref.at[j], rs_buf.at[me_op], send_rs.at[d], recv_rs.at[me_op], op_peer(j))

    pl.semaphore_wait(barrier, greeted)
    a_args = (n_op, me_op, t_out, op_buf, send_a, recv_a, op_peer)
    start_gather(*a_args)
    for d in range(1, n_op):
        rs_copy(d).start()
    rs_buf[me_op] = x_ref[me_op]


    wait_gather(*a_args)
    mid[...] = ordered_sum(op_buf, n_op)
    settle(mid, mid_out, local_sem.at[0])
    start_rows(mid_out, sec_buf, send_b, recv_b)
    operators = copy_to(piece_ref, got_ref, send_w.at[send_w.shape[0] - 1],
                        recv_w.at[recv_w.shape[0] - 1], (next_sec, me_op))
    operators.start()

    for d in range(1, n_op):
        slot = (me_op + n_op - d) % n_op
        copy_to(x_ref.at[me_op], rs_buf.at[slot], send_rs.at[d], recv_rs.at[slot],
                op_peer(slot)).wait_recv()
    red[...] = ordered_sum(rs_buf, n_op)

    sums = finish_sec(mid_out, sec_buf, send_b, recv_b, part, part_out, local_sem.at[5])
    energy_sum = sums[0:1, 0:1]
    norm_sum = sums[0:1, 1:2]
    state_wide = st_ref[n_op + me_op].astype(jnp.float32)
    sigma = red[...] + sh_ref[me_op] * state_wide
    updated = state_wide - step_size * (sigma - (energy_sum / norm_sum) * state_wide)
    factor = jnp.sqrt(count / norm_sum)
    if final:
        square = total_of(updated * updated)
    new_buf[...] = (updated * factor).astype(new_buf.dtype)
    settle(new_buf, new_out, local_sem.at[2])

    sides = ((next_sec, 0),) if final else ((next_sec, 0), (prev_sec, 2 * n_op))
    sent = 0
    for side, base in sides:
        for j in range(n_op):
            copy_to(new_out, win_buf.at[base + me_op], send_w.at[sent],
                    recv_w.at[base + me_op], (side, j)).start()
            sent += 1
    for d in range(1, n_op):
        j = (me_op + d) % n_op
        copy_to(new_out, win_buf.at[n_op + me_op], send_w.at[sent],
                recv_w.at[n_op + me_op], op_peer(j)).start()
        sent += 1
    win_buf[n_op + me_op] = new_out[...]

    if final:
        mid2[...] = jnp.where(lane == 0, square, 0.0)
        settle(mid2, mid2_out, local_sem.at[1])
        a2_args = (n_op, me_op, mid2_out, op_buf2, send_a2, recv_a2, op_peer)
        start_gather(*a2_args)
        wait_gather(*a2_args)
        mid3[...] = ordered_sum(op_buf2, n_op)
        settle(mid3, mid3_out, local_sem.at[3])
        start_rows(mid3_out, sec_buf2, send_b2, recv_b2)
        new_norm = finish_sec(mid3_out, sec_buf2, send_b2, recv_b2, part2, part2_out,
                              local_sem.at[6])[0:1, 0:1]
        rescale = jnp.sqrt(count / new_norm) / factor

    from_sides = ((prev_sec, 0),) if final else ((prev_sec, 0), (next_sec, 2 * n_op))
    for side, base in from_sides:
        for j in range(n_op):
            copy_to(new_out, win_buf.at[base + j], send_w.at[0], recv_w.at[base + j],
                    (side, j)).wait_recv()
    for d in range(1, n_op):
        slot = (me_op + n_op - d) % n_op
        copy_to(new_out, win_buf.at[n_op + slot], send_w.at[0], recv_w.at[n_op + slot],
                op_peer(slot)).wait_recv()
    if final:
        for k in range(win_ref.shape[0]):
            win_ref[k] = (win_buf[k].astype(jnp.float32) * rescale).astype(win_ref.dtype)
    else:
        win_ref[...] = win_buf[...]
    operators.wait_recv()

    operators.wait_send()
    for d in range(1, n_op):
        rs_copy(d).wait_send()
    drain_gather(*a_args)
    drain_sec(mid_out, sec_buf, send_b, recv_b, part_out)
    if final:
        drain_gather(*a2_args)
        drain_sec(mid3_out, sec_buf2, send_b2, recv_b2, part2_out)
    for k in range(sent):
        copy_to(new_out, win_buf.at[n_op + me_op], send_w.at[k], recv_w.at[n_op + me_op],
                op_peer((me_op + 1) % n_op)).wait_send()


def step(partial, window, shift, piece, count, final, n_sec, n_op):
    shape = partial.shape
    rows = shape[0] * shape[1] // n_op
    chunks = partial.reshape(n_op, rows, shape[2])
    state_chunks = window.reshape(-1, rows, shape[2])
    shift_chunks = jnp.repeat(shift, n_op // shape[0])[:, None, None]
    slots = (2 if final else 3) * n_op
    tile_shape = (rows, shape[2])
    scalar_bufs = [
        pltpu.VMEM((n_op, 8, 128), jnp.float32),
        pltpu.VMEM((n_sec, 8, 128), jnp.float32),
        pltpu.VMEM((8, 128), jnp.float32),
        pltpu.VMEM((8, 128), jnp.float32),
    ]
    scratch = [
        pltpu.VMEM((8, 128), jnp.float32),
        pltpu.VMEM((8, 128), jnp.float32),
        pltpu.VMEM(chunks.shape, jnp.float32),
        pltpu.VMEM(tile_shape, jnp.float32),
    ] + scalar_bufs + (scalar_bufs + scalar_bufs[2:] if final else []) + [
        pltpu.VMEM(tile_shape, jnp.bfloat16),
        pltpu.VMEM(tile_shape, jnp.bfloat16),
        pltpu.VMEM((slots, rows, shape[2]), jnp.bfloat16),
    ] + [pltpu.VMEM((8, 128), jnp.float32)] * (4 if final else 2) + [
        pltpu.SemaphoreType.DMA((n_op,)),
        pltpu.SemaphoreType.DMA((n_op,)),
        pltpu.SemaphoreType.DMA((n_op,)),
        pltpu.SemaphoreType.DMA((n_op,)),
        pltpu.SemaphoreType.DMA((n_sec,)),
        pltpu.SemaphoreType.DMA((n_sec,)),
    ] + ([
        pltpu.SemaphoreType.DMA((n_op,)),
        pltpu.SemaphoreType.DMA((n_op,)),
        pltpu.SemaphoreType.DMA((n_sec,)),
        pltpu.SemaphoreType.DMA((n_sec,)),
    ] if final else []) + [
        pltpu.SemaphoreType.DMA((slots + n_op + 1,)),
        pltpu.SemaphoreType.DMA((slots + 1,)),
        pltpu.SemaphoreType.DMA((7,)),
    ]
    vmem = pl.BlockSpec(memory_space=pltpu.VMEM)
    anywhere = pl.BlockSpec(memory_space=pl.ANY)
    window, got = pl.pallas_call(
        functools.partial(step_kernel, n_sec, n_op, count, final),
        out_shape=(
            jax.ShapeDtypeStruct((slots, rows, shape[2]), jnp.bfloat16),
            jax.ShapeDtypeStruct(piece.shape, piece.dtype),
        ),
        in_specs=[vmem, vmem, vmem, anywhere],
        out_specs=(vmem, anywhere),
        scratch_shapes=scratch,
        compiler_params=pltpu.CompilerParams(
            collective_id=3 if final else 2, has_side_effects=True
        ),
    )(chunks, state_chunks, shift_chunks, piece)
    return window.reshape(slots // (n_op // shape[0]), shape[1], shape[2]), got


def sigma_part_kernel(partner_ref, win_ref, left_ref, right_ref, o_ref):
    b = pl.program_id(0)
    total = jnp.zeros(o_ref.shape[1:], jnp.float32)
    for t in range(left_ref.shape[0]):
        source = win_ref[partner_ref[t, b]]
        halfway = jnp.dot(left_ref[t, 0], source, preferred_element_type=jnp.float32)
        total = total + jnp.dot(halfway.astype(jnp.bfloat16), right_ref[t, 0],
                                preferred_element_type=jnp.float32)
    o_ref[0] = total


def sigma_part(window, left_ops, right_ops, partner):
    terms, sectors, m, _ = left_ops.shape
    op_spec = pl.BlockSpec((terms, 1, m, m), lambda b, p: (0, b, 0, 0))
    return pl.pallas_call(
        sigma_part_kernel,
        out_shape=jax.ShapeDtypeStruct((sectors, m, m), jnp.float32),
        grid_spec=pltpu.PrefetchScalarGridSpec(
            num_scalar_prefetch=1,
            grid=(sectors,),
            in_specs=[
                pl.BlockSpec(window.shape, lambda b, p: (0, 0, 0)),
                op_spec,
                op_spec,
            ],
            out_specs=pl.BlockSpec((1, m, m), lambda b, p: (b, 0, 0)),
        ),
        cost_estimate=pl.CostEstimate(
            flops=4 * terms * sectors * m * m * m,
            bytes_accessed=2 * left_ops.size * 2 + window.size * 2 + sectors * m * m * 4,
            transcendentals=0,
        ),
    )(partner, window, left_ops, right_ops)


def shifted(block, axis, distance):
    devices = range(lax.axis_size(axis))
    route = [((i - distance) % len(devices), i) for i in devices]
    return lax.ppermute(block, axis, route)


def per_device(state_start, left_ops, right_ops, shift, partner, kept):
    sector_local = state_start.shape[0]
    width = state_start.shape[1]
    count = float(sector_local * lax.axis_size("sec") * width * width)
    n_sec = lax.axis_size("sec")
    n_op = lax.axis_size("op")
    kept_prev = shifted(kept, "sec", 1)
    state = state_start
    window = padded(state, (("sec", 0),), sector_local)
    terms = left_ops.shape[0]
    cuts = [terms * k // ITERS for k in range(ITERS + 1)]
    left_pieces = []
    for iteration in range(ITERS):
        partial_sigma = sigma_part(window, left_ops, right_ops, partner)
        final = iteration == ITERS - 1
        window, got = step(
            partial_sigma, window, shift,
            left_ops[cuts[iteration] : cuts[iteration + 1]], count, final, n_sec, n_op,
        )
        left_pieces.append(got)
        state = window[sector_local : 2 * sector_local]
    state_prev = window[:sector_local]
    left_prev = jnp.concatenate(left_pieces, axis=0)
    columns = jnp.arange(width, dtype=jnp.int32)
    keep_mask = (columns[None, :] < kept_prev[:, None]).astype(jnp.bfloat16)
    kept_block = state_prev * keep_mask[:, None, :]
    out_scale = 1.0 / float(width) ** 0.5
    projected = jnp.einsum(
        "tbij,bjk->tbik", left_prev, kept_block, preferred_element_type=jnp.float32
    ).astype(jnp.bfloat16)
    kept_turned = jnp.broadcast_to(
        jnp.swapaxes(kept_block, 1, 2)[None], left_prev.shape
    )
    new_ops = (
        jnp.einsum("tbij,tbjk->tbik", kept_turned, projected, preferred_element_type=jnp.float32)
        * out_scale
    ).astype(jnp.bfloat16)
    return (state, new_ops)


def solution(mesh):
    in_specs = (
        P("sec", None, None),
        P("op", "sec", None, None),
        P("op", "sec", None, None),
        P("sec"),
        P("op", "sec"),
        P("sec"),
    )
    out_specs = (P("sec", None, None), P("op", "sec", None, None))
    return jax.shard_map(
        per_device, mesh=mesh, in_specs=in_specs, out_specs=out_specs, check_vma=False
    )
```

```python
import functools

import jax
import jax.numpy as jnp
from jax import lax
from jax.experimental import pallas as pl
from jax.experimental.pallas import tpu as pltpu
from jax.sharding import PartitionSpec as P

MESH = pl.DeviceIdType.MESH

ITERS = 4


step_size = 0.5


def padded(cells, sides, width):
    for axis, dim in sides:
        count = lax.axis_size(axis)
        head = lax.slice_in_dim(cells, 0, width, axis=dim)
        tail = lax.slice_in_dim(cells, cells.shape[dim] - width, cells.shape[dim], axis=dim)
        cells = jnp.concatenate(
            [
                lax.ppermute(tail, axis, [(i, (i + 1) % count) for i in range(count)]),
                cells,
                lax.ppermute(head, axis, [((i + 1) % count, i) for i in range(count)]),
            ],
            axis=dim,
        )
    return cells


def all_sum_kernel(n_sec, n_op, x_ref, o_ref, op_buf, sec_buf, mid, out_buf,
                   send_a, recv_a, send_b, recv_b, local_sem):
    me_sec = lax.axis_index("sec")
    me_op = lax.axis_index("op")
    barrier = pltpu.get_barrier_semaphore()
    for d in range(1, n_op):
        pl.semaphore_signal(barrier, 1, device_id=(me_sec, (me_op + d) % n_op),
                            device_id_type=MESH)
    for d in range(1, n_sec):
        pl.semaphore_signal(barrier, 1, device_id=((me_sec + d) % n_sec, me_op),
                            device_id_type=MESH)
    pl.semaphore_wait(barrier, n_op - 1 + n_sec - 1)

    def stage(n, me, src, buf, send, recv, peer_of):
        for d in range(1, n):
            pltpu.make_async_remote_copy(
                src_ref=src, dst_ref=buf.at[me], send_sem=send.at[d],
                recv_sem=recv.at[me], device_id=peer_of((me + d) % n),
                device_id_type=MESH).start()
        buf[me] = src[...]
        for d in range(1, n):
            slot = (me + n - d) % n
            pltpu.make_async_remote_copy(
                src_ref=src, dst_ref=buf.at[slot], send_sem=send.at[d],
                recv_sem=recv.at[slot], device_id=peer_of(slot),
                device_id_type=MESH).wait_recv()
        for d in range(1, n):
            pltpu.make_async_remote_copy(
                src_ref=src, dst_ref=buf.at[me], send_sem=send.at[d],
                recv_sem=recv.at[me], device_id=peer_of((me + d) % n),
                device_id_type=MESH).wait_send()
        total = buf[0]
        for j in range(1, n):
            total = total + buf[j]
        return total

    mid[...] = stage(n_op, me_op, x_ref, op_buf, send_a, recv_a,
                     lambda j: (me_sec, j))
    local = pltpu.make_async_copy(mid, out_buf, local_sem)
    local.start()
    local.wait()
    o_ref[...] = stage(n_sec, me_sec, out_buf, sec_buf, send_b, recv_b,
                       lambda j: (j, me_op))


def all_sum(values, n_sec, n_op):
    lane = lax.broadcasted_iota(jnp.int32, (8, 128), 1)
    tile = jnp.zeros((8, 128), jnp.float32)
    for k, v in enumerate(values):
        tile = jnp.where(lane == k, v, tile)
    tile_spec = pl.BlockSpec(memory_space=pltpu.VMEM)
    out = pl.pallas_call(
        functools.partial(all_sum_kernel, n_sec, n_op),
        out_shape=jax.ShapeDtypeStruct((8, 128), jnp.float32),
        in_specs=[tile_spec],
        out_specs=tile_spec,
        scratch_shapes=[
            pltpu.VMEM((n_op, 8, 128), jnp.float32),
            pltpu.VMEM((n_sec, 8, 128), jnp.float32),
            pltpu.VMEM((8, 128), jnp.float32),
            pltpu.VMEM((8, 128), jnp.float32),
            pltpu.SemaphoreType.DMA((n_op,)),
            pltpu.SemaphoreType.DMA((n_op,)),
            pltpu.SemaphoreType.DMA((n_sec,)),
            pltpu.SemaphoreType.DMA((n_sec,)),
            pltpu.SemaphoreType.DMA(()),
        ],
        compiler_params=pltpu.CompilerParams(collective_id=0, has_side_effects=True),
    )(tile)
    return tuple(out[0, k] for k in range(len(values)))


def sigma_sum_kernel(n_sec, n_op, x_ref, t_ref, o_ref, s_ref,
                     rs_buf, red, red_out, ag_buf, op_buf, sec_buf, mid, mid_out,
                     send_rs, recv_rs, send_ag, recv_ag, send_a, recv_a,
                     send_b, recv_b, local_sem):
    me_sec = lax.axis_index("sec")
    me_op = lax.axis_index("op")
    barrier = pltpu.get_barrier_semaphore()
    for d in range(1, n_op):
        pl.semaphore_signal(barrier, 1, device_id=(me_sec, (me_op + d) % n_op),
                            device_id_type=MESH)
    for d in range(1, n_sec):
        pl.semaphore_signal(barrier, 1, device_id=((me_sec + d) % n_sec, me_op),
                            device_id_type=MESH)
    pl.semaphore_wait(barrier, n_op - 1 + n_sec - 1)

    def op_peer(j):
        return (me_sec, j)

    def sec_peer(j):
        return (j, me_op)

    def total_of(v):
        return jnp.sum(jnp.sum(v, axis=1, keepdims=True), axis=0, keepdims=True)

    lane = lax.broadcasted_iota(jnp.int32, (8, 128), 1)
    own = st_ref[n_op + me_op].astype(jnp.float32)
    own_square = total_of(own * own)
    energy = sh_ref[me_op] * own_square
    for j in range(n_op):
        energy = energy + total_of(x_ref[j] * st_ref[n_op + j].astype(jnp.float32))
    t_ref[...] = jnp.where(lane == 0, energy, jnp.where(lane == 1, own_square, 0.0))
    settle(t_ref, t_out, local_sem.at[4])

    def rs_copy(d):
        j = (me_op + d) % n_op
        return pltpu.make_async_remote_copy(
            src_ref=x_ref.at[j], dst_ref=rs_buf.at[me_op], send_sem=send_rs.at[d],
            recv_sem=recv_rs.at[me_op], device_id=op_peer(j), device_id_type=MESH)

    def rs_recv(d):
        slot = (me_op + n_op - d) % n_op
        return pltpu.make_async_remote_copy(
            src_ref=x_ref.at[me_op], dst_ref=rs_buf.at[slot], send_sem=send_rs.at[d],
            recv_sem=recv_rs.at[slot], device_id=op_peer(slot), device_id_type=MESH)

    def gather_copy(n, me, src, buf, send, recv, peer_of, d):
        return pltpu.make_async_remote_copy(
            src_ref=src, dst_ref=buf.at[me], send_sem=send.at[d],
            recv_sem=recv.at[me], device_id=peer_of((me + d) % n), device_id_type=MESH)

    def gather_recv(n, me, src, buf, send, recv, peer_of, d):
        slot = (me + n - d) % n
        return pltpu.make_async_remote_copy(
            src_ref=src, dst_ref=buf.at[slot], send_sem=send.at[d],
            recv_sem=recv.at[slot], device_id=peer_of(slot), device_id_type=MESH)

    def ordered_sum(buf, n):
        total = buf[0]
        for j in range(1, n):
            total = total + buf[j]
        return total

    for d in range(1, n_op):
        rs_copy(d).start()
    a_args = (n_op, me_op, t_out, op_buf, send_a, recv_a, op_peer)
    for d in range(1, n_op):
        gather_copy(*a_args, d).start()
    rs_buf[me_op] = x_ref[me_op]
    op_buf[me_op] = t_ref[...]

    for d in range(1, n_op):
        gather_recv(*a_args, d).wait_recv()
    mid[...] = ordered_sum(op_buf, n_op)
    local = pltpu.make_async_copy(mid, mid_out, local_sem.at[0])
    local.start()
    local.wait()
    b_args = (n_sec, me_sec, mid_out, sec_buf, send_b, recv_b, sec_peer)
    for d in range(1, n_sec):
        gather_copy(*b_args, d).start()
    sec_buf[me_sec] = mid_out[...]

    for d in range(1, n_op):
        rs_recv(d).wait_recv()
    red[...] = ordered_sum(rs_buf, n_op)
    local = pltpu.make_async_copy(red, red_out, local_sem.at[1])
    local.start()
    local.wait()
    g_args = (n_op, me_op, red_out, ag_buf, send_ag, recv_ag, op_peer)
    for d in range(1, n_op):
        gather_copy(*g_args, d).start()
    ag_buf[me_op] = red_out[...]

    for d in range(1, n_sec):
        gather_recv(*b_args, d).wait_recv()
    s_ref[...] = ordered_sum(sec_buf, n_sec)
    for d in range(1, n_op):
        gather_recv(*g_args, d).wait_recv()
    o_ref[...] = ag_buf[...]

    for d in range(1, n_op):
        rs_copy(d).wait_send()
        gather_copy(*a_args, d).wait_send()
        gather_copy(*g_args, d).wait_send()
    for d in range(1, n_sec):
        gather_copy(*b_args, d).wait_send()


def sigma_sum(partial, values, n_sec, n_op):
    shape = partial.shape
    rows = shape[0] * shape[1] // n_op
    chunks = partial.reshape(n_op, rows, shape[2])
    lane = lax.broadcasted_iota(jnp.int32, (8, 128), 1)
    tile = jnp.zeros((8, 128), jnp.float32)
    for k, v in enumerate(values):
        tile = jnp.where(lane == k, v, tile)
    vmem = pl.BlockSpec(memory_space=pltpu.VMEM)
    total, sums = pl.pallas_call(
        functools.partial(sigma_sum_kernel, n_sec, n_op),
        out_shape=(
            jax.ShapeDtypeStruct(chunks.shape, jnp.float32),
            jax.ShapeDtypeStruct((8, 128), jnp.float32),
        ),
        in_specs=[vmem, vmem],
        out_specs=(vmem, vmem),
        scratch_shapes=[
            pltpu.VMEM(chunks.shape, jnp.float32),
            pltpu.VMEM((rows, shape[2]), jnp.float32),
            pltpu.VMEM((rows, shape[2]), jnp.float32),
            pltpu.VMEM(chunks.shape, jnp.float32),
            pltpu.VMEM((n_op, 8, 128), jnp.float32),
            pltpu.VMEM((n_sec, 8, 128), jnp.float32),
            pltpu.VMEM((8, 128), jnp.float32),
            pltpu.VMEM((8, 128), jnp.float32),
            pltpu.SemaphoreType.DMA((n_op,)),
            pltpu.SemaphoreType.DMA((n_op,)),
            pltpu.SemaphoreType.DMA((n_op,)),
            pltpu.SemaphoreType.DMA((n_op,)),
            pltpu.SemaphoreType.DMA((n_op,)),
            pltpu.SemaphoreType.DMA((n_op,)),
            pltpu.SemaphoreType.DMA((n_sec,)),
            pltpu.SemaphoreType.DMA((n_sec,)),
            pltpu.SemaphoreType.DMA((2,)),
        ],
        compiler_params=pltpu.CompilerParams(collective_id=1, has_side_effects=True),
    )(chunks, tile)
    return total.reshape(shape), tuple(sums[0, k] for k in range(len(values)))


def step_kernel(n_sec, n_op, count, final, x_ref, st_ref, sh_ref, piece_ref, *refs):
    if final:
        (win_ref, got_ref, t_ref, t_out, rs_buf, red, op_buf, sec_buf, mid, mid_out,
         op_buf2, sec_buf2, mid2, mid2_out, mid3, mid3_out, new_buf, new_out, win_buf,
         part, part_out, part2, part2_out,
         send_rs, recv_rs, send_a, recv_a, send_b, recv_b, send_a2, recv_a2, send_b2,
         recv_b2, send_w, recv_w, local_sem) = refs
    else:
        (win_ref, got_ref, t_ref, t_out, rs_buf, red, op_buf, sec_buf, mid, mid_out,
         new_buf, new_out, win_buf, part, part_out, send_rs, recv_rs, send_a, recv_a, send_b, recv_b, send_w,
         recv_w, local_sem) = refs
    me_sec = lax.axis_index("sec")
    me_op = lax.axis_index("op")
    prev_sec = (me_sec + n_sec - 1) % n_sec
    next_sec = (me_sec + 1) % n_sec
    barrier = pltpu.get_barrier_semaphore()
    row_len = 8 if n_sec % 8 == 0 else (2 if n_sec % 2 == 0 else n_sec)
    n_rows = n_sec // row_len
    row = me_sec // row_len
    col = me_sec % row_len
    greet = [(me_sec, (me_op + d) % n_op) for d in range(1, n_op)]
    greet += [(row * row_len + (col + d) % row_len, me_op) for d in range(1, row_len)]
    greet += [(((row + d) % n_rows) * row_len + col, me_op) for d in range(1, n_rows)]
    greet += [(side, j) for side in (prev_sec, next_sec) for j in range(n_op)]
    for peer in greet:
        pl.semaphore_signal(barrier, 1, device_id=peer, device_id_type=MESH)
    greeted = len(greet)

    def op_peer(j):
        return (me_sec, j)

    def sec_peer(j):
        return (j, me_op)

    def copy_to(src, dst, send, recv, peer):
        return pltpu.make_async_remote_copy(
            src_ref=src, dst_ref=dst, send_sem=send, recv_sem=recv,
            device_id=peer, device_id_type=MESH)

    def ordered_sum(buf, n):
        total = buf[0]
        for j in range(1, n):
            total = total + buf[j]
        return total

    def start_gather(n, me, src, buf, send, recv, peer_of):
        for d in range(1, n):
            copy_to(src, buf.at[me], send.at[d], recv.at[me], peer_of((me + d) % n)).start()
        buf[me] = src[...]

    def wait_gather(n, me, src, buf, send, recv, peer_of):
        for d in range(1, n):
            slot = (me + n - d) % n
            copy_to(src, buf.at[slot], send.at[d], recv.at[slot], peer_of(slot)).wait_recv()

    def drain_gather(n, me, src, buf, send, recv, peer_of):
        for d in range(1, n):
            copy_to(src, buf.at[me], send.at[d], recv.at[me], peer_of((me + d) % n)).wait_send()

    def settle(src, dst, sem):
        local = pltpu.make_async_copy(src, dst, sem)
        local.start()
        local.wait()

    def total_of(v):
        return jnp.sum(jnp.sum(v, axis=1, keepdims=True), axis=0, keepdims=True)

    lane = lax.broadcasted_iota(jnp.int32, (8, 128), 1)
    own = st_ref[n_op + me_op].astype(jnp.float32)
    own_square = total_of(own * own)
    energy = sh_ref[me_op] * own_square
    for j in range(n_op):
        energy = energy + total_of(x_ref[j] * st_ref[n_op + j].astype(jnp.float32))
    t_ref[...] = jnp.where(lane == 0, energy, jnp.where(lane == 1, own_square, 0.0))
    settle(t_ref, t_out, local_sem.at[4])

    def row_peer(c):
        return (row * row_len + c, me_op)

    def col_peer(r):
        return (r * row_len + col, me_op)

    def start_rows(src, buf, send, recv):
        for d in range(1, row_len):
            copy_to(src, buf.at[col], send.at[d], recv.at[col],
                    row_peer((col + d) % row_len)).start()
        buf[col] = src[...]

    def finish_sec(src, buf, send, recv, mid_sum, mid_out, sem):
        for d in range(1, row_len):
            slot = (col + row_len - d) % row_len
            copy_to(src, buf.at[slot], send.at[d], recv.at[slot], row_peer(slot)).wait_recv()
        mid_sum[...] = ordered_sum(buf, row_len)
        settle(mid_sum, mid_out, sem)
        for d in range(1, n_rows):
            copy_to(mid_out, buf.at[row_len + row], send.at[row_len + d],
                    recv.at[row_len + row], col_peer((row + d) % n_rows)).start()
        buf[row_len + row] = mid_out[...]
        for d in range(1, n_rows):
            slot = (row + n_rows - d) % n_rows
            copy_to(mid_out, buf.at[row_len + slot], send.at[row_len + d],
                    recv.at[row_len + slot], col_peer(slot)).wait_recv()
        total = buf[row_len]
        for r in range(1, n_rows):
            total = total + buf[row_len + r]
        return total

    def drain_sec(src, buf, send, recv, mid_out):
        for d in range(1, row_len):
            copy_to(src, buf.at[col], send.at[d], recv.at[col],
                    row_peer((col + d) % row_len)).wait_send()
        for d in range(1, n_rows):
            copy_to(mid_out, buf.at[row_len + row], send.at[row_len + d],
                    recv.at[row_len + row], col_peer((row + d) % n_rows)).wait_send()

    def rs_copy(d):
        j = (me_op + d) % n_op
        return copy_to(x_ref.at[j], rs_buf.at[me_op], send_rs.at[d], recv_rs.at[me_op], op_peer(j))

    pl.semaphore_wait(barrier, greeted)
    for d in range(1, n_op):
        rs_copy(d).start()
    a_args = (n_op, me_op, t_out, op_buf, send_a, recv_a, op_peer)
    start_gather(*a_args)
    rs_buf[me_op] = x_ref[me_op]

    operators = copy_to(piece_ref, got_ref, send_w.at[send_w.shape[0] - 1],
                        recv_w.at[recv_w.shape[0] - 1], (next_sec, me_op))
    operators.start()

    wait_gather(*a_args)
    mid[...] = ordered_sum(op_buf, n_op)
    settle(mid, mid_out, local_sem.at[0])
    start_rows(mid_out, sec_buf, send_b, recv_b)

    for d in range(1, n_op):
        slot = (me_op + n_op - d) % n_op
        copy_to(x_ref.at[me_op], rs_buf.at[slot], send_rs.at[d], recv_rs.at[slot],
                op_peer(slot)).wait_recv()
    red[...] = ordered_sum(rs_buf, n_op)

    sums = finish_sec(mid_out, sec_buf, send_b, recv_b, part, part_out, local_sem.at[5])
    energy_sum = sums[0:1, 0:1]
    norm_sum = sums[0:1, 1:2]
    state_wide = st_ref[n_op + me_op].astype(jnp.float32)
    sigma = red[...] + sh_ref[me_op] * state_wide
    updated = state_wide - step_size * (sigma - (energy_sum / norm_sum) * state_wide)
    factor = jnp.sqrt(count / norm_sum)
    if final:
        square = total_of(updated * updated)
    new_buf[...] = (updated * factor).astype(new_buf.dtype)
    settle(new_buf, new_out, local_sem.at[2])

    sides = ((next_sec, 0),) if final else ((prev_sec, 2 * n_op), (next_sec, 0))
    sent = 0
    for side, base in sides:
        for j in range(n_op):
            copy_to(new_out, win_buf.at[base + me_op], send_w.at[sent],
                    recv_w.at[base + me_op], (side, j)).start()
            sent += 1
    for d in range(1, n_op):
        j = (me_op + d) % n_op
        copy_to(new_out, win_buf.at[n_op + me_op], send_w.at[sent],
                recv_w.at[n_op + me_op], op_peer(j)).start()
        sent += 1
    win_buf[n_op + me_op] = new_out[...]

    if final:
        mid2[...] = jnp.where(lane == 0, square, 0.0)
        settle(mid2, mid2_out, local_sem.at[1])
        a2_args = (n_op, me_op, mid2_out, op_buf2, send_a2, recv_a2, op_peer)
        start_gather(*a2_args)
        wait_gather(*a2_args)
        mid3[...] = ordered_sum(op_buf2, n_op)
        settle(mid3, mid3_out, local_sem.at[3])
        start_rows(mid3_out, sec_buf2, send_b2, recv_b2)
        new_norm = finish_sec(mid3_out, sec_buf2, send_b2, recv_b2, part2, part2_out,
                              local_sem.at[6])[0:1, 0:1]
        rescale = jnp.sqrt(count / new_norm) / factor

    from_sides = ((prev_sec, 0),) if final else ((prev_sec, 0), (next_sec, 2 * n_op))
    for side, base in from_sides:
        for j in range(n_op):
            copy_to(new_out, win_buf.at[base + j], send_w.at[0], recv_w.at[base + j],
                    (side, j)).wait_recv()
    for d in range(1, n_op):
        slot = (me_op + n_op - d) % n_op
        copy_to(new_out, win_buf.at[n_op + slot], send_w.at[0], recv_w.at[n_op + slot],
                op_peer(slot)).wait_recv()
    if final:
        for k in range(win_ref.shape[0]):
            win_ref[k] = (win_buf[k].astype(jnp.float32) * rescale).astype(win_ref.dtype)
    else:
        win_ref[...] = win_buf[...]
    operators.wait_recv()

    operators.wait_send()
    for d in range(1, n_op):
        rs_copy(d).wait_send()
    drain_gather(*a_args)
    drain_sec(mid_out, sec_buf, send_b, recv_b, part_out)
    if final:
        drain_gather(*a2_args)
        drain_sec(mid3_out, sec_buf2, send_b2, recv_b2, part2_out)
    for k in range(sent):
        copy_to(new_out, win_buf.at[n_op + me_op], send_w.at[k], recv_w.at[n_op + me_op],
                op_peer((me_op + 1) % n_op)).wait_send()


def step(partial, window, shift, piece, count, final, n_sec, n_op):
    shape = partial.shape
    rows = shape[0] * shape[1] // n_op
    chunks = partial.reshape(n_op, rows, shape[2])
    state_chunks = window.reshape(-1, rows, shape[2])
    shift_chunks = jnp.repeat(shift, n_op // shape[0])[:, None, None]
    slots = (2 if final else 3) * n_op
    tile_shape = (rows, shape[2])
    scalar_bufs = [
        pltpu.VMEM((n_op, 8, 128), jnp.float32),
        pltpu.VMEM((n_sec, 8, 128), jnp.float32),
        pltpu.VMEM((8, 128), jnp.float32),
        pltpu.VMEM((8, 128), jnp.float32),
    ]
    scratch = [
        pltpu.VMEM((8, 128), jnp.float32),
        pltpu.VMEM((8, 128), jnp.float32),
        pltpu.VMEM(chunks.shape, jnp.float32),
        pltpu.VMEM(tile_shape, jnp.float32),
    ] + scalar_bufs + (scalar_bufs + scalar_bufs[2:] if final else []) + [
        pltpu.VMEM(tile_shape, jnp.bfloat16),
        pltpu.VMEM(tile_shape, jnp.bfloat16),
        pltpu.VMEM((slots, rows, shape[2]), jnp.bfloat16),
    ] + [pltpu.VMEM((8, 128), jnp.float32)] * (4 if final else 2) + [
        pltpu.SemaphoreType.DMA((n_op,)),
        pltpu.SemaphoreType.DMA((n_op,)),
        pltpu.SemaphoreType.DMA((n_op,)),
        pltpu.SemaphoreType.DMA((n_op,)),
        pltpu.SemaphoreType.DMA((n_sec,)),
        pltpu.SemaphoreType.DMA((n_sec,)),
    ] + ([
        pltpu.SemaphoreType.DMA((n_op,)),
        pltpu.SemaphoreType.DMA((n_op,)),
        pltpu.SemaphoreType.DMA((n_sec,)),
        pltpu.SemaphoreType.DMA((n_sec,)),
    ] if final else []) + [
        pltpu.SemaphoreType.DMA((slots + n_op + 1,)),
        pltpu.SemaphoreType.DMA((slots + 1,)),
        pltpu.SemaphoreType.DMA((7,)),
    ]
    vmem = pl.BlockSpec(memory_space=pltpu.VMEM)
    anywhere = pl.BlockSpec(memory_space=pl.ANY)
    window, got = pl.pallas_call(
        functools.partial(step_kernel, n_sec, n_op, count, final),
        out_shape=(
            jax.ShapeDtypeStruct((slots, rows, shape[2]), jnp.bfloat16),
            jax.ShapeDtypeStruct(piece.shape, piece.dtype),
        ),
        in_specs=[vmem, vmem, vmem, anywhere],
        out_specs=(vmem, anywhere),
        scratch_shapes=scratch,
        compiler_params=pltpu.CompilerParams(
            collective_id=3 if final else 2, has_side_effects=True
        ),
    )(chunks, state_chunks, shift_chunks, piece)
    return window.reshape(slots // (n_op // shape[0]), shape[1], shape[2]), got


def sigma_part_kernel(partner_ref, win_ref, left_ref, right_ref, o_ref):
    b = pl.program_id(0)
    total = jnp.zeros(o_ref.shape[1:], jnp.float32)
    for t in range(left_ref.shape[0]):
        source = win_ref[partner_ref[t, b]]
        halfway = jnp.dot(left_ref[t, 0], source, preferred_element_type=jnp.float32)
        total = total + jnp.dot(halfway.astype(jnp.bfloat16), right_ref[t, 0],
                                preferred_element_type=jnp.float32)
    o_ref[0] = total


def sigma_part(window, left_ops, right_ops, partner):
    terms, sectors, m, _ = left_ops.shape
    op_spec = pl.BlockSpec((terms, 1, m, m), lambda b, p: (0, b, 0, 0))
    return pl.pallas_call(
        sigma_part_kernel,
        out_shape=jax.ShapeDtypeStruct((sectors, m, m), jnp.float32),
        grid_spec=pltpu.PrefetchScalarGridSpec(
            num_scalar_prefetch=1,
            grid=(sectors,),
            in_specs=[
                pl.BlockSpec(window.shape, lambda b, p: (0, 0, 0)),
                op_spec,
                op_spec,
            ],
            out_specs=pl.BlockSpec((1, m, m), lambda b, p: (b, 0, 0)),
        ),
        cost_estimate=pl.CostEstimate(
            flops=4 * terms * sectors * m * m * m,
            bytes_accessed=2 * left_ops.size * 2 + window.size * 2 + sectors * m * m * 4,
            transcendentals=0,
        ),
    )(partner, window, left_ops, right_ops)


def shifted(block, axis, distance):
    devices = range(lax.axis_size(axis))
    route = [((i - distance) % len(devices), i) for i in devices]
    return lax.ppermute(block, axis, route)


def per_device(state_start, left_ops, right_ops, shift, partner, kept):
    sector_local = state_start.shape[0]
    width = state_start.shape[1]
    count = float(sector_local * lax.axis_size("sec") * width * width)
    n_sec = lax.axis_size("sec")
    n_op = lax.axis_size("op")
    kept_prev = shifted(kept, "sec", 1)
    state = state_start
    window = padded(state, (("sec", 0),), sector_local)
    terms = left_ops.shape[0]
    cuts = [terms * k // ITERS for k in range(ITERS + 1)]
    left_pieces = []
    for iteration in range(ITERS):
        partial_sigma = sigma_part(window, left_ops, right_ops, partner)
        final = iteration == ITERS - 1
        window, got = step(
            partial_sigma, window, shift,
            left_ops[cuts[iteration] : cuts[iteration + 1]], count, final, n_sec, n_op,
        )
        left_pieces.append(got)
        state = window[sector_local : 2 * sector_local]
    state_prev = window[:sector_local]
    left_prev = jnp.concatenate(left_pieces, axis=0)
    columns = jnp.arange(width, dtype=jnp.int32)
    keep_mask = (columns[None, :] < kept_prev[:, None]).astype(jnp.bfloat16)
    kept_block = state_prev * keep_mask[:, None, :]
    out_scale = 1.0 / float(width) ** 0.5
    projected = jnp.einsum(
        "tbij,bjk->tbik", left_prev, kept_block, preferred_element_type=jnp.float32
    ).astype(jnp.bfloat16)
    kept_turned = jnp.broadcast_to(
        jnp.swapaxes(kept_block, 1, 2)[None], left_prev.shape
    )
    new_ops = (
        jnp.einsum("tbij,tbjk->tbik", kept_turned, projected, preferred_element_type=jnp.float32)
        * out_scale
    ).astype(jnp.bfloat16)
    return (state, new_ops)


def solution(mesh):
    in_specs = (
        P("sec", None, None),
        P("op", "sec", None, None),
        P("op", "sec", None, None),
        P("sec"),
        P("op", "sec"),
        P("sec"),
    )
    out_specs = (P("sec", None, None), P("op", "sec", None, None))
    return jax.shard_map(
        per_device, mesh=mesh, in_specs=in_specs, out_specs=out_specs, check_vma=False
    )
```

```python
import functools

import jax
import jax.numpy as jnp
from jax import lax
from jax.experimental import pallas as pl
from jax.experimental.pallas import tpu as pltpu
from jax.sharding import PartitionSpec as P

MESH = pl.DeviceIdType.MESH

ITERS = 4


step_size = 0.5


def padded(cells, sides, width):
    for axis, dim in sides:
        count = lax.axis_size(axis)
        head = lax.slice_in_dim(cells, 0, width, axis=dim)
        tail = lax.slice_in_dim(cells, cells.shape[dim] - width, cells.shape[dim], axis=dim)
        cells = jnp.concatenate(
            [
                lax.ppermute(tail, axis, [(i, (i + 1) % count) for i in range(count)]),
                cells,
                lax.ppermute(head, axis, [((i + 1) % count, i) for i in range(count)]),
            ],
            axis=dim,
        )
    return cells


def all_sum_kernel(n_sec, n_op, x_ref, o_ref, op_buf, sec_buf, mid, out_buf,
                   send_a, recv_a, send_b, recv_b, local_sem):
    me_sec = lax.axis_index("sec")
    me_op = lax.axis_index("op")
    barrier = pltpu.get_barrier_semaphore()
    for d in range(1, n_op):
        pl.semaphore_signal(barrier, 1, device_id=(me_sec, (me_op + d) % n_op),
                            device_id_type=MESH)
    for d in range(1, n_sec):
        pl.semaphore_signal(barrier, 1, device_id=((me_sec + d) % n_sec, me_op),
                            device_id_type=MESH)
    pl.semaphore_wait(barrier, n_op - 1 + n_sec - 1)

    def stage(n, me, src, buf, send, recv, peer_of):
        for d in range(1, n):
            pltpu.make_async_remote_copy(
                src_ref=src, dst_ref=buf.at[me], send_sem=send.at[d],
                recv_sem=recv.at[me], device_id=peer_of((me + d) % n),
                device_id_type=MESH).start()
        buf[me] = src[...]
        for d in range(1, n):
            slot = (me + n - d) % n
            pltpu.make_async_remote_copy(
                src_ref=src, dst_ref=buf.at[slot], send_sem=send.at[d],
                recv_sem=recv.at[slot], device_id=peer_of(slot),
                device_id_type=MESH).wait_recv()
        for d in range(1, n):
            pltpu.make_async_remote_copy(
                src_ref=src, dst_ref=buf.at[me], send_sem=send.at[d],
                recv_sem=recv.at[me], device_id=peer_of((me + d) % n),
                device_id_type=MESH).wait_send()
        total = buf[0]
        for j in range(1, n):
            total = total + buf[j]
        return total

    mid[...] = stage(n_op, me_op, x_ref, op_buf, send_a, recv_a,
                     lambda j: (me_sec, j))
    local = pltpu.make_async_copy(mid, out_buf, local_sem)
    local.start()
    local.wait()
    o_ref[...] = stage(n_sec, me_sec, out_buf, sec_buf, send_b, recv_b,
                       lambda j: (j, me_op))


def all_sum(values, n_sec, n_op):
    lane = lax.broadcasted_iota(jnp.int32, (8, 128), 1)
    tile = jnp.zeros((8, 128), jnp.float32)
    for k, v in enumerate(values):
        tile = jnp.where(lane == k, v, tile)
    tile_spec = pl.BlockSpec(memory_space=pltpu.VMEM)
    out = pl.pallas_call(
        functools.partial(all_sum_kernel, n_sec, n_op),
        out_shape=jax.ShapeDtypeStruct((8, 128), jnp.float32),
        in_specs=[tile_spec],
        out_specs=tile_spec,
        scratch_shapes=[
            pltpu.VMEM((n_op, 8, 128), jnp.float32),
            pltpu.VMEM((n_sec, 8, 128), jnp.float32),
            pltpu.VMEM((8, 128), jnp.float32),
            pltpu.VMEM((8, 128), jnp.float32),
            pltpu.SemaphoreType.DMA((n_op,)),
            pltpu.SemaphoreType.DMA((n_op,)),
            pltpu.SemaphoreType.DMA((n_sec,)),
            pltpu.SemaphoreType.DMA((n_sec,)),
            pltpu.SemaphoreType.DMA(()),
        ],
        compiler_params=pltpu.CompilerParams(collective_id=0, has_side_effects=True),
    )(tile)
    return tuple(out[0, k] for k in range(len(values)))


def sigma_sum_kernel(n_sec, n_op, x_ref, t_ref, o_ref, s_ref,
                     rs_buf, red, red_out, ag_buf, op_buf, sec_buf, mid, mid_out,
                     send_rs, recv_rs, send_ag, recv_ag, send_a, recv_a,
                     send_b, recv_b, local_sem):
    me_sec = lax.axis_index("sec")
    me_op = lax.axis_index("op")
    barrier = pltpu.get_barrier_semaphore()
    for d in range(1, n_op):
        pl.semaphore_signal(barrier, 1, device_id=(me_sec, (me_op + d) % n_op),
                            device_id_type=MESH)
    for d in range(1, n_sec):
        pl.semaphore_signal(barrier, 1, device_id=((me_sec + d) % n_sec, me_op),
                            device_id_type=MESH)
    pl.semaphore_wait(barrier, n_op - 1 + n_sec - 1)

    def op_peer(j):
        return (me_sec, j)

    def sec_peer(j):
        return (j, me_op)

    def total_of(v):
        return jnp.sum(jnp.sum(v, axis=1, keepdims=True), axis=0, keepdims=True)

    lane = lax.broadcasted_iota(jnp.int32, (8, 128), 1)
    own = st_ref[n_op + me_op].astype(jnp.float32)
    own_square = total_of(own * own)
    energy = sh_ref[me_op] * own_square
    for j in range(n_op):
        energy = energy + total_of(x_ref[j] * st_ref[n_op + j].astype(jnp.float32))
    t_ref[...] = jnp.where(lane == 0, energy, jnp.where(lane == 1, own_square, 0.0))
    settle(t_ref, t_out, local_sem.at[4])

    def rs_copy(d):
        j = (me_op + d) % n_op
        return pltpu.make_async_remote_copy(
            src_ref=x_ref.at[j], dst_ref=rs_buf.at[me_op], send_sem=send_rs.at[d],
            recv_sem=recv_rs.at[me_op], device_id=op_peer(j), device_id_type=MESH)

    def rs_recv(d):
        slot = (me_op + n_op - d) % n_op
        return pltpu.make_async_remote_copy(
            src_ref=x_ref.at[me_op], dst_ref=rs_buf.at[slot], send_sem=send_rs.at[d],
            recv_sem=recv_rs.at[slot], device_id=op_peer(slot), device_id_type=MESH)

    def gather_copy(n, me, src, buf, send, recv, peer_of, d):
        return pltpu.make_async_remote_copy(
            src_ref=src, dst_ref=buf.at[me], send_sem=send.at[d],
            recv_sem=recv.at[me], device_id=peer_of((me + d) % n), device_id_type=MESH)

    def gather_recv(n, me, src, buf, send, recv, peer_of, d):
        slot = (me + n - d) % n
        return pltpu.make_async_remote_copy(
            src_ref=src, dst_ref=buf.at[slot], send_sem=send.at[d],
            recv_sem=recv.at[slot], device_id=peer_of(slot), device_id_type=MESH)

    def ordered_sum(buf, n):
        total = buf[0]
        for j in range(1, n):
            total = total + buf[j]
        return total

    for d in range(1, n_op):
        rs_copy(d).start()
    a_args = (n_op, me_op, t_out, op_buf, send_a, recv_a, op_peer)
    for d in range(1, n_op):
        gather_copy(*a_args, d).start()
    rs_buf[me_op] = x_ref[me_op]
    op_buf[me_op] = t_ref[...]

    for d in range(1, n_op):
        gather_recv(*a_args, d).wait_recv()
    mid[...] = ordered_sum(op_buf, n_op)
    local = pltpu.make_async_copy(mid, mid_out, local_sem.at[0])
    local.start()
    local.wait()
    b_args = (n_sec, me_sec, mid_out, sec_buf, send_b, recv_b, sec_peer)
    for d in range(1, n_sec):
        gather_copy(*b_args, d).start()
    sec_buf[me_sec] = mid_out[...]

    for d in range(1, n_op):
        rs_recv(d).wait_recv()
    red[...] = ordered_sum(rs_buf, n_op)
    local = pltpu.make_async_copy(red, red_out, local_sem.at[1])
    local.start()
    local.wait()
    g_args = (n_op, me_op, red_out, ag_buf, send_ag, recv_ag, op_peer)
    for d in range(1, n_op):
        gather_copy(*g_args, d).start()
    ag_buf[me_op] = red_out[...]

    for d in range(1, n_sec):
        gather_recv(*b_args, d).wait_recv()
    s_ref[...] = ordered_sum(sec_buf, n_sec)
    for d in range(1, n_op):
        gather_recv(*g_args, d).wait_recv()
    o_ref[...] = ag_buf[...]

    for d in range(1, n_op):
        rs_copy(d).wait_send()
        gather_copy(*a_args, d).wait_send()
        gather_copy(*g_args, d).wait_send()
    for d in range(1, n_sec):
        gather_copy(*b_args, d).wait_send()


def sigma_sum(partial, values, n_sec, n_op):
    shape = partial.shape
    rows = shape[0] * shape[1] // n_op
    chunks = partial.reshape(n_op, rows, shape[2])
    lane = lax.broadcasted_iota(jnp.int32, (8, 128), 1)
    tile = jnp.zeros((8, 128), jnp.float32)
    for k, v in enumerate(values):
        tile = jnp.where(lane == k, v, tile)
    vmem = pl.BlockSpec(memory_space=pltpu.VMEM)
    total, sums = pl.pallas_call(
        functools.partial(sigma_sum_kernel, n_sec, n_op),
        out_shape=(
            jax.ShapeDtypeStruct(chunks.shape, jnp.float32),
            jax.ShapeDtypeStruct((8, 128), jnp.float32),
        ),
        in_specs=[vmem, vmem],
        out_specs=(vmem, vmem),
        scratch_shapes=[
            pltpu.VMEM(chunks.shape, jnp.float32),
            pltpu.VMEM((rows, shape[2]), jnp.float32),
            pltpu.VMEM((rows, shape[2]), jnp.float32),
            pltpu.VMEM(chunks.shape, jnp.float32),
            pltpu.VMEM((n_op, 8, 128), jnp.float32),
            pltpu.VMEM((n_sec, 8, 128), jnp.float32),
            pltpu.VMEM((8, 128), jnp.float32),
            pltpu.VMEM((8, 128), jnp.float32),
            pltpu.SemaphoreType.DMA((n_op,)),
            pltpu.SemaphoreType.DMA((n_op,)),
            pltpu.SemaphoreType.DMA((n_op,)),
            pltpu.SemaphoreType.DMA((n_op,)),
            pltpu.SemaphoreType.DMA((n_op,)),
            pltpu.SemaphoreType.DMA((n_op,)),
            pltpu.SemaphoreType.DMA((n_sec,)),
            pltpu.SemaphoreType.DMA((n_sec,)),
            pltpu.SemaphoreType.DMA((2,)),
        ],
        compiler_params=pltpu.CompilerParams(collective_id=1, has_side_effects=True),
    )(chunks, tile)
    return total.reshape(shape), tuple(sums[0, k] for k in range(len(values)))


def step_kernel(n_sec, n_op, count, final, x_ref, st_ref, sh_ref, piece_ref, *refs):
    if final:
        (win_ref, got_ref, t_ref, t_out, rs_buf, red, op_buf, sec_buf, mid, mid_out,
         op_buf2, sec_buf2, mid2, mid2_out, mid3, mid3_out, new_buf, new_out, win_buf,
         part, part_out, part2, part2_out,
         send_rs, recv_rs, send_a, recv_a, send_b, recv_b, send_a2, recv_a2, send_b2,
         recv_b2, send_w, recv_w, local_sem) = refs
    else:
        (win_ref, got_ref, t_ref, t_out, rs_buf, red, op_buf, sec_buf, mid, mid_out,
         new_buf, new_out, win_buf, part, part_out, send_rs, recv_rs, send_a, recv_a, send_b, recv_b, send_w,
         recv_w, local_sem) = refs
    me_sec = lax.axis_index("sec")
    me_op = lax.axis_index("op")
    prev_sec = (me_sec + n_sec - 1) % n_sec
    next_sec = (me_sec + 1) % n_sec
    barrier = pltpu.get_barrier_semaphore()
    row_len = 8 if n_sec % 8 == 0 else (2 if n_sec % 2 == 0 else n_sec)
    n_rows = n_sec // row_len
    row = me_sec // row_len
    col = me_sec % row_len
    greet = [(me_sec, (me_op + d) % n_op) for d in range(1, n_op)]
    greet += [(row * row_len + (col + d) % row_len, me_op) for d in range(1, row_len)]
    greet += [(((row + d) % n_rows) * row_len + col, me_op) for d in range(1, n_rows)]
    greet += [(side, j) for side in (prev_sec, next_sec) for j in range(n_op)]
    for peer in greet:
        pl.semaphore_signal(barrier, 1, device_id=peer, device_id_type=MESH)
    greeted = len(greet)

    def op_peer(j):
        return (me_sec, j)

    def sec_peer(j):
        return (j, me_op)

    def copy_to(src, dst, send, recv, peer):
        return pltpu.make_async_remote_copy(
            src_ref=src, dst_ref=dst, send_sem=send, recv_sem=recv,
            device_id=peer, device_id_type=MESH)

    def ordered_sum(buf, n):
        total = buf[0]
        for j in range(1, n):
            total = total + buf[j]
        return total

    def start_gather(n, me, src, buf, send, recv, peer_of):
        for d in range(1, n):
            copy_to(src, buf.at[me], send.at[d], recv.at[me], peer_of((me + d) % n)).start()
        buf[me] = src[...]

    def wait_gather(n, me, src, buf, send, recv, peer_of):
        for d in range(1, n):
            slot = (me + n - d) % n
            copy_to(src, buf.at[slot], send.at[d], recv.at[slot], peer_of(slot)).wait_recv()

    def drain_gather(n, me, src, buf, send, recv, peer_of):
        for d in range(1, n):
            copy_to(src, buf.at[me], send.at[d], recv.at[me], peer_of((me + d) % n)).wait_send()

    def settle(src, dst, sem):
        local = pltpu.make_async_copy(src, dst, sem)
        local.start()
        local.wait()

    def total_of(v):
        return jnp.sum(jnp.sum(v, axis=1, keepdims=True), axis=0, keepdims=True)

    lane = lax.broadcasted_iota(jnp.int32, (8, 128), 1)
    own = st_ref[n_op + me_op].astype(jnp.float32)
    own_square = total_of(own * own)
    energy = sh_ref[me_op] * own_square
    for j in range(n_op):
        energy = energy + total_of(x_ref[j] * st_ref[n_op + j].astype(jnp.float32))
    t_ref[...] = jnp.where(lane == 0, energy, jnp.where(lane == 1, own_square, 0.0))
    settle(t_ref, t_out, local_sem.at[4])

    def row_peer(c):
        return (row * row_len + c, me_op)

    def col_peer(r):
        return (r * row_len + col, me_op)

    def start_rows(src, buf, send, recv):
        for d in range(1, row_len):
            copy_to(src, buf.at[col], send.at[d], recv.at[col],
                    row_peer((col + d) % row_len)).start()
        buf[col] = src[...]

    def finish_sec(src, buf, send, recv, mid_sum, mid_out, sem):
        for d in range(1, row_len):
            slot = (col + row_len - d) % row_len
            copy_to(src, buf.at[slot], send.at[d], recv.at[slot], row_peer(slot)).wait_recv()
        mid_sum[...] = ordered_sum(buf, row_len)
        settle(mid_sum, mid_out, sem)
        for d in range(1, n_rows):
            copy_to(mid_out, buf.at[row_len + row], send.at[row_len + d],
                    recv.at[row_len + row], col_peer((row + d) % n_rows)).start()
        buf[row_len + row] = mid_out[...]
        for d in range(1, n_rows):
            slot = (row + n_rows - d) % n_rows
            copy_to(mid_out, buf.at[row_len + slot], send.at[row_len + d],
                    recv.at[row_len + slot], col_peer(slot)).wait_recv()
        total = buf[row_len]
        for r in range(1, n_rows):
            total = total + buf[row_len + r]
        return total

    def drain_sec(src, buf, send, recv, mid_out):
        for d in range(1, row_len):
            copy_to(src, buf.at[col], send.at[d], recv.at[col],
                    row_peer((col + d) % row_len)).wait_send()
        for d in range(1, n_rows):
            copy_to(mid_out, buf.at[row_len + row], send.at[row_len + d],
                    recv.at[row_len + row], col_peer((row + d) % n_rows)).wait_send()

    def rs_copy(d):
        j = (me_op + d) % n_op
        return copy_to(x_ref.at[j], rs_buf.at[me_op], send_rs.at[d], recv_rs.at[me_op], op_peer(j))

    pl.semaphore_wait(barrier, greeted)
    operators = copy_to(piece_ref, got_ref, send_w.at[send_w.shape[0] - 1],
                        recv_w.at[recv_w.shape[0] - 1], (next_sec, me_op))
    operators.start()
    for d in range(1, n_op):
        rs_copy(d).start()
    a_args = (n_op, me_op, t_out, op_buf, send_a, recv_a, op_peer)
    start_gather(*a_args)
    rs_buf[me_op] = x_ref[me_op]


    wait_gather(*a_args)
    mid[...] = ordered_sum(op_buf, n_op)
    settle(mid, mid_out, local_sem.at[0])
    start_rows(mid_out, sec_buf, send_b, recv_b)

    for d in range(1, n_op):
        slot = (me_op + n_op - d) % n_op
        copy_to(x_ref.at[me_op], rs_buf.at[slot], send_rs.at[d], recv_rs.at[slot],
                op_peer(slot)).wait_recv()
    red[...] = ordered_sum(rs_buf, n_op)

    sums = finish_sec(mid_out, sec_buf, send_b, recv_b, part, part_out, local_sem.at[5])
    energy_sum = sums[0:1, 0:1]
    norm_sum = sums[0:1, 1:2]
    state_wide = st_ref[n_op + me_op].astype(jnp.float32)
    sigma = red[...] + sh_ref[me_op] * state_wide
    updated = state_wide - step_size * (sigma - (energy_sum / norm_sum) * state_wide)
    factor = jnp.sqrt(count / norm_sum)
    if final:
        square = total_of(updated * updated)
    new_buf[...] = (updated * factor).astype(new_buf.dtype)
    settle(new_buf, new_out, local_sem.at[2])

    sides = ((next_sec, 0),) if final else ((next_sec, 0), (prev_sec, 2 * n_op))
    sent = 0
    for side, base in sides:
        for j in range(n_op):
            copy_to(new_out, win_buf.at[base + me_op], send_w.at[sent],
                    recv_w.at[base + me_op], (side, j)).start()
            sent += 1
    for d in range(1, n_op):
        j = (me_op + d) % n_op
        copy_to(new_out, win_buf.at[n_op + me_op], send_w.at[sent],
                recv_w.at[n_op + me_op], op_peer(j)).start()
        sent += 1
    win_buf[n_op + me_op] = new_out[...]

    if final:
        mid2[...] = jnp.where(lane == 0, square, 0.0)
        settle(mid2, mid2_out, local_sem.at[1])
        a2_args = (n_op, me_op, mid2_out, op_buf2, send_a2, recv_a2, op_peer)
        start_gather(*a2_args)
        wait_gather(*a2_args)
        mid3[...] = ordered_sum(op_buf2, n_op)
        settle(mid3, mid3_out, local_sem.at[3])
        start_rows(mid3_out, sec_buf2, send_b2, recv_b2)
        new_norm = finish_sec(mid3_out, sec_buf2, send_b2, recv_b2, part2, part2_out,
                              local_sem.at[6])[0:1, 0:1]
        rescale = jnp.sqrt(count / new_norm) / factor

    from_sides = ((prev_sec, 0),) if final else ((prev_sec, 0), (next_sec, 2 * n_op))
    for side, base in from_sides:
        for j in range(n_op):
            copy_to(new_out, win_buf.at[base + j], send_w.at[0], recv_w.at[base + j],
                    (side, j)).wait_recv()
    for d in range(1, n_op):
        slot = (me_op + n_op - d) % n_op
        copy_to(new_out, win_buf.at[n_op + slot], send_w.at[0], recv_w.at[n_op + slot],
                op_peer(slot)).wait_recv()
    if final:
        for k in range(win_ref.shape[0]):
            win_ref[k] = (win_buf[k].astype(jnp.float32) * rescale).astype(win_ref.dtype)
    else:
        win_ref[...] = win_buf[...]
    operators.wait_recv()

    operators.wait_send()
    for d in range(1, n_op):
        rs_copy(d).wait_send()
    drain_gather(*a_args)
    drain_sec(mid_out, sec_buf, send_b, recv_b, part_out)
    if final:
        drain_gather(*a2_args)
        drain_sec(mid3_out, sec_buf2, send_b2, recv_b2, part2_out)
    for k in range(sent):
        copy_to(new_out, win_buf.at[n_op + me_op], send_w.at[k], recv_w.at[n_op + me_op],
                op_peer((me_op + 1) % n_op)).wait_send()


def step(partial, window, shift, piece, count, final, n_sec, n_op):
    shape = partial.shape
    rows = shape[0] * shape[1] // n_op
    chunks = partial.reshape(n_op, rows, shape[2])
    state_chunks = window.reshape(-1, rows, shape[2])
    shift_chunks = jnp.repeat(shift, n_op // shape[0])[:, None, None]
    slots = (2 if final else 3) * n_op
    tile_shape = (rows, shape[2])
    scalar_bufs = [
        pltpu.VMEM((n_op, 8, 128), jnp.float32),
        pltpu.VMEM((n_sec, 8, 128), jnp.float32),
        pltpu.VMEM((8, 128), jnp.float32),
        pltpu.VMEM((8, 128), jnp.float32),
    ]
    scratch = [
        pltpu.VMEM((8, 128), jnp.float32),
        pltpu.VMEM((8, 128), jnp.float32),
        pltpu.VMEM(chunks.shape, jnp.float32),
        pltpu.VMEM(tile_shape, jnp.float32),
    ] + scalar_bufs + (scalar_bufs + scalar_bufs[2:] if final else []) + [
        pltpu.VMEM(tile_shape, jnp.bfloat16),
        pltpu.VMEM(tile_shape, jnp.bfloat16),
        pltpu.VMEM((slots, rows, shape[2]), jnp.bfloat16),
    ] + [pltpu.VMEM((8, 128), jnp.float32)] * (4 if final else 2) + [
        pltpu.SemaphoreType.DMA((n_op,)),
        pltpu.SemaphoreType.DMA((n_op,)),
        pltpu.SemaphoreType.DMA((n_op,)),
        pltpu.SemaphoreType.DMA((n_op,)),
        pltpu.SemaphoreType.DMA((n_sec,)),
        pltpu.SemaphoreType.DMA((n_sec,)),
    ] + ([
        pltpu.SemaphoreType.DMA((n_op,)),
        pltpu.SemaphoreType.DMA((n_op,)),
        pltpu.SemaphoreType.DMA((n_sec,)),
        pltpu.SemaphoreType.DMA((n_sec,)),
    ] if final else []) + [
        pltpu.SemaphoreType.DMA((slots + n_op + 1,)),
        pltpu.SemaphoreType.DMA((slots + 1,)),
        pltpu.SemaphoreType.DMA((7,)),
    ]
    vmem = pl.BlockSpec(memory_space=pltpu.VMEM)
    anywhere = pl.BlockSpec(memory_space=pl.ANY)
    window, got = pl.pallas_call(
        functools.partial(step_kernel, n_sec, n_op, count, final),
        out_shape=(
            jax.ShapeDtypeStruct((slots, rows, shape[2]), jnp.bfloat16),
            jax.ShapeDtypeStruct(piece.shape, piece.dtype),
        ),
        in_specs=[vmem, vmem, vmem, anywhere],
        out_specs=(vmem, anywhere),
        scratch_shapes=scratch,
        compiler_params=pltpu.CompilerParams(
            collective_id=3 if final else 2, has_side_effects=True
        ),
    )(chunks, state_chunks, shift_chunks, piece)
    return window.reshape(slots // (n_op // shape[0]), shape[1], shape[2]), got


def sigma_part_kernel(partner_ref, win_ref, left_ref, right_ref, o_ref):
    b = pl.program_id(0)
    total = jnp.zeros(o_ref.shape[1:], jnp.float32)
    for t in range(left_ref.shape[0]):
        source = win_ref[partner_ref[t, b]]
        halfway = jnp.dot(left_ref[t, 0], source, preferred_element_type=jnp.float32)
        total = total + jnp.dot(halfway.astype(jnp.bfloat16), right_ref[t, 0],
                                preferred_element_type=jnp.float32)
    o_ref[0] = total


def sigma_part(window, left_ops, right_ops, partner):
    terms, sectors, m, _ = left_ops.shape
    op_spec = pl.BlockSpec((terms, 1, m, m), lambda b, p: (0, b, 0, 0))
    return pl.pallas_call(
        sigma_part_kernel,
        out_shape=jax.ShapeDtypeStruct((sectors, m, m), jnp.float32),
        grid_spec=pltpu.PrefetchScalarGridSpec(
            num_scalar_prefetch=1,
            grid=(sectors,),
            in_specs=[
                pl.BlockSpec(window.shape, lambda b, p: (0, 0, 0)),
                op_spec,
                op_spec,
            ],
            out_specs=pl.BlockSpec((1, m, m), lambda b, p: (b, 0, 0)),
        ),
        cost_estimate=pl.CostEstimate(
            flops=4 * terms * sectors * m * m * m,
            bytes_accessed=2 * left_ops.size * 2 + window.size * 2 + sectors * m * m * 4,
            transcendentals=0,
        ),
    )(partner, window, left_ops, right_ops)


def shifted(block, axis, distance):
    devices = range(lax.axis_size(axis))
    route = [((i - distance) % len(devices), i) for i in devices]
    return lax.ppermute(block, axis, route)


def per_device(state_start, left_ops, right_ops, shift, partner, kept):
    sector_local = state_start.shape[0]
    width = state_start.shape[1]
    count = float(sector_local * lax.axis_size("sec") * width * width)
    n_sec = lax.axis_size("sec")
    n_op = lax.axis_size("op")
    kept_prev = shifted(kept, "sec", 1)
    state = state_start
    window = padded(state, (("sec", 0),), sector_local)
    terms = left_ops.shape[0]
    cuts = [terms * k // ITERS for k in range(ITERS + 1)]
    left_pieces = []
    for iteration in range(ITERS):
        partial_sigma = sigma_part(window, left_ops, right_ops, partner)
        final = iteration == ITERS - 1
        window, got = step(
            partial_sigma, window, shift,
            left_ops[cuts[iteration] : cuts[iteration + 1]], count, final, n_sec, n_op,
        )
        left_pieces.append(got)
        state = window[sector_local : 2 * sector_local]
    state_prev = window[:sector_local]
    left_prev = jnp.concatenate(left_pieces, axis=0)
    columns = jnp.arange(width, dtype=jnp.int32)
    keep_mask = (columns[None, :] < kept_prev[:, None]).astype(jnp.bfloat16)
    kept_block = state_prev * keep_mask[:, None, :]
    out_scale = 1.0 / float(width) ** 0.5
    projected = jnp.einsum(
        "tbij,bjk->tbik", left_prev, kept_block, preferred_element_type=jnp.float32
    ).astype(jnp.bfloat16)
    kept_turned = jnp.broadcast_to(
        jnp.swapaxes(kept_block, 1, 2)[None], left_prev.shape
    )
    new_ops = (
        jnp.einsum("tbij,tbjk->tbik", kept_turned, projected, preferred_element_type=jnp.float32)
        * out_scale
    ).astype(jnp.bfloat16)
    return (state, new_ops)


def solution(mesh):
    in_specs = (
        P("sec", None, None),
        P("op", "sec", None, None),
        P("op", "sec", None, None),
        P("sec"),
        P("op", "sec"),
        P("sec"),
    )
    out_specs = (P("sec", None, None), P("op", "sec", None, None))
    return jax.shard_map(
        per_device, mesh=mesh, in_specs=in_specs, out_specs=out_specs, check_vma=False
    )
```
